32 devices in a mesh: replica: 16 (over z, x, core), group: 2 (over y).
Axes of the slice: x: 2, y: 2, z: 4, core: 2. Of those that a mesh axis runs over, the one named last changes fastest.
Arguments:
- layer_input: bfloat16 [16384, 1024], P(('replica', 'group')), may hold values from -6 to 6
- document_numbers: int32 [16384], P(('replica', 'group')), may hold values from 0 to 63, never falling along the last dimension, each value on 1 to 1024 neighbouring positions
- routes: int32 [16384, 8], P(('replica', 'group')), may hold values from 0 to 15, all different within a row; in each aligned block of 512 rows (0 to 511, 512 to 1023, ...) at most 384 rows name the same one
- norm_attn: bfloat16 [1024], P('group'), may hold values from 0.5 to 1.5
- w_query: bfloat16 [1024, 1024], P('group'), may hold values from -0.375 to 0.375
- key_weight: bfloat16 [1024, 512], P('group'), may hold values from -0.1875 to 0.1875
- value_weight: bfloat16 [1024, 512], P('group'), may hold values from -0.1875 to 0.1875
- w_out: bfloat16 [1024, 1024], P('group'), may hold values from -0.75 to 0.75
- norm_moe: bfloat16 [1024], P('group'), may hold values from 0.5 to 1.5
- w_router: bfloat16 [1024, 16], P('group'), may hold values from -0.09375 to 0.09375
- expert_in: bfloat16 [16, 1024, 1024], P('group'), may hold values from -0.1875 to 0.1875
- expert_out: bfloat16 [16, 512, 1024], P('group'), may hold values from -1 to 1
- cotangent: bfloat16 [16384, 1024], P(('replica', 'group')), may hold values from -6 to 6
Outputs:
- layer_output: bfloat16 [16384, 1024], P(('replica', 'group'))
- grad_input: float32 [16384, 1024], P(('replica', 'group'))
- grad_norm_attn: float32 [1024], P('group')
- grad_query: float32 [1024, 1024], P('group')
- grad_key: float32 [1024, 512], P('group')
- grad_value: float32 [1024, 512], P('group')
- grad_out: float32 [1024, 1024], P('group')
- grad_norm_moe: float32 [1024], P('group')
- grad_router: float32 [1024, 16], P('group')
- grad_expert_in: float32 [16, 1024, 1024], P('group')
- grad_expert_out: float32 [16, 512, 1024], P('group')
The draws below stay inside these ranges and needn't reach their ends.
Inputs may be any that keep to these rules, and one draw needn't show every extreme that they name: `routes`: each token names 8 different experts; the tokens of one device name one expert at most 384 times, and in every draw some expert is named exactly 384 times by the tokens of some device. `document_numbers`: never falling along the tokens; a document holds 1 to 1024 tokens and one holds exactly 1024.
All inputs are finite; a program needn't handle non-finite values.
Results may differ from the reference program's by a relative error of at most 0.023.
Values may be sent and summed in bfloat16 or wider, within the bound.
A program may use at most 320 MiB of HBM per device.

```python
import math
from functools import partial
import jax
import jax.numpy as jnp
import numpy as np
from jax import lax

MODEL_WIDTH = 1024
QUERY_HEADS = 16
KEY_VALUE_HEADS = 8
HEAD_SIZE = 64
FF = 512
TOP = 8
EXPERTS = 16
SEQUENCE_TOKENS = 1024
TOK_DEV = 512
CAP = 384
TOKENS = 16384


def shard_levels(stream_key, extent, cuts, low, top_value):
    gain = 1.0
    for position, parts in cuts:
        draws = jax.random.uniform(jax.random.fold_in(jax.random.fold_in(stream_key, 6), position), (parts,), jnp.float32, low / len(cuts), top_value / len(cuts))
        gain = gain * jnp.repeat(jnp.exp(draws), extent[position] // parts).reshape((-1,) + (1,) * (len(extent) - 1 - position))
    return gain


def profile(count, total, limit, slope):
    portions = [(1 << 20) // math.isqrt(standing ** slope) + 1 for standing in range(2, count + 1)]
    spare, holding = total - limit - (count - 1), [1] * (count - 1)
    while spare > 0:
        candidates = [i for i in range(count - 1) if holding[i] < limit]
        whole, left = sum([portions[i] for i in candidates]), spare
        for i in candidates:
            extra = min(limit - holding[i], max(1, left * portions[i] // whole), spare)
            holding[i] = holding[i] + extra
            spare = spare - extra
    return np.array([limit] + holding)


def ragged(key, amount, total, reach, skew):
    if amount == 2:
        one = jax.random.randint(key, (), max(1, total - reach), min(reach, total - 1) + 1)
        return jnp.stack([one, total - one])
    sizes = jnp.asarray(profile(amount, total, reach, skew), jnp.int32)
    twos = (amount - 1) // 2
    giver, receiver = sizes[1:1 + 2 * twos:2], sizes[2:2 + 2 * twos:2]
    slack = jnp.minimum(giver - 1, reach - receiver)
    moved = jax.random.randint(jax.random.fold_in(key, 1), (twos,), 0, 1 << 20) % (slack + 1)
    sizes = sizes.at[1:1 + 2 * twos:2].set(giver - moved).at[2:2 + 2 * twos:2].set(receiver + moved)
    return sizes[jax.random.permutation(jax.random.fold_in(key, 2), amount)]


def routed_block(own_key, own, number, rows, number_of, top, reach, lean):
    sequence = jax.random.permutation(own_key, number_of)
    heavy_load, common = load_shares(number_of, rows * top, reach, lean, True), load_shares(number_of, rows * top, reach, lean, False)
    places = jnp.arange(number_of)

    def named(sizes, offset_by):
        used = int((sizes > 0).sum())
        fixed = max(1, used // 4)
        moved = fixed + (places - fixed + offset_by * (used - fixed)) % max(1, number_of - fixed)
        return jnp.zeros((number_of,), jnp.int32).at[sequence[jnp.where(places < fixed, places, moved)]].set(jnp.asarray(sizes, jnp.int32))

    sizes = jnp.where(number % 4 == 0, named(heavy_load, number // 4), named(common, number - number // 4 - 1))
    mixed = jax.random.permutation(jax.random.fold_in(own, 3), number_of)
    giver, receiver = mixed[0:number_of // 2 * 2:2], mixed[1:number_of // 2 * 2:2]
    room = jnp.minimum(sizes[giver] - 1, reach - sizes[receiver]) // 2
    room = jnp.where((giver == sequence[0]) | (receiver == sequence[0]) | (sizes[receiver] == 0), 0, jnp.maximum(room, 0))
    moved = jax.random.randint(jax.random.fold_in(own, 4), (number_of // 2,), 0, 1 << 20) % (room + 1)
    sizes = sizes.at[giver].add(-moved).at[receiver].add(moved)
    items = jnp.searchsorted(jnp.cumsum(sizes), jnp.arange(rows * top), side="right").astype(jnp.int32)
    table = items.reshape(top, rows).T
    table = table[jax.random.permutation(jax.random.fold_in(own, 1), rows)]
    offset_by = jax.random.randint(jax.random.fold_in(own, 2), (rows, 1), 0, top)
    return jnp.take_along_axis(table, (jnp.arange(top)[None, :] + offset_by) % top, axis=1)


def load_shares(amount, total, limit, slope, full):
    loads = [(1 << 20) // math.isqrt(rank ** slope) + 1 for rank in range(1, amount + 1)]
    largest = limit if full else min(limit, max(-(-total // amount), total * loads[0] // sum(loads)))
    least = 1 if total - largest >= amount - 1 else 0
    holding, rest = [largest] + [least] * (amount - 1), total - largest - least * (amount - 1)
    while rest > 0:
        free = [i for i in range(1, amount) if holding[i] < largest] or [i for i in range(1, amount) if holding[i] < limit]
        whole, remaining = sum([loads[i] for i in free]), rest
        for i in free:
            more = min(limit - holding[i], max(1, remaining * loads[i] // whole), rest)
            holding[i] = holding[i] + more
            rest = rest - more
    return np.array(holding)


def centred(key, extent, deviation, reach, shards=(), kind=jnp.bfloat16):
    entries = deviation * jax.random.normal(key, extent, jnp.float32)
    if shards:
        entries = entries * shard_levels(key, extent, shards, -0.22, 0.18)
    return jnp.clip(entries, -reach, reach).astype(kind)


def setup_inputs(seed: int = 0) -> dict:
    key_list = jax.random.split(jax.random.key(seed), 14)
    layer_input = centred(key_list[0], (TOKENS, MODEL_WIDTH), 1.0, 6.0, ((0, 32),))
    document_numbers = jnp.searchsorted(jnp.cumsum(ragged(key_list[1], TOKENS * 4 // SEQUENCE_TOKENS, TOKENS, SEQUENCE_TOKENS, 2)), jnp.arange(TOKENS), side="right").astype(jnp.int32)
    routes_keys = jax.random.split(jax.random.fold_in(key_list[2], 1), TOKENS // TOK_DEV)
    routes_turns = jax.random.permutation(jax.random.fold_in(key_list[2], 3), TOKENS // TOK_DEV)
    routes = jax.vmap(lambda own, number: routed_block(jax.random.fold_in(key_list[2], 2), own, number, TOK_DEV, EXPERTS, TOP, CAP, 1))(routes_keys, routes_turns).reshape((TOKENS, TOP))
    norm_attn = jnp.clip(1.0 + 0.1 * jax.random.normal(key_list[3], (MODEL_WIDTH,), jnp.float32), 0.5, 1.5).astype(jnp.bfloat16)
    w_query = centred(key_list[4], (MODEL_WIDTH, QUERY_HEADS * HEAD_SIZE), (MODEL_WIDTH // 4) ** -0.5, 0.375, ((0, 2),))
    key_weight = centred(key_list[5], (MODEL_WIDTH, KEY_VALUE_HEADS * HEAD_SIZE), MODEL_WIDTH ** -0.5, 0.1875, ((0, 2),))
    value_weight = centred(key_list[6], (MODEL_WIDTH, KEY_VALUE_HEADS * HEAD_SIZE), MODEL_WIDTH ** -0.5, 0.1875, ((0, 2),))
    w_out = centred(key_list[7], (QUERY_HEADS * HEAD_SIZE, MODEL_WIDTH), (QUERY_HEADS * HEAD_SIZE // 16) ** -0.5, 0.75, ((0, 2),))
    norm_moe = jnp.clip(1.0 + 0.1 * jax.random.normal(key_list[8], (MODEL_WIDTH,), jnp.float32), 0.5, 1.5).astype(jnp.bfloat16)
    w_router = centred(key_list[9], (MODEL_WIDTH, EXPERTS), (4 * MODEL_WIDTH) ** -0.5, 0.09375, ((0, 2),))
    expert_in = centred(key_list[10], (EXPERTS, MODEL_WIDTH, 2 * FF), MODEL_WIDTH ** -0.5, 0.1875, ((0, 2),))
    expert_out = centred(key_list[11], (EXPERTS, FF, MODEL_WIDTH), (FF // 16) ** -0.5, 1.0, ((0, 2),))
    cotangent = centred(key_list[12], (TOKENS, MODEL_WIDTH), 1.0, 6.0, ((0, 32),))
    return {"layer_input": layer_input, "document_numbers": document_numbers, "routes": routes, "norm_attn": norm_attn, "w_query": w_query, "key_weight": key_weight, "value_weight": value_weight, "w_out": w_out, "norm_moe": norm_moe, "w_router": w_router, "expert_in": expert_in, "expert_out": expert_out, "cotangent": cotangent}


@jax.custom_vjp
def lower_precision(v):
    return lax.optimization_barrier(v.astype(jnp.bfloat16)).astype(jnp.float32)

@jax.custom_vjp
def lower_precision_backward(v):
    return v

def low_keep(v):
    return (lower_precision(v), None)

def low_pass(kept, grad):
    return (grad,)

def back_keep(v):
    return (v, None)

def back_low(kept, grad):
    return (lower_precision(grad),)
lower_precision.defvjp(low_keep, low_pass)
lower_precision_backward.defvjp(back_keep, back_low)
epsilon = 1e-06
masked_value = -1e+30
highest = lax.Precision.HIGHEST

def matrix_multiply(left_side, right_side):
    return jnp.dot(left_side, right_side, precision=highest, preferred_element_type=jnp.float32)

def rms_normed(values, gain_vec):
    factor = lax.rsqrt(lax.optimization_barrier(jnp.mean(values * values, axis=-1, keepdims=True)) + epsilon)
    return values * factor * gain_vec

def doc_positions(seg_ids):
    sequence_length = seg_ids.shape[0]
    token_index = jnp.arange(sequence_length, dtype=jnp.int32)
    previous = jnp.concatenate([seg_ids[:1] - 1, seg_ids[:-1]])
    is_start = (seg_ids != previous) | (token_index % SEQUENCE_TOKENS == 0)
    doc_start = lax.cummax(jnp.where(is_start, token_index, 0), axis=0)
    return token_index - doc_start

def apply_rotary(vectors, token_position):
    half_dim = vectors.shape[-1] // 2
    exponent = jnp.arange(half_dim, dtype=jnp.float32) * (-2.0 / vectors.shape[-1])
    inv_freq = jnp.power(10000.0, exponent)
    angles = token_position.astype(jnp.float32)[:, None] * inv_freq[None, :]
    cosine = jnp.cos(angles)[:, None, :]
    sine_part = jnp.sin(angles)[:, None, :]
    first_half = vectors[..., :half_dim]
    second_half = vectors[..., half_dim:]
    return jnp.concatenate([first_half * cosine - second_half * sine_part, second_half * cosine + first_half * sine_part], axis=-1)

def attend_packed_sequence(packed):
    query_rows, keys_seq, values_seq, seg_seq = packed
    sequence_length = query_rows.shape[0]
    heads_grouped = query_rows.reshape(sequence_length, KEY_VALUE_HEADS, QUERY_HEADS // KEY_VALUE_HEADS, HEAD_SIZE)
    raw_scores = lower_precision_backward(jnp.einsum('shgd,thd->hgst', heads_grouped, keys_seq, precision=highest))
    scores = raw_scores * HEAD_SIZE ** (-0.5)
    token_index = jnp.arange(sequence_length, dtype=jnp.int32)
    visible = (seg_seq[:, None] == seg_seq[None, :]) & (token_index[:, None] >= token_index[None, :])
    scores = jnp.where(visible[None, None], scores, masked_value)
    weights = lower_precision(jax.nn.softmax(scores, axis=-1))
    mixture = jnp.einsum('hgst,thd->shgd', weights, values_seq, precision=highest)
    return mixture.reshape(sequence_length, QUERY_HEADS * HEAD_SIZE)

def layer_forward(x_in, norm_attn, w_query, key_weight, value_weight, w_out, norm_moe, w_router, expert_in, expert_out, document_numbers, routes):
    token_total = x_in.shape[0]
    token_position = doc_positions(document_numbers)
    first_normalized = lower_precision(rms_normed(x_in, norm_attn))
    query_rows = lower_precision(apply_rotary(lower_precision_backward(matrix_multiply(first_normalized, w_query)).reshape(token_total, QUERY_HEADS, HEAD_SIZE), token_position))
    keys_gathered = lower_precision(apply_rotary(lower_precision_backward(matrix_multiply(first_normalized, key_weight)).reshape(token_total, KEY_VALUE_HEADS, HEAD_SIZE), token_position))
    values_gathered = lower_precision(lower_precision_backward(matrix_multiply(first_normalized, value_weight))).reshape(token_total, KEY_VALUE_HEADS, HEAD_SIZE)
    sequence_count = token_total // SEQUENCE_TOKENS
    attention_output = lax.map(jax.checkpoint(attend_packed_sequence), (query_rows.reshape(sequence_count, SEQUENCE_TOKENS, QUERY_HEADS, HEAD_SIZE), keys_gathered.reshape(sequence_count, SEQUENCE_TOKENS, KEY_VALUE_HEADS, HEAD_SIZE), values_gathered.reshape(sequence_count, SEQUENCE_TOKENS, KEY_VALUE_HEADS, HEAD_SIZE), document_numbers.reshape(sequence_count, SEQUENCE_TOKENS)))
    attn_rows = lower_precision_backward(lower_precision(attention_output.reshape(token_total, QUERY_HEADS * HEAD_SIZE)))
    hidden = x_in + lower_precision_backward(matrix_multiply(attn_rows, w_out))
    normed_two = lower_precision(rms_normed(hidden, norm_moe))
    logits = lower_precision_backward(matrix_multiply(normed_two, w_router))
    chosen = (routes[:, :, None] == jnp.arange(EXPERTS, dtype=jnp.int32)[None, None, :]).astype(jnp.float32)
    picked = lax.optimization_barrier(jnp.sum(chosen * logits[:, None, :], axis=2))
    gate_probs = jax.nn.softmax(picked, axis=1)
    share_table = lax.optimization_barrier(jnp.sum(gate_probs[:, :, None] * chosen, axis=1))

    def expert_step(running, expert_args):
        weight_in, weight_down, expert_share = expert_args
        inputs = lower_precision_backward(normed_two)
        gate_up = lower_precision_backward(matrix_multiply(inputs, weight_in))
        active = lower_precision(jax.nn.silu(gate_up[:, :FF]) * gate_up[:, FF:])
        result = lower_precision_backward(lower_precision(matrix_multiply(active, weight_down)))
        return (running + expert_share[:, None] * result, None)
    moe_sum, unused = lax.scan(jax.checkpoint(expert_step), jnp.zeros_like(hidden), (expert_in, expert_out, share_table.T))
    return hidden + moe_sum

def reference(layer_input, document_numbers, routes, norm_attn, w_query, key_weight, value_weight, w_out, norm_moe, w_router, expert_in, expert_out, cotangent):
    forward = partial(layer_forward, document_numbers=document_numbers, routes=routes)
    output, pullback = jax.vjp(forward, layer_input.astype(jnp.float32), norm_attn.astype(jnp.float32), w_query.astype(jnp.float32), key_weight.astype(jnp.float32), value_weight.astype(jnp.float32), w_out.astype(jnp.float32), norm_moe.astype(jnp.float32), w_router.astype(jnp.float32), expert_in.astype(jnp.float32), expert_out.astype(jnp.float32))
    grads = pullback(cotangent.astype(jnp.float32))
    return (output.astype(jnp.bfloat16), grads[0], grads[1], grads[2], grads[3], grads[4], grads[5], grads[6], grads[7], grads[8], grads[9])
```

```python
import functools

import jax
import jax.numpy as jnp
from jax import lax
from jax.experimental import pallas as pl
from jax.experimental.pallas import tpu as pltpu
from jax.sharding import PartitionSpec as P

QUERY_HEADS = 16
KEY_VALUE_HEADS = 8
HEAD_SIZE = 64
EXPERTS = 16
EPS = 1e-06
MASKED = -1e30
SCALE = HEAD_SIZE ** (-0.5)

f32 = jnp.float32
bf16 = jnp.bfloat16
MIB = 1 << 20


def mm(a, b):
    return lax.dot_general(a, b, (((1,), (0,)), ((), ())), preferred_element_type=f32)


def mm_nt(a, b):
    return lax.dot_general(a, b, (((1,), (1,)), ((), ())), preferred_element_type=f32)


def mm_tn(a, b):
    return lax.dot_general(a, b, (((0,), (0,)), ((), ())), preferred_element_type=f32)


def params(mib):
    return pltpu.CompilerParams(vmem_limit_bytes=mib * MIB)


def cost(flops, moved):
    return pl.CostEstimate(flops=int(flops), bytes_accessed=int(moved), transcendentals=0)


def doc_positions(seg_ids):
    length = seg_ids.shape[0]
    index = jnp.arange(length, dtype=jnp.int32)
    previous = jnp.concatenate([seg_ids[:1] - 1, seg_ids[:-1]])
    is_start = (seg_ids != previous) | (index == 0)
    start = lax.cummax(jnp.where(is_start, index, 0), axis=0)
    return index - start


def turn_tables(position):
    half = HEAD_SIZE // 2
    exponent = jnp.arange(half, dtype=f32) * (-2.0 / HEAD_SIZE)
    inv_freq = jnp.power(10000.0, exponent)
    angles = position.astype(f32)[:, None] * inv_freq[None, :]
    cosine, sine = jnp.cos(angles), jnp.sin(angles)
    return (
        jnp.concatenate([cosine] * 4, axis=1),
        jnp.concatenate([-sine, sine, -sine, sine], axis=1),
    )


def swap_halves(t):
    lane = lax.broadcasted_iota(jnp.int32, t.shape, 1)
    return jnp.where(
        lane % HEAD_SIZE < HEAD_SIZE // 2, pltpu.roll(t, 96, 1), pltpu.roll(t, 32, 1)
    )


def qkv_kernel(x_ref, gain_ref, w_ref, cos_ref, sin_ref, n1_ref, q_ref, k_ref, v_ref):
    x = x_ref[...].astype(f32)
    factor = lax.rsqrt(jnp.mean(x * x, axis=-1, keepdims=True) + EPS)
    n1 = (x * factor * gain_ref[...]).astype(bf16)
    n1_ref[...] = n1
    cosine, sine = cos_ref[...], sin_ref[...]
    q_width, k_width = q_ref.shape[1], k_ref.shape[1]
    for start in range(0, q_width + k_width, 256):
        lin = mm(n1, w_ref[:, start : start + 256])
        for part in (0, 128):
            t = lin[:, part : part + 128]
            turned = (t * cosine + swap_halves(t) * sine).astype(bf16)
            at = start + part
            if at < q_width:
                q_ref[:, at : at + 128] = turned
            else:
                k_ref[:, at - q_width : at - q_width + 128] = turned
    v_ref[...] = mm(n1, w_ref[:, q_width + k_width :]).astype(bf16)


def project(x, gain, w, cosine, sine):
    rows, width = x.shape
    q_width, k_width = QUERY_HEADS * HEAD_SIZE, KEY_VALUE_HEADS * HEAD_SIZE
    shape = jax.ShapeDtypeStruct
    return pl.pallas_call(
        qkv_kernel,
        out_shape=(
            shape((rows, width), bf16),
            shape((rows, q_width), bf16),
            shape((rows, k_width), bf16),
            shape((rows, k_width), bf16),
        ),
        compiler_params=params(40),
        cost_estimate=cost(2 * rows * width * w.shape[1], 2 * w.size + 8 * x.size),
        name="project",
    )(x, gain, w, cosine, sine)


def qkv_grad_kernel(
    dq_ref, dk_ref, dv_ref, n1_ref, w_ref, cos_ref, sin_ref, x_ref, gain_ref, dh_ref,
    gw_ref, gx_ref, gg_ref, lin_ref,
):
    cosine, sine = cos_ref[...], sin_ref[...]
    q_width, k_width = dq_ref.shape[1], dk_ref.shape[1]
    for ref, width, base in ((dq_ref, q_width, 0), (dk_ref, k_width, q_width)):
        for at in range(0, width, 128):
            t = ref[:, at : at + 128].astype(f32)
            turned = (t * cosine - swap_halves(t) * sine).astype(bf16)
            lin_ref[:, base + at : base + at + 128] = turned
    lin_ref[:, q_width + k_width :] = dv_ref[...].astype(bf16)
    total = q_width + 2 * k_width
    n1 = n1_ref[...]
    for at in range(0, total, 512):
        gw_ref[:, at : at + 512] = mm_tn(n1, lin_ref[:, at : at + 512]).astype(bf16)
    dn1 = mm_nt(lin_ref[...], w_ref[...])
    x = x_ref[...].astype(f32)
    factor = lax.rsqrt(jnp.mean(x * x, axis=-1, keepdims=True) + EPS)
    gg_ref[...] = jnp.sum(x * factor * dn1, axis=0, keepdims=True)
    c = dn1 * gain_ref[...]
    mean = jnp.mean(c * x, axis=-1, keepdims=True)
    gx_ref[...] = dh_ref[...] + factor * (c - x * (factor * factor * mean))


def project_grad(dq, dk, dv, n1, w, cosine, sine, x, gain, dh):
    rows, width = x.shape
    shape = jax.ShapeDtypeStruct
    return pl.pallas_call(
        qkv_grad_kernel,
        out_shape=(
            shape(w.shape, bf16),
            shape((rows, width), f32),
            shape((1, width), f32),
        ),
        scratch_shapes=[pltpu.VMEM((rows, w.shape[1]), bf16)],
        compiler_params=params(56),
        cost_estimate=cost(4 * rows * width * w.shape[1], 4 * w.size + 16 * x.size),
        name="project_grad",
    )(dq, dk, dv, n1, w, cosine, sine, x, gain, dh)


def visible_bias(first_ref, seg_q_ref, seg_k_ref, bias_ref):
    rows, keys = bias_ref.shape
    row = first_ref[0] + lax.broadcasted_iota(jnp.int32, (rows, keys), 0)
    col = lax.broadcasted_iota(jnp.int32, (rows, keys), 1)
    seen = (seg_q_ref[...] == seg_k_ref[...]) & (row >= col)
    bias_ref[...] = jnp.where(seen, 0.0, MASKED).astype(f32)


def attend_kernel(first_ref, q_ref, k_ref, v_ref, seg_q_ref, seg_k_ref, o_ref, bias_ref):
    @pl.when(pl.program_id(0) == 0)
    def _():
        visible_bias(first_ref, seg_q_ref, seg_k_ref, bias_ref)

    bias = bias_ref[...]
    for head in range(4):
        at, kv = head * HEAD_SIZE, head // 2 * HEAD_SIZE
        s = mm_nt(q_ref[:, at : at + HEAD_SIZE], k_ref[:, kv : kv + HEAD_SIZE]) * SCALE + bias
        e = jnp.exp(s - jnp.max(s, axis=1, keepdims=True))
        total = jnp.sum(e, axis=1, keepdims=True)
        o = mm(e.astype(bf16), v_ref[:, kv : kv + HEAD_SIZE]) / total
        o_ref[:, at : at + HEAD_SIZE] = o.astype(bf16)


def attend(first, q, k, v, seg_q, seg_k):
    rows, width = q.shape
    keys = k.shape[0]
    wide = pl.BlockSpec((rows, 256), lambda i, first: (0, i))
    narrow = pl.BlockSpec((keys, 128), lambda i, first: (0, i))
    return pl.pallas_call(
        attend_kernel,
        out_shape=jax.ShapeDtypeStruct((rows, width), bf16),
        grid_spec=pltpu.PrefetchScalarGridSpec(
            num_scalar_prefetch=1,
            grid=(width // 256,),
            in_specs=[
                wide,
                narrow,
                narrow,
                pl.BlockSpec((rows, 1), lambda i, first: (0, 0)),
                pl.BlockSpec((1, keys), lambda i, first: (0, 0)),
            ],
            out_specs=wide,
            scratch_shapes=[pltpu.VMEM((rows, keys), f32)],
        ),
        compiler_params=params(48),
        cost_estimate=cost(16 * rows * keys * width, 4 * q.size + 4 * k.size),
        name="attend",
    )(first, q, k, v, seg_q, seg_k)


def attend_grad_kernel(
    first_ref, q_ref, k_ref, v_ref, do_ref, seg_q_ref, seg_k_ref,
    dq_ref, dk_ref, dv_ref, bias_ref,
):
    @pl.when(pl.program_id(0) == 0)
    def _():
        visible_bias(first_ref, seg_q_ref, seg_k_ref, bias_ref)

    bias = bias_ref[...]
    for pair in range(2):
        kv = pair * HEAD_SIZE
        k, v = k_ref[:, kv : kv + HEAD_SIZE], v_ref[:, kv : kv + HEAD_SIZE]
        dk = dv = None
        for head in (2 * pair, 2 * pair + 1):
            at = head * HEAD_SIZE
            q, do = q_ref[:, at : at + HEAD_SIZE], do_ref[:, at : at + HEAD_SIZE]
            s = mm_nt(q, k) * SCALE + bias
            e = jnp.exp(s - jnp.max(s, axis=1, keepdims=True))
            p = e * (1.0 / jnp.sum(e, axis=1, keepdims=True))
            dp = mm_nt(do, v)
            delta = jnp.sum(p * dp, axis=1, keepdims=True)
            ds = (p * (dp - delta) * SCALE).astype(bf16)
            dq_ref[:, at : at + HEAD_SIZE] = mm(ds, k)
            dk_part, dv_part = mm_tn(ds, q), mm_tn(p.astype(bf16), do)
            dk = dk_part if dk is None else dk + dk_part
            dv = dv_part if dv is None else dv + dv_part
        dk_ref[:, kv : kv + HEAD_SIZE] = dk.astype(bf16)
        dv_ref[:, kv : kv + HEAD_SIZE] = dv.astype(bf16)


def attend_grad(first, q, k, v, do, seg_q, seg_k):
    rows, width = q.shape
    keys = k.shape[0]
    wide = pl.BlockSpec((rows, 256), lambda i, first: (0, i))
    narrow = pl.BlockSpec((keys, 128), lambda i, first: (0, i))
    shape = jax.ShapeDtypeStruct
    return pl.pallas_call(
        attend_grad_kernel,
        out_shape=(
            shape((rows, width), f32),
            shape(k.shape, bf16),
            shape(k.shape, bf16),
        ),
        grid_spec=pltpu.PrefetchScalarGridSpec(
            num_scalar_prefetch=1,
            grid=(width // 256,),
            in_specs=[
                wide,
                narrow,
                narrow,
                wide,
                pl.BlockSpec((rows, 1), lambda i, first: (0, 0)),
                pl.BlockSpec((1, keys), lambda i, first: (0, 0)),
            ],
            out_specs=[wide, narrow, narrow],
            scratch_shapes=[pltpu.VMEM((rows, keys), f32)],
        ),
        compiler_params=params(56),
        cost_estimate=cost(40 * rows * keys * width // 4, 8 * q.size + 8 * k.size),
        name="attend_grad",
    )(first, q, k, v, do, seg_q, seg_k)


def gather(value):
    return lax.all_gather(value, "group", axis=0, tiled=True)


def owner_sum(value):
    return lax.psum_scatter(value.astype(bf16), "group", scatter_dimension=0, tiled=True)


def rms_factor(values):
    return lax.rsqrt(jnp.mean(values * values, axis=-1, keepdims=True) + EPS)


def expert_pass(n2, grad, share, w_in, w_out):
    half = w_out.shape[0]
    gu = mm(n2, w_in)
    z, w = gu[:, :half], gu[:, half:]
    sg = jax.nn.sigmoid(z)
    act = (z * sg * w).astype(bf16)
    ye = mm(act, w_out).astype(bf16).astype(f32)
    d_gate = jnp.sum(grad * ye, axis=1)
    d_ye = (share * grad).astype(bf16)
    g_out = mm_tn(act, d_ye).astype(bf16)
    d_act = mm_nt(d_ye, w_out)
    d_gu = jnp.concatenate(
        [d_act * w * sg * (1.0 + z * (1.0 - sg)), d_act * z * sg], axis=1
    ).astype(bf16)
    g_in = mm_tn(n2, d_gu).astype(bf16)
    d_xe = mm_nt(d_gu, w_in).astype(bf16).astype(f32)
    return share * ye, d_gate, g_in, g_out, d_xe


def on_device(
    layer_input, document_numbers, routes, norm_attn, w_query, key_weight, value_weight, w_out,
    norm_moe, w_router, expert_in, expert_out, cotangent,
):
    rows, width = layer_input.shape
    group = lax.axis_index("group")
    first = group * rows
    owned = expert_in.shape[0]
    kv_width = KEY_VALUE_HEADS * HEAD_SIZE

    seg_all = gather(document_numbers)
    position = lax.dynamic_slice_in_dim(doc_positions(seg_all), first, rows, 0)
    cosine, sine = turn_tables(position)
    small = gather(jnp.concatenate([norm_attn[:, None], norm_moe[:, None], w_router], axis=1))
    gain_attn = small[:, 0].astype(f32)[None, :]
    gain_moe = small[:, 1].astype(f32)[None, :]
    router = small[:, 2:]
    w_qkv = gather(jnp.concatenate([w_query, key_weight, value_weight], axis=1))
    wo = gather(w_out)
    grad_all = gather(cotangent).astype(f32)

    n1, q, k, v = project(layer_input, gain_attn, w_qkv, cosine, sine)
    kv_all = gather(jnp.concatenate([k, v], axis=1))
    k_all, v_all = kv_all[:, :kv_width], kv_all[:, kv_width:]
    first_row = jnp.full((1,), first, jnp.int32)
    seg_q, seg_k = document_numbers[:, None], seg_all[None, :]
    ao = attend(first_row, q, k_all, v_all, seg_q, seg_k)

    x = layer_input.astype(f32)
    h = x + mm(ao, wo)
    r2 = rms_factor(h)
    n2 = (h * r2 * gain_moe).astype(bf16)
    logits = mm(n2, router)
    chosen = jnp.any(routes[:, :, None] == jnp.arange(EXPERTS, dtype=jnp.int32), axis=1)
    picked = jnp.where(chosen, logits, MASKED)
    e = jnp.where(chosen, jnp.exp(picked - jnp.max(picked, axis=1, keepdims=True)), 0.0)
    share = e / jnp.sum(e, axis=1, keepdims=True)

    n2_all = gather(n2)
    share_all = lax.dynamic_slice_in_dim(gather(share), group * owned, owned, 1)
    moe = jnp.zeros((n2_all.shape[0], width), f32)
    d_n2_all = jnp.zeros_like(moe)
    d_gate, g_in, g_out = [], [], []
    for i in range(owned):
        y, dg, gi, go, dx = expert_pass(
            n2_all, grad_all, share_all[:, i : i + 1], expert_in[i], expert_out[i]
        )
        moe, d_n2_all = moe + y, d_n2_all + dx
        d_gate.append(dg)
        g_in.append(gi)
        g_out.append(go)
    d_gate = jnp.zeros((n2_all.shape[0], EXPERTS), f32).at[:, :].set(
        lax.dynamic_update_slice_in_dim(
            jnp.zeros((n2_all.shape[0], EXPERTS), f32), jnp.stack(d_gate, 1), group * owned, 1
        )
    )
    d_gate = lax.psum_scatter(d_gate, "group", scatter_dimension=0, tiled=True)
    layer_output = (h + owner_sum(moe).astype(f32)).astype(bf16)

    d_logits = (share * (d_gate - jnp.sum(share * d_gate, axis=1, keepdims=True))).astype(bf16)
    g_router = mm_tn(n2, d_logits)
    d_n2 = owner_sum(d_n2_all).astype(f32) + mm_nt(d_logits, router)
    g_gain_moe = jnp.sum(h * r2 * d_n2, axis=0)
    c = d_n2 * gain_moe
    d_h = cotangent.astype(f32) + r2 * (
        c - h * r2 * r2 * jnp.mean(c * h, axis=-1, keepdims=True)
    )
    d_y = d_h.astype(bf16)
    g_wo = mm_tn(ao, d_y).astype(bf16)
    d_o = mm_nt(d_y, wo).astype(bf16)

    dq, dk_all, dv_all = attend_grad(first_row, q, k_all, v_all, d_o, seg_q, seg_k)
    dkv = owner_sum(jnp.concatenate([dk_all, dv_all], axis=1))
    g_qkv, grad_input, g_gain_attn = project_grad(
        dq, dkv[:, :kv_width], dkv[:, kv_width:], n1, w_qkv, cosine, sine, layer_input,
        gain_attn, d_h,
    )

    g_attn = owner_sum(jnp.concatenate([g_qkv, g_wo], axis=1))
    g_small = owner_sum(
        jnp.concatenate([g_gain_attn.reshape(-1, 1), g_gain_moe[:, None], g_router], axis=1)
    )
    sums = lax.psum((*g_in, *g_out, g_attn, g_small), "replica")
    sums = [s.astype(f32) for s in sums]
    g_in, g_out = jnp.stack(sums[:owned]), jnp.stack(sums[owned : 2 * owned])
    g_attn, g_small = sums[-2:]
    q_width = QUERY_HEADS * HEAD_SIZE
    return (
        layer_output,
        grad_input,
        g_small[:, 0],
        g_attn[:, :q_width],
        g_attn[:, q_width : q_width + kv_width],
        g_attn[:, q_width + kv_width : q_width + 2 * kv_width],
        g_attn[:, q_width + 2 * kv_width :],
        g_small[:, 1],
        g_small[:, 2:],
        g_in,
        g_out,
    )


def solution(mesh):
    tokens, weights = P(("replica", "group"), None), P("group", None)
    in_specs = (
        tokens, P(("replica", "group")), tokens, P("group"), weights, weights, weights, weights,
        P("group"), weights, P("group", None, None), P("group", None, None), tokens,
    )
    out_specs = (
        tokens, tokens, P("group"), weights, weights, weights, weights, P("group"), weights,
        P("group", None, None), P("group", None, None),
    )
    return jax.shard_map(
        on_device, mesh=mesh, in_specs=in_specs, out_specs=out_specs, check_vma=False
    )
```

```python
import functools

import jax
import jax.numpy as jnp
from jax import lax
from jax.experimental import pallas as pl
from jax.experimental.pallas import tpu as pltpu
from jax.sharding import PartitionSpec as P

QUERY_HEADS = 16
KEY_VALUE_HEADS = 8
HEAD_SIZE = 64
EXPERTS = 16
EPS = 1e-06
MASKED = -1e30
SCALE = HEAD_SIZE ** (-0.5)

f32 = jnp.float32
bf16 = jnp.bfloat16
MIB = 1 << 20


def mm(a, b):
    return lax.dot_general(a, b, (((1,), (0,)), ((), ())), preferred_element_type=f32)


def mm_nt(a, b):
    return lax.dot_general(a, b, (((1,), (1,)), ((), ())), preferred_element_type=f32)


def mm_tn(a, b):
    return lax.dot_general(a, b, (((0,), (0,)), ((), ())), preferred_element_type=f32)


def params(mib):
    return pltpu.CompilerParams(vmem_limit_bytes=mib * MIB)


def cost(flops, moved):
    return pl.CostEstimate(flops=int(flops), bytes_accessed=int(moved), transcendentals=0)


def doc_positions(seg_ids):
    length = seg_ids.shape[0]
    index = jnp.arange(length, dtype=jnp.int32)
    previous = jnp.concatenate([seg_ids[:1] - 1, seg_ids[:-1]])
    is_start = (seg_ids != previous) | (index == 0)
    start = lax.cummax(jnp.where(is_start, index, 0), axis=0)
    return index - start


def turn_tables(position):
    half = HEAD_SIZE // 2
    exponent = jnp.arange(half, dtype=f32) * (-2.0 / HEAD_SIZE)
    inv_freq = jnp.power(10000.0, exponent)
    angles = position.astype(f32)[:, None] * inv_freq[None, :]
    cosine, sine = jnp.cos(angles), jnp.sin(angles)
    return (
        jnp.concatenate([cosine] * 4, axis=1),
        jnp.concatenate([-sine, sine, -sine, sine], axis=1),
    )


def swap_halves(t):
    lane = lax.broadcasted_iota(jnp.int32, t.shape, 1)
    return jnp.where(
        lane % HEAD_SIZE < HEAD_SIZE // 2, pltpu.roll(t, 96, 1), pltpu.roll(t, 32, 1)
    )


def qkv_kernel(x_ref, gain_ref, w_ref, cos_ref, sin_ref, n1_ref, q_ref, k_ref, v_ref):
    x = x_ref[...].astype(f32)
    factor = lax.rsqrt(jnp.mean(x * x, axis=-1, keepdims=True) + EPS)
    n1 = (x * factor * gain_ref[...]).astype(bf16)
    n1_ref[...] = n1
    cosine, sine = cos_ref[...], sin_ref[...]
    q_width, k_width = q_ref.shape[1], k_ref.shape[1]
    for start in range(0, q_width + k_width, 256):
        lin = mm(n1, w_ref[:, start : start + 256])
        for part in (0, 128):
            t = lin[:, part : part + 128]
            turned = (t * cosine + swap_halves(t) * sine).astype(bf16)
            at = start + part
            if at < q_width:
                q_ref[:, at : at + 128] = turned
            else:
                k_ref[:, at - q_width : at - q_width + 128] = turned
    v_ref[...] = mm(n1, w_ref[:, q_width + k_width :]).astype(bf16)


def project(x, gain, w, cosine, sine):
    rows, width = x.shape
    q_width, k_width = QUERY_HEADS * HEAD_SIZE, KEY_VALUE_HEADS * HEAD_SIZE
    shape = jax.ShapeDtypeStruct
    return pl.pallas_call(
        qkv_kernel,
        out_shape=(
            shape((rows, width), bf16),
            shape((rows, q_width), bf16),
            shape((rows, k_width), bf16),
            shape((rows, k_width), bf16),
        ),
        compiler_params=params(40),
        cost_estimate=cost(2 * rows * width * w.shape[1], 2 * w.size + 8 * x.size),
        name="project",
    )(x, gain, w, cosine, sine)


def qkv_grad_kernel(
    dq_ref, dk_ref, dv_ref, n1_ref, w_ref, cos_ref, sin_ref, x_ref, gain_ref, dh_ref,
    gw_ref, gx_ref, gg_ref, lin_ref,
):
    cosine, sine = cos_ref[...], sin_ref[...]
    q_width, k_width = dq_ref.shape[1], dk_ref.shape[1]
    for ref, width, base in ((dq_ref, q_width, 0), (dk_ref, k_width, q_width)):
        for at in range(0, width, 128):
            t = ref[:, at : at + 128].astype(f32)
            turned = (t * cosine - swap_halves(t) * sine).astype(bf16)
            lin_ref[:, base + at : base + at + 128] = turned
    lin_ref[:, q_width + k_width :] = dv_ref[...].astype(bf16)
    total = q_width + 2 * k_width
    n1 = n1_ref[...]
    for at in range(0, total, 512):
        gw_ref[:, at : at + 512] = mm_tn(n1, lin_ref[:, at : at + 512]).astype(bf16)
    dn1 = mm_nt(lin_ref[...], w_ref[...])
    x = x_ref[...].astype(f32)
    factor = lax.rsqrt(jnp.mean(x * x, axis=-1, keepdims=True) + EPS)
    gg_ref[...] = jnp.sum(x * factor * dn1, axis=0, keepdims=True)
    c = dn1 * gain_ref[...]
    mean = jnp.mean(c * x, axis=-1, keepdims=True)
    gx_ref[...] = dh_ref[...] + factor * (c - x * (factor * factor * mean))


def project_grad(dq, dk, dv, n1, w, cosine, sine, x, gain, dh):
    rows, width = x.shape
    shape = jax.ShapeDtypeStruct
    return pl.pallas_call(
        qkv_grad_kernel,
        out_shape=(
            shape(w.shape, bf16),
            shape((rows, width), f32),
            shape((1, width), f32),
        ),
        scratch_shapes=[pltpu.VMEM((rows, w.shape[1]), bf16)],
        compiler_params=params(56),
        cost_estimate=cost(4 * rows * width * w.shape[1], 4 * w.size + 16 * x.size),
        name="project_grad",
    )(dq, dk, dv, n1, w, cosine, sine, x, gain, dh)


def visible_bias(first_ref, seg_q_ref, seg_k_ref, bias_ref):
    rows, keys = bias_ref.shape
    row = first_ref[0] + lax.broadcasted_iota(jnp.int32, (rows, keys), 0)
    col = lax.broadcasted_iota(jnp.int32, (rows, keys), 1)
    seen = (seg_q_ref[...] == seg_k_ref[...]) & (row >= col)
    bias_ref[...] = jnp.where(seen, 0.0, MASKED).astype(f32)


def attend_kernel(first_ref, q_ref, k_ref, v_ref, seg_q_ref, seg_k_ref, o_ref, bias_ref):
    @pl.when(pl.program_id(0) == 0)
    def _():
        visible_bias(first_ref, seg_q_ref, seg_k_ref, bias_ref)

    bias = bias_ref[...]
    for head in range(4):
        at, kv = head * HEAD_SIZE, head // 2 * HEAD_SIZE
        s = mm_nt(q_ref[:, at : at + HEAD_SIZE], k_ref[:, kv : kv + HEAD_SIZE]) * SCALE + bias
        e = jnp.exp(s - jnp.max(s, axis=1, keepdims=True))
        total = jnp.sum(e, axis=1, keepdims=True)
        o = mm(e.astype(bf16), v_ref[:, kv : kv + HEAD_SIZE]) / total
        o_ref[:, at : at + HEAD_SIZE] = o.astype(bf16)


def attend(first, q, k, v, seg_q, seg_k):
    rows, width = q.shape
    keys = k.shape[0]
    wide = pl.BlockSpec((rows, 256), lambda i, first: (0, i))
    narrow = pl.BlockSpec((keys, 128), lambda i, first: (0, i))
    return pl.pallas_call(
        attend_kernel,
        out_shape=jax.ShapeDtypeStruct((rows, width), bf16),
        grid_spec=pltpu.PrefetchScalarGridSpec(
            num_scalar_prefetch=1,
            grid=(width // 256,),
            in_specs=[
                wide,
                narrow,
                narrow,
                pl.BlockSpec((rows, 1), lambda i, first: (0, 0)),
                pl.BlockSpec((1, keys), lambda i, first: (0, 0)),
            ],
            out_specs=wide,
            scratch_shapes=[pltpu.VMEM((rows, keys), f32)],
        ),
        compiler_params=params(48),
        cost_estimate=cost(16 * rows * keys * width, 4 * q.size + 4 * k.size),
        name="attend",
    )(first, q, k, v, seg_q, seg_k)


def attend_grad_kernel(
    first_ref, q_ref, k_ref, v_ref, do_ref, seg_q_ref, seg_k_ref,
    dq_ref, dk_ref, dv_ref, bias_ref,
):
    @pl.when(pl.program_id(0) == 0)
    def _():
        visible_bias(first_ref, seg_q_ref, seg_k_ref, bias_ref)

    bias = bias_ref[...]
    for pair in range(2):
        kv = pair * HEAD_SIZE
        k, v = k_ref[:, kv : kv + HEAD_SIZE], v_ref[:, kv : kv + HEAD_SIZE]
        dk = dv = None
        for head in (2 * pair, 2 * pair + 1):
            at = head * HEAD_SIZE
            q, do = q_ref[:, at : at + HEAD_SIZE], do_ref[:, at : at + HEAD_SIZE]
            s = mm_nt(q, k) * SCALE + bias
            e = jnp.exp(s - jnp.max(s, axis=1, keepdims=True))
            p = e * (1.0 / jnp.sum(e, axis=1, keepdims=True))
            dp = mm_nt(do, v)
            delta = jnp.sum(p * dp, axis=1, keepdims=True)
            ds = (p * (dp - delta) * SCALE).astype(bf16)
            dq_ref[:, at : at + HEAD_SIZE] = mm(ds, k)
            dk_part, dv_part = mm_tn(ds, q), mm_tn(p.astype(bf16), do)
            dk = dk_part if dk is None else dk + dk_part
            dv = dv_part if dv is None else dv + dv_part
        dk_ref[:, kv : kv + HEAD_SIZE] = dk.astype(bf16)
        dv_ref[:, kv : kv + HEAD_SIZE] = dv.astype(bf16)


def attend_grad(first, q, k, v, do, seg_q, seg_k):
    rows, width = q.shape
    keys = k.shape[0]
    wide = pl.BlockSpec((rows, 256), lambda i, first: (0, i))
    narrow = pl.BlockSpec((keys, 128), lambda i, first: (0, i))
    shape = jax.ShapeDtypeStruct
    return pl.pallas_call(
        attend_grad_kernel,
        out_shape=(
            shape((rows, width), f32),
            shape(k.shape, bf16),
            shape(k.shape, bf16),
        ),
        grid_spec=pltpu.PrefetchScalarGridSpec(
            num_scalar_prefetch=1,
            grid=(width // 256,),
            in_specs=[
                wide,
                narrow,
                narrow,
                wide,
                pl.BlockSpec((rows, 1), lambda i, first: (0, 0)),
                pl.BlockSpec((1, keys), lambda i, first: (0, 0)),
            ],
            out_specs=[wide, narrow, narrow],
            scratch_shapes=[pltpu.VMEM((rows, keys), f32)],
        ),
        compiler_params=params(56),
        cost_estimate=cost(40 * rows * keys * width // 4, 8 * q.size + 8 * k.size),
        name="attend_grad",
    )(first, q, k, v, do, seg_q, seg_k)


def gather(value):
    return lax.all_gather(value, "group", axis=0, tiled=True)


def owner_sum(value):
    return lax.psum_scatter(value.astype(bf16), "group", scatter_dimension=0, tiled=True)


def rms_factor(values):
    return lax.rsqrt(jnp.mean(values * values, axis=-1, keepdims=True) + EPS)


LAG = 2
PHASES = 7
SEMS = 8
(CORE, X_A, IN_B, IN_A, HALF_B, MID_A, RUNG_B, OUT_A, BACK_B, SPREAD_A, OUT_B, JOIN, KINDS) = range(13)


def engine_scratch(quarter, width):
    def vmem(*shape):
        return pltpu.VMEM((*shape, quarter, width), bf16)

    return [
        vmem(4, 2, 4),
        vmem(4, 4),
        vmem(4),
        vmem(8, 2),
        vmem(8),
        vmem(4),
        vmem(4),
        vmem(4),
        vmem(LAG, 4),
        vmem(LAG),
        vmem(LAG, 2),
        vmem(LAG),
        vmem(LAG),
        vmem(LAG),
        vmem(LAG),
        pltpu.SemaphoreType.DMA((KINDS, SEMS)),
        pltpu.SemaphoreType.DMA((KINDS, SEMS)),
        pltpu.SemaphoreType.DMA((2, SEMS)),
    ]


def replica_place():
    r = lax.axis_index("replica")
    core, x, z = lax.rem(r, 2), lax.rem(r // 2, 2), r // 4
    inner = (z == 1) | (z == 2)
    late = z // 2
    return r, core, x, z, inner, late


def greet(with_group):
    r, core, x, z, inner, late = replica_place()
    barrier = pltpu.get_barrier_semaphore()

    def signal(target):
        pl.semaphore_signal(
            barrier, inc=1, device_id={"replica": target}, device_id_type=pl.DeviceIdType.MESH
        )

    signal(r + 1 - 2 * core)
    signal(r + 2 - 4 * x)
    if with_group:
        pl.semaphore_signal(
            barrier, inc=1, device_id={"group": 1 - lax.axis_index("group")},
            device_id_type=pl.DeviceIdType.MESH,
        )
    extra = 1 if with_group else 0

    @pl.when(inner)
    def _():
        signal(r + 4)
        signal(r - 4)
        pl.semaphore_wait(barrier, 4 + extra)

    @pl.when(jnp.logical_not(inner))
    def _():
        signal(jnp.where(z == 0, r + 4, r - 4))
        pl.semaphore_wait(barrier, 3 + extra)


def make_engine(count, out, scratch):
    (staged, got_core, got_x, got_end_b, got_end_a, got_mid_b, got_mid_a, got_rung,
     summed, a_x, b_end, a_end, b_mid, a_all, b_all, send_sem, recv_sem, copy_sem) = scratch
    r, core, x, z, inner, late = replica_place()
    outer = jnp.logical_not(inner)
    core_peer, x_peer = r + 1 - 2 * core, r + 2 - 4 * x
    mid_peer = jnp.where(z == 1, r + 4, r - 4)
    line_peer = jnp.where(z < 2, jnp.where(z == 0, r + 4, r - 4), jnp.where(z == 3, r - 4, r + 4))

    def remote(kind, k, src, dst, peer):
        slot = lax.rem(k, SEMS)
        return pltpu.make_async_remote_copy(
            src_ref=src, dst_ref=dst, send_sem=send_sem.at[kind, slot],
            recv_sem=recv_sem.at[kind, slot], device_id={"replica": peer},
            device_id_type=pl.DeviceIdType.MESH,
        )

    def core_copy(k):
        return remote(
            CORE, k, staged.at[lax.rem(k, 4), 1 - core], got_core.at[lax.rem(k, 4)], core_peer
        )

    def x_copy(k):
        return remote(X_A, k, summed.at[lax.rem(k, LAG), 1 - x], got_x.at[lax.rem(k, 4)], x_peer)

    def in_b_copy(k):
        return remote(
            IN_B, k, summed.at[lax.rem(k, LAG), pl.ds(2, 2)], got_end_b.at[lax.rem(k, 8)], line_peer
        )

    def in_a_copy(k):
        return remote(IN_A, k, a_x.at[lax.rem(k, LAG)], got_end_a.at[lax.rem(k, 8)], line_peer)

    def half_b_copy(k):
        return remote(
            HALF_B, k, b_end.at[lax.rem(k, LAG), 1 - late], got_mid_b.at[lax.rem(k, 4)], mid_peer
        )

    def mid_a_copy(k):
        return remote(MID_A, k, a_end.at[lax.rem(k, LAG)], got_mid_a.at[lax.rem(k, 4)], mid_peer)

    def rung_copy(k):
        return remote(RUNG_B, k, b_mid.at[lax.rem(k, LAG)], got_rung.at[lax.rem(k, 4)], x_peer)

    def out_a_copy(k):
        return remote(OUT_A, k, a_all.at[lax.rem(k, LAG)], out.at[k, core, x], line_peer)

    def back_b_copy(k):
        return remote(BACK_B, k, b_all.at[lax.rem(k, LAG)], out.at[k, core, 2 + late], mid_peer)

    def back_b_arrival(k):
        return remote(BACK_B, k, b_all.at[lax.rem(k, LAG)], out.at[k, core, 3 - late], mid_peer)

    def spread_copy(k):
        return remote(SPREAD_A, k, out.at[k, core, x], out.at[k, core, x], x_peer)

    def spread_arrival(k):
        return remote(SPREAD_A, k, out.at[k, core, x], out.at[k, core, 1 - x], x_peer)

    def out_b_copy(k):
        part = out.at[k, core, pl.ds(2, 2)]
        return remote(OUT_B, k, part, part, line_peer)

    def join_copy(k):
        return remote(JOIN, k, out.at[k, core], out.at[k, core], core_peer)

    def join_arrival(k):
        return remote(JOIN, k, out.at[k, core], out.at[k, 1 - core], core_peer)

    def keep_a(k):
        return pltpu.make_async_copy(
            a_all.at[lax.rem(k, LAG)], out.at[k, core, x], copy_sem.at[0, lax.rem(k, SEMS)]
        )

    def keep_b(k):
        return pltpu.make_async_copy(
            b_all.at[lax.rem(k, LAG)], out.at[k, core, 2 + late], copy_sem.at[1, lax.rem(k, SEMS)]
        )

    def phase1(k):
        core_copy(k).wait()
        summed[lax.rem(k, LAG)] = staged[lax.rem(k, 4), core] + got_core[lax.rem(k, 4)]
        x_copy(k).start()

        @pl.when(outer)
        def _():
            in_b_copy(k).start()

    def phase2(k):
        i = lax.rem(k, LAG)
        x_copy(k).wait()
        a_x[i] = summed[i, x] + got_x[lax.rem(k, 4)]

        @pl.when(outer)
        def _():
            in_a_copy(k).start()
            in_b_copy(k).wait_send()

        @pl.when(inner)
        def _():
            in_b_copy(k).wait_recv()
            b_end[i] = summed[i, 2:4] + got_end_b[lax.rem(k, 8)]
            half_b_copy(k).start()

    def phase3(k):
        i = lax.rem(k, LAG)

        @pl.when(outer)
        def _():
            in_a_copy(k).wait_send()

        @pl.when(inner)
        def _():
            in_a_copy(k).wait_recv()
            a_end[i] = a_x[i] + got_end_a[lax.rem(k, 8)]
            mid_a_copy(k).start()
            half_b_copy(k).wait()
            b_mid[i] = b_end[i, late] + got_mid_b[lax.rem(k, 4)]
            rung_copy(k).start()

    def phase4(k):
        i = lax.rem(k, LAG)

        @pl.when(inner)
        def _():
            mid_a_copy(k).wait()
            a_all[i] = a_end[i] + got_mid_a[lax.rem(k, 4)]
            out_a_copy(k).start()
            keep_a(k).start()
            rung_copy(k).wait()
            b_all[i] = b_mid[i] + got_rung[lax.rem(k, 4)]
            back_b_copy(k).start()
            keep_b(k).start()

    def phase5(k):
        @pl.when(outer)
        def _():
            out_a_copy(k).wait_recv()

        @pl.when(inner)
        def _():
            keep_a(k).wait()
            out_a_copy(k).wait_send()

        spread_copy(k).start()

        @pl.when(inner)
        def _():
            keep_b(k).wait()
            back_b_copy(k).wait_send()
            back_b_arrival(k).wait_recv()
            out_b_copy(k).start()

    def phase6(k):
        spread_copy(k).wait_send()
        spread_arrival(k).wait_recv()

        @pl.when(outer)
        def _():
            out_b_copy(k).wait_recv()

        @pl.when(inner)
        def _():
            out_b_copy(k).wait_send()

        join_copy(k).start()

    def phase7(k):
        join_copy(k).wait_send()
        join_arrival(k).wait_recv()

    def tick(t):
        for number, phase in reversed(
            list(enumerate((phase1, phase2, phase3, phase4, phase5, phase6, phase7), 1))
        ):
            k = t - LAG * number

            @pl.when((k >= 0) & (k < count))
            def _():
                phase(k)

    def send(k):
        core_copy(k).start()

    return tick, send, staged


TILE = 256


def experts_kernel(
    n2_ref, g_ref, share_ref, w1_hbm, w2_hbm, moe_ref, dn2_ref, gate_ref, out,
    n2_turned, moe, dn2, act, d_ye, d_gu, w1, w2, w_sem, *scratch,
):
    tokens, width = n2_ref.shape
    owned, half = w2_hbm.shape[0], w2_hbm.shape[1]
    count = 3 * owned
    tiles = tokens // TILE
    lanes = gate_ref.shape[1]

    def fetch(e):
        slot = lax.rem(e, 2)
        return (
            pltpu.make_async_copy(w1_hbm.at[e], w1.at[slot], w_sem.at[0, slot]),
            pltpu.make_async_copy(w2_hbm.at[e], w2.at[slot], w_sem.at[1, slot]),
        )

    for copy in fetch(0):
        copy.start()
    greet(False)
    tick, send, staged = make_engine(count, out, scratch)
    gate_ref[...] = jnp.zeros_like(gate_ref)

    def over_tiles(body):
        @pl.loop(0, tiles)
        def _(i):
            body(pl.ds(pl.multiple_of(i * TILE, TILE), TILE))

    def prepare(rows):
        n2_turned[:, rows] = n2_ref[rows, :].T
        moe[rows, :] = jnp.zeros((TILE, width), f32)
        dn2[rows, :] = jnp.zeros((TILE, width), f32)

    over_tiles(prepare)

    def pick(table, e):
        lane = lax.broadcasted_iota(jnp.int32, table.shape, 1)
        return jnp.sum(jnp.where(lane == e, table, 0.0), axis=1, keepdims=True)

    def work(k):
        e, sub = k // 3, lax.rem(k, 3)
        slot = lax.rem(e, 2)

        @pl.when(sub == 0)
        def _():
            for copy in fetch(e):
                copy.wait()

            @pl.when(e + 1 < owned)
            def _():
                for copy in fetch(e + 1):
                    copy.start()

            def body(rows):
                gu = mm(n2_ref[rows, :], w1[slot])
                z, w = gu[:, :half], gu[:, half:]
                sg = jax.nn.sigmoid(z)
                silu = z * sg
                act[rows, :] = (silu * w).astype(bf16)
                dy = (pick(share_ref[rows, :], e) * g_ref[rows, :].astype(f32)).astype(bf16)
                d_ye[rows, :] = dy
                d_act = mm_nt(dy, w2[slot])
                d_gu[rows, :half] = (d_act * w * sg * (1.0 + z * (1.0 - sg))).astype(bf16)
                d_gu[rows, half:] = (d_act * silu).astype(bf16)

            over_tiles(body)
            for part in range(2):
                columns = slice(part * half // 2, (part + 1) * half // 2)
                grad = mm_tn(act[:, columns], d_ye[...])
                staged[lax.rem(k, 4), part] = grad.astype(bf16).reshape(staged.shape[2:])

        @pl.when(sub == 1)
        def _():
            def body(rows):
                ye = mm(act[rows, :], w2[slot]).astype(bf16).astype(f32)
                gate = jnp.sum(g_ref[rows, :].astype(f32) * ye, axis=1, keepdims=True)
                lane = lax.broadcasted_iota(jnp.int32, (TILE, lanes), 1)
                gate_ref[rows, :] = jnp.where(lane == e, gate, gate_ref[rows, :])
                moe[rows, :] += pick(share_ref[rows, :], e) * ye

            over_tiles(body)

        @pl.when(sub == 2)
        def _():
            def body(rows):
                dn2[rows, :] += mm_nt(d_gu[rows, :], w1[slot]).astype(bf16).astype(f32)

            over_tiles(body)

        @pl.when(sub > 0)
        def _():
            @pl.loop(0, 2)
            def _(part):
                first = pl.multiple_of((2 * (sub - 1) + part) * (half // 2), half // 2)
                grad = mm(n2_turned[pl.ds(first, half // 2), :], d_gu[...])
                staged[lax.rem(k, 4), part] = grad.astype(bf16).reshape(staged.shape[2:])

    @pl.loop(0, count + PHASES * LAG)
    def _(t):
        tick(t)

        @pl.when(t < count)
        def _():
            work(t)
            send(t)

        @pl.when(t == count)
        def _():
            def finish(rows):
                moe_ref[rows, :] = moe[rows, :].astype(bf16)
                dn2_ref[rows, :] = dn2[rows, :].astype(bf16)

            over_tiles(finish)


def experts(n2, grad, share, w_in, w_out):
    tokens, width = n2.shape
    owned, half = w_out.shape[:2]
    quarter = half // 8
    shape = jax.ShapeDtypeStruct
    vmem = pl.BlockSpec(memory_space=pltpu.VMEM)
    hbm = pl.BlockSpec(memory_space=pl.ANY)
    return pl.pallas_call(
        experts_kernel,
        out_shape=(
            shape((tokens, width), bf16),
            shape((tokens, width), bf16),
            shape((tokens, owned), f32),
            shape((3 * owned, 2, 4, quarter, width), bf16),
        ),
        in_specs=[vmem, vmem, vmem, hbm, hbm],
        out_specs=[vmem, vmem, vmem, hbm],
        scratch_shapes=[
            pltpu.VMEM((width, tokens), bf16),
            pltpu.VMEM((tokens, width), f32),
            pltpu.VMEM((tokens, width), f32),
            pltpu.VMEM((tokens, half), bf16),
            pltpu.VMEM((tokens, width), bf16),
            pltpu.VMEM((tokens, 2 * half), bf16),
            pltpu.VMEM((2, width, 2 * half), bf16),
            pltpu.VMEM((2, half, width), bf16),
            pltpu.SemaphoreType.DMA((2, 2)),
            *engine_scratch(quarter, width),
        ],
        compiler_params=pltpu.CompilerParams(
            collective_id=1, has_side_effects=True, vmem_limit_bytes=62 * MIB
        ),
        cost_estimate=cost(18 * tokens * width * half * owned, 6 * w_in.size),
        name="experts",
    )(n2, grad, share, w_in, w_out)


def expert_pass(n2, grad, share, w_in, w_out):
    half = w_out.shape[0]
    gu = mm(n2, w_in)
    z, w = gu[:, :half], gu[:, half:]
    sg = jax.nn.sigmoid(z)
    act = (z * sg * w).astype(bf16)
    ye = mm(act, w_out).astype(bf16).astype(f32)
    d_gate = jnp.sum(grad * ye, axis=1)
    d_ye = (share * grad).astype(bf16)
    g_out = mm_tn(act, d_ye).astype(bf16)
    d_act = mm_nt(d_ye, w_out)
    d_gu = jnp.concatenate(
        [d_act * w * sg * (1.0 + z * (1.0 - sg)), d_act * z * sg], axis=1
    ).astype(bf16)
    g_in = mm_tn(n2, d_gu).astype(bf16)
    d_xe = mm_nt(d_gu, w_in).astype(bf16).astype(f32)
    return share * ye, d_gate, g_in, g_out, d_xe


def all_experts(n2, grad, share, w_in, w_out):
    moe = jnp.zeros(n2.shape, f32)
    d_n2 = jnp.zeros_like(moe)
    d_gate, g_in, g_out = [], [], []
    for i in range(w_in.shape[0]):
        y, dg, gi, go, dx = expert_pass(
            n2, grad.astype(f32), share[:, i : i + 1], w_in[i], w_out[i]
        )
        moe, d_n2 = moe + y, d_n2 + dx
        d_gate.append(dg)
        g_in.append(gi)
        g_out.append(go)
    g_in, g_out = lax.psum((jnp.stack(g_in), jnp.stack(g_out)), "replica")
    return moe, d_n2, jnp.stack(d_gate, 1), g_in.astype(f32), g_out.astype(f32)


def on_device(
    layer_input, document_numbers, routes, norm_attn, w_query, key_weight, value_weight, w_out,
    norm_moe, w_router, expert_in, expert_out, cotangent,
):
    rows, width = layer_input.shape
    group = lax.axis_index("group")
    first = group * rows
    owned = expert_in.shape[0]
    kv_width = KEY_VALUE_HEADS * HEAD_SIZE

    seg_all = gather(document_numbers)
    position = lax.dynamic_slice_in_dim(doc_positions(seg_all), first, rows, 0)
    cosine, sine = turn_tables(position)
    small = gather(jnp.concatenate([norm_attn[:, None], norm_moe[:, None], w_router], axis=1))
    gain_attn = small[:, 0].astype(f32)[None, :]
    gain_moe = small[:, 1].astype(f32)[None, :]
    router = small[:, 2:]
    w_qkv = gather(jnp.concatenate([w_query, key_weight, value_weight], axis=1))
    wo = gather(w_out)
    grad_all = gather(cotangent)

    n1, q, k, v = project(layer_input, gain_attn, w_qkv, cosine, sine)
    kv_all = gather(jnp.concatenate([k, v], axis=1))
    k_all, v_all = kv_all[:, :kv_width], kv_all[:, kv_width:]
    first_row = jnp.full((1,), first, jnp.int32)
    seg_q, seg_k = document_numbers[:, None], seg_all[None, :]
    ao = attend(first_row, q, k_all, v_all, seg_q, seg_k)

    x = layer_input.astype(f32)
    h = x + mm(ao, wo)
    r2 = rms_factor(h)
    n2 = (h * r2 * gain_moe).astype(bf16)
    logits = mm(n2, router)
    chosen = jnp.any(routes[:, :, None] == jnp.arange(EXPERTS, dtype=jnp.int32), axis=1)
    picked = jnp.where(chosen, logits, MASKED)
    e = jnp.where(chosen, jnp.exp(picked - jnp.max(picked, axis=1, keepdims=True)), 0.0)
    share = e / jnp.sum(e, axis=1, keepdims=True)

    n2_all = gather(n2)
    share_all = lax.dynamic_slice_in_dim(gather(share), group * owned, owned, 1)
    if lax.axis_size("replica") == 16 and n2_all.shape[0] % TILE == 0:
        moe, d_n2_all, d_gate, summed = experts(n2_all, grad_all, share_all, expert_in, expert_out)
        summed = summed.reshape(owned, 3, -1, width).astype(f32)
        g_out, g_in = summed[:, 0], summed[:, 1:].reshape(expert_in.shape)
    else:
        moe, d_n2_all, d_gate, g_in, g_out = all_experts(
            n2_all, grad_all, share_all, expert_in, expert_out
        )
    d_gate = lax.dynamic_update_slice_in_dim(
        jnp.zeros((n2_all.shape[0], EXPERTS), f32), d_gate, group * owned, 1
    )
    d_gate = lax.psum_scatter(d_gate, "group", scatter_dimension=0, tiled=True)
    layer_output = (h + owner_sum(moe).astype(f32)).astype(bf16)

    d_logits = (share * (d_gate - jnp.sum(share * d_gate, axis=1, keepdims=True))).astype(bf16)
    g_router = mm_tn(n2, d_logits)
    d_n2 = owner_sum(d_n2_all).astype(f32) + mm_nt(d_logits, router)
    g_gain_moe = jnp.sum(h * r2 * d_n2, axis=0)
    c = d_n2 * gain_moe
    d_h = cotangent.astype(f32) + r2 * (
        c - h * r2 * r2 * jnp.mean(c * h, axis=-1, keepdims=True)
    )
    d_y = d_h.astype(bf16)
    g_wo = mm_tn(ao, d_y).astype(bf16)
    d_o = mm_nt(d_y, wo).astype(bf16)

    dq, dk_all, dv_all = attend_grad(first_row, q, k_all, v_all, d_o, seg_q, seg_k)
    dkv = owner_sum(jnp.concatenate([dk_all, dv_all], axis=1))
    g_qkv, grad_input, g_gain_attn = project_grad(
        dq, dkv[:, :kv_width], dkv[:, kv_width:], n1, w_qkv, cosine, sine, layer_input,
        gain_attn, d_h,
    )

    g_attn = owner_sum(jnp.concatenate([g_qkv, g_wo], axis=1))
    g_small = owner_sum(
        jnp.concatenate([g_gain_attn.reshape(-1, 1), g_gain_moe[:, None], g_router], axis=1)
    )
    g_attn, g_small = (t.astype(f32) for t in lax.psum((g_attn, g_small), "replica"))
    q_width = QUERY_HEADS * HEAD_SIZE
    return (
        layer_output,
        grad_input,
        g_small[:, 0],
        g_attn[:, :q_width],
        g_attn[:, q_width : q_width + kv_width],
        g_attn[:, q_width + kv_width : q_width + 2 * kv_width],
        g_attn[:, q_width + 2 * kv_width :],
        g_small[:, 1],
        g_small[:, 2:],
        g_in,
        g_out,
    )


def solution(mesh):
    tokens, weights = P(("replica", "group"), None), P("group", None)
    in_specs = (
        tokens, P(("replica", "group")), tokens, P("group"), weights, weights, weights, weights,
        P("group"), weights, P("group", None, None), P("group", None, None), tokens,
    )
    out_specs = (
        tokens, tokens, P("group"), weights, weights, weights, weights, P("group"), weights,
        P("group", None, None), P("group", None, None),
    )
    return jax.shard_map(
        on_device, mesh=mesh, in_specs=in_specs, out_specs=out_specs, check_vma=False
    )
```

```python
import functools

import jax
import jax.numpy as jnp
from jax import lax
from jax.experimental import pallas as pl
from jax.experimental.pallas import tpu as pltpu
from jax.sharding import PartitionSpec as P

QUERY_HEADS = 16
KEY_VALUE_HEADS = 8
HEAD_SIZE = 64
EXPERTS = 16
EPS = 1e-06
MASKED = -1e30
SCALE = HEAD_SIZE ** (-0.5)

f32 = jnp.float32
bf16 = jnp.bfloat16
MIB = 1 << 20


def mm(a, b):
    return lax.dot_general(a, b, (((1,), (0,)), ((), ())), preferred_element_type=f32)


def mm_nt(a, b):
    return lax.dot_general(a, b, (((1,), (1,)), ((), ())), preferred_element_type=f32)


def mm_tn(a, b):
    return lax.dot_general(a, b, (((0,), (0,)), ((), ())), preferred_element_type=f32)


def params(mib):
    return pltpu.CompilerParams(vmem_limit_bytes=mib * MIB)


def cost(flops, moved):
    return pl.CostEstimate(flops=int(flops), bytes_accessed=int(moved), transcendentals=0)


def doc_positions(seg_ids):
    length = seg_ids.shape[0]
    index = jnp.arange(length, dtype=jnp.int32)
    previous = jnp.concatenate([seg_ids[:1] - 1, seg_ids[:-1]])
    is_start = (seg_ids != previous) | (index == 0)
    start = lax.cummax(jnp.where(is_start, index, 0), axis=0)
    return index - start


def turn_tables(position):
    half = HEAD_SIZE // 2
    exponent = jnp.arange(half, dtype=f32) * (-2.0 / HEAD_SIZE)
    inv_freq = jnp.power(10000.0, exponent)
    angles = position.astype(f32)[:, None] * inv_freq[None, :]
    cosine, sine = jnp.cos(angles), jnp.sin(angles)
    return (
        jnp.concatenate([cosine] * 4, axis=1),
        jnp.concatenate([-sine, sine, -sine, sine], axis=1),
    )


def swap_halves(t):
    lane = lax.broadcasted_iota(jnp.int32, t.shape, 1)
    return jnp.where(
        lane % HEAD_SIZE < HEAD_SIZE // 2, pltpu.roll(t, 96, 1), pltpu.roll(t, 32, 1)
    )


def qkv_kernel(x_ref, gain_ref, w_ref, cos_ref, sin_ref, n1_ref, q_ref, k_ref, v_ref):
    x = x_ref[...].astype(f32)
    factor = lax.rsqrt(jnp.mean(x * x, axis=-1, keepdims=True) + EPS)
    n1 = (x * factor * gain_ref[...]).astype(bf16)
    n1_ref[...] = n1
    cosine, sine = cos_ref[...], sin_ref[...]
    q_width, k_width = q_ref.shape[1], k_ref.shape[1]
    for start in range(0, q_width + k_width, 256):
        lin = mm(n1, w_ref[:, start : start + 256])
        for part in (0, 128):
            t = lin[:, part : part + 128]
            turned = (t * cosine + swap_halves(t) * sine).astype(bf16)
            at = start + part
            if at < q_width:
                q_ref[:, at : at + 128] = turned
            else:
                k_ref[:, at - q_width : at - q_width + 128] = turned
    v_ref[...] = mm(n1, w_ref[:, q_width + k_width :]).astype(bf16)


def project(x, gain, w, cosine, sine):
    rows, width = x.shape
    q_width, k_width = QUERY_HEADS * HEAD_SIZE, KEY_VALUE_HEADS * HEAD_SIZE
    shape = jax.ShapeDtypeStruct
    return pl.pallas_call(
        qkv_kernel,
        out_shape=(
            shape((rows, width), bf16),
            shape((rows, q_width), bf16),
            shape((rows, k_width), bf16),
            shape((rows, k_width), bf16),
        ),
        compiler_params=params(40),
        cost_estimate=cost(2 * rows * width * w.shape[1], 2 * w.size + 8 * x.size),
        name="project",
    )(x, gain, w, cosine, sine)


def qkv_grad_kernel(
    dq_ref, dk_ref, dv_ref, n1_ref, w_ref, cos_ref, sin_ref, x_ref, gain_ref, dh_ref,
    gw_ref, gx_ref, gg_ref, lin_ref,
):
    cosine, sine = cos_ref[...], sin_ref[...]
    q_width, k_width = dq_ref.shape[1], dk_ref.shape[1]
    for ref, width, base in ((dq_ref, q_width, 0), (dk_ref, k_width, q_width)):
        for at in range(0, width, 128):
            t = ref[:, at : at + 128].astype(f32)
            turned = (t * cosine - swap_halves(t) * sine).astype(bf16)
            lin_ref[:, base + at : base + at + 128] = turned
    lin_ref[:, q_width + k_width :] = dv_ref[...].astype(bf16)
    total = q_width + 2 * k_width
    n1 = n1_ref[...]
    for at in range(0, total, 512):
        gw_ref[:, at : at + 512] = mm_tn(n1, lin_ref[:, at : at + 512]).astype(bf16)
    dn1 = mm_nt(lin_ref[...], w_ref[...])
    x = x_ref[...].astype(f32)
    factor = lax.rsqrt(jnp.mean(x * x, axis=-1, keepdims=True) + EPS)
    gg_ref[...] = jnp.sum(x * factor * dn1, axis=0, keepdims=True)
    c = dn1 * gain_ref[...]
    mean = jnp.mean(c * x, axis=-1, keepdims=True)
    gx_ref[...] = dh_ref[...] + factor * (c - x * (factor * factor * mean))


def project_grad(dq, dk, dv, n1, w, cosine, sine, x, gain, dh):
    rows, width = x.shape
    shape = jax.ShapeDtypeStruct
    return pl.pallas_call(
        qkv_grad_kernel,
        out_shape=(
            shape(w.shape, bf16),
            shape((rows, width), f32),
            shape((1, width), f32),
        ),
        scratch_shapes=[pltpu.VMEM((rows, w.shape[1]), bf16)],
        compiler_params=params(56),
        cost_estimate=cost(4 * rows * width * w.shape[1], 4 * w.size + 16 * x.size),
        name="project_grad",
    )(dq, dk, dv, n1, w, cosine, sine, x, gain, dh)


def visible_bias(first_ref, seg_q_ref, seg_k_ref, bias_ref):
    rows, keys = bias_ref.shape
    row = first_ref[0] + lax.broadcasted_iota(jnp.int32, (rows, keys), 0)
    col = lax.broadcasted_iota(jnp.int32, (rows, keys), 1)
    seen = (seg_q_ref[...] == seg_k_ref[...]) & (row >= col)
    bias_ref[...] = jnp.where(seen, 0.0, MASKED).astype(f32)


def attend_kernel(first_ref, q_ref, k_ref, v_ref, seg_q_ref, seg_k_ref, o_ref, bias_ref):
    @pl.when(pl.program_id(0) == 0)
    def _():
        visible_bias(first_ref, seg_q_ref, seg_k_ref, bias_ref)

    bias = bias_ref[...]
    for head in range(4):
        at, kv = head * HEAD_SIZE, head // 2 * HEAD_SIZE
        s = mm_nt(q_ref[:, at : at + HEAD_SIZE], k_ref[:, kv : kv + HEAD_SIZE]) * SCALE + bias
        e = jnp.exp(s - jnp.max(s, axis=1, keepdims=True))
        total = jnp.sum(e, axis=1, keepdims=True)
        o = mm(e.astype(bf16), v_ref[:, kv : kv + HEAD_SIZE]) / total
        o_ref[:, at : at + HEAD_SIZE] = o.astype(bf16)


def attend(first, q, k, v, seg_q, seg_k):
    rows, width = q.shape
    keys = k.shape[0]
    wide = pl.BlockSpec((rows, 256), lambda i, first: (0, i))
    narrow = pl.BlockSpec((keys, 128), lambda i, first: (0, i))
    return pl.pallas_call(
        attend_kernel,
        out_shape=jax.ShapeDtypeStruct((rows, width), bf16),
        grid_spec=pltpu.PrefetchScalarGridSpec(
            num_scalar_prefetch=1,
            grid=(width // 256,),
            in_specs=[
                wide,
                narrow,
                narrow,
                pl.BlockSpec((rows, 1), lambda i, first: (0, 0)),
                pl.BlockSpec((1, keys), lambda i, first: (0, 0)),
            ],
            out_specs=wide,
            scratch_shapes=[pltpu.VMEM((rows, keys), f32)],
        ),
        compiler_params=params(48),
        cost_estimate=cost(16 * rows * keys * width, 4 * q.size + 4 * k.size),
        name="attend",
    )(first, q, k, v, seg_q, seg_k)


def attend_grad_kernel(
    first_ref, q_ref, k_ref, v_ref, do_ref, seg_q_ref, seg_k_ref,
    dq_ref, dk_ref, dv_ref, bias_ref,
):
    @pl.when(pl.program_id(0) == 0)
    def _():
        visible_bias(first_ref, seg_q_ref, seg_k_ref, bias_ref)

    bias = bias_ref[...]
    for pair in range(2):
        kv = pair * HEAD_SIZE
        k, v = k_ref[:, kv : kv + HEAD_SIZE], v_ref[:, kv : kv + HEAD_SIZE]
        dk = dv = None
        for head in (2 * pair, 2 * pair + 1):
            at = head * HEAD_SIZE
            q, do = q_ref[:, at : at + HEAD_SIZE], do_ref[:, at : at + HEAD_SIZE]
            s = mm_nt(q, k) * SCALE + bias
            e = jnp.exp(s - jnp.max(s, axis=1, keepdims=True))
            p = e * (1.0 / jnp.sum(e, axis=1, keepdims=True))
            dp = mm_nt(do, v)
            delta = jnp.sum(p * dp, axis=1, keepdims=True)
            ds = (p * (dp - delta) * SCALE).astype(bf16)
            dq_ref[:, at : at + HEAD_SIZE] = mm(ds, k)
            dk_part, dv_part = mm_tn(ds, q), mm_tn(p.astype(bf16), do)
            dk = dk_part if dk is None else dk + dk_part
            dv = dv_part if dv is None else dv + dv_part
        dk_ref[:, kv : kv + HEAD_SIZE] = dk.astype(bf16)
        dv_ref[:, kv : kv + HEAD_SIZE] = dv.astype(bf16)


def attend_grad(first, q, k, v, do, seg_q, seg_k):
    rows, width = q.shape
    keys = k.shape[0]
    wide = pl.BlockSpec((rows, 256), lambda i, first: (0, i))
    narrow = pl.BlockSpec((keys, 128), lambda i, first: (0, i))
    shape = jax.ShapeDtypeStruct
    return pl.pallas_call(
        attend_grad_kernel,
        out_shape=(
            shape((rows, width), f32),
            shape(k.shape, bf16),
            shape(k.shape, bf16),
        ),
        grid_spec=pltpu.PrefetchScalarGridSpec(
            num_scalar_prefetch=1,
            grid=(width // 256,),
            in_specs=[
                wide,
                narrow,
                narrow,
                wide,
                pl.BlockSpec((rows, 1), lambda i, first: (0, 0)),
                pl.BlockSpec((1, keys), lambda i, first: (0, 0)),
            ],
            out_specs=[wide, narrow, narrow],
            scratch_shapes=[pltpu.VMEM((rows, keys), f32)],
        ),
        compiler_params=params(56),
        cost_estimate=cost(40 * rows * keys * width // 4, 8 * q.size + 8 * k.size),
        name="attend_grad",
    )(first, q, k, v, do, seg_q, seg_k)


def gather(value):
    return lax.all_gather(value, "group", axis=0, tiled=True)


def owner_sum(value):
    return lax.psum_scatter(value.astype(bf16), "group", scatter_dimension=0, tiled=True)


def rms_factor(values):
    return lax.rsqrt(jnp.mean(values * values, axis=-1, keepdims=True) + EPS)


LAG = 2
PHASES = 7
SEMS = 8
(CORE, X_A, IN_B, IN_A, HALF_B, MID_A, RUNG_B, OUT_A, BACK_B, SPREAD_A, OUT_B, JOIN, KINDS) = range(13)
(Y_N2, Y_SHARE, Y_DN2, Y_MOE, Y_GATE, Y_DKV, Y_WEIGHT, Y_KINDS) = (0, 1, 2, 3, 4, 5, 6, 9)


def engine_scratch(quarter, width):
    def vmem(*shape):
        return pltpu.VMEM((*shape, quarter, width), bf16)

    return [
        vmem(4, 4),
        vmem(4, 4),
        vmem(4),
        vmem(8, 2),
        vmem(8),
        vmem(4),
        vmem(4),
        vmem(4),
        vmem(LAG, 4),
        vmem(LAG),
        vmem(LAG, 2),
        vmem(LAG),
        vmem(LAG),
        vmem(LAG),
        vmem(LAG),
        pltpu.SemaphoreType.DMA((KINDS, SEMS)),
        pltpu.SemaphoreType.DMA((KINDS, SEMS)),
        pltpu.SemaphoreType.DMA((3, SEMS)),
    ]


class Place:
    def __init__(self):
        r = lax.axis_index("replica")
        self.core, self.x, z = lax.rem(r, 2), lax.rem(r // 2, 2), r // 4
        self.group = lax.axis_index("group")
        self.inner = (z == 1) | (z == 2)
        self.outer = jnp.logical_not(self.inner)
        self.late = z // 2
        up = (z == 0) | (z == 2)
        self.core_peer = {"replica": r + 1 - 2 * self.core}
        self.x_peer = {"replica": r + 2 - 4 * self.x}
        self.line_peer = {"replica": jnp.where(up, r + 4, r - 4)}
        self.mid_peer = {"replica": jnp.where(z == 1, r + 4, r - 4)}
        self.y_peer = {"group": 1 - self.group}

    def greet(self):
        barrier = pltpu.get_barrier_semaphore()

        def signal(peer):
            pl.semaphore_signal(
                barrier, inc=1, device_id=peer, device_id_type=pl.DeviceIdType.MESH
            )

        for peer in (self.core_peer, self.x_peer, self.line_peer, self.y_peer):
            signal(peer)

        @pl.when(self.inner)
        def _():
            signal(self.mid_peer)
            pl.semaphore_wait(barrier, 5)

        @pl.when(self.outer)
        def _():
            pl.semaphore_wait(barrier, 4)


def remote_copy(src, dst, send_sem, recv_sem, peer):
    return pltpu.make_async_remote_copy(
        src_ref=src, dst_ref=dst, send_sem=send_sem, recv_sem=recv_sem, device_id=peer,
        device_id_type=pl.DeviceIdType.MESH,
    )


def make_engine(place, count, split, stage, out, scratch, late_piece):
    (mine, got_core, got_x, got_end_b, got_end_a, got_mid_b, got_mid_a, got_rung,
     summed, a_x, b_end, a_end, b_mid, a_all, b_all, send_sem, recv_sem, copy_sem) = scratch
    core, x, inner, outer, late = place.core, place.x, place.inner, place.outer, place.late

    def remote(kind, k, src, dst, peer):
        slot = lax.rem(k, SEMS)
        return remote_copy(src, dst, send_sem.at[kind, slot], recv_sem.at[kind, slot], peer)

    def local(kind, k, src, dst):
        return pltpu.make_async_copy(src, dst, copy_sem.at[kind, lax.rem(k, SEMS)])

    def core_copy(k):
        return remote(
            CORE, k, stage.at[k, 1 - core], got_core.at[lax.rem(k, 4)], place.core_peer
        )

    def mine_copy(k):
        return local(2, k, stage.at[k, core], mine.at[lax.rem(k, 4)])

    def x_copy(k):
        return remote(
            X_A, k, summed.at[lax.rem(k, LAG), 1 - x], got_x.at[lax.rem(k, 4)], place.x_peer
        )

    def in_b_copy(k):
        return remote(
            IN_B, k, summed.at[lax.rem(k, LAG), pl.ds(2, 2)], got_end_b.at[lax.rem(k, 8)],
            place.line_peer,
        )

    def in_a_copy(k):
        return remote(
            IN_A, k, a_x.at[lax.rem(k, LAG)], got_end_a.at[lax.rem(k, 8)], place.line_peer
        )

    def half_b_copy(k):
        return remote(
            HALF_B, k, b_end.at[lax.rem(k, LAG), 1 - late], got_mid_b.at[lax.rem(k, 4)],
            place.mid_peer,
        )

    def mid_a_copy(k):
        return remote(
            MID_A, k, a_end.at[lax.rem(k, LAG)], got_mid_a.at[lax.rem(k, 4)], place.mid_peer
        )

    def rung_copy(k):
        return remote(
            RUNG_B, k, b_mid.at[lax.rem(k, LAG)], got_rung.at[lax.rem(k, 4)], place.x_peer
        )

    def out_a_copy(k):
        return remote(OUT_A, k, a_all.at[lax.rem(k, LAG)], out.at[k, core, x], place.line_peer)

    def back_b_copy(k, quarter):
        return remote(
            BACK_B, k, b_all.at[lax.rem(k, LAG)], out.at[k, core, quarter], place.mid_peer
        )

    def spread_copy(k, quarter):
        return remote(SPREAD_A, k, out.at[k, core, x], out.at[k, core, quarter], place.x_peer)

    def out_b_copy(k):
        part = out.at[k, core, pl.ds(2, 2)]
        return remote(OUT_B, k, part, part, place.line_peer)

    def join_copy(k, half):
        return remote(JOIN, k, out.at[k, core], out.at[k, half], place.core_peer)

    def keep_a(k):
        return local(0, k, a_all.at[lax.rem(k, LAG)], out.at[k, core, x])

    def keep_b(k):
        return local(1, k, b_all.at[lax.rem(k, LAG)], out.at[k, core, 2 + late])

    def phase1(k):
        i = lax.rem(k, LAG)

        @pl.when(k < split)
        def _():
            mine_copy(k).wait()
            core_copy(k).wait()
            summed[i] = mine[lax.rem(k, 4)] + got_core[lax.rem(k, 4)]

        if count > split:

            @pl.when(k >= split)
            def _():
                copy, own, other = late_piece(k)
                copy.wait()
                summed[i] = own[...] + other[...]

        x_copy(k).start()

        @pl.when(outer)
        def _():
            in_b_copy(k).start()

    def phase2(k):
        i = lax.rem(k, LAG)
        x_copy(k).wait()
        a_x[i] = summed[i, x] + got_x[lax.rem(k, 4)]

        @pl.when(outer)
        def _():
            in_a_copy(k).start()
            in_b_copy(k).wait_send()

        @pl.when(inner)
        def _():
            in_b_copy(k).wait_recv()
            b_end[i] = summed[i, 2:4] + got_end_b[lax.rem(k, 8)]
            half_b_copy(k).start()

    def phase3(k):
        i = lax.rem(k, LAG)

        @pl.when(outer)
        def _():
            in_a_copy(k).wait_send()

        @pl.when(inner)
        def _():
            in_a_copy(k).wait_recv()
            a_end[i] = a_x[i] + got_end_a[lax.rem(k, 8)]
            mid_a_copy(k).start()
            half_b_copy(k).wait()
            b_mid[i] = b_end[i, late] + got_mid_b[lax.rem(k, 4)]
            rung_copy(k).start()

    def phase4(k):
        i = lax.rem(k, LAG)

        @pl.when(inner)
        def _():
            mid_a_copy(k).wait()
            a_all[i] = a_end[i] + got_mid_a[lax.rem(k, 4)]
            out_a_copy(k).start()
            keep_a(k).start()
            rung_copy(k).wait()
            b_all[i] = b_mid[i] + got_rung[lax.rem(k, 4)]
            back_b_copy(k, 2 + late).start()
            keep_b(k).start()

    def phase5(k):
        @pl.when(outer)
        def _():
            out_a_copy(k).wait_recv()

        @pl.when(inner)
        def _():
            keep_a(k).wait()
            out_a_copy(k).wait_send()

        spread_copy(k, x).start()

        @pl.when(inner)
        def _():
            keep_b(k).wait()
            back_b_copy(k, 2 + late).wait_send()
            back_b_copy(k, 3 - late).wait_recv()
            out_b_copy(k).start()

    def phase6(k):
        spread_copy(k, x).wait_send()
        spread_copy(k, 1 - x).wait_recv()

        @pl.when(outer)
        def _():
            out_b_copy(k).wait_recv()

        @pl.when(inner)
        def _():
            out_b_copy(k).wait_send()

        join_copy(k, core).start()

    def phase7(k):
        join_copy(k, core).wait_send()
        join_copy(k, 1 - core).wait_recv()

    phases = (phase1, phase2, phase3, phase4, phase5, phase6, phase7)

    def tick(t):
        for number in range(PHASES, 0, -1):
            k = t - LAG * number

            @pl.when((k >= 0) & (k < count))
            def _():
                phases[number - 1](k)

    def send(k):
        @pl.when(k < split)
        def _():
            core_copy(k).start()
            mine_copy(k).start()

        if count > split:

            @pl.when((k >= split) & (k < count))
            def _():
                late_piece(k)[0].start()

    return tick, send


def make_small_sum(place, values, got, send_sem, recv_sem):
    def copy(i, peer):
        return remote_copy(values.at[i], got.at[i], send_sem.at[i], recv_sem.at[i], peer)

    peers = (
        place.core_peer, place.x_peer, place.y_peer, place.line_peer, place.mid_peer,
        place.line_peer,
    )

    def add(i):
        values[i + 1] = values[i] + got[i]

    def step(i):
        if 1 <= i <= 3:
            copy(i - 1, peers[i - 1]).wait()
            add(i - 1)
        if i <= 2:
            copy(i, peers[i]).start()
        if i == 3:

            @pl.when(place.outer)
            def _():
                copy(3, peers[3]).start()

        if i == 4:

            @pl.when(place.outer)
            def _():
                copy(3, peers[3]).wait_send()

            @pl.when(place.inner)
            def _():
                copy(3, peers[3]).wait_recv()
                add(3)
                copy(4, peers[4]).start()

        if i == 5:

            @pl.when(place.inner)
            def _():
                copy(4, peers[4]).wait()
                add(4)
                copy(5, peers[5]).start()

        if i == 6:

            @pl.when(place.inner)
            def _():
                copy(5, peers[5]).wait_send()

            @pl.when(place.outer)
            def _():
                copy(5, peers[5]).wait_recv()
                values[5] = got[5]

    return step


TILE = 256


def backward_kernel(
    n2_hbm, g_hbm, h_hbm, ao_hbm, wo_hbm, q_hbm, kv_hbm, n1_hbm, wqkv_hbm, x_hbm, w1_hbm, w2_hbm,
    share_own, router, gain_moe, gain_attn, seg_q, seg_k, cosine, sine,
    y_ref, gx_ref, small_ref, out, stage,
    moe, dn2, share, gate, got_gate, y_send, y_got, got_kv, got_core_w, got_y_w, small, got_small,
    piece, piece_sem, w_sem, load_sem, ys_sem, yr_sem, cs_sem, cr_sem, ss_sem, sr_sem, *scratch,
):
    rows, width = n2_hbm.shape
    tokens = 2 * rows
    owned, half = w2_hbm.shape[0], w2_hbm.shape[1]
    pieces = 3 * owned
    count = pieces + 3
    place = Place()
    group, core = place.group, place.core
    here = pl.multiple_of(group * rows, rows)
    there = pl.multiple_of((1 - group) * rows, rows)

    def load(*pairs):
        copies = [
            pltpu.make_async_copy(src, dst, load_sem.at[i]) for i, (src, dst) in enumerate(pairs)
        ]
        for copy in copies:
            copy.start()
        for copy in copies:
            copy.wait()

    def y_copy(kind, src, dst):
        return remote_copy(src, dst, ys_sem.at[kind], yr_sem.at[kind], place.y_peer)

    def over_tiles(first, number, body):
        @pl.loop(0, number)
        def _(i):
            body(pl.ds(pl.multiple_of(first + i * TILE, TILE), TILE))

    def shifted(tile, by):
        return pl.ds(pl.multiple_of(tile.start + by, TILE), TILE)

    def after_core(gw):
        def late_piece(k):
            j = k - pieces
            copy = y_copy(Y_WEIGHT + j, gw.at[j, 1 - group, core], got_y_w.at[j])
            return copy, gw.at[j, group, core], got_y_w.at[j]

        return late_piece

    def fetch(w1, w2, e):
        slot = lax.rem(e, 2)
        return (
            pltpu.make_async_copy(w1_hbm.at[e], w1.at[slot], w_sem.at[0, slot]),
            pltpu.make_async_copy(w2_hbm.at[e], w2.at[slot], w_sem.at[1, slot]),
        )

    tick, send = make_engine(place, count, count, stage, out, scratch, None)

    def advance(t):
        tick(t)

        @pl.when(t < pieces)
        def _():
            send(t)

    def advance_all(first, number):
        @pl.loop(first, first + number)
        def _(t):
            advance(t)

    def expert_part(n2, n2_turned, g, act, d_ye, d_gu, w1, w2):
        for copy in fetch(w1, w2, 0):
            copy.start()
        place.greet()
        n2_copy = y_copy(Y_N2, n2_hbm, n2.at[pl.ds(here, rows)])
        n2_copy.start()
        share[pl.ds(here, rows), :] = share_own[...]
        share_copy = y_copy(
            Y_SHARE, share.at[pl.ds(here, rows)], share.at[pl.ds(here, rows)]
        )
        share_copy.start()
        load((g_hbm, g), (n2_hbm, n2.at[pl.ds(here, rows)]))
        gate[...] = jnp.zeros_like(gate)

        def prepare(tile):
            n2_turned[:, tile] = n2[tile, :].T
            moe[tile, :] = jnp.zeros((TILE, width), f32)
            dn2[tile, :] = jnp.zeros((TILE, width), f32)

        over_tiles(here, rows // TILE, prepare)
        n2_copy.wait()
        share_copy.wait()
        over_tiles(there, rows // TILE, prepare)

        def pick(table, e):
            lane = lax.broadcasted_iota(jnp.int32, table.shape, 1)
            return jnp.sum(
                jnp.where(lane == group * owned + e, table, 0.0), axis=1, keepdims=True
            )

        def keep(k):
            slot = lax.rem(k, 2)
            return pltpu.make_async_copy(piece.at[slot], stage.at[k], piece_sem.at[slot])

        def work(k):
            e, sub = k // 3, lax.rem(k, 3)
            slot = lax.rem(e, 2)

            @pl.when(k == 2)
            def _():
                keep(1).wait()

            @pl.when(k >= 4)
            def _():
                keep(k - 2).wait()

            @pl.when(sub == 0)
            def _():
                for copy in fetch(w1, w2, e):
                    copy.wait()

                @pl.when(e + 1 < owned)
                def _():
                    for copy in fetch(w1, w2, e + 1):
                        copy.start()

                def body(tile):
                    gu = mm(n2[tile, :], w1[slot])
                    z, w = gu[:, :half], gu[:, half:]
                    sg = jax.nn.sigmoid(z)
                    silu = z * sg
                    act[tile, :] = (silu * w).astype(bf16)
                    dy = (pick(share[tile, :], e) * g[tile, :].astype(f32)).astype(bf16)
                    d_ye[tile, :] = dy
                    d_act = mm_nt(dy, w2[slot])
                    d_gu[tile, :half] = (d_act * w * sg * (1.0 + z * (1.0 - sg))).astype(bf16)
                    d_gu[tile, half:] = (d_act * silu).astype(bf16)

                over_tiles(0, tokens // TILE, body)
                for part in range(2):
                    columns = slice(part * half // 2, (part + 1) * half // 2)
                    grad = mm_tn(act[:, columns], d_ye[...])
                    piece[lax.rem(k, 2), part] = grad.astype(bf16).reshape(piece.shape[2:])

            @pl.when(sub == 1)
            def _():
                def body(tile):
                    ye = mm(act[tile, :], w2[slot]).astype(bf16).astype(f32)
                    value = jnp.sum(g[tile, :].astype(f32) * ye, axis=1, keepdims=True)
                    lane = lax.broadcasted_iota(jnp.int32, (TILE, gate.shape[1]), 1)
                    gate[tile, :] = jnp.where(lane == group * owned + e, value, gate[tile, :])
                    moe[tile, :] += pick(share[tile, :], e) * ye

                over_tiles(0, tokens // TILE, body)

            @pl.when(sub == 2)
            def _():
                def body(tile):
                    dn2[tile, :] += mm_nt(d_gu[tile, :], w1[slot]).astype(bf16).astype(f32)

                over_tiles(0, tokens // TILE, body)

            @pl.when(sub > 0)
            def _():
                @pl.loop(0, 2)
                def _(part):
                    first = pl.multiple_of((2 * (sub - 1) + part) * (half // 2), half // 2)
                    grad = mm(n2_turned[pl.ds(first, half // 2), :], d_gu[...])
                    piece[lax.rem(k, 2), part] = grad.astype(bf16).reshape(piece.shape[2:])

            keep(k).start()

            @pl.when(k == 0)
            def _():
                keep(0).wait()

        @pl.loop(0, pieces)
        def _(k):
            work(k)

            @pl.when(lax.rem(k, 2) == 0)
            def _():
                advance(k // 2)

        keep(pieces - 2).wait()
        keep(pieces - 1).wait()

        def leave(tile):
            to = shifted(tile, -there)
            y_send[0, to, :] = dn2[tile, :].astype(bf16)
            y_send[1, to, :] = moe[tile, :].astype(bf16)

        over_tiles(there, rows // TILE, leave)

    wide = (tokens, width)
    pl.run_scoped(
        expert_part,
        pltpu.VMEM(wide, bf16),
        pltpu.VMEM((width, tokens), bf16),
        pltpu.VMEM(wide, bf16),
        pltpu.VMEM((tokens, half), bf16),
        pltpu.VMEM(wide, bf16),
        pltpu.VMEM((tokens, 2 * half), bf16),
        pltpu.VMEM((2, width, 2 * half), bf16),
        pltpu.VMEM((2, half, width), bf16),
    )
    t = pieces // 2
    dn2_copy = y_copy(Y_DN2, y_send.at[0], y_got.at[0])
    gate_copy = y_copy(Y_GATE, gate.at[pl.ds(there, rows)], got_gate)
    moe_copy = y_copy(Y_MOE, y_send.at[1], y_got.at[1])
    dn2_copy.start()
    gate_copy.start()
    moe_copy.start()
    advance_all(t, 3)
    t += 3

    def attention_part(gw, d_o, dkv):
        tail = gw.shape[3:]

        def store_rows(j, i, grad):
            gw[j, i // 2, i % 2] = grad.astype(bf16).reshape(tail)

        def middle(h, g, n2, ao, wo, d_y):
            load(
                (h_hbm, h), (g_hbm.at[pl.ds(here, rows)], g), (n2_hbm, n2), (ao_hbm, ao),
                (wo_hbm, wo),
            )
            dn2_copy.wait()
            gate_copy.wait()
            moe_copy.wait()
            small[0] = jnp.zeros(small.shape[1:], f32)

            def body(tile):
                own = shifted(tile, here)
                s = share_own[tile, :]
                dg = gate[own, :] + got_gate[tile, :]
                d_logits = (s * (dg - jnp.sum(s * dg, axis=1, keepdims=True))).astype(bf16)
                d_n2 = dn2[own, :] + y_got[0, tile, :].astype(f32) + mm_nt(d_logits, router[...])
                hidden = h[tile, :]
                factor = lax.rsqrt(jnp.mean(hidden * hidden, axis=-1, keepdims=True) + EPS)
                small[0, 0:EXPERTS, :] += mm_tn(d_logits, n2[tile, :])
                small[0, EXPERTS : EXPERTS + 1, :] += jnp.sum(
                    hidden * factor * d_n2, axis=0, keepdims=True
                )
                c = d_n2 * gain_moe[...]
                mean = jnp.mean(c * hidden, axis=-1, keepdims=True)
                d_h = g[tile, :].astype(f32) + factor * (c - hidden * (factor * factor * mean))
                dn2[shifted(tile, there), :] = d_h
                d_y[tile, :] = d_h.astype(bf16)
                d_o[tile, :] = mm_nt(d_h.astype(bf16), wo[...]).astype(bf16)
                y_ref[tile, :] = (
                    hidden + moe[own, :] + y_got[1, tile, :].astype(f32)
                ).astype(bf16)

            over_tiles(0, rows // TILE, body)
            for i in range(4):
                columns = slice(i * width // 4, (i + 1) * width // 4)
                store_rows(2, i, mm_tn(ao[:, columns], d_y[...]))

        pl.run_scoped(
            middle,
            pltpu.VMEM((rows, width), f32),
            *[pltpu.VMEM((rows, width), bf16)] * 3,
            pltpu.VMEM((width, width), bf16),
            pltpu.VMEM((rows, width), bf16),
        )
        advance(t)

        def heads(q, kv, bias):
            load((q_hbm, q), (kv_hbm, kv))
            row = here + lax.broadcasted_iota(jnp.int32, bias.shape, 0)
            col = lax.broadcasted_iota(jnp.int32, bias.shape, 1)
            seen = (seg_q[...] == seg_k[...]) & (row >= col)
            bias[...] = jnp.where(seen, 0.0, MASKED).astype(f32)

            @pl.loop(0, 4)
            def _(i):
                at_k = pl.ds(pl.multiple_of(i * 128, 128), 128)
                at_v = pl.ds(pl.multiple_of(width // 2 + i * 128, 128), 128)
                keys, values = kv[:, at_k], kv[:, at_v]
                dks, dvs = [], []
                for pair in range(2):
                    lanes = slice(pair * HEAD_SIZE, (pair + 1) * HEAD_SIZE)
                    key, value = keys[:, lanes], values[:, lanes]
                    at_q = pl.ds(pl.multiple_of(i * 256 + pair * 128, 128), 128)

                    def body(part, sums):
                        dk, dv = sums
                        tile = pl.ds(pl.multiple_of(part * TILE, TILE), TILE)
                        qs, dos = q[tile, at_q], d_o[tile, at_q]
                        dqs = []
                        for head in range(2):
                            lane = slice(head * HEAD_SIZE, (head + 1) * HEAD_SIZE)
                            qh, doh = qs[:, lane], dos[:, lane]
                            s = mm_nt(qh, key) * SCALE + bias[tile, :]
                            e = jnp.exp(s - jnp.max(s, axis=1, keepdims=True))
                            p = e * (1.0 / jnp.sum(e, axis=1, keepdims=True))
                            dp = mm_nt(doh, value)
                            delta = jnp.sum(p * dp, axis=1, keepdims=True)
                            ds = (p * (dp - delta) * SCALE).astype(bf16)
                            dqs.append(mm(ds, key))
                            dk = dk + mm_tn(ds, qh)
                            dv = dv + mm_tn(p.astype(bf16), doh)
                        moe[shifted(tile, there), at_q] = jnp.concatenate(dqs, axis=1)
                        return dk, dv

                    zero = jnp.zeros((kv.shape[0], HEAD_SIZE), f32)
                    dk, dv = lax.fori_loop(0, rows // TILE, body, (zero, zero))
                    dks.append(dk)
                    dvs.append(dv)
                dkv[:, at_k] = jnp.concatenate(dks, axis=1).astype(bf16)
                dkv[:, at_v] = jnp.concatenate(dvs, axis=1).astype(bf16)
                advance(t + 1 + i)

        pl.run_scoped(
            heads,
            pltpu.VMEM((rows, width), bf16),
            pltpu.VMEM((tokens, width), bf16),
            pltpu.VMEM((rows, tokens), f32),
        )

        def kv_copy():
            return y_copy(Y_DKV, dkv.at[pl.ds(0, rows)], got_kv)

        @pl.when(group == 1)
        def _():
            kv_copy().start()

        advance_all(t + 5, 3)

        @pl.when(group == 1)
        def _():
            kv_copy().wait_send()

        @pl.when(group == 0)
        def _():
            kv_copy().wait_recv()
            dkv[0:rows, :] = (dkv[0:rows, :].astype(f32) + got_kv[...].astype(f32)).astype(bf16)

        def projections(n1, wqkv, x_in, lin):
            load((n1_hbm, n1), (wqkv_hbm, wqkv), (x_hbm, x_in))
            own = pl.ds(here, rows)
            tiles = [(j, moe, pl.ds(there, rows), j) for j in range(0, width, 128)]
            tiles += [(width + j, dkv, own, j) for j in range(0, width // 2, 128)]
            for to, source, where, at in tiles:
                value = source[where, at : at + 128].astype(f32)
                turned = value * cosine[...] - swap_halves(value) * sine[...]
                lin[:, to : to + 128] = turned.astype(bf16)
            lin[:, 3 * width // 2 :] = dkv[own, width // 2 :]
            for j in range(2):
                for i in range(4):
                    columns = slice(i * width // 4, (i + 1) * width // 4)
                    store_rows(
                        j, i, mm_tn(n1[:, columns], lin[:, j * width : (j + 1) * width])
                    )
            for j in range(3):
                core_weight(j).start()

            def body(tile):
                dn1 = mm_nt(lin[tile, :], wqkv[...])
                xs = x_in[tile, :].astype(f32)
                factor = lax.rsqrt(jnp.mean(xs * xs, axis=-1, keepdims=True) + EPS)
                small[0, EXPERTS + 1 : EXPERTS + 2, :] += jnp.sum(
                    xs * factor * dn1, axis=0, keepdims=True
                )
                c = dn1 * gain_attn[...]
                mean = jnp.mean(c * xs, axis=-1, keepdims=True)
                gx_ref[tile, :] = dn2[shifted(tile, there), :] + factor * (
                    c - xs * (factor * factor * mean)
                )

            over_tiles(0, rows // TILE, body)

        def core_weight(j):
            return remote_copy(
                gw.at[j, :, 1 - core], got_core_w.at[j], cs_sem.at[j], cr_sem.at[j],
                place.core_peer,
            )

        pl.run_scoped(
            projections,
            pltpu.VMEM((rows, width), bf16),
            pltpu.VMEM((width, 2 * width), bf16),
            pltpu.VMEM((rows, width), bf16),
            pltpu.VMEM((rows, 2 * width), bf16),
        )
        advance_all(t + 8, pieces - t - 8)
        for j in range(3):
            core_weight(j).wait()
            for member in range(2):
                gw[j, member, core] += got_core_w[j, member]

        last_tick, last_send = make_engine(
            place, count, pieces, stage, out, scratch, after_core(gw)
        )
        small_step = make_small_sum(place, small, got_small, ss_sem, sr_sem)

        @pl.loop(pieces, count + PHASES * LAG)
        def _(now):
            last_tick(now)
            last_send(now)
            for i in range(7):

                @pl.when(now == pieces + i)
                def _():
                    small_step(i)

    pl.run_scoped(
        attention_part,
        pltpu.VMEM((3, 2, 2, *piece.shape[2:]), bf16),
        pltpu.VMEM((rows, width), bf16),
        pltpu.VMEM((tokens, width), bf16),
    )
    small_ref[...] = small[5]


def backward(
    n2, g_all, h, ao, wo, q, kv_all, n1, w_qkv, x, w_in, w_out, share, router, gain_moe, gain_attn,
    seg_q, seg_k, cosine, sine,
):
    rows, width = n2.shape
    owned, half = w_out.shape[:2]
    tokens, quarter = 2 * rows, half // 8
    pieces = 3 * owned
    shape = jax.ShapeDtypeStruct
    vmem = pl.BlockSpec(memory_space=pltpu.VMEM)
    hbm = pl.BlockSpec(memory_space=pl.ANY)
    dma = pltpu.SemaphoreType.DMA
    small_rows = EXPERTS + 8
    return pl.pallas_call(
        backward_kernel,
        out_shape=(
            shape((rows, width), bf16),
            shape((rows, width), f32),
            shape((small_rows, width), f32),
            shape((pieces + 3, 2, 4, quarter, width), bf16),
            shape((pieces, 2, 4, quarter, width), bf16),
        ),
        in_specs=[hbm] * 12 + [vmem] * 8,
        out_specs=[vmem, vmem, vmem, hbm, hbm],
        scratch_shapes=[
            pltpu.VMEM((tokens, width), f32),
            pltpu.VMEM((tokens, width), f32),
            pltpu.VMEM((tokens, EXPERTS), f32),
            pltpu.VMEM((tokens, EXPERTS), f32),
            pltpu.VMEM((rows, EXPERTS), f32),
            pltpu.VMEM((2, rows, width), bf16),
            pltpu.VMEM((2, rows, width), bf16),
            pltpu.VMEM((rows, width), bf16),
            pltpu.VMEM((3, 2, 4, quarter, width), bf16),
            pltpu.VMEM((3, 4, quarter, width), bf16),
            pltpu.VMEM((6, small_rows, width), f32),
            pltpu.VMEM((6, small_rows, width), f32),
            pltpu.VMEM((2, 2, 4, quarter, width), bf16),
            dma((2,)),
            dma((2, 2)),
            dma((5,)),
            dma((Y_KINDS,)),
            dma((Y_KINDS,)),
            dma((3,)),
            dma((3,)),
            dma((6,)),
            dma((6,)),
            *engine_scratch(quarter, width),
        ],
        compiler_params=pltpu.CompilerParams(
            collective_id=1, has_side_effects=True, vmem_limit_bytes=63 * MIB
        ),
        cost_estimate=cost(18 * tokens * width * half * owned, 6 * w_in.size),
        name="backward",
    )(
        n2, g_all, h, ao, wo, q, kv_all, n1, w_qkv, x, w_in, w_out, share, router, gain_moe,
        gain_attn, seg_q, seg_k, cosine, sine,
    )


def expert_pass(n2, grad, share, w_in, w_out):
    half = w_out.shape[0]
    gu = mm(n2, w_in)
    z, w = gu[:, :half], gu[:, half:]
    sg = jax.nn.sigmoid(z)
    act = (z * sg * w).astype(bf16)
    ye = mm(act, w_out).astype(bf16).astype(f32)
    d_gate = jnp.sum(grad * ye, axis=1)
    d_ye = (share * grad).astype(bf16)
    g_out = mm_tn(act, d_ye).astype(bf16)
    d_act = mm_nt(d_ye, w_out)
    d_gu = jnp.concatenate(
        [d_act * w * sg * (1.0 + z * (1.0 - sg)), d_act * z * sg], axis=1
    ).astype(bf16)
    g_in = mm_tn(n2, d_gu).astype(bf16)
    d_xe = mm_nt(d_gu, w_in).astype(bf16).astype(f32)
    return share * ye, d_gate, g_in, g_out, d_xe


def all_experts(n2, grad, share, w_in, w_out):
    moe = jnp.zeros(n2.shape, f32)
    d_n2 = jnp.zeros_like(moe)
    d_gate, g_in, g_out = [], [], []
    for i in range(w_in.shape[0]):
        y, dg, gi, go, dx = expert_pass(
            n2, grad.astype(f32), share[:, i : i + 1], w_in[i], w_out[i]
        )
        moe, d_n2 = moe + y, d_n2 + dx
        d_gate.append(dg)
        g_in.append(gi)
        g_out.append(go)
    g_in, g_out = lax.psum((jnp.stack(g_in), jnp.stack(g_out)), "replica")
    return moe, d_n2, jnp.stack(d_gate, 1), g_in.astype(f32), g_out.astype(f32)


def on_device(
    layer_input, document_numbers, routes, norm_attn, w_query, key_weight, value_weight, w_out,
    norm_moe, w_router, expert_in, expert_out, cotangent,
):
    rows, width = layer_input.shape
    group = lax.axis_index("group")
    first = group * rows
    owned = expert_in.shape[0]
    kv_width = KEY_VALUE_HEADS * HEAD_SIZE

    seg_all = gather(document_numbers)
    position = lax.dynamic_slice_in_dim(doc_positions(seg_all), first, rows, 0)
    cosine, sine = turn_tables(position)
    small = gather(jnp.concatenate([norm_attn[:, None], norm_moe[:, None], w_router], axis=1))
    gain_attn = small[:, 0].astype(f32)[None, :]
    gain_moe = small[:, 1].astype(f32)[None, :]
    router = small[:, 2:]
    w_qkv = gather(jnp.concatenate([w_query, key_weight, value_weight], axis=1))
    wo = gather(w_out)
    grad_all = gather(cotangent)

    n1, q, k, v = project(layer_input, gain_attn, w_qkv, cosine, sine)
    kv_all = gather(jnp.concatenate([k, v], axis=1))
    k_all, v_all = kv_all[:, :kv_width], kv_all[:, kv_width:]
    first_row = jnp.full((1,), first, jnp.int32)
    seg_q, seg_k = document_numbers[:, None], seg_all[None, :]
    ao = attend(first_row, q, k_all, v_all, seg_q, seg_k)

    x = layer_input.astype(f32)
    h = x + mm(ao, wo)
    r2 = rms_factor(h)
    n2 = (h * r2 * gain_moe).astype(bf16)
    logits = mm(n2, router)
    chosen = jnp.any(routes[:, :, None] == jnp.arange(EXPERTS, dtype=jnp.int32), axis=1)
    picked = jnp.where(chosen, logits, MASKED)
    e = jnp.where(chosen, jnp.exp(picked - jnp.max(picked, axis=1, keepdims=True)), 0.0)
    share = e / jnp.sum(e, axis=1, keepdims=True)

    q_width = QUERY_HEADS * HEAD_SIZE
    if lax.axis_size("replica") == 16 and lax.axis_size("group") == 2:
        layer_output, grad_input, small_sum, sums, _ = backward(
            n2, grad_all, h, ao, wo, q, kv_all, n1, w_qkv, layer_input, expert_in, expert_out,
            share, router, gain_moe, gain_attn, seg_q, seg_k, cosine, sine,
        )
        half = expert_out.shape[1]
        sums = sums.reshape(-1, half, width)
        pieces = sums[: 3 * owned].reshape(owned, 3, half, width)
        g_small = lax.dynamic_slice_in_dim(small_sum, group * (width // 2), width // 2, 1)
        return (
            layer_output,
            grad_input,
            g_small[EXPERTS + 1],
            sums[3 * owned].astype(f32),
            sums[3 * owned + 1][:, :kv_width].astype(f32),
            sums[3 * owned + 1][:, kv_width:].astype(f32),
            sums[3 * owned + 2].astype(f32),
            g_small[EXPERTS],
            g_small[:EXPERTS].T,
            pieces[:, 1:].reshape(expert_in.shape).astype(f32),
            pieces[:, 0].astype(f32),
        )

    n2_all = gather(n2)
    share_all = lax.dynamic_slice_in_dim(gather(share), group * owned, owned, 1)
    moe, d_n2_all, d_gate, g_in, g_out = all_experts(
        n2_all, grad_all, share_all, expert_in, expert_out
    )
    d_gate = lax.dynamic_update_slice_in_dim(
        jnp.zeros((n2_all.shape[0], EXPERTS), f32), d_gate, group * owned, 1
    )
    d_gate = lax.psum_scatter(d_gate, "group", scatter_dimension=0, tiled=True)
    layer_output = (h + owner_sum(moe).astype(f32)).astype(bf16)

    d_logits = (share * (d_gate - jnp.sum(share * d_gate, axis=1, keepdims=True))).astype(bf16)
    g_router = mm_tn(n2, d_logits)
    d_n2 = owner_sum(d_n2_all).astype(f32) + mm_nt(d_logits, router)
    g_gain_moe = jnp.sum(h * r2 * d_n2, axis=0)
    c = d_n2 * gain_moe
    d_h = cotangent.astype(f32) + r2 * (
        c - h * r2 * r2 * jnp.mean(c * h, axis=-1, keepdims=True)
    )
    d_y = d_h.astype(bf16)
    g_wo = mm_tn(ao, d_y).astype(bf16)
    d_o = mm_nt(d_y, wo).astype(bf16)

    dq, dk_all, dv_all = attend_grad(first_row, q, k_all, v_all, d_o, seg_q, seg_k)
    dkv = owner_sum(jnp.concatenate([dk_all, dv_all], axis=1))
    g_qkv, grad_input, g_gain_attn = project_grad(
        dq, dkv[:, :kv_width], dkv[:, kv_width:], n1, w_qkv, cosine, sine, layer_input,
        gain_attn, d_h,
    )

    g_attn = owner_sum(jnp.concatenate([g_qkv, g_wo], axis=1))
    g_small = owner_sum(
        jnp.concatenate([g_gain_attn.reshape(-1, 1), g_gain_moe[:, None], g_router], axis=1)
    )
    g_attn, g_small = (t.astype(f32) for t in lax.psum((g_attn, g_small), "replica"))
    return (
        layer_output,
        grad_input,
        g_small[:, 0],
        g_attn[:, :q_width],
        g_attn[:, q_width : q_width + kv_width],
        g_attn[:, q_width + kv_width : q_width + 2 * kv_width],
        g_attn[:, q_width + 2 * kv_width :],
        g_small[:, 1],
        g_small[:, 2:],
        g_in,
        g_out,
    )


def solution(mesh):
    tokens, weights = P(("replica", "group"), None), P("group", None)
    in_specs = (
        tokens, P(("replica", "group")), tokens, P("group"), weights, weights, weights, weights,
        P("group"), weights, P("group", None, None), P("group", None, None), tokens,
    )
    out_specs = (
        tokens, tokens, P("group"), weights, weights, weights, weights, P("group"), weights,
        P("group", None, None), P("group", None, None),
    )
    return jax.shard_map(
        on_device, mesh=mesh, in_specs=in_specs, out_specs=out_specs, check_vma=False
    )
```

```python
import functools

import jax
import jax.numpy as jnp
from jax import lax
from jax.experimental import pallas as pl
from jax.experimental.pallas import tpu as pltpu
from jax.sharding import PartitionSpec as P

QUERY_HEADS = 16
KEY_VALUE_HEADS = 8
HEAD_SIZE = 64
EXPERTS = 16
EPS = 1e-06
MASKED = -1e30
SCALE = HEAD_SIZE ** (-0.5)

f32 = jnp.float32
bf16 = jnp.bfloat16
MIB = 1 << 20


def mm(a, b):
    return lax.dot_general(a, b, (((1,), (0,)), ((), ())), preferred_element_type=f32)


def mm_nt(a, b):
    return lax.dot_general(a, b, (((1,), (1,)), ((), ())), preferred_element_type=f32)


def mm_tn(a, b):
    return lax.dot_general(a, b, (((0,), (0,)), ((), ())), preferred_element_type=f32)


def params(mib):
    return pltpu.CompilerParams(vmem_limit_bytes=mib * MIB)


def cost(flops, moved):
    return pl.CostEstimate(flops=int(flops), bytes_accessed=int(moved), transcendentals=0)


def doc_positions(seg_ids):
    length = seg_ids.shape[0]
    index = jnp.arange(length, dtype=jnp.int32)
    previous = jnp.concatenate([seg_ids[:1] - 1, seg_ids[:-1]])
    is_start = (seg_ids != previous) | (index == 0)
    start = lax.cummax(jnp.where(is_start, index, 0), axis=0)
    return index - start


def turn_tables(position):
    half = HEAD_SIZE // 2
    exponent = jnp.arange(half, dtype=f32) * (-2.0 / HEAD_SIZE)
    inv_freq = jnp.power(10000.0, exponent)
    angles = position.astype(f32)[:, None] * inv_freq[None, :]
    cosine, sine = jnp.cos(angles), jnp.sin(angles)
    return (
        jnp.concatenate([cosine] * 4, axis=1),
        jnp.concatenate([-sine, sine, -sine, sine], axis=1),
    )


def swap_halves(t):
    lane = lax.broadcasted_iota(jnp.int32, t.shape, 1)
    return jnp.where(
        lane % HEAD_SIZE < HEAD_SIZE // 2, pltpu.roll(t, 96, 1), pltpu.roll(t, 32, 1)
    )


def qkv_kernel(x_ref, gain_ref, w_ref, cos_ref, sin_ref, n1_ref, q_ref, k_ref, v_ref):
    x = x_ref[...].astype(f32)
    factor = lax.rsqrt(jnp.mean(x * x, axis=-1, keepdims=True) + EPS)
    n1 = (x * factor * gain_ref[...]).astype(bf16)
    n1_ref[...] = n1
    cosine, sine = cos_ref[...], sin_ref[...]
    q_width, k_width = q_ref.shape[1], k_ref.shape[1]
    for start in range(0, q_width + k_width, 256):
        lin = mm(n1, w_ref[:, start : start + 256])
        for part in (0, 128):
            t = lin[:, part : part + 128]
            turned = (t * cosine + swap_halves(t) * sine).astype(bf16)
            at = start + part
            if at < q_width:
                q_ref[:, at : at + 128] = turned
            else:
                k_ref[:, at - q_width : at - q_width + 128] = turned
    v_ref[...] = mm(n1, w_ref[:, q_width + k_width :]).astype(bf16)


def project(x, gain, w, cosine, sine):
    rows, width = x.shape
    q_width, k_width = QUERY_HEADS * HEAD_SIZE, KEY_VALUE_HEADS * HEAD_SIZE
    shape = jax.ShapeDtypeStruct
    return pl.pallas_call(
        qkv_kernel,
        out_shape=(
            shape((rows, width), bf16),
            shape((rows, q_width), bf16),
            shape((rows, k_width), bf16),
            shape((rows, k_width), bf16),
        ),
        compiler_params=params(40),
        cost_estimate=cost(2 * rows * width * w.shape[1], 2 * w.size + 8 * x.size),
        name="project",
    )(x, gain, w, cosine, sine)


def qkv_grad_kernel(
    dq_ref, dk_ref, dv_ref, n1_ref, w_ref, cos_ref, sin_ref, x_ref, gain_ref, dh_ref,
    gw_ref, gx_ref, gg_ref, lin_ref,
):
    cosine, sine = cos_ref[...], sin_ref[...]
    q_width, k_width = dq_ref.shape[1], dk_ref.shape[1]
    for ref, width, base in ((dq_ref, q_width, 0), (dk_ref, k_width, q_width)):
        for at in range(0, width, 128):
            t = ref[:, at : at + 128].astype(f32)
            turned = (t * cosine - swap_halves(t) * sine).astype(bf16)
            lin_ref[:, base + at : base + at + 128] = turned
    lin_ref[:, q_width + k_width :] = dv_ref[...].astype(bf16)
    total = q_width + 2 * k_width
    n1 = n1_ref[...]
    for at in range(0, total, 512):
        gw_ref[:, at : at + 512] = mm_tn(n1, lin_ref[:, at : at + 512]).astype(bf16)
    dn1 = mm_nt(lin_ref[...], w_ref[...])
    x = x_ref[...].astype(f32)
    factor = lax.rsqrt(jnp.mean(x * x, axis=-1, keepdims=True) + EPS)
    gg_ref[...] = jnp.sum(x * factor * dn1, axis=0, keepdims=True)
    c = dn1 * gain_ref[...]
    mean = jnp.mean(c * x, axis=-1, keepdims=True)
    gx_ref[...] = dh_ref[...] + factor * (c - x * (factor * factor * mean))


def project_grad(dq, dk, dv, n1, w, cosine, sine, x, gain, dh):
    rows, width = x.shape
    shape = jax.ShapeDtypeStruct
    return pl.pallas_call(
        qkv_grad_kernel,
        out_shape=(
            shape(w.shape, bf16),
            shape((rows, width), f32),
            shape((1, width), f32),
        ),
        scratch_shapes=[pltpu.VMEM((rows, w.shape[1]), bf16)],
        compiler_params=params(56),
        cost_estimate=cost(4 * rows * width * w.shape[1], 4 * w.size + 16 * x.size),
        name="project_grad",
    )(dq, dk, dv, n1, w, cosine, sine, x, gain, dh)


def visible_bias(first_ref, seg_q_ref, seg_k_ref, bias_ref):
    rows, keys = bias_ref.shape
    row = first_ref[0] + lax.broadcasted_iota(jnp.int32, (rows, keys), 0)
    col = lax.broadcasted_iota(jnp.int32, (rows, keys), 1)
    seen = (seg_q_ref[...] == seg_k_ref[...]) & (row >= col)
    bias_ref[...] = jnp.where(seen, 0.0, MASKED).astype(f32)


def attend_kernel(first_ref, q_ref, k_ref, v_ref, seg_q_ref, seg_k_ref, o_ref, bias_ref):
    @pl.when(pl.program_id(0) == 0)
    def _():
        visible_bias(first_ref, seg_q_ref, seg_k_ref, bias_ref)

    bias = bias_ref[...]
    for head in range(4):
        at, kv = head * HEAD_SIZE, head // 2 * HEAD_SIZE
        s = mm_nt(q_ref[:, at : at + HEAD_SIZE], k_ref[:, kv : kv + HEAD_SIZE]) * SCALE + bias
        e = jnp.exp(s - jnp.max(s, axis=1, keepdims=True))
        total = jnp.sum(e, axis=1, keepdims=True)
        o = mm(e.astype(bf16), v_ref[:, kv : kv + HEAD_SIZE]) / total
        o_ref[:, at : at + HEAD_SIZE] = o.astype(bf16)


def attend(first, q, k, v, seg_q, seg_k):
    rows, width = q.shape
    keys = k.shape[0]
    wide = pl.BlockSpec((rows, 256), lambda i, first: (0, i))
    narrow = pl.BlockSpec((keys, 128), lambda i, first: (0, i))
    return pl.pallas_call(
        attend_kernel,
        out_shape=jax.ShapeDtypeStruct((rows, width), bf16),
        grid_spec=pltpu.PrefetchScalarGridSpec(
            num_scalar_prefetch=1,
            grid=(width // 256,),
            in_specs=[
                wide,
                narrow,
                narrow,
                pl.BlockSpec((rows, 1), lambda i, first: (0, 0)),
                pl.BlockSpec((1, keys), lambda i, first: (0, 0)),
            ],
            out_specs=wide,
            scratch_shapes=[pltpu.VMEM((rows, keys), f32)],
        ),
        compiler_params=params(48),
        cost_estimate=cost(16 * rows * keys * width, 4 * q.size + 4 * k.size),
        name="attend",
    )(first, q, k, v, seg_q, seg_k)


def attend_grad_kernel(
    first_ref, q_ref, k_ref, v_ref, do_ref, seg_q_ref, seg_k_ref,
    dq_ref, dk_ref, dv_ref, bias_ref,
):
    @pl.when(pl.program_id(0) == 0)
    def _():
        visible_bias(first_ref, seg_q_ref, seg_k_ref, bias_ref)

    bias = bias_ref[...]
    for pair in range(2):
        kv = pair * HEAD_SIZE
        k, v = k_ref[:, kv : kv + HEAD_SIZE], v_ref[:, kv : kv + HEAD_SIZE]
        dk = dv = None
        for head in (2 * pair, 2 * pair + 1):
            at = head * HEAD_SIZE
            q, do = q_ref[:, at : at + HEAD_SIZE], do_ref[:, at : at + HEAD_SIZE]
            s = mm_nt(q, k) * SCALE + bias
            e = jnp.exp(s - jnp.max(s, axis=1, keepdims=True))
            p = e * (1.0 / jnp.sum(e, axis=1, keepdims=True))
            dp = mm_nt(do, v)
            delta = jnp.sum(p * dp, axis=1, keepdims=True)
            ds = (p * (dp - delta) * SCALE).astype(bf16)
            dq_ref[:, at : at + HEAD_SIZE] = mm(ds, k)
            dk_part, dv_part = mm_tn(ds, q), mm_tn(p.astype(bf16), do)
            dk = dk_part if dk is None else dk + dk_part
            dv = dv_part if dv is None else dv + dv_part
        dk_ref[:, kv : kv + HEAD_SIZE] = dk.astype(bf16)
        dv_ref[:, kv : kv + HEAD_SIZE] = dv.astype(bf16)


def attend_grad(first, q, k, v, do, seg_q, seg_k):
    rows, width = q.shape
    keys = k.shape[0]
    wide = pl.BlockSpec((rows, 256), lambda i, first: (0, i))
    narrow = pl.BlockSpec((keys, 128), lambda i, first: (0, i))
    shape = jax.ShapeDtypeStruct
    return pl.pallas_call(
        attend_grad_kernel,
        out_shape=(
            shape((rows, width), f32),
            shape(k.shape, bf16),
            shape(k.shape, bf16),
        ),
        grid_spec=pltpu.PrefetchScalarGridSpec(
            num_scalar_prefetch=1,
            grid=(width // 256,),
            in_specs=[
                wide,
                narrow,
                narrow,
                wide,
                pl.BlockSpec((rows, 1), lambda i, first: (0, 0)),
                pl.BlockSpec((1, keys), lambda i, first: (0, 0)),
            ],
            out_specs=[wide, narrow, narrow],
            scratch_shapes=[pltpu.VMEM((rows, keys), f32)],
        ),
        compiler_params=params(56),
        cost_estimate=cost(40 * rows * keys * width // 4, 8 * q.size + 8 * k.size),
        name="attend_grad",
    )(first, q, k, v, do, seg_q, seg_k)


def gather(value):
    return lax.all_gather(value, "group", axis=0, tiled=True)


def owner_sum(value):
    return lax.psum_scatter(value.astype(bf16), "group", scatter_dimension=0, tiled=True)


def rms_factor(values):
    return lax.rsqrt(jnp.mean(values * values, axis=-1, keepdims=True) + EPS)


LAG = 2
PHASES = 7
SEMS = 8
(CORE, X_A, IN_B, IN_A, HALF_B, MID_A, RUNG_B, OUT_A, BACK_B, SPREAD_A, OUT_B, JOIN, KINDS) = range(13)
(Y_N2, Y_SHARE, Y_DN2, Y_MOE, Y_GATE, Y_DKV, Y_WEIGHT, Y_KINDS) = (0, 1, 2, 3, 4, 5, 6, 9)


def engine_scratch(quarter, width):
    def vmem(*shape):
        return pltpu.VMEM((*shape, quarter, width), bf16)

    return [
        vmem(4, 4),
        vmem(4, 4),
        vmem(4),
        vmem(8, 2),
        vmem(8),
        vmem(4),
        vmem(4),
        vmem(4),
        vmem(LAG, 4),
        vmem(LAG),
        vmem(LAG, 2),
        vmem(LAG),
        vmem(LAG),
        vmem(LAG),
        vmem(LAG),
        pltpu.SemaphoreType.DMA((KINDS, SEMS)),
        pltpu.SemaphoreType.DMA((KINDS, SEMS)),
        pltpu.SemaphoreType.DMA((3, SEMS)),
    ]


class Place:
    def __init__(self):
        r = lax.axis_index("replica")
        self.core, self.x, z = lax.rem(r, 2), lax.rem(r // 2, 2), r // 4
        self.group = lax.axis_index("group")
        self.inner = (z == 1) | (z == 2)
        self.outer = jnp.logical_not(self.inner)
        self.late = z // 2
        up = (z == 0) | (z == 2)
        self.core_peer = {"replica": r + 1 - 2 * self.core}
        self.x_peer = {"replica": r + 2 - 4 * self.x}
        self.line_peer = {"replica": jnp.where(up, r + 4, r - 4)}
        self.mid_peer = {"replica": jnp.where(z == 1, r + 4, r - 4)}
        self.y_peer = {"group": 1 - self.group}

    def greet(self):
        barrier = pltpu.get_barrier_semaphore()

        def signal(peer):
            pl.semaphore_signal(
                barrier, inc=1, device_id=peer, device_id_type=pl.DeviceIdType.MESH
            )

        for peer in (self.core_peer, self.x_peer, self.line_peer, self.y_peer):
            signal(peer)

        @pl.when(self.inner)
        def _():
            signal(self.mid_peer)
            pl.semaphore_wait(barrier, 5)

        @pl.when(self.outer)
        def _():
            pl.semaphore_wait(barrier, 4)


def remote_copy(src, dst, send_sem, recv_sem, peer):
    return pltpu.make_async_remote_copy(
        src_ref=src, dst_ref=dst, send_sem=send_sem, recv_sem=recv_sem, device_id=peer,
        device_id_type=pl.DeviceIdType.MESH,
    )


def make_engine(place, count, split, split_of, stage, out, scratch, late_piece):
    (mine, got_core, got_x, got_end_b, got_end_a, got_mid_b, got_mid_a, got_rung,
     summed, a_x, b_end, a_end, b_mid, a_all, b_all, send_sem, recv_sem, copy_sem) = scratch
    core, x, inner, outer, late = place.core, place.x, place.inner, place.outer, place.late

    owned = split_of // 3

    def spot(k):
        e, sub = k // 3, lax.rem(k, 3)
        inner_spot = jnp.where(sub == 0, 2 * owned + e, 2 * e + sub - 1)
        return jnp.where(k < split_of, inner_spot, k)

    def remote(kind, k, src, dst, peer):
        slot = lax.rem(k, SEMS)
        return remote_copy(src, dst, send_sem.at[kind, slot], recv_sem.at[kind, slot], peer)

    def local(kind, k, src, dst):
        return pltpu.make_async_copy(src, dst, copy_sem.at[kind, lax.rem(k, SEMS)])

    def core_copy(k):
        return remote(
            CORE, k, stage.at[k, 1 - core], got_core.at[lax.rem(k, 4)], place.core_peer
        )

    def mine_copy(k):
        return local(2, k, stage.at[k, core], mine.at[lax.rem(k, 4)])

    def x_copy(k):
        return remote(
            X_A, k, summed.at[lax.rem(k, LAG), 1 - x], got_x.at[lax.rem(k, 4)], place.x_peer
        )

    def in_b_copy(k):
        return remote(
            IN_B, k, summed.at[lax.rem(k, LAG), pl.ds(2, 2)], got_end_b.at[lax.rem(k, 8)],
            place.line_peer,
        )

    def in_a_copy(k):
        return remote(
            IN_A, k, a_x.at[lax.rem(k, LAG)], got_end_a.at[lax.rem(k, 8)], place.line_peer
        )

    def half_b_copy(k):
        return remote(
            HALF_B, k, b_end.at[lax.rem(k, LAG), 1 - late], got_mid_b.at[lax.rem(k, 4)],
            place.mid_peer,
        )

    def mid_a_copy(k):
        return remote(
            MID_A, k, a_end.at[lax.rem(k, LAG)], got_mid_a.at[lax.rem(k, 4)], place.mid_peer
        )

    def rung_copy(k):
        return remote(
            RUNG_B, k, b_mid.at[lax.rem(k, LAG)], got_rung.at[lax.rem(k, 4)], place.x_peer
        )

    def out_a_copy(k):
        return remote(OUT_A, k, a_all.at[lax.rem(k, LAG)], out.at[spot(k), core, x], place.line_peer)

    def back_b_copy(k, quarter):
        return remote(
            BACK_B, k, b_all.at[lax.rem(k, LAG)], out.at[spot(k), core, quarter], place.mid_peer
        )

    def spread_copy(k, quarter):
        return remote(SPREAD_A, k, out.at[spot(k), core, x], out.at[spot(k), core, quarter], place.x_peer)

    def out_b_copy(k):
        part = out.at[spot(k), core, pl.ds(2, 2)]
        return remote(OUT_B, k, part, part, place.line_peer)

    def join_copy(k, half):
        return remote(JOIN, k, out.at[spot(k), core], out.at[spot(k), half], place.core_peer)

    def keep_a(k):
        return local(0, k, a_all.at[lax.rem(k, LAG)], out.at[spot(k), core, x])

    def keep_b(k):
        return local(1, k, b_all.at[lax.rem(k, LAG)], out.at[spot(k), core, 2 + late])

    def phase1(k):
        i = lax.rem(k, LAG)

        @pl.when(k < split)
        def _():
            mine_copy(k).wait()
            core_copy(k).wait()
            summed[i] = mine[lax.rem(k, 4)] + got_core[lax.rem(k, 4)]

        if count > split:

            @pl.when(k >= split)
            def _():
                copy, own, other = late_piece(k)
                copy.wait()
                summed[i] = own[...] + other[...]

        x_copy(k).start()

        @pl.when(outer)
        def _():
            in_b_copy(k).start()

    def phase2(k):
        i = lax.rem(k, LAG)
        x_copy(k).wait()
        a_x[i] = summed[i, x] + got_x[lax.rem(k, 4)]

        @pl.when(outer)
        def _():
            in_a_copy(k).start()
            in_b_copy(k).wait_send()

        @pl.when(inner)
        def _():
            in_b_copy(k).wait_recv()
            b_end[i] = summed[i, 2:4] + got_end_b[lax.rem(k, 8)]
            half_b_copy(k).start()

    def phase3(k):
        i = lax.rem(k, LAG)

        @pl.when(outer)
        def _():
            in_a_copy(k).wait_send()

        @pl.when(inner)
        def _():
            in_a_copy(k).wait_recv()
            a_end[i] = a_x[i] + got_end_a[lax.rem(k, 8)]
            mid_a_copy(k).start()
            half_b_copy(k).wait()
            b_mid[i] = b_end[i, late] + got_mid_b[lax.rem(k, 4)]
            rung_copy(k).start()

    def phase4(k):
        i = lax.rem(k, LAG)

        @pl.when(inner)
        def _():
            mid_a_copy(k).wait()
            a_all[i] = a_end[i] + got_mid_a[lax.rem(k, 4)]
            out_a_copy(k).start()
            keep_a(k).start()
            rung_copy(k).wait()
            b_all[i] = b_mid[i] + got_rung[lax.rem(k, 4)]
            back_b_copy(k, 2 + late).start()
            keep_b(k).start()

    def phase5(k):
        @pl.when(outer)
        def _():
            out_a_copy(k).wait_recv()

        @pl.when(inner)
        def _():
            keep_a(k).wait()
            out_a_copy(k).wait_send()

        spread_copy(k, x).start()

        @pl.when(inner)
        def _():
            keep_b(k).wait()
            back_b_copy(k, 2 + late).wait_send()
            back_b_copy(k, 3 - late).wait_recv()
            out_b_copy(k).start()

    def phase6(k):
        spread_copy(k, x).wait_send()
        spread_copy(k, 1 - x).wait_recv()

        @pl.when(outer)
        def _():
            out_b_copy(k).wait_recv()

        @pl.when(inner)
        def _():
            out_b_copy(k).wait_send()

        join_copy(k, core).start()

    def phase7(k):
        join_copy(k, core).wait_send()
        join_copy(k, 1 - core).wait_recv()

    phases = (phase1, phase2, phase3, phase4, phase5, phase6, phase7)

    def tick(t):
        for number in range(PHASES, 0, -1):
            k = t - LAG * number

            @pl.when((k >= 0) & (k < count))
            def _():
                phases[number - 1](k)

    def send(k):
        @pl.when(k < split)
        def _():
            core_copy(k).start()
            mine_copy(k).start()

        if count > split:

            @pl.when((k >= split) & (k < count))
            def _():
                late_piece(k)[0].start()

    return tick, send


def make_small_sum(place, values, got, send_sem, recv_sem):
    def copy(i, peer):
        return remote_copy(values.at[i], got.at[i], send_sem.at[i], recv_sem.at[i], peer)

    peers = (
        place.core_peer, place.x_peer, place.y_peer, place.line_peer, place.mid_peer,
        place.line_peer,
    )

    def add(i):
        values[i + 1] = values[i] + got[i]

    def step(i):
        if 1 <= i <= 3:
            copy(i - 1, peers[i - 1]).wait()
            add(i - 1)
        if i <= 2:
            copy(i, peers[i]).start()
        if i == 3:

            @pl.when(place.outer)
            def _():
                copy(3, peers[3]).start()

        if i == 4:

            @pl.when(place.outer)
            def _():
                copy(3, peers[3]).wait_send()

            @pl.when(place.inner)
            def _():
                copy(3, peers[3]).wait_recv()
                add(3)
                copy(4, peers[4]).start()

        if i == 5:

            @pl.when(place.inner)
            def _():
                copy(4, peers[4]).wait()
                add(4)
                copy(5, peers[5]).start()

        if i == 6:

            @pl.when(place.inner)
            def _():
                copy(5, peers[5]).wait_send()

            @pl.when(place.outer)
            def _():
                copy(5, peers[5]).wait_recv()
                values[5] = got[5]

    return step


TILE = 256
WIDE = 512


(F_SMALL, F_SEG, F_WQ, F_WK, F_WV, F_WO, F_GRAD, F_KV) = range(8)
F_KINDS = F_KV + 8
W_QKV, W_OUT = 0, 1
SMALL_ROWS = 32


def forward_kernel(
    x_hbm, wq_hbm, wk_hbm, wv_hbm, wo_hbm, g_hbm, small_own, seg_own, seg_column, routes, inv_freq,
    n1_ref, q_ref, ao_ref, h_ref, n2_ref, share_ref, lse_ref, cos_ref, sin_ref, seg_ref, router_ref,
    gain_ref, kv_hbm, g_all, w_all,
    x_in, w, kv, bias, small, seg, y_send, y_recv, x_send, x_recv, c_send, c_recv, load_sem,
):
    rows, width = x_in.shape
    own_rows = wq_hbm.shape[0]
    part = own_rows // 4
    kv_width = wk_hbm.shape[1]
    qkv_width = width + 2 * kv_width
    place = Place()
    group, core, x = place.group, place.core, place.x
    here = pl.multiple_of(group * rows, rows)
    there = pl.multiple_of((1 - group) * rows, rows)
    w_here = pl.multiple_of(group * own_rows, own_rows)
    w_there = pl.multiple_of((1 - group) * own_rows, own_rows)
    quarter = pl.multiple_of((2 * core + x) * part, part)

    loads = [
        (x_hbm, x_in),
        (wk_hbm, w.at[pl.ds(w_here, own_rows), pl.ds(width, kv_width)]),
        (wv_hbm, w.at[pl.ds(w_here, own_rows), pl.ds(width + kv_width, kv_width)]),
        (wq_hbm, w.at[pl.ds(w_here, own_rows), pl.ds(0, width)]),
        (wo_hbm, w.at[pl.ds(w_here, own_rows), pl.ds(qkv_width, width)]),
        (g_hbm, g_all.at[pl.ds(here, rows)]),
    ]
    loads = [
        pltpu.make_async_copy(src, dst, load_sem.at[i]) for i, (src, dst) in enumerate(loads)
    ]
    for copy in loads:
        copy.start()
    place.greet()

    def y_copy(kind, src, dst):
        return remote_copy(src, dst, y_send.at[kind], y_recv.at[kind], place.y_peer)

    def weight_copy(kind, src, column, columns):
        return y_copy(
            kind, src.at[pl.ds(quarter, part)],
            w.at[pl.ds(w_here + quarter, part), pl.ds(column, columns)],
        )

    def x_copy(i, column, columns):
        block = w.at[pl.ds(w_there + quarter, part), pl.ds(column, columns)]
        return remote_copy(block, block, x_send.at[i], x_recv.at[i], place.x_peer)

    def core_copy(i, column, columns):
        first = pl.multiple_of(w_there + 2 * core * part, 2 * part)
        block = w.at[pl.ds(first, 2 * part), pl.ds(column, columns)]
        return remote_copy(block, block, c_send.at[i], c_recv.at[i], place.core_peer)

    small_copy = y_copy(F_SMALL, small_own, small.at[group])
    seg_copy = y_copy(F_SEG, seg_own, seg.at[group])
    qkv_copies = [
        weight_copy(F_WK, wk_hbm, width, kv_width),
        weight_copy(F_WV, wv_hbm, width + kv_width, kv_width),
        weight_copy(F_WQ, wq_hbm, 0, width),
    ]
    wo_copy = weight_copy(F_WO, wo_hbm, qkv_width, width)
    grad_copy = y_copy(F_GRAD, g_hbm, g_all.at[pl.ds(here, rows)])
    for copy in (small_copy, seg_copy, *qkv_copies):
        copy.start()
    small[group] = small_own[...]
    seg[group] = seg_own[...]

    small_copy.wait()
    seg_copy.wait()
    seg_row = jnp.concatenate([seg[0, 0:1, :], seg[1, 0:1, :]], axis=1)
    seg_ref[...] = seg_row
    router_ref[...] = jnp.concatenate([small[0, 0:EXPERTS, :], small[1, 0:EXPERTS, :]], axis=1)
    gain_ref[...] = jnp.concatenate(
        [small[0, EXPERTS:, :], small[1, EXPERTS:, :]], axis=1
    ).astype(f32)[0 : gain_ref.shape[0]]
    row = here + lax.broadcasted_iota(jnp.int32, bias.shape, 0)
    col = lax.broadcasted_iota(jnp.int32, bias.shape, 1)
    same = seg_column[...] == seg_row
    bias[...] = jnp.where(same & (row >= col), 0.0, MASKED).astype(f32)
    position = jnp.sum(jnp.where(same & (row > col), 1.0, 0.0), axis=1, keepdims=True)
    angle = position * inv_freq[...]
    lane = lax.broadcasted_iota(jnp.int32, angle.shape, 1)
    cos_ref[...] = jnp.cos(angle)
    sine = jnp.sin(angle)
    sin_ref[...] = jnp.where(lax.rem(lane, HEAD_SIZE) < HEAD_SIZE // 2, -sine, sine)

    for copy in loads:
        copy.wait()
    xs = x_in[...].astype(f32)
    factor = lax.rsqrt(jnp.mean(xs * xs, axis=-1, keepdims=True) + EPS)
    n1_ref[...] = (xs * factor * gain_ref[0:1, :]).astype(bf16)

    for copy in qkv_copies:
        copy.wait()
    x_copy(W_QKV, 0, qkv_width).start()
    wo_copy.start()
    x_copy(W_QKV, 0, qkv_width).wait()
    core_copy(W_QKV, 0, qkv_width).start()
    core_copy(W_QKV, 0, qkv_width).wait()

    n1 = n1_ref[...]
    cosine, sine = cos_ref[...], sin_ref[...]

    def turned(column):
        lin = mm(n1, w[:, column : column + 256])
        return [
            (t * cosine + swap_halves(t) * sine).astype(bf16)
            for t in (lin[:, :128], lin[:, 128:])
        ]

    own = pl.ds(here, rows)

    def kv_copies(i):
        first = pl.multiple_of(i * 128, 128)
        return [
            y_copy(
                F_KV + 2 * i + j,
                kv.at[own, pl.ds(first + j * kv_width, 128)],
                kv.at[own, pl.ds(first + j * kv_width, 128)],
            )
            for j in range(2)
        ]

    for i in range(2):
        at = 256 * i
        kv[own, at : at + 128], kv[own, at + 128 : at + 256] = turned(width + at)
        lin = mm(n1, w[:, width + kv_width + at : width + kv_width + at + 256])
        kv[own, kv_width + at : kv_width + at + 256] = lin.astype(bf16)

        @pl.when(group == 0)
        def _():
            for j in (2 * i, 2 * i + 1):
                for copy in kv_copies(j):
                    copy.start()

    @pl.when(group == 0)
    def _():
        kv[rows:, :] = jnp.zeros((rows, kv.shape[1]), bf16)

    for at in range(0, width, 256):
        q_ref[:, at : at + 128], q_ref[:, at + 128 : at + 256] = turned(at)
    wo_copy.wait()
    x_copy(W_OUT, qkv_width, width).start()
    grad_copy.start()
    lse_ref[...] = jnp.zeros_like(lse_ref)

    @pl.loop(0, 4)
    def _(i):
        @pl.when(group == 1)
        def _():
            for copy in kv_copies(i):
                copy.wait_recv()

        @pl.when(i == 2)
        def _():
            x_copy(W_OUT, qkv_width, width).wait()
            core_copy(W_OUT, qkv_width, width).start()

        at_k = pl.ds(pl.multiple_of(i * 128, 128), 128)
        at_v = pl.ds(pl.multiple_of(kv_width + i * 128, 128), 128)
        keys, values = kv[:, at_k], kv[:, at_v]
        for pair in range(2):
            lanes = slice(pair * HEAD_SIZE, (pair + 1) * HEAD_SIZE)
            key, value = keys[:, lanes], values[:, lanes]
            at_q = pl.ds(pl.multiple_of(i * 256 + pair * 128, 128), 128)

            @pl.loop(0, rows // TILE)
            def _(number):
                tile = pl.ds(pl.multiple_of(number * TILE, TILE), TILE)
                s = mm_nt(two_heads(q_ref[tile, at_q]) * SCALE, key)
                s = s.reshape(2, TILE, -1) + bias[tile, :][None]
                peak = jnp.max(s, axis=2, keepdims=True)
                e = jnp.exp(s - peak)
                total = jnp.sum(e, axis=2, keepdims=True)
                o = mm(e.astype(bf16).reshape(2 * TILE, -1), value)
                o = o / total.reshape(2 * TILE, 1)
                ao_ref[tile, at_q] = side_by_side(o).astype(bf16)
                lse = peak + jnp.log(total)
                lane = lax.broadcasted_iota(jnp.int32, (TILE, QUERY_HEADS), 1)
                head = 4 * i + 2 * pair
                lse_ref[tile, :] = jnp.where(
                    lane == head, lse[0], jnp.where(lane == head + 1, lse[1], lse_ref[tile, :])
                )

    core_copy(W_OUT, qkv_width, width).wait()
    keep_w = pltpu.make_async_copy(w, w_all, load_sem.at[0])
    keep_kv = pltpu.make_async_copy(kv, kv_hbm, load_sem.at[1])
    keep_w.start()
    keep_kv.start()

    @pl.loop(0, rows // TILE)
    def _(number):
        tile = pl.ds(pl.multiple_of(number * TILE, TILE), TILE)
        h = x_in[tile, :].astype(f32) + mm(ao_ref[tile, :], w[:, qkv_width:])
        h_ref[tile, :] = h
        factor = lax.rsqrt(jnp.mean(h * h, axis=-1, keepdims=True) + EPS)
        n2 = (h * factor * gain_ref[1:2, :]).astype(bf16)
        n2_ref[tile, :] = n2
        logits = mm_nt(n2, router_ref[...])
        lane = lax.broadcasted_iota(jnp.int32, logits.shape, 1)
        named = routes[tile, :]
        chosen = named[:, 0:1] == lane
        for k in range(1, named.shape[1]):
            chosen = chosen | (named[:, k : k + 1] == lane)
        picked = jnp.where(chosen, logits, MASKED)
        e = jnp.exp(picked - jnp.max(picked, axis=1, keepdims=True))
        e = jnp.where(chosen, e, 0.0)
        share_ref[tile, :] = e / jnp.sum(e, axis=1, keepdims=True)

    keep_w.wait()
    keep_kv.wait()
    grad_copy.wait()

    @pl.when(group == 0)
    def _():
        for i in range(4):
            for copy in kv_copies(i):
                copy.wait_send()


def two_heads(t):
    return jnp.concatenate([t[:, :HEAD_SIZE], t[:, HEAD_SIZE:]], axis=0)


def side_by_side(t):
    half = t.shape[0] // 2
    return jnp.concatenate([t[:half], t[half:]], axis=1)


def forward(x, document_numbers, routes, gains, w_router, wq, wk, wv, wo, grad):
    rows, width = x.shape
    tokens, own_rows = 2 * rows, wq.shape[0]
    kv_width = wk.shape[1]
    small = jnp.concatenate(
        [w_router.T, *[gain[None] for gain in gains],
         jnp.zeros((SMALL_ROWS - EXPERTS - 2, own_rows), bf16)], axis=0,
    )
    exponent = (jnp.arange(128, dtype=jnp.int32) % (HEAD_SIZE // 2)).astype(f32)
    inv_freq = jnp.power(10000.0, exponent * (-2.0 / HEAD_SIZE))[None]
    shape = jax.ShapeDtypeStruct
    vmem = pl.BlockSpec(memory_space=pltpu.VMEM)
    hbm = pl.BlockSpec(memory_space=pl.ANY)
    dma = pltpu.SemaphoreType.DMA
    total = 2 * width + 2 * kv_width
    return pl.pallas_call(
        forward_kernel,
        out_shape=(
            shape((rows, width), bf16),
            shape((rows, width), bf16),
            shape((rows, width), bf16),
            shape((rows, width), f32),
            shape((rows, width), bf16),
            shape((rows, EXPERTS), f32),
            shape((rows, QUERY_HEADS), f32),
            shape((rows, 128), f32),
            shape((rows, 128), f32),
            shape((1, tokens), jnp.int32),
            shape((EXPERTS, width), bf16),
            shape((8, width), f32),
            shape((tokens, 2 * kv_width), bf16),
            shape((tokens, width), bf16),
            shape((width, total), bf16),
        ),
        in_specs=[hbm] * 6 + [vmem] * 5,
        out_specs=[vmem] * 12 + [hbm] * 3,
        scratch_shapes=[
            pltpu.VMEM((rows, width), bf16),
            pltpu.VMEM((width, total), bf16),
            pltpu.VMEM((tokens, 2 * kv_width), bf16),
            pltpu.VMEM((rows, tokens), f32),
            pltpu.VMEM((2, SMALL_ROWS, own_rows), bf16),
            pltpu.VMEM((2, 8, rows), jnp.int32),
            dma((F_KINDS,)),
            dma((F_KINDS,)),
            *[dma((2,))] * 4,
            dma((6,)),
        ],
        compiler_params=pltpu.CompilerParams(
            collective_id=2, has_side_effects=True, vmem_limit_bytes=56 * MIB
        ),
        cost_estimate=cost(2 * rows * width * total, 8 * width * total),
        name="forward",
    )(
        x, wq, wk, wv, wo, grad, small, jnp.broadcast_to(document_numbers[None], (8, rows)),
        document_numbers[:, None], routes, inv_freq,
    )


def backward_kernel(
    n2_hbm, g_hbm, h_hbm, ao_hbm, q_hbm, kv_hbm, n1_hbm, w_hbm, x_hbm, w1_hbm, w2_hbm,
    share_own, router, gains, lse, seg_q, seg_k, cosine, sine,
    y_ref, gx_ref, small_ref, out, stage,
    moe, dn2, share, gate, got_gate, y_send, y_got, got_kv, got_core_w, got_y_w, small, got_small,
    piece, piece_sem, w_sem, load_sem, ys_sem, yr_sem, cs_sem, cr_sem, ss_sem, sr_sem, *scratch,
):
    rows, width = n2_hbm.shape
    tokens = 2 * rows
    owned, half = w2_hbm.shape[0], w2_hbm.shape[1]
    pieces = 3 * owned
    count = pieces + 3
    place = Place()
    group, core = place.group, place.core
    here = pl.multiple_of(group * rows, rows)
    there = pl.multiple_of((1 - group) * rows, rows)

    def load(*pairs):
        copies = [
            pltpu.make_async_copy(src, dst, load_sem.at[i]) for i, (src, dst) in enumerate(pairs)
        ]
        for copy in copies:
            copy.start()
        for copy in copies:
            copy.wait()

    def y_copy(kind, src, dst):
        return remote_copy(src, dst, ys_sem.at[kind], yr_sem.at[kind], place.y_peer)

    def over_tiles(first, number, body, size=TILE):
        @pl.loop(0, number)
        def _(i):
            body(pl.ds(pl.multiple_of(first + i * size, size), size))

    def shifted(tile, by):
        return pl.ds(pl.multiple_of(tile.start + by, TILE), TILE)

    def after_core(gw):
        def late_piece(k):
            j = k - pieces
            copy = y_copy(Y_WEIGHT + j, gw.at[j, 1 - group, core], got_y_w.at[j])
            return copy, gw.at[j, group, core], got_y_w.at[j]

        return late_piece

    def fetch(w1, w2, e):
        slot = lax.rem(e, 2)
        return (
            pltpu.make_async_copy(w1_hbm.at[e], w1.at[slot], w_sem.at[0, slot]),
            pltpu.make_async_copy(w2_hbm.at[e], w2.at[slot], w_sem.at[1, slot]),
        )

    tick, send = make_engine(place, count, count, pieces, stage, out, scratch, None)

    def advance(t):
        tick(t)

        @pl.when(t < pieces)
        def _():
            send(t)

    def advance_all(first, number):
        @pl.loop(first, first + number)
        def _(t):
            advance(t)

    def expert_part(n2, n2_turned, g, act, d_ye, d_gu, w1, w2):
        for copy in fetch(w1, w2, 0):
            copy.start()
        place.greet()
        n2_copy = y_copy(Y_N2, n2_hbm, n2.at[pl.ds(here, rows)])
        n2_copy.start()
        share[pl.ds(here, rows), :] = share_own[...]
        share_copy = y_copy(
            Y_SHARE, share.at[pl.ds(here, rows)], share.at[pl.ds(here, rows)]
        )
        share_copy.start()
        load((g_hbm, g), (n2_hbm, n2.at[pl.ds(here, rows)]))
        gate[...] = jnp.zeros_like(gate)

        def prepare(tile):
            n2_turned[:, tile] = n2[tile, :].T
            moe[tile, :] = jnp.zeros((TILE, width), f32)
            dn2[tile, :] = jnp.zeros((TILE, width), f32)

        over_tiles(here, rows // TILE, prepare)
        n2_copy.wait()
        share_copy.wait()
        over_tiles(there, rows // TILE, prepare)

        def pick(table, e):
            lane = lax.broadcasted_iota(jnp.int32, table.shape, 1)
            return jnp.sum(
                jnp.where(lane == group * owned + e, table, 0.0), axis=1, keepdims=True
            )

        def keep(k):
            slot = lax.rem(k, 2)
            return pltpu.make_async_copy(piece.at[slot], stage.at[k], piece_sem.at[slot])

        def work(k):
            e, sub = k // 3, lax.rem(k, 3)
            slot = lax.rem(e, 2)

            @pl.when(k == 2)
            def _():
                keep(1).wait()

            @pl.when(k >= 4)
            def _():
                keep(k - 2).wait()

            @pl.when(sub == 0)
            def _():
                for copy in fetch(w1, w2, e):
                    copy.wait()

                @pl.when(e + 1 < owned)
                def _():
                    for copy in fetch(w1, w2, e + 1):
                        copy.start()

                def body(tile):
                    gu = mm(n2[tile, :], w1[slot])
                    z, w = gu[:, :half], gu[:, half:]
                    sg = jax.nn.sigmoid(z)
                    silu = z * sg
                    act[tile, :] = (silu * w).astype(bf16)
                    dy = (pick(share[tile, :], e) * g[tile, :].astype(f32)).astype(bf16)
                    d_ye[tile, :] = dy
                    d_act = mm_nt(dy, w2[slot])
                    d_gu[tile, :half] = (d_act * w * sg * (1.0 + z * (1.0 - sg))).astype(bf16)
                    d_gu[tile, half:] = (d_act * silu).astype(bf16)

                over_tiles(0, tokens // WIDE, body, WIDE)
                for part in range(2):
                    columns = slice(part * half // 2, (part + 1) * half // 2)
                    grad = mm_tn(act[:, columns], d_ye[...])
                    piece[lax.rem(k, 2), part] = grad.astype(bf16).reshape(piece.shape[2:])

            @pl.when(sub == 1)
            def _():
                def body(tile):
                    ye = mm(act[tile, :], w2[slot]).astype(bf16).astype(f32)
                    value = jnp.sum(g[tile, :].astype(f32) * ye, axis=1, keepdims=True)
                    lane = lax.broadcasted_iota(jnp.int32, (WIDE, gate.shape[1]), 1)
                    gate[tile, :] = jnp.where(lane == group * owned + e, value, gate[tile, :])
                    moe[tile, :] += pick(share[tile, :], e) * ye

                over_tiles(0, tokens // WIDE, body, WIDE)

            @pl.when(sub == 2)
            def _():
                def body(tile):
                    dn2[tile, :] += mm_nt(d_gu[tile, :], w1[slot]).astype(bf16).astype(f32)

                over_tiles(0, tokens // WIDE, body, WIDE)

            @pl.when(sub > 0)
            def _():
                @pl.loop(0, 2)
                def _(part):
                    first = pl.multiple_of((2 * (sub - 1) + part) * (half // 2), half // 2)
                    grad = mm(n2_turned[pl.ds(first, half // 2), :], d_gu[...])
                    piece[lax.rem(k, 2), part] = grad.astype(bf16).reshape(piece.shape[2:])

            keep(k).start()

            @pl.when(k == 0)
            def _():
                keep(0).wait()

        @pl.loop(0, pieces)
        def _(k):
            work(k)

            @pl.when(lax.rem(k, 2) == 0)
            def _():
                advance(k // 2)

        keep(pieces - 2).wait()
        keep(pieces - 1).wait()

        def leave(tile):
            to = shifted(tile, -there)
            y_send[0, to, :] = dn2[tile, :].astype(bf16)
            y_send[1, to, :] = moe[tile, :].astype(bf16)

        over_tiles(there, rows // TILE, leave)

    wide = (tokens, width)
    pl.run_scoped(
        expert_part,
        pltpu.VMEM(wide, bf16),
        pltpu.VMEM((width, tokens), bf16),
        pltpu.VMEM(wide, bf16),
        pltpu.VMEM((tokens, half), bf16),
        pltpu.VMEM(wide, bf16),
        pltpu.VMEM((tokens, 2 * half), bf16),
        pltpu.VMEM((2, width, 2 * half), bf16),
        pltpu.VMEM((2, half, width), bf16),
    )
    t = pieces // 2
    dn2_copy = y_copy(Y_DN2, y_send.at[0], y_got.at[0])
    gate_copy = y_copy(Y_GATE, gate.at[pl.ds(there, rows)], got_gate)
    moe_copy = y_copy(Y_MOE, y_send.at[1], y_got.at[1])
    dn2_copy.start()
    gate_copy.start()
    moe_copy.start()
    advance_all(t, 3)
    t += 3

    def attention_part(gw, d_o, dkv):
        tail = gw.shape[3:]

        def store_rows(j, i, grad):
            gw[j, i // 2, i % 2] = grad.astype(bf16).reshape(tail)

        def middle(h, g, n2, ao, wo, d_y):
            load(
                (h_hbm, h), (g_hbm.at[pl.ds(here, rows)], g), (n2_hbm, n2), (ao_hbm, ao),
                (w_hbm.at[:, pl.ds(2 * width, width)], wo),
            )
            dn2_copy.wait()
            gate_copy.wait()
            small[0] = jnp.zeros(small.shape[1:], f32)

            def body(tile):
                own = shifted(tile, here)
                s = share_own[tile, :]
                dg = gate[own, :] + got_gate[tile, :]
                d_logits = (s * (dg - jnp.sum(s * dg, axis=1, keepdims=True))).astype(bf16)
                d_n2 = dn2[own, :] + y_got[0, tile, :].astype(f32) + mm(d_logits, router[...])
                hidden = h[tile, :]
                factor = lax.rsqrt(jnp.mean(hidden * hidden, axis=-1, keepdims=True) + EPS)
                small[0, 0:EXPERTS, :] += mm_tn(d_logits, n2[tile, :])
                small[0, EXPERTS : EXPERTS + 1, :] += jnp.sum(
                    hidden * factor * d_n2, axis=0, keepdims=True
                )
                c = d_n2 * gains[1:2, :]
                mean = jnp.mean(c * hidden, axis=-1, keepdims=True)
                d_h = g[tile, :].astype(f32) + factor * (c - hidden * (factor * factor * mean))
                dn2[shifted(tile, there), :] = d_h
                d_y[tile, :] = d_h.astype(bf16)
                d_o[tile, :] = mm_nt(d_h.astype(bf16), wo[...]).astype(bf16)
                moe[own, :] += hidden

            over_tiles(0, rows // TILE, body)
            for i in range(4):
                columns = slice(i * width // 4, (i + 1) * width // 4)
                store_rows(2, i, mm_tn(ao[:, columns], d_y[...]))

        pl.run_scoped(
            middle,
            pltpu.VMEM((rows, width), f32),
            *[pltpu.VMEM((rows, width), bf16)] * 3,
            pltpu.VMEM((width, width), bf16),
            pltpu.VMEM((rows, width), bf16),
        )
        advance(t)

        def heads(q, ao, kv, bias):
            load((q_hbm, q), (kv_hbm, kv), (ao_hbm, ao))
            row = here + lax.broadcasted_iota(jnp.int32, bias.shape, 0)
            col = lax.broadcasted_iota(jnp.int32, bias.shape, 1)
            seen = (seg_q[...] == seg_k[...]) & (row >= col)
            bias[...] = jnp.where(seen, 0.0, MASKED).astype(f32)

            @pl.loop(0, 4)
            def _(i):
                at_k = pl.ds(pl.multiple_of(i * 128, 128), 128)
                at_v = pl.ds(pl.multiple_of(width // 2 + i * 128, 128), 128)
                keys, values = kv[:, at_k], kv[:, at_v]
                dks, dvs = [], []
                for pair in range(2):
                    lanes = slice(pair * HEAD_SIZE, (pair + 1) * HEAD_SIZE)
                    key, value = keys[:, lanes], values[:, lanes]
                    at_q = pl.ds(pl.multiple_of(i * 256 + pair * 128, 128), 128)

                    def body(part, sums):
                        dk, dv = sums
                        tile = pl.ds(pl.multiple_of(part * TILE, TILE), TILE)
                        qs = two_heads(q[tile, at_q]) * SCALE
                        dos = two_heads(d_o[tile, at_q])
                        os = two_heads(ao[tile, at_q])
                        delta = jnp.sum(
                            dos.astype(f32) * os.astype(f32), axis=1, keepdims=True
                        )
                        lane = lax.broadcasted_iota(jnp.int32, (TILE, QUERY_HEADS), 1)
                        peaks = jnp.concatenate(
                            [
                                jnp.sum(
                                    jnp.where(lane == 4 * i + 2 * pair + head, lse[tile, :], 0.0),
                                    axis=1, keepdims=True,
                                )
                                for head in range(2)
                            ],
                            axis=0,
                        )
                        s = mm_nt(qs, key) - peaks
                        s = s.reshape(2, TILE, -1) + bias[tile, :][None]
                        p = jnp.exp(s).reshape(2 * TILE, -1)
                        dp = mm_nt(dos, value)
                        ds = (p * (dp - delta)).astype(bf16)
                        dq = mm(ds, key) * SCALE
                        moe[shifted(tile, there), at_q] = side_by_side(dq)
                        return dk + mm_tn(qs, ds), dv + mm_tn(dos, p.astype(bf16))

                    zero = jnp.zeros((HEAD_SIZE, kv.shape[0]), f32)
                    dk, dv = lax.fori_loop(0, rows // TILE, body, (zero, zero))
                    dks.append(dk)
                    dvs.append(dv)
                dkv[:, at_k] = jnp.concatenate(dks, axis=0).T.astype(bf16)
                dkv[:, at_v] = jnp.concatenate(dvs, axis=0).T.astype(bf16)
                advance(t + 1 + i)

        pl.run_scoped(
            heads,
            pltpu.VMEM((rows, width), bf16),
            pltpu.VMEM((rows, width), bf16),
            pltpu.VMEM((tokens, width), bf16),
            pltpu.VMEM((rows, tokens), f32),
        )

        def kv_copy():
            return y_copy(Y_DKV, dkv.at[pl.ds(0, rows)], got_kv)

        @pl.when(group == 1)
        def _():
            kv_copy().start()

        advance_all(t + 5, 3)

        @pl.when(group == 1)
        def _():
            kv_copy().wait_send()

        @pl.when(group == 0)
        def _():
            kv_copy().wait_recv()
            dkv[0:rows, :] = (dkv[0:rows, :].astype(f32) + got_kv[...].astype(f32)).astype(bf16)

        def projections(n1, wqkv, x_in, lin):
            load((n1_hbm, n1), (w_hbm.at[:, pl.ds(0, 2 * width)], wqkv), (x_hbm, x_in))
            own = pl.ds(here, rows)
            tiles = [(j, moe, pl.ds(there, rows), j) for j in range(0, width, 128)]
            tiles += [(width + j, dkv, own, j) for j in range(0, width // 2, 128)]
            for to, source, where, at in tiles:
                value = source[where, at : at + 128].astype(f32)
                turned = value * cosine[...] - swap_halves(value) * sine[...]
                lin[:, to : to + 128] = turned.astype(bf16)
            lin[:, 3 * width // 2 :] = dkv[own, width // 2 :]
            for j in range(2):
                for i in range(4):
                    columns = slice(i * width // 4, (i + 1) * width // 4)
                    store_rows(
                        j, i, mm_tn(n1[:, columns], lin[:, j * width : (j + 1) * width])
                    )
            for j in range(3):
                core_weight(j).start()

            def body(tile):
                dn1 = mm_nt(lin[tile, :], wqkv[...])
                xs = x_in[tile, :].astype(f32)
                factor = lax.rsqrt(jnp.mean(xs * xs, axis=-1, keepdims=True) + EPS)
                small[0, EXPERTS + 1 : EXPERTS + 2, :] += jnp.sum(
                    xs * factor * dn1, axis=0, keepdims=True
                )
                c = dn1 * gains[0:1, :]
                mean = jnp.mean(c * xs, axis=-1, keepdims=True)
                gx_ref[tile, :] = dn2[shifted(tile, there), :] + factor * (
                    c - xs * (factor * factor * mean)
                )
                total = moe[shifted(tile, here), :] + y_got[1, tile, :].astype(f32)
                y_ref[tile, :] = total.astype(bf16)

            moe_copy.wait()
            over_tiles(0, rows // TILE, body)

        def core_weight(j):
            return remote_copy(
                gw.at[j, :, 1 - core], got_core_w.at[j], cs_sem.at[j], cr_sem.at[j],
                place.core_peer,
            )

        pl.run_scoped(
            projections,
            pltpu.VMEM((rows, width), bf16),
            pltpu.VMEM((width, 2 * width), bf16),
            pltpu.VMEM((rows, width), bf16),
            pltpu.VMEM((rows, 2 * width), bf16),
        )
        advance_all(t + 8, pieces - t - 8)
        for j in range(3):
            core_weight(j).wait()
            for member in range(2):
                gw[j, member, core] += got_core_w[j, member]

        last_tick, last_send = make_engine(
            place, count, pieces, pieces, stage, out, scratch, after_core(gw)
        )
        small_step = make_small_sum(place, small, got_small, ss_sem, sr_sem)

        @pl.loop(pieces, count + PHASES * LAG)
        def _(now):
            last_tick(now)
            last_send(now)
            for i in range(7):

                @pl.when(now == pieces + i)
                def _():
                    small_step(i)

    pl.run_scoped(
        attention_part,
        pltpu.VMEM((3, 2, 2, *piece.shape[2:]), bf16),
        pltpu.VMEM((rows, width), bf16),
        pltpu.VMEM((tokens, width), bf16),
    )
    small_ref[...] = small[5]


def widen_kernel(narrow_ref, wide_ref):
    wide_ref[...] = narrow_ref[...].astype(f32)


def widen(pieces, first, number):
    block = (1, *pieces.shape[1:])
    return pl.pallas_call(
        widen_kernel,
        out_shape=jax.ShapeDtypeStruct((number, *pieces.shape[1:]), f32),
        grid=(number,),
        in_specs=[pl.BlockSpec(block, lambda i: (first + i, 0, 0))],
        out_specs=pl.BlockSpec(block, lambda i: (i, 0, 0)),
        compiler_params=params(32),
        cost_estimate=cost(0, 6 * number * pieces[0].size),
        name="widen",
    )(pieces)


def backward(
    n2, g_all, h, ao, q, kv_all, n1, w_all, x, w_in, w_out, share, router, gains, lse, seg_q, seg_k,
    cosine, sine,
):
    rows, width = n2.shape
    owned, half = w_out.shape[:2]
    tokens, quarter = 2 * rows, half // 8
    pieces = 3 * owned
    shape = jax.ShapeDtypeStruct
    vmem = pl.BlockSpec(memory_space=pltpu.VMEM)
    hbm = pl.BlockSpec(memory_space=pl.ANY)
    dma = pltpu.SemaphoreType.DMA
    small_rows = EXPERTS + 8
    return pl.pallas_call(
        backward_kernel,
        out_shape=(
            shape((rows, width), bf16),
            shape((rows, width), f32),
            shape((small_rows, width), f32),
            shape((pieces + 3, 2, 4, quarter, width), bf16),
            shape((pieces, 2, 4, quarter, width), bf16),
        ),
        in_specs=[hbm] * 11 + [vmem] * 8,
        out_specs=[vmem, vmem, vmem, hbm, hbm],
        scratch_shapes=[
            pltpu.VMEM((tokens, width), f32),
            pltpu.VMEM((tokens, width), f32),
            pltpu.VMEM((tokens, EXPERTS), f32),
            pltpu.VMEM((tokens, EXPERTS), f32),
            pltpu.VMEM((rows, EXPERTS), f32),
            pltpu.VMEM((2, rows, width), bf16),
            pltpu.VMEM((2, rows, width), bf16),
            pltpu.VMEM((rows, width), bf16),
            pltpu.VMEM((3, 2, 4, quarter, width), bf16),
            pltpu.VMEM((3, 4, quarter, width), bf16),
            pltpu.VMEM((6, small_rows, width), f32),
            pltpu.VMEM((6, small_rows, width), f32),
            pltpu.VMEM((2, 2, 4, quarter, width), bf16),
            dma((2,)),
            dma((2, 2)),
            dma((5,)),
            dma((Y_KINDS,)),
            dma((Y_KINDS,)),
            dma((3,)),
            dma((3,)),
            dma((6,)),
            dma((6,)),
            *engine_scratch(quarter, width),
        ],
        compiler_params=pltpu.CompilerParams(
            collective_id=1, has_side_effects=True, vmem_limit_bytes=63 * MIB
        ),
        cost_estimate=cost(18 * tokens * width * half * owned, 6 * w_in.size),
        name="backward",
    )(
        n2, g_all, h, ao, q, kv_all, n1, w_all, x, w_in, w_out, share, router, gains, lse, seg_q,
        seg_k, cosine, sine,
    )


def expert_pass(n2, grad, share, w_in, w_out):
    half = w_out.shape[0]
    gu = mm(n2, w_in)
    z, w = gu[:, :half], gu[:, half:]
    sg = jax.nn.sigmoid(z)
    act = (z * sg * w).astype(bf16)
    ye = mm(act, w_out).astype(bf16).astype(f32)
    d_gate = jnp.sum(grad * ye, axis=1)
    d_ye = (share * grad).astype(bf16)
    g_out = mm_tn(act, d_ye).astype(bf16)
    d_act = mm_nt(d_ye, w_out)
    d_gu = jnp.concatenate(
        [d_act * w * sg * (1.0 + z * (1.0 - sg)), d_act * z * sg], axis=1
    ).astype(bf16)
    g_in = mm_tn(n2, d_gu).astype(bf16)
    d_xe = mm_nt(d_gu, w_in).astype(bf16).astype(f32)
    return share * ye, d_gate, g_in, g_out, d_xe


def all_experts(n2, grad, share, w_in, w_out):
    moe = jnp.zeros(n2.shape, f32)
    d_n2 = jnp.zeros_like(moe)
    d_gate, g_in, g_out = [], [], []
    for i in range(w_in.shape[0]):
        y, dg, gi, go, dx = expert_pass(
            n2, grad.astype(f32), share[:, i : i + 1], w_in[i], w_out[i]
        )
        moe, d_n2 = moe + y, d_n2 + dx
        d_gate.append(dg)
        g_in.append(gi)
        g_out.append(go)
    g_in, g_out = lax.psum((jnp.stack(g_in), jnp.stack(g_out)), "replica")
    return moe, d_n2, jnp.stack(d_gate, 1), g_in.astype(f32), g_out.astype(f32)


def on_device(
    layer_input, document_numbers, routes, norm_attn, w_query, key_weight, value_weight, w_out,
    norm_moe, w_router, expert_in, expert_out, cotangent,
):
    rows, width = layer_input.shape
    group = lax.axis_index("group")
    first = group * rows
    owned = expert_in.shape[0]
    kv_width = KEY_VALUE_HEADS * HEAD_SIZE

    q_width = QUERY_HEADS * HEAD_SIZE
    if lax.axis_size("replica") == 16 and lax.axis_size("group") == 2:
        (n1, q, ao, h, n2, share, lse, cosine, sine, seg_k, router, gains, kv_all, grad_all, w_all) = (
            forward(
                layer_input, document_numbers, routes, (norm_attn, norm_moe), w_router, w_query,
                key_weight, value_weight, w_out, cotangent,
            )
        )
        layer_output, grad_input, small_sum, sums, _ = backward(
            n2, grad_all, h, ao, q, kv_all, n1, w_all, layer_input, expert_in, expert_out, share,
            router, gains, lse, document_numbers[:, None], seg_k, cosine, sine,
        )
        half = expert_out.shape[1]
        sums = sums.reshape(-1, half, width)
        g_small = lax.dynamic_slice_in_dim(small_sum, group * (width // 2), width // 2, 1)
        return (
            layer_output,
            grad_input,
            g_small[EXPERTS + 1],
            widen(sums, 3 * owned, 1)[0],
            sums[3 * owned + 1][:, :kv_width].astype(f32),
            sums[3 * owned + 1][:, kv_width:].astype(f32),
            widen(sums, 3 * owned + 2, 1)[0],
            g_small[EXPERTS],
            g_small[:EXPERTS].T,
            widen(sums, 0, 2 * owned).reshape(expert_in.shape),
            widen(sums, 2 * owned, owned),
        )

    seg_all = gather(document_numbers)
    position = lax.dynamic_slice_in_dim(doc_positions(seg_all), first, rows, 0)
    cosine, sine = turn_tables(position)
    small = gather(jnp.concatenate([norm_attn[:, None], norm_moe[:, None], w_router], axis=1))
    gain_attn = small[:, 0].astype(f32)[None, :]
    gain_moe = small[:, 1].astype(f32)[None, :]
    router = small[:, 2:]
    w_qkv = gather(jnp.concatenate([w_query, key_weight, value_weight], axis=1))
    wo = gather(w_out)
    grad_all = gather(cotangent)

    n1, q, k, v = project(layer_input, gain_attn, w_qkv, cosine, sine)
    kv_all = gather(jnp.concatenate([k, v], axis=1))
    k_all, v_all = kv_all[:, :kv_width], kv_all[:, kv_width:]
    first_row = jnp.full((1,), first, jnp.int32)
    seg_q, seg_k = document_numbers[:, None], seg_all[None, :]
    ao = attend(first_row, q, k_all, v_all, seg_q, seg_k)

    x = layer_input.astype(f32)
    h = x + mm(ao, wo)
    r2 = rms_factor(h)
    n2 = (h * r2 * gain_moe).astype(bf16)
    logits = mm(n2, router)
    chosen = jnp.any(routes[:, :, None] == jnp.arange(EXPERTS, dtype=jnp.int32), axis=1)
    picked = jnp.where(chosen, logits, MASKED)
    e = jnp.where(chosen, jnp.exp(picked - jnp.max(picked, axis=1, keepdims=True)), 0.0)
    share = e / jnp.sum(e, axis=1, keepdims=True)

    n2_all = gather(n2)
    share_all = lax.dynamic_slice_in_dim(gather(share), group * owned, owned, 1)
    moe, d_n2_all, d_gate, g_in, g_out = all_experts(
        n2_all, grad_all, share_all, expert_in, expert_out
    )
    d_gate = lax.dynamic_update_slice_in_dim(
        jnp.zeros((n2_all.shape[0], EXPERTS), f32), d_gate, group * owned, 1
    )
    d_gate = lax.psum_scatter(d_gate, "group", scatter_dimension=0, tiled=True)
    layer_output = (h + owner_sum(moe).astype(f32)).astype(bf16)

    d_logits = (share * (d_gate - jnp.sum(share * d_gate, axis=1, keepdims=True))).astype(bf16)
    g_router = mm_tn(n2, d_logits)
    d_n2 = owner_sum(d_n2_all).astype(f32) + mm_nt(d_logits, router)
    g_gain_moe = jnp.sum(h * r2 * d_n2, axis=0)
    c = d_n2 * gain_moe
    d_h = cotangent.astype(f32) + r2 * (
        c - h * r2 * r2 * jnp.mean(c * h, axis=-1, keepdims=True)
    )
    d_y = d_h.astype(bf16)
    g_wo = mm_tn(ao, d_y).astype(bf16)
    d_o = mm_nt(d_y, wo).astype(bf16)

    dq, dk_all, dv_all = attend_grad(first_row, q, k_all, v_all, d_o, seg_q, seg_k)
    dkv = owner_sum(jnp.concatenate([dk_all, dv_all], axis=1))
    g_qkv, grad_input, g_gain_attn = project_grad(
        dq, dkv[:, :kv_width], dkv[:, kv_width:], n1, w_qkv, cosine, sine, layer_input,
        gain_attn, d_h,
    )

    g_attn = owner_sum(jnp.concatenate([g_qkv, g_wo], axis=1))
    g_small = owner_sum(
        jnp.concatenate([g_gain_attn.reshape(-1, 1), g_gain_moe[:, None], g_router], axis=1)
    )
    g_attn, g_small = (t.astype(f32) for t in lax.psum((g_attn, g_small), "replica"))
    return (
        layer_output,
        grad_input,
        g_small[:, 0],
        g_attn[:, :q_width],
        g_attn[:, q_width : q_width + kv_width],
        g_attn[:, q_width + kv_width : q_width + 2 * kv_width],
        g_attn[:, q_width + 2 * kv_width :],
        g_small[:, 1],
        g_small[:, 2:],
        g_in,
        g_out,
    )


def solution(mesh):
    tokens, weights = P(("replica", "group"), None), P("group", None)
    in_specs = (
        tokens, P(("replica", "group")), tokens, P("group"), weights, weights, weights, weights,
        P("group"), weights, P("group", None, None), P("group", None, None), tokens,
    )
    out_specs = (
        tokens, tokens, P("group"), weights, weights, weights, weights, P("group"), weights,
        P("group", None, None), P("group", None, None),
    )
    return jax.shard_map(
        on_device, mesh=mesh, in_specs=in_specs, out_specs=out_specs, check_vma=False
    )
```

```python
import functools

import jax
import jax.numpy as jnp
import numpy as np
from jax import lax
from jax.experimental import pallas as pl
from jax.experimental.pallas import tpu as pltpu
from jax.sharding import PartitionSpec as P

QUERY_HEADS = 16
KEY_VALUE_HEADS = 8
HEAD_SIZE = 64
EXPERTS = 16
EPS = 1e-06
MASKED = -1e30
SCALE = HEAD_SIZE ** (-0.5)

f32 = jnp.float32
bf16 = jnp.bfloat16
MIB = 1 << 20


def mm(a, b):
    return lax.dot_general(a, b, (((1,), (0,)), ((), ())), preferred_element_type=f32)


def mm_nt(a, b):
    return lax.dot_general(a, b, (((1,), (1,)), ((), ())), preferred_element_type=f32)


def mm_tn(a, b):
    return lax.dot_general(a, b, (((0,), (0,)), ((), ())), preferred_element_type=f32)


def params(mib):
    return pltpu.CompilerParams(vmem_limit_bytes=mib * MIB)


def cost(flops, moved):
    return pl.CostEstimate(flops=int(flops), bytes_accessed=int(moved), transcendentals=0)


def doc_positions(seg_ids):
    length = seg_ids.shape[0]
    index = jnp.arange(length, dtype=jnp.int32)
    previous = jnp.concatenate([seg_ids[:1] - 1, seg_ids[:-1]])
    is_start = (seg_ids != previous) | (index == 0)
    start = lax.cummax(jnp.where(is_start, index, 0), axis=0)
    return index - start


def turn_tables(position):
    half = HEAD_SIZE // 2
    exponent = jnp.arange(half, dtype=f32) * (-2.0 / HEAD_SIZE)
    inv_freq = jnp.power(10000.0, exponent)
    angles = position.astype(f32)[:, None] * inv_freq[None, :]
    cosine, sine = jnp.cos(angles), jnp.sin(angles)
    return (
        jnp.concatenate([cosine] * 4, axis=1),
        jnp.concatenate([-sine, sine, -sine, sine], axis=1),
    )


def swap_halves(t):
    lane = lax.broadcasted_iota(jnp.int32, t.shape, 1)
    return jnp.where(
        lane % HEAD_SIZE < HEAD_SIZE // 2, pltpu.roll(t, 96, 1), pltpu.roll(t, 32, 1)
    )


def qkv_kernel(x_ref, gain_ref, w_ref, cos_ref, sin_ref, n1_ref, q_ref, k_ref, v_ref):
    x = x_ref[...].astype(f32)
    factor = lax.rsqrt(jnp.mean(x * x, axis=-1, keepdims=True) + EPS)
    n1 = (x * factor * gain_ref[...]).astype(bf16)
    n1_ref[...] = n1
    cosine, sine = cos_ref[...], sin_ref[...]
    q_width, k_width = q_ref.shape[1], k_ref.shape[1]
    for start in range(0, q_width + k_width, 256):
        lin = mm(n1, w_ref[:, start : start + 256])
        for part in (0, 128):
            t = lin[:, part : part + 128]
            turned = (t * cosine + swap_halves(t) * sine).astype(bf16)
            at = start + part
            if at < q_width:
                q_ref[:, at : at + 128] = turned
            else:
                k_ref[:, at - q_width : at - q_width + 128] = turned
    v_ref[...] = mm(n1, w_ref[:, q_width + k_width :]).astype(bf16)


def project(x, gain, w, cosine, sine):
    rows, width = x.shape
    q_width, k_width = QUERY_HEADS * HEAD_SIZE, KEY_VALUE_HEADS * HEAD_SIZE
    shape = jax.ShapeDtypeStruct
    return pl.pallas_call(
        qkv_kernel,
        out_shape=(
            shape((rows, width), bf16),
            shape((rows, q_width), bf16),
            shape((rows, k_width), bf16),
            shape((rows, k_width), bf16),
        ),
        compiler_params=params(40),
        cost_estimate=cost(2 * rows * width * w.shape[1], 2 * w.size + 8 * x.size),
        name="project",
    )(x, gain, w, cosine, sine)


def qkv_grad_kernel(
    dq_ref, dk_ref, dv_ref, n1_ref, w_ref, cos_ref, sin_ref, x_ref, gain_ref, dh_ref,
    gw_ref, gx_ref, gg_ref, lin_ref,
):
    cosine, sine = cos_ref[...], sin_ref[...]
    q_width, k_width = dq_ref.shape[1], dk_ref.shape[1]
    for ref, width, base in ((dq_ref, q_width, 0), (dk_ref, k_width, q_width)):
        for at in range(0, width, 128):
            t = ref[:, at : at + 128].astype(f32)
            turned = (t * cosine - swap_halves(t) * sine).astype(bf16)
            lin_ref[:, base + at : base + at + 128] = turned
    lin_ref[:, q_width + k_width :] = dv_ref[...].astype(bf16)
    total = q_width + 2 * k_width
    n1 = n1_ref[...]
    for at in range(0, total, 512):
        gw_ref[:, at : at + 512] = mm_tn(n1, lin_ref[:, at : at + 512]).astype(bf16)
    dn1 = mm_nt(lin_ref[...], w_ref[...])
    x = x_ref[...].astype(f32)
    factor = lax.rsqrt(jnp.mean(x * x, axis=-1, keepdims=True) + EPS)
    gg_ref[...] = jnp.sum(x * factor * dn1, axis=0, keepdims=True)
    c = dn1 * gain_ref[...]
    mean = jnp.mean(c * x, axis=-1, keepdims=True)
    gx_ref[...] = dh_ref[...] + factor * (c - x * (factor * factor * mean))


def project_grad(dq, dk, dv, n1, w, cosine, sine, x, gain, dh):
    rows, width = x.shape
    shape = jax.ShapeDtypeStruct
    return pl.pallas_call(
        qkv_grad_kernel,
        out_shape=(
            shape(w.shape, bf16),
            shape((rows, width), f32),
            shape((1, width), f32),
        ),
        scratch_shapes=[pltpu.VMEM((rows, w.shape[1]), bf16)],
        compiler_params=params(56),
        cost_estimate=cost(4 * rows * width * w.shape[1], 4 * w.size + 16 * x.size),
        name="project_grad",
    )(dq, dk, dv, n1, w, cosine, sine, x, gain, dh)


def visible_bias(first_ref, seg_q_ref, seg_k_ref, bias_ref):
    rows, keys = bias_ref.shape
    row = first_ref[0] + lax.broadcasted_iota(jnp.int32, (rows, keys), 0)
    col = lax.broadcasted_iota(jnp.int32, (rows, keys), 1)
    seen = (seg_q_ref[...] == seg_k_ref[...]) & (row >= col)
    bias_ref[...] = jnp.where(seen, 0.0, MASKED).astype(f32)


def attend_kernel(first_ref, q_ref, k_ref, v_ref, seg_q_ref, seg_k_ref, o_ref, bias_ref):
    @pl.when(pl.program_id(0) == 0)
    def _():
        visible_bias(first_ref, seg_q_ref, seg_k_ref, bias_ref)

    bias = bias_ref[...]
    for head in range(4):
        at, kv = head * HEAD_SIZE, head // 2 * HEAD_SIZE
        s = mm_nt(q_ref[:, at : at + HEAD_SIZE], k_ref[:, kv : kv + HEAD_SIZE]) * SCALE + bias
        e = jnp.exp(s - jnp.max(s, axis=1, keepdims=True))
        total = jnp.sum(e, axis=1, keepdims=True)
        o = mm(e.astype(bf16), v_ref[:, kv : kv + HEAD_SIZE]) / total
        o_ref[:, at : at + HEAD_SIZE] = o.astype(bf16)


def attend(first, q, k, v, seg_q, seg_k):
    rows, width = q.shape
    keys = k.shape[0]
    wide = pl.BlockSpec((rows, 256), lambda i, first: (0, i))
    narrow = pl.BlockSpec((keys, 128), lambda i, first: (0, i))
    return pl.pallas_call(
        attend_kernel,
        out_shape=jax.ShapeDtypeStruct((rows, width), bf16),
        grid_spec=pltpu.PrefetchScalarGridSpec(
            num_scalar_prefetch=1,
            grid=(width // 256,),
            in_specs=[
                wide,
                narrow,
                narrow,
                pl.BlockSpec((rows, 1), lambda i, first: (0, 0)),
                pl.BlockSpec((1, keys), lambda i, first: (0, 0)),
            ],
            out_specs=wide,
            scratch_shapes=[pltpu.VMEM((rows, keys), f32)],
        ),
        compiler_params=params(48),
        cost_estimate=cost(16 * rows * keys * width, 4 * q.size + 4 * k.size),
        name="attend",
    )(first, q, k, v, seg_q, seg_k)


def attend_grad_kernel(
    first_ref, q_ref, k_ref, v_ref, do_ref, seg_q_ref, seg_k_ref,
    dq_ref, dk_ref, dv_ref, bias_ref,
):
    @pl.when(pl.program_id(0) == 0)
    def _():
        visible_bias(first_ref, seg_q_ref, seg_k_ref, bias_ref)

    bias = bias_ref[...]
    for pair in range(2):
        kv = pair * HEAD_SIZE
        k, v = k_ref[:, kv : kv + HEAD_SIZE], v_ref[:, kv : kv + HEAD_SIZE]
        dk = dv = None
        for head in (2 * pair, 2 * pair + 1):
            at = head * HEAD_SIZE
            q, do = q_ref[:, at : at + HEAD_SIZE], do_ref[:, at : at + HEAD_SIZE]
            s = mm_nt(q, k) * SCALE + bias
            e = jnp.exp(s - jnp.max(s, axis=1, keepdims=True))
            p = e * (1.0 / jnp.sum(e, axis=1, keepdims=True))
            dp = mm_nt(do, v)
            delta = jnp.sum(p * dp, axis=1, keepdims=True)
            ds = (p * (dp - delta) * SCALE).astype(bf16)
            dq_ref[:, at : at + HEAD_SIZE] = mm(ds, k)
            dk_part, dv_part = mm_tn(ds, q), mm_tn(p.astype(bf16), do)
            dk = dk_part if dk is None else dk + dk_part
            dv = dv_part if dv is None else dv + dv_part
        dk_ref[:, kv : kv + HEAD_SIZE] = dk.astype(bf16)
        dv_ref[:, kv : kv + HEAD_SIZE] = dv.astype(bf16)


def attend_grad(first, q, k, v, do, seg_q, seg_k):
    rows, width = q.shape
    keys = k.shape[0]
    wide = pl.BlockSpec((rows, 256), lambda i, first: (0, i))
    narrow = pl.BlockSpec((keys, 128), lambda i, first: (0, i))
    shape = jax.ShapeDtypeStruct
    return pl.pallas_call(
        attend_grad_kernel,
        out_shape=(
            shape((rows, width), f32),
            shape(k.shape, bf16),
            shape(k.shape, bf16),
        ),
        grid_spec=pltpu.PrefetchScalarGridSpec(
            num_scalar_prefetch=1,
            grid=(width // 256,),
            in_specs=[
                wide,
                narrow,
                narrow,
                wide,
                pl.BlockSpec((rows, 1), lambda i, first: (0, 0)),
                pl.BlockSpec((1, keys), lambda i, first: (0, 0)),
            ],
            out_specs=[wide, narrow, narrow],
            scratch_shapes=[pltpu.VMEM((rows, keys), f32)],
        ),
        compiler_params=params(56),
        cost_estimate=cost(40 * rows * keys * width // 4, 8 * q.size + 8 * k.size),
        name="attend_grad",
    )(first, q, k, v, do, seg_q, seg_k)


def gather(value):
    return lax.all_gather(value, "group", axis=0, tiled=True)


def owner_sum(value):
    return lax.psum_scatter(value.astype(bf16), "group", scatter_dimension=0, tiled=True)


def rms_factor(values):
    return lax.rsqrt(jnp.mean(values * values, axis=-1, keepdims=True) + EPS)


LAG = 2
PHASES = 7
SEMS = 8
(CORE, X_A, IN_B, IN_A, HALF_B, MID_A, RUNG_B, OUT_A, BACK_B, SPREAD_A, OUT_B, JOIN, KINDS) = range(13)
(Y_N2, Y_SHARE, Y_DN2, Y_MOE, Y_GATE, Y_DKV, Y_WEIGHT, Y_KINDS) = (0, 1, 2, 3, 4, 5, 13, 19)


def engine_scratch(quarter, width):
    def vmem(*shape):
        return pltpu.VMEM((*shape, quarter, width), bf16)

    return [
        vmem(4, 4),
        vmem(4, 4),
        vmem(4),
        vmem(8, 2),
        vmem(8),
        vmem(4),
        vmem(4),
        vmem(4),
        vmem(LAG, 4),
        vmem(LAG),
        vmem(LAG, 2),
        vmem(LAG),
        vmem(LAG),
        vmem(LAG),
        vmem(LAG),
        pltpu.SemaphoreType.DMA((KINDS, SEMS)),
        pltpu.SemaphoreType.DMA((KINDS, SEMS)),
        pltpu.SemaphoreType.DMA((3, SEMS)),
    ]


class Place:
    def __init__(self):
        r = lax.axis_index("replica")
        self.core, self.x, z = lax.rem(r, 2), lax.rem(r // 2, 2), r // 4
        self.group = lax.axis_index("group")
        self.inner = (z == 1) | (z == 2)
        self.outer = jnp.logical_not(self.inner)
        self.late = z // 2
        up = (z == 0) | (z == 2)
        self.core_peer = {"replica": r + 1 - 2 * self.core}
        self.x_peer = {"replica": r + 2 - 4 * self.x}
        self.line_peer = {"replica": jnp.where(up, r + 4, r - 4)}
        self.mid_peer = {"replica": jnp.where(z == 1, r + 4, r - 4)}
        self.y_peer = {"group": 1 - self.group}

    def greet(self):
        barrier = pltpu.get_barrier_semaphore()

        def signal(peer):
            pl.semaphore_signal(
                barrier, inc=1, device_id=peer, device_id_type=pl.DeviceIdType.MESH
            )

        for peer in (self.core_peer, self.x_peer, self.line_peer, self.y_peer):
            signal(peer)

        @pl.when(self.inner)
        def _():
            signal(self.mid_peer)
            pl.semaphore_wait(barrier, 5)

        @pl.when(self.outer)
        def _():
            pl.semaphore_wait(barrier, 4)


def remote_copy(src, dst, send_sem, recv_sem, peer):
    return pltpu.make_async_remote_copy(
        src_ref=src, dst_ref=dst, send_sem=send_sem, recv_sem=recv_sem, device_id=peer,
        device_id_type=pl.DeviceIdType.MESH,
    )


def make_engine(place, count, split, split_of, stage, out, scratch, late_piece):
    (mine, got_core, got_x, got_end_b, got_end_a, got_mid_b, got_mid_a, got_rung,
     summed, a_x, b_end, a_end, b_mid, a_all, b_all, send_sem, recv_sem, copy_sem) = scratch
    core, x, inner, outer, late = place.core, place.x, place.inner, place.outer, place.late

    owned = split_of // 6

    def spot(k):
        e, sub, part = k // 6, lax.rem(k // 2, 3), lax.rem(k, 2)
        inner_spot = jnp.where(sub == 0, 4 * owned + 2 * e, 4 * e + 2 * sub - 2) + part
        return jnp.where(k < split_of, inner_spot, k)

    def remote(kind, k, src, dst, peer):
        slot = lax.rem(k, SEMS)
        return remote_copy(src, dst, send_sem.at[kind, slot], recv_sem.at[kind, slot], peer)

    def local(kind, k, src, dst):
        return pltpu.make_async_copy(src, dst, copy_sem.at[kind, lax.rem(k, SEMS)])

    def core_copy(k):
        return remote(
            CORE, k, stage.at[k, 1 - core], got_core.at[lax.rem(k, 4)], place.core_peer
        )

    def mine_copy(k):
        return local(2, k, stage.at[k, core], mine.at[lax.rem(k, 4)])

    def x_copy(k):
        return remote(
            X_A, k, summed.at[lax.rem(k, LAG), 1 - x], got_x.at[lax.rem(k, 4)], place.x_peer
        )

    def in_b_copy(k):
        return remote(
            IN_B, k, summed.at[lax.rem(k, LAG), pl.ds(2, 2)], got_end_b.at[lax.rem(k, 8)],
            place.line_peer,
        )

    def in_a_copy(k):
        return remote(
            IN_A, k, a_x.at[lax.rem(k, LAG)], got_end_a.at[lax.rem(k, 8)], place.line_peer
        )

    def half_b_copy(k):
        return remote(
            HALF_B, k, b_end.at[lax.rem(k, LAG), 1 - late], got_mid_b.at[lax.rem(k, 4)],
            place.mid_peer,
        )

    def mid_a_copy(k):
        return remote(
            MID_A, k, a_end.at[lax.rem(k, LAG)], got_mid_a.at[lax.rem(k, 4)], place.mid_peer
        )

    def rung_copy(k):
        return remote(
            RUNG_B, k, b_mid.at[lax.rem(k, LAG)], got_rung.at[lax.rem(k, 4)], place.x_peer
        )

    def out_a_copy(k):
        return remote(OUT_A, k, a_all.at[lax.rem(k, LAG)], out.at[spot(k), core, x], place.line_peer)

    def back_b_copy(k, quarter):
        return remote(
            BACK_B, k, b_all.at[lax.rem(k, LAG)], out.at[spot(k), core, quarter], place.mid_peer
        )

    def spread_copy(k, quarter):
        return remote(SPREAD_A, k, out.at[spot(k), core, x], out.at[spot(k), core, quarter], place.x_peer)

    def out_b_copy(k):
        part = out.at[spot(k), core, pl.ds(2, 2)]
        return remote(OUT_B, k, part, part, place.line_peer)

    def join_copy(k, half):
        return remote(JOIN, k, out.at[spot(k), core], out.at[spot(k), half], place.core_peer)

    def keep_a(k):
        return local(0, k, a_all.at[lax.rem(k, LAG)], out.at[spot(k), core, x])

    def keep_b(k):
        return local(1, k, b_all.at[lax.rem(k, LAG)], out.at[spot(k), core, 2 + late])

    def phase1(k):
        i = lax.rem(k, LAG)

        @pl.when(k < split)
        def _():
            mine_copy(k).wait()
            core_copy(k).wait()
            summed[i] = mine[lax.rem(k, 4)] + got_core[lax.rem(k, 4)]

        if count > split:

            @pl.when(k >= split)
            def _():
                copy, own, other = late_piece(k)
                copy.wait()
                summed[i] = own[...] + other[...]

        x_copy(k).start()

        @pl.when(outer)
        def _():
            in_b_copy(k).start()

    def phase2(k):
        i = lax.rem(k, LAG)
        x_copy(k).wait()
        a_x[i] = summed[i, x] + got_x[lax.rem(k, 4)]

        @pl.when(outer)
        def _():
            in_a_copy(k).start()
            in_b_copy(k).wait_send()

        @pl.when(inner)
        def _():
            in_b_copy(k).wait_recv()
            b_end[i] = summed[i, 2:4] + got_end_b[lax.rem(k, 8)]
            half_b_copy(k).start()

    def phase3(k):
        i = lax.rem(k, LAG)

        @pl.when(outer)
        def _():
            in_a_copy(k).wait_send()

        @pl.when(inner)
        def _():
            in_a_copy(k).wait_recv()
            a_end[i] = a_x[i] + got_end_a[lax.rem(k, 8)]
            mid_a_copy(k).start()
            half_b_copy(k).wait()
            b_mid[i] = b_end[i, late] + got_mid_b[lax.rem(k, 4)]
            rung_copy(k).start()

    def phase4(k):
        i = lax.rem(k, LAG)

        @pl.when(inner)
        def _():
            mid_a_copy(k).wait()
            a_all[i] = a_end[i] + got_mid_a[lax.rem(k, 4)]
            out_a_copy(k).start()
            keep_a(k).start()
            rung_copy(k).wait()
            b_all[i] = b_mid[i] + got_rung[lax.rem(k, 4)]
            back_b_copy(k, 2 + late).start()
            keep_b(k).start()

    def phase5(k):
        @pl.when(outer)
        def _():
            out_a_copy(k).wait_recv()

        @pl.when(inner)
        def _():
            keep_a(k).wait()
            out_a_copy(k).wait_send()

        spread_copy(k, x).start()

        @pl.when(inner)
        def _():
            keep_b(k).wait()
            back_b_copy(k, 2 + late).wait_send()
            back_b_copy(k, 3 - late).wait_recv()
            out_b_copy(k).start()

    def phase6(k):
        spread_copy(k, x).wait_send()
        spread_copy(k, 1 - x).wait_recv()

        @pl.when(outer)
        def _():
            out_b_copy(k).wait_recv()

        @pl.when(inner)
        def _():
            out_b_copy(k).wait_send()

        join_copy(k, core).start()

    def phase7(k):
        join_copy(k, core).wait_send()
        join_copy(k, 1 - core).wait_recv()

    phases = (phase1, phase2, phase3, phase4, phase5, phase6, phase7)

    def tick(t):
        for number in range(PHASES, 0, -1):
            k = t - LAG * number

            @pl.when((k >= 0) & (k < count))
            def _():
                phases[number - 1](k)

    def send(k):
        @pl.when(k < split)
        def _():
            core_copy(k).start()
            mine_copy(k).start()

    return tick, send


def make_small_sum(place, values, got, send_sem, recv_sem):
    def copy(i, peer):
        return remote_copy(values.at[i], got.at[i], send_sem.at[i], recv_sem.at[i], peer)

    peers = (
        place.core_peer, place.x_peer, place.y_peer, place.line_peer, place.mid_peer,
        place.line_peer,
    )

    def add(i):
        values[i + 1] = values[i] + got[i]

    def step(i):
        if 1 <= i <= 3:
            copy(i - 1, peers[i - 1]).wait()
            add(i - 1)
        if i <= 2:
            copy(i, peers[i]).start()
        if i == 3:

            @pl.when(place.outer)
            def _():
                copy(3, peers[3]).start()

        if i == 4:

            @pl.when(place.outer)
            def _():
                copy(3, peers[3]).wait_send()

            @pl.when(place.inner)
            def _():
                copy(3, peers[3]).wait_recv()
                add(3)
                copy(4, peers[4]).start()

        if i == 5:

            @pl.when(place.inner)
            def _():
                copy(4, peers[4]).wait()
                add(4)
                copy(5, peers[5]).start()

        if i == 6:

            @pl.when(place.inner)
            def _():
                copy(5, peers[5]).wait_send()

            @pl.when(place.outer)
            def _():
                copy(5, peers[5]).wait_recv()
                values[5] = got[5]

    return step


TILE = 256
WIDE = 1024


(F_SMALL, F_SEG, F_WQ, F_WK, F_WV, F_WO, F_GRAD, F_KV) = range(8)
F_KINDS = F_KV + 8
W_KV, W_Q, W_OUT = 0, 1, 2
SMALL_ROWS = 32


def forward_kernel(
    x_hbm, wq_hbm, wk_hbm, wv_hbm, wo_hbm, g_hbm, small_own, seg_own, routes, inv_freq,
    n1_ref, q_ref, ao_ref, h_ref, n2_ref, share_ref, lse_ref, cos_ref, sin_ref, seg_ref, column_ref,
    router_ref, gain_ref, kv_hbm, g_all, w_all,
    x_in, w, kv, bias, small, seg, y_send, y_recv, x_send, x_recv, c_send, c_recv, load_sem,
):
    rows, width = x_in.shape
    own_rows = wq_hbm.shape[0]
    part = own_rows // 4
    kv_width = wk_hbm.shape[1]
    qkv_width = width + 2 * kv_width
    place = Place()
    group, core, x = place.group, place.core, place.x
    here = pl.multiple_of(group * rows, rows)
    there = pl.multiple_of((1 - group) * rows, rows)
    w_here = pl.multiple_of(group * own_rows, own_rows)
    w_there = pl.multiple_of((1 - group) * own_rows, own_rows)
    quarter = pl.multiple_of((2 * core + x) * part, part)

    loads = [
        (x_hbm, x_in),
        (wk_hbm, w.at[pl.ds(w_here, own_rows), pl.ds(width, kv_width)]),
        (wv_hbm, w.at[pl.ds(w_here, own_rows), pl.ds(width + kv_width, kv_width)]),
        (wq_hbm, w.at[pl.ds(w_here, own_rows), pl.ds(0, width)]),
        (wo_hbm, w.at[pl.ds(w_here, own_rows), pl.ds(qkv_width, width)]),
        (g_hbm, g_all.at[pl.ds(here, rows)]),
    ]
    loads = [
        pltpu.make_async_copy(src, dst, load_sem.at[i]) for i, (src, dst) in enumerate(loads)
    ]
    for copy in loads:
        copy.start()
    place.greet()

    def y_copy(kind, src, dst):
        return remote_copy(src, dst, y_send.at[kind], y_recv.at[kind], place.y_peer)

    def weight_copy(kind, src, column, columns):
        return y_copy(
            kind, src.at[pl.ds(quarter, part)],
            w.at[pl.ds(w_here + quarter, part), pl.ds(column, columns)],
        )

    def x_copy(i, column, columns):
        block = w.at[pl.ds(w_there + quarter, part), pl.ds(column, columns)]
        return remote_copy(block, block, x_send.at[i], x_recv.at[i], place.x_peer)

    def core_copy(i, column, columns):
        first = pl.multiple_of(w_there + 2 * core * part, 2 * part)
        block = w.at[pl.ds(first, 2 * part), pl.ds(column, columns)]
        return remote_copy(block, block, c_send.at[i], c_recv.at[i], place.core_peer)

    small_copy = y_copy(F_SMALL, small_own, small.at[group])
    seg_copy = y_copy(F_SEG, seg_own, seg.at[group])
    kv_weights = [
        weight_copy(F_WK, wk_hbm, width, kv_width),
        weight_copy(F_WV, wv_hbm, width + kv_width, kv_width),
    ]
    wq_copy = weight_copy(F_WQ, wq_hbm, 0, width)
    wo_copy = weight_copy(F_WO, wo_hbm, qkv_width, width)
    grad_copy = y_copy(F_GRAD, g_hbm, g_all.at[pl.ds(here, rows)])
    for copy in (small_copy, seg_copy, *kv_weights):
        copy.start()
    small[group] = small_own[...]
    seg[group] = seg_own[...]

    small_copy.wait()
    seg_copy.wait()
    seg_row = jnp.concatenate([seg[0, 0:1, :], seg[1, 0:1, :]], axis=1)
    seg_ref[...] = seg_row
    router_ref[...] = jnp.concatenate([small[0, 0:EXPERTS, :], small[1, 0:EXPERTS, :]], axis=1)
    gain_ref[...] = jnp.concatenate(
        [small[0, EXPERTS:, :], small[1, EXPERTS:, :]], axis=1
    ).astype(f32)[0 : gain_ref.shape[0]]
    row = here + lax.broadcasted_iota(jnp.int32, bias.shape, 0)
    col = lax.broadcasted_iota(jnp.int32, bias.shape, 1)
    seg_column = seg_own[...].astype(f32).T[:, 0:1].astype(jnp.int32)
    column_ref[...] = seg_column
    same = seg_column == seg_row
    bias[...] = jnp.where(same & (row >= col), 0.0, MASKED).astype(f32)
    position = jnp.sum(jnp.where(same & (row > col), 1.0, 0.0), axis=1, keepdims=True)

    for copy in kv_weights:
        copy.wait()
    x_copy(W_KV, width, 2 * kv_width).start()
    wq_copy.start()

    expert = lax.broadcasted_iota(jnp.int32, (EXPERTS, rows), 0)
    named = jnp.zeros((EXPERTS, rows), f32)
    for k in range(routes.shape[0]):
        named = jnp.where(routes[k : k + 1, :] == expert, 1.0, named)
    share_ref[...] = named.T

    angle = position * inv_freq[...]
    lane = lax.broadcasted_iota(jnp.int32, angle.shape, 1)
    cos_ref[...] = jnp.cos(angle)
    sine = jnp.sin(angle)
    sin_ref[...] = jnp.where(lax.rem(lane, HEAD_SIZE) < HEAD_SIZE // 2, -sine, sine)

    for copy in loads:
        copy.wait()
    xs = x_in[...].astype(f32)
    factor = lax.rsqrt(jnp.mean(xs * xs, axis=-1, keepdims=True) + EPS)
    n1_ref[...] = (xs * factor * gain_ref[0:1, :]).astype(bf16)

    x_copy(W_KV, width, 2 * kv_width).wait()
    core_copy(W_KV, width, 2 * kv_width).start()
    wq_copy.wait()
    x_copy(W_Q, 0, width).start()
    wo_copy.start()
    core_copy(W_KV, width, 2 * kv_width).wait()

    n1 = n1_ref[...]
    cosine, sine = cos_ref[...], sin_ref[...]

    def turned(column):
        lin = mm(n1, w[:, column : column + 256])
        return [
            (t * cosine + swap_halves(t) * sine).astype(bf16)
            for t in (lin[:, :128], lin[:, 128:])
        ]

    own = pl.ds(here, rows)

    def kv_copies(i):
        first = pl.multiple_of(i * 128, 128)
        return [
            y_copy(
                F_KV + 2 * i + j,
                kv.at[own, pl.ds(first + j * kv_width, 128)],
                kv.at[own, pl.ds(first + j * kv_width, 128)],
            )
            for j in range(2)
        ]

    for i in range(2):
        at = 256 * i
        kv[own, at : at + 128], kv[own, at + 128 : at + 256] = turned(width + at)
        lin = mm(n1, w[:, width + kv_width + at : width + kv_width + at + 256])
        kv[own, kv_width + at : kv_width + at + 256] = lin.astype(bf16)

        @pl.when(group == 0)
        def _():
            for j in (2 * i, 2 * i + 1):
                for copy in kv_copies(j):
                    copy.start()

    @pl.when(group == 0)
    def _():
        kv[rows:, :] = jnp.zeros((rows, kv.shape[1]), bf16)

    x_copy(W_Q, 0, width).wait()
    core_copy(W_Q, 0, width).start()
    wo_copy.wait()
    x_copy(W_OUT, qkv_width, width).start()

    @pl.when(group == 1)
    def _():
        grad_copy.start()

    core_copy(W_Q, 0, width).wait()
    for at in range(0, width, 256):
        q_ref[:, at : at + 128], q_ref[:, at + 128 : at + 256] = turned(at)
    lse_ref[...] = jnp.zeros_like(lse_ref)

    @pl.loop(0, 4)
    def _(i):
        @pl.when(group == 1)
        def _():
            for copy in kv_copies(i):
                copy.wait_recv()

        @pl.when(i == 2)
        def _():
            x_copy(W_OUT, qkv_width, width).wait()
            core_copy(W_OUT, qkv_width, width).start()

        at_k = pl.ds(pl.multiple_of(i * 128, 128), 128)
        at_v = pl.ds(pl.multiple_of(kv_width + i * 128, 128), 128)
        keys, values = kv[:, at_k], kv[:, at_v]
        for pair in range(2):
            lanes = slice(pair * HEAD_SIZE, (pair + 1) * HEAD_SIZE)
            key, value = keys[:, lanes], values[:, lanes]
            at_q = pl.ds(pl.multiple_of(i * 256 + pair * 128, 128), 128)

            @pl.loop(0, rows // TILE)
            def _(number):
                tile = pl.ds(pl.multiple_of(number * TILE, TILE), TILE)
                s = mm_nt(two_heads(q_ref[tile, at_q]) * SCALE, key)
                s = s.reshape(2, TILE, -1) + bias[tile, :][None]
                peak = jnp.max(s, axis=2, keepdims=True)
                e = jnp.exp(s - peak)
                total = jnp.sum(e, axis=2, keepdims=True)
                o = mm(e.astype(bf16).reshape(2 * TILE, -1), value)
                o = o / total.reshape(2 * TILE, 1)
                ao_ref[tile, at_q] = side_by_side(o).astype(bf16)
                lse = peak + jnp.log(total)
                lane = lax.broadcasted_iota(jnp.int32, (TILE, QUERY_HEADS), 1)
                head = 4 * i + 2 * pair
                lse_ref[tile, :] = jnp.where(
                    lane == head, lse[0], jnp.where(lane == head + 1, lse[1], lse_ref[tile, :])
                )

    @pl.when(group == 0)
    def _():
        for i in range(4):
            for copy in kv_copies(i):
                copy.wait_send()
        grad_copy.start()

    core_copy(W_OUT, qkv_width, width).wait()
    keep_w = pltpu.make_async_copy(w, w_all, load_sem.at[0])
    keep_kv = pltpu.make_async_copy(kv, kv_hbm, load_sem.at[1])
    keep_w.start()
    keep_kv.start()

    @pl.loop(0, rows // TILE)
    def _(number):
        tile = pl.ds(pl.multiple_of(number * TILE, TILE), TILE)
        h = x_in[tile, :].astype(f32) + mm(ao_ref[tile, :], w[:, qkv_width:])
        h_ref[tile, :] = h
        factor = lax.rsqrt(jnp.mean(h * h, axis=-1, keepdims=True) + EPS)
        n2 = (h * factor * gain_ref[1:2, :]).astype(bf16)
        n2_ref[tile, :] = n2
        logits = mm_nt(n2, router_ref[...])
        chosen = share_ref[tile, :] > 0.0
        picked = jnp.where(chosen, logits, MASKED)
        e = jnp.exp(picked - jnp.max(picked, axis=1, keepdims=True))
        e = jnp.where(chosen, e, 0.0)
        share_ref[tile, :] = e / jnp.sum(e, axis=1, keepdims=True)

    keep_w.wait()
    keep_kv.wait()
    grad_copy.wait()


def two_heads(t):
    return jnp.concatenate([t[:, :HEAD_SIZE], t[:, HEAD_SIZE:]], axis=0)


def side_by_side(t):
    half = t.shape[0] // 2
    return jnp.concatenate([t[:half], t[half:]], axis=1)


def forward(x, document_numbers, routes, gains, w_router, wq, wk, wv, wo, grad):
    rows, width = x.shape
    tokens, own_rows = 2 * rows, wq.shape[0]
    kv_width = wk.shape[1]
    small = jnp.concatenate(
        [w_router.T, *[gain[None] for gain in gains],
         jnp.zeros((SMALL_ROWS - EXPERTS - 2, own_rows), bf16)], axis=0,
    )
    exponent = (np.arange(128) % (HEAD_SIZE // 2)) * (-2.0 / HEAD_SIZE)
    inv_freq = jnp.asarray(np.power(10000.0, exponent)[None], f32)
    shape = jax.ShapeDtypeStruct
    vmem = pl.BlockSpec(memory_space=pltpu.VMEM)
    hbm = pl.BlockSpec(memory_space=pl.ANY)
    dma = pltpu.SemaphoreType.DMA
    total = 2 * width + 2 * kv_width
    return pl.pallas_call(
        forward_kernel,
        out_shape=(
            shape((rows, width), bf16),
            shape((rows, width), bf16),
            shape((rows, width), bf16),
            shape((rows, width), f32),
            shape((rows, width), bf16),
            shape((rows, EXPERTS), f32),
            shape((rows, QUERY_HEADS), f32),
            shape((rows, 128), f32),
            shape((rows, 128), f32),
            shape((1, tokens), jnp.int32),
            shape((rows, 1), jnp.int32),
            shape((EXPERTS, width), bf16),
            shape((8, width), f32),
            shape((tokens, 2 * kv_width), bf16),
            shape((tokens, width), bf16),
            shape((width, total), bf16),
        ),
        in_specs=[hbm] * 6 + [vmem] * 4,
        out_specs=[vmem] * 13 + [hbm] * 3,
        scratch_shapes=[
            pltpu.VMEM((rows, width), bf16),
            pltpu.VMEM((width, total), bf16),
            pltpu.VMEM((tokens, 2 * kv_width), bf16),
            pltpu.VMEM((rows, tokens), f32),
            pltpu.VMEM((2, SMALL_ROWS, own_rows), bf16),
            pltpu.VMEM((2, 8, rows), jnp.int32),
            dma((F_KINDS,)),
            dma((F_KINDS,)),
            *[dma((3,))] * 4,
            dma((6,)),
        ],
        compiler_params=pltpu.CompilerParams(
            collective_id=2, has_side_effects=True, vmem_limit_bytes=56 * MIB
        ),
        cost_estimate=cost(2 * rows * width * total, 8 * width * total),
        name="forward",
    )(
        x, wq, wk, wv, wo, grad, small, jnp.broadcast_to(document_numbers[None], (8, rows)),
        routes.T, inv_freq,
    )


def backward_kernel(
    n2_hbm, g_hbm, h_hbm, ao_hbm, q_hbm, kv_hbm, n1_hbm, w_hbm, x_hbm, w1_hbm, w2_hbm,
    share_own, router, gains, lse, seg_q, seg_k, cosine, sine,
    y_ref, gx_ref, small_ref, out, stage,
    moe, dn2, share, gate, got_gate, y_send, y_got, got_kv, got_core_w, got_y_w, small, got_small,
    piece, piece_sem, w_sem, load_sem, ys_sem, yr_sem, cs_sem, cr_sem, ss_sem, sr_sem, *scratch,
):
    rows, width = n2_hbm.shape
    tokens = 2 * rows
    owned, half = w2_hbm.shape[0], w2_hbm.shape[1]
    works = 3 * owned
    pieces = 2 * works
    count = pieces + 6
    place = Place()
    group, core = place.group, place.core
    here = pl.multiple_of(group * rows, rows)
    there = pl.multiple_of((1 - group) * rows, rows)

    def load(*pairs):
        copies = [
            pltpu.make_async_copy(src, dst, load_sem.at[i]) for i, (src, dst) in enumerate(pairs)
        ]
        for copy in copies:
            copy.start()
        for copy in copies:
            copy.wait()

    def y_copy(kind, src, dst):
        return remote_copy(src, dst, ys_sem.at[kind], yr_sem.at[kind], place.y_peer)

    def over_tiles(first, number, body, size=TILE):
        @pl.loop(0, number)
        def _(i):
            body(pl.ds(pl.multiple_of(first + i * size, size), size))

    def shifted(tile, by):
        return pl.ds(pl.multiple_of(tile.start + by, TILE), TILE)

    def after_core(gw):
        def late_piece(k):
            j, part = (k - pieces) // 2, lax.rem(k - pieces, 2)
            return (
                y_weight(gw, k - pieces), gw.at[j, group, part, core], got_y_w.at[j, part]
            )

        return late_piece

    def y_weight(gw, i):
        j, part = i // 2, i % 2
        return y_copy(Y_WEIGHT + i, gw.at[j, 1 - group, part, core], got_y_w.at[j, part])

    def fetch(w1, w2, e):
        slot = lax.rem(e, 2)
        return (
            pltpu.make_async_copy(w1_hbm.at[e], w1.at[slot], w_sem.at[0, slot]),
            pltpu.make_async_copy(w2_hbm.at[e], w2.at[slot], w_sem.at[1, slot]),
        )

    tick, send = make_engine(place, count, count, pieces, stage, out, scratch, None)

    def advance(t):
        tick(t)

        @pl.when(t < pieces)
        def _():
            send(t)

    def advance_all(first, number):
        @pl.loop(first, first + number)
        def _(t):
            advance(t)

    def expert_part(n2, n2_turned, g, act, d_ye, d_gu, w1, w2):
        for copy in fetch(w1, w2, 0):
            copy.start()
        place.greet()
        n2_copy = y_copy(Y_N2, n2_hbm, n2.at[pl.ds(here, rows)])
        n2_copy.start()
        share[pl.ds(here, rows), :] = share_own[...]
        share_copy = y_copy(
            Y_SHARE, share.at[pl.ds(here, rows)], share.at[pl.ds(here, rows)]
        )
        share_copy.start()
        load((g_hbm, g), (n2_hbm, n2.at[pl.ds(here, rows)]))
        gate[...] = jnp.zeros_like(gate)

        def prepare(tile):
            n2_turned[:, tile] = n2[tile, :].T
            moe[tile, :] = jnp.zeros((TILE, width), f32)
            dn2[tile, :] = jnp.zeros((TILE, width), f32)

        over_tiles(here, rows // TILE, prepare)
        n2_copy.wait()
        share_copy.wait()
        over_tiles(there, rows // TILE, prepare)

        def pick(table, e):
            lane = lax.broadcasted_iota(jnp.int32, table.shape, 1)
            return jnp.sum(
                jnp.where(lane == group * owned + e, table, 0.0), axis=1, keepdims=True
            )

        def keep(k):
            slot = lax.rem(k, 2)
            return pltpu.make_async_copy(piece.at[slot], stage.at[pl.ds(2 * k, 2)], piece_sem.at[slot])

        def work(k):
            e, sub = k // 3, lax.rem(k, 3)
            slot = lax.rem(e, 2)

            @pl.when(k == 2)
            def _():
                keep(1).wait()

            @pl.when(k >= 4)
            def _():
                keep(k - 2).wait()

            @pl.when(sub == 0)
            def _():
                for copy in fetch(w1, w2, e):
                    copy.wait()

                @pl.when(e + 1 < owned)
                def _():
                    for copy in fetch(w1, w2, e + 1):
                        copy.start()

                def body(tile):
                    gu = mm(n2[tile, :], w1[slot])
                    z, w = gu[:, :half], gu[:, half:]
                    sg = jax.nn.sigmoid(z)
                    silu = z * sg
                    act[tile, :] = (silu * w).astype(bf16)
                    dy = (pick(share[tile, :], e) * g[tile, :].astype(f32)).astype(bf16)
                    d_ye[tile, :] = dy
                    d_act = mm_nt(dy, w2[slot])
                    d_gu[tile, :half] = (d_act * w * sg * (1.0 + z * (1.0 - sg))).astype(bf16)
                    d_gu[tile, half:] = (d_act * silu).astype(bf16)

                over_tiles(0, tokens // WIDE, body, WIDE)
                for part in range(2):
                    columns = slice(part * half // 2, (part + 1) * half // 2)
                    grad = mm_tn(act[:, columns], d_ye[...])
                    piece[lax.rem(k, 2), part] = grad.astype(bf16).reshape(piece.shape[2:])

            @pl.when(sub == 1)
            def _():
                def body(tile):
                    ye = mm(act[tile, :], w2[slot]).astype(bf16).astype(f32)
                    value = jnp.sum(g[tile, :].astype(f32) * ye, axis=1, keepdims=True)
                    lane = lax.broadcasted_iota(jnp.int32, (WIDE, gate.shape[1]), 1)
                    gate[tile, :] = jnp.where(lane == group * owned + e, value, gate[tile, :])
                    moe[tile, :] += pick(share[tile, :], e) * ye

                over_tiles(0, tokens // WIDE, body, WIDE)

            @pl.when(sub == 2)
            def _():
                def body(tile):
                    dn2[tile, :] += mm_nt(d_gu[tile, :], w1[slot]).astype(bf16).astype(f32)

                over_tiles(0, tokens // WIDE, body, WIDE)

            @pl.when(sub > 0)
            def _():
                @pl.loop(0, 2)
                def _(part):
                    first = pl.multiple_of((2 * (sub - 1) + part) * (half // 2), half // 2)
                    grad = mm(n2_turned[pl.ds(first, half // 2), :], d_gu[...])
                    piece[lax.rem(k, 2), part] = grad.astype(bf16).reshape(piece.shape[2:])

            keep(k).start()

            @pl.when(k == 0)
            def _():
                keep(0).wait()

        @pl.loop(0, works)
        def _(k):
            work(k)
            advance(k)

        keep(works - 2).wait()
        keep(works - 1).wait()

        def leave(tile):
            to = shifted(tile, -there)
            y_send[0, to, :] = dn2[tile, :].astype(bf16)
            y_send[1, to, :] = moe[tile, :].astype(bf16)

        over_tiles(there, rows // TILE, leave)

    wide = (tokens, width)
    pl.run_scoped(
        expert_part,
        pltpu.VMEM(wide, bf16),
        pltpu.VMEM((width, tokens), bf16),
        pltpu.VMEM(wide, bf16),
        pltpu.VMEM((tokens, half), bf16),
        pltpu.VMEM(wide, bf16),
        pltpu.VMEM((tokens, 2 * half), bf16),
        pltpu.VMEM((2, width, 2 * half), bf16),
        pltpu.VMEM((2, half, width), bf16),
    )
    t = works
    dn2_copy = y_copy(Y_DN2, y_send.at[0], y_got.at[0])
    gate_copy = y_copy(Y_GATE, gate.at[pl.ds(there, rows)], got_gate)
    moe_copy = y_copy(Y_MOE, y_send.at[1], y_got.at[1])
    dn2_copy.start()
    gate_copy.start()
    advance_all(t, 5)
    t += 5

    def attention_part(gw, d_o, dkv):
        tail = gw.shape[3:]

        def store_rows(j, i, grad):
            gw[j, i // 2, i % 2] = grad.astype(bf16).reshape(tail)

        def core_weight(j):
            return remote_copy(
                gw.at[j, :, :, 1 - core], got_core_w.at[j], cs_sem.at[j], cr_sem.at[j],
                place.core_peer,
            )

        def to_owner(j):
            core_weight(j).wait()
            for member in range(2):
                for part in range(2):
                    gw[j, member, part, core] += got_core_w[j, member, part]
            for part in range(2):
                y_weight(gw, 2 * j + part).start()

        def kv_copies(i):
            first = pl.multiple_of(i * 128, 128)
            return [
                y_copy(
                    Y_DKV + 2 * i + j,
                    dkv.at[pl.ds(0, rows), pl.ds(first + j * (width // 2), 128)],
                    got_kv.at[:, pl.ds(first + j * (width // 2), 128)],
                )
                for j in range(2)
            ]

        def middle(h, g, n2, ao, wo, d_y):
            load(
                (h_hbm, h), (g_hbm.at[pl.ds(here, rows)], g), (n2_hbm, n2), (ao_hbm, ao),
                (w_hbm.at[:, pl.ds(2 * width, width)], wo),
            )
            dn2_copy.wait()
            gate_copy.wait()
            moe_copy.start()
            small[0] = jnp.zeros(small.shape[1:], f32)

            def body(tile):
                own = shifted(tile, here)
                s = share_own[tile, :]
                dg = gate[own, :] + got_gate[tile, :]
                d_logits = (s * (dg - jnp.sum(s * dg, axis=1, keepdims=True))).astype(bf16)
                d_n2 = dn2[own, :] + y_got[0, tile, :].astype(f32) + mm(d_logits, router[...])
                hidden = h[tile, :]
                factor = lax.rsqrt(jnp.mean(hidden * hidden, axis=-1, keepdims=True) + EPS)
                small[0, 0:EXPERTS, :] += mm_tn(d_logits, n2[tile, :])
                small[0, EXPERTS : EXPERTS + 1, :] += jnp.sum(
                    hidden * factor * d_n2, axis=0, keepdims=True
                )
                c = d_n2 * gains[1:2, :]
                mean = jnp.mean(c * hidden, axis=-1, keepdims=True)
                d_h = g[tile, :].astype(f32) + factor * (c - hidden * (factor * factor * mean))
                dn2[shifted(tile, there), :] = d_h
                d_y[tile, :] = d_h.astype(bf16)
                d_o[tile, :] = mm_nt(d_h.astype(bf16), wo[...]).astype(bf16)
                moe[own, :] += hidden

            @pl.loop(0, rows // TILE)
            def _(i):
                body(pl.ds(pl.multiple_of(i * TILE, TILE), TILE))
                advance(t + i)

            for i in range(4):
                columns = slice(i * width // 4, (i + 1) * width // 4)
                store_rows(0, i, mm_tn(ao[:, columns], d_y[...]))
            core_weight(0).start()

        pl.run_scoped(
            middle,
            pltpu.VMEM((rows, width), f32),
            *[pltpu.VMEM((rows, width), bf16)] * 3,
            pltpu.VMEM((width, width), bf16),
            pltpu.VMEM((rows, width), bf16),
        )
        advance(t + 2)
        to_owner(0)

        def heads(q, ao, kv, bias):
            load((q_hbm, q), (kv_hbm, kv), (ao_hbm, ao))
            row = here + lax.broadcasted_iota(jnp.int32, bias.shape, 0)
            col = lax.broadcasted_iota(jnp.int32, bias.shape, 1)
            seen = (seg_q[...] == seg_k[...]) & (row >= col)
            bias[...] = jnp.where(seen, 0.0, MASKED).astype(f32)

            @pl.loop(0, 4)
            def _(i):
                at_k = pl.ds(pl.multiple_of(i * 128, 128), 128)
                at_v = pl.ds(pl.multiple_of(width // 2 + i * 128, 128), 128)
                keys, values = kv[:, at_k], kv[:, at_v]
                dks, dvs = [], []
                for pair in range(2):
                    lanes = slice(pair * HEAD_SIZE, (pair + 1) * HEAD_SIZE)
                    key, value = keys[:, lanes], values[:, lanes]
                    at_q = pl.ds(pl.multiple_of(i * 256 + pair * 128, 128), 128)

                    def body(part, sums):
                        dk, dv = sums
                        tile = pl.ds(pl.multiple_of(part * TILE, TILE), TILE)
                        qs = two_heads(q[tile, at_q]) * SCALE
                        dos = two_heads(d_o[tile, at_q])
                        os = two_heads(ao[tile, at_q])
                        delta = jnp.sum(
                            dos.astype(f32) * os.astype(f32), axis=1, keepdims=True
                        )
                        lane = lax.broadcasted_iota(jnp.int32, (TILE, QUERY_HEADS), 1)
                        peaks = jnp.concatenate(
                            [
                                jnp.sum(
                                    jnp.where(lane == 4 * i + 2 * pair + head, lse[tile, :], 0.0),
                                    axis=1, keepdims=True,
                                )
                                for head in range(2)
                            ],
                            axis=0,
                        )
                        s = mm_nt(qs, key) - peaks
                        s = s.reshape(2, TILE, -1) + bias[tile, :][None]
                        p = jnp.exp(s).reshape(2 * TILE, -1)
                        dp = mm_nt(dos, value)
                        ds = (p * (dp - delta)).astype(bf16)
                        dq = mm(ds, key) * SCALE
                        moe[shifted(tile, there), at_q] = side_by_side(dq)
                        return dk + mm_tn(qs, ds), dv + mm_tn(dos, p.astype(bf16))

                    zero = jnp.zeros((HEAD_SIZE, kv.shape[0]), f32)
                    dk, dv = lax.fori_loop(0, rows // TILE, body, (zero, zero))
                    dks.append(dk)
                    dvs.append(dv)
                dkv[:, at_k] = jnp.concatenate(dks, axis=0).T.astype(bf16)
                dkv[:, at_v] = jnp.concatenate(dvs, axis=0).T.astype(bf16)

                @pl.when(group == 1)
                def _():
                    for copy in kv_copies(i):
                        copy.start()

                advance(t + 3 + 2 * i)
                advance(t + 4 + 2 * i)

        pl.run_scoped(
            heads,
            pltpu.VMEM((rows, width), bf16),
            pltpu.VMEM((rows, width), bf16),
            pltpu.VMEM((tokens, width), bf16),
            pltpu.VMEM((rows, tokens), f32),
        )

        def projections(n1, wqkv, x_in, lin):
            load((n1_hbm, n1), (w_hbm.at[:, pl.ds(0, 2 * width)], wqkv), (x_hbm, x_in))
            own = pl.ds(here, rows)

            def turn_back(to, source, where, at):
                value = source[where, at : at + 128].astype(f32)
                turned = value * cosine[...] - swap_halves(value) * sine[...]
                lin[:, to : to + 128] = turned.astype(bf16)

            def weight_grad(j, first):
                for i in range(4):
                    columns = slice(i * width // 4, (i + 1) * width // 4)
                    store_rows(j, i, mm_tn(n1[:, columns], lin[:, first : first + width]))
                core_weight(j).start()

            for j in range(0, width, 128):
                turn_back(j, moe, pl.ds(there, rows), j)
            weight_grad(1, 0)
            advance(t + 11)
            to_owner(1)
            advance(t + 12)

            @pl.when(group == 1)
            def _():
                for i in range(4):
                    for copy in kv_copies(i):
                        copy.wait_send()

            @pl.when(group == 0)
            def _():
                for i in range(4):
                    for copy in kv_copies(i):
                        copy.wait_recv()
                total = dkv[0:rows, :].astype(f32) + got_kv[...].astype(f32)
                dkv[0:rows, :] = total.astype(bf16)

            for j in range(0, width // 2, 128):
                turn_back(width + j, dkv, own, j)
            lin[:, 3 * width // 2 :] = dkv[own, width // 2 :]
            weight_grad(2, width)
            advance(t + 13)
            to_owner(2)
            advance(t + 14)

            def body(tile):
                dn1 = mm_nt(lin[tile, :], wqkv[...])
                xs = x_in[tile, :].astype(f32)
                factor = lax.rsqrt(jnp.mean(xs * xs, axis=-1, keepdims=True) + EPS)
                small[0, EXPERTS + 1 : EXPERTS + 2, :] += jnp.sum(
                    xs * factor * dn1, axis=0, keepdims=True
                )
                c = dn1 * gains[0:1, :]
                mean = jnp.mean(c * xs, axis=-1, keepdims=True)
                gx_ref[tile, :] = dn2[shifted(tile, there), :] + factor * (
                    c - xs * (factor * factor * mean)
                )
                total = moe[shifted(tile, here), :] + y_got[1, tile, :].astype(f32)
                y_ref[tile, :] = total.astype(bf16)

            moe_copy.wait()
            over_tiles(0, rows // TILE, body)

        pl.run_scoped(
            projections,
            pltpu.VMEM((rows, width), bf16),
            pltpu.VMEM((width, 2 * width), bf16),
            pltpu.VMEM((rows, width), bf16),
            pltpu.VMEM((rows, 2 * width), bf16),
        )
        last_tick, last_send = make_engine(
            place, count, pieces, pieces, stage, out, scratch, after_core(gw)
        )
        small_step = make_small_sum(place, small, got_small, ss_sem, sr_sem)

        first_last = t + 15

        @pl.loop(first_last, count + PHASES * LAG)
        def _(now):
            last_tick(now)

            @pl.when(now < pieces)
            def _():
                last_send(now)

            for i in range(7):

                @pl.when(now == first_last + 1 + 2 * i)
                def _():
                    small_step(i)

    pl.run_scoped(
        attention_part,
        pltpu.VMEM((3, 2, 2, *piece.shape[2:]), bf16),
        pltpu.VMEM((rows, width), bf16),
        pltpu.VMEM((tokens, width), bf16),
    )
    small_ref[...] = small[5]


def finish_kernel(
    owned, pieces_ref, small_ref, g_in_ref, g_out_ref, g_q_ref, g_k_ref, g_v_ref, g_wo_ref,
    router_ref, gain_ref,
):
    i = pl.program_id(0)

    def copy_at(condition, *outputs):
        @pl.when(condition)
        def _():
            at = 0
            for ref in outputs:
                width = ref.shape[-1]
                value = pieces_ref[0, :, at : at + width].astype(f32)
                ref[...] = value.reshape(ref.shape)
                at += width

    copy_at(i < 2 * owned, g_in_ref)
    copy_at((i >= 2 * owned) & (i < 3 * owned), g_out_ref)
    copy_at(i == 3 * owned, g_wo_ref)
    copy_at(i == 3 * owned + 1, g_q_ref)
    copy_at(i == 3 * owned + 2, g_k_ref, g_v_ref)

    @pl.when(i == 0)
    def _():
        columns = router_ref.shape[1]
        first = pl.multiple_of(lax.axis_index("group") * columns, columns)
        router_ref[...] = small_ref[0:EXPERTS, pl.ds(first, columns)]
        gain_ref[...] = small_ref[EXPERTS:, pl.ds(first, columns)]


def finish(pieces, small, owned, kv_width):
    number, half, width = pieces.shape
    shape = jax.ShapeDtypeStruct

    def whole(*size):
        return pl.BlockSpec(size, lambda i: (0,) * len(size))

    return pl.pallas_call(
        functools.partial(finish_kernel, owned),
        out_shape=(
            shape((2 * owned, half, width), f32),
            shape((owned, half, width), f32),
            shape((half, width), f32),
            shape((half, kv_width), f32),
            shape((half, kv_width), f32),
            shape((half, width), f32),
            shape((EXPERTS, width // 2), f32),
            shape((8, width // 2), f32),
        ),
        grid=(number,),
        in_specs=[
            pl.BlockSpec((1, half, width), lambda i: (i, 0, 0)),
            whole(*small.shape),
        ],
        out_specs=[
            pl.BlockSpec((1, half, width), lambda i: (jnp.minimum(i, 2 * owned - 1), 0, 0)),
            pl.BlockSpec(
                (1, half, width), lambda i: (jnp.clip(i - 2 * owned, 0, owned - 1), 0, 0)
            ),
            whole(half, width),
            whole(half, kv_width),
            whole(half, kv_width),
            whole(half, width),
            whole(EXPERTS, width // 2),
            whole(8, width // 2),
        ],
        compiler_params=params(48),
        cost_estimate=cost(0, 6 * pieces.size),
        name="finish",
    )(pieces, small)


def backward(
    n2, g_all, h, ao, q, kv_all, n1, w_all, x, w_in, w_out, share, router, gains, lse, seg_q, seg_k,
    cosine, sine,
):
    rows, width = n2.shape
    owned, half = w_out.shape[:2]
    tokens, quarter = 2 * rows, half // 16
    pieces = 6 * owned
    shape = jax.ShapeDtypeStruct
    vmem = pl.BlockSpec(memory_space=pltpu.VMEM)
    hbm = pl.BlockSpec(memory_space=pl.ANY)
    dma = pltpu.SemaphoreType.DMA
    small_rows = EXPERTS + 8
    return pl.pallas_call(
        backward_kernel,
        out_shape=(
            shape((rows, width), bf16),
            shape((rows, width), f32),
            shape((small_rows, width), f32),
            shape((pieces + 6, 2, 4, quarter, width), bf16),
            shape((pieces, 2, 4, quarter, width), bf16),
        ),
        in_specs=[hbm] * 11 + [vmem] * 8,
        out_specs=[vmem, vmem, vmem, hbm, hbm],
        scratch_shapes=[
            pltpu.VMEM((tokens, width), f32),
            pltpu.VMEM((tokens, width), f32),
            pltpu.VMEM((tokens, EXPERTS), f32),
            pltpu.VMEM((tokens, EXPERTS), f32),
            pltpu.VMEM((rows, EXPERTS), f32),
            pltpu.VMEM((2, rows, width), bf16),
            pltpu.VMEM((2, rows, width), bf16),
            pltpu.VMEM((rows, width), bf16),
            pltpu.VMEM((3, 2, 2, 4, quarter, width), bf16),
            pltpu.VMEM((3, 2, 4, quarter, width), bf16),
            pltpu.VMEM((6, small_rows, width), f32),
            pltpu.VMEM((6, small_rows, width), f32),
            pltpu.VMEM((2, 2, 2, 4, quarter, width), bf16),
            dma((2,)),
            dma((2, 2)),
            dma((5,)),
            dma((Y_KINDS,)),
            dma((Y_KINDS,)),
            dma((3,)),
            dma((3,)),
            dma((6,)),
            dma((6,)),
            *engine_scratch(quarter, width),
        ],
        compiler_params=pltpu.CompilerParams(
            collective_id=1, has_side_effects=True, vmem_limit_bytes=63 * MIB
        ),
        cost_estimate=cost(18 * tokens * width * half * owned, 6 * w_in.size),
        name="backward",
    )(
        n2, g_all, h, ao, q, kv_all, n1, w_all, x, w_in, w_out, share, router, gains, lse, seg_q,
        seg_k, cosine, sine,
    )


def expert_pass(n2, grad, share, w_in, w_out):
    half = w_out.shape[0]
    gu = mm(n2, w_in)
    z, w = gu[:, :half], gu[:, half:]
    sg = jax.nn.sigmoid(z)
    act = (z * sg * w).astype(bf16)
    ye = mm(act, w_out).astype(bf16).astype(f32)
    d_gate = jnp.sum(grad * ye, axis=1)
    d_ye = (share * grad).astype(bf16)
    g_out = mm_tn(act, d_ye).astype(bf16)
    d_act = mm_nt(d_ye, w_out)
    d_gu = jnp.concatenate(
        [d_act * w * sg * (1.0 + z * (1.0 - sg)), d_act * z * sg], axis=1
    ).astype(bf16)
    g_in = mm_tn(n2, d_gu).astype(bf16)
    d_xe = mm_nt(d_gu, w_in).astype(bf16).astype(f32)
    return share * ye, d_gate, g_in, g_out, d_xe


def all_experts(n2, grad, share, w_in, w_out):
    moe = jnp.zeros(n2.shape, f32)
    d_n2 = jnp.zeros_like(moe)
    d_gate, g_in, g_out = [], [], []
    for i in range(w_in.shape[0]):
        y, dg, gi, go, dx = expert_pass(
            n2, grad.astype(f32), share[:, i : i + 1], w_in[i], w_out[i]
        )
        moe, d_n2 = moe + y, d_n2 + dx
        d_gate.append(dg)
        g_in.append(gi)
        g_out.append(go)
    g_in, g_out = lax.psum((jnp.stack(g_in), jnp.stack(g_out)), "replica")
    return moe, d_n2, jnp.stack(d_gate, 1), g_in.astype(f32), g_out.astype(f32)


def on_device(
    layer_input, document_numbers, routes, norm_attn, w_query, key_weight, value_weight, w_out,
    norm_moe, w_router, expert_in, expert_out, cotangent,
):
    rows, width = layer_input.shape
    group = lax.axis_index("group")
    first = group * rows
    owned = expert_in.shape[0]
    kv_width = KEY_VALUE_HEADS * HEAD_SIZE

    q_width = QUERY_HEADS * HEAD_SIZE
    if lax.axis_size("replica") == 16 and lax.axis_size("group") == 2:
        (n1, q, ao, h, n2, share, lse, cosine, sine, seg_k, seg_q, router, gains, kv_all, grad_all,
         w_all) = (
            forward(
                layer_input, document_numbers, routes, (norm_attn, norm_moe), w_router, w_query,
                key_weight, value_weight, w_out, cotangent,
            )
        )
        layer_output, grad_input, small_sum, sums, _ = backward(
            n2, grad_all, h, ao, q, kv_all, n1, w_all, layer_input, expert_in, expert_out, share,
            router, gains, lse, seg_q, seg_k, cosine, sine,
        )
        half = expert_out.shape[1]
        g_in, g_out, g_q, g_k, g_v, g_wo, g_router, g_gains = finish(
            sums.reshape(-1, half, width), small_sum, owned, kv_width
        )
        return (
            layer_output,
            grad_input,
            g_gains[1],
            g_q,
            g_k,
            g_v,
            g_wo,
            g_gains[0],
            g_router.T,
            g_in.reshape(expert_in.shape),
            g_out,
        )

    seg_all = gather(document_numbers)
    position = lax.dynamic_slice_in_dim(doc_positions(seg_all), first, rows, 0)
    cosine, sine = turn_tables(position)
    small = gather(jnp.concatenate([norm_attn[:, None], norm_moe[:, None], w_router], axis=1))
    gain_attn = small[:, 0].astype(f32)[None, :]
    gain_moe = small[:, 1].astype(f32)[None, :]
    router = small[:, 2:]
    w_qkv = gather(jnp.concatenate([w_query, key_weight, value_weight], axis=1))
    wo = gather(w_out)
    grad_all = gather(cotangent)

    n1, q, k, v = project(layer_input, gain_attn, w_qkv, cosine, sine)
    kv_all = gather(jnp.concatenate([k, v], axis=1))
    k_all, v_all = kv_all[:, :kv_width], kv_all[:, kv_width:]
    first_row = jnp.full((1,), first, jnp.int32)
    seg_q, seg_k = document_numbers[:, None], seg_all[None, :]
    ao = attend(first_row, q, k_all, v_all, seg_q, seg_k)

    x = layer_input.astype(f32)
    h = x + mm(ao, wo)
    r2 = rms_factor(h)
    n2 = (h * r2 * gain_moe).astype(bf16)
    logits = mm(n2, router)
    chosen = jnp.any(routes[:, :, None] == jnp.arange(EXPERTS, dtype=jnp.int32), axis=1)
    picked = jnp.where(chosen, logits, MASKED)
    e = jnp.where(chosen, jnp.exp(picked - jnp.max(picked, axis=1, keepdims=True)), 0.0)
    share = e / jnp.sum(e, axis=1, keepdims=True)

    n2_all = gather(n2)
    share_all = lax.dynamic_slice_in_dim(gather(share), group * owned, owned, 1)
    moe, d_n2_all, d_gate, g_in, g_out = all_experts(
        n2_all, grad_all, share_all, expert_in, expert_out
    )
    d_gate = lax.dynamic_update_slice_in_dim(
        jnp.zeros((n2_all.shape[0], EXPERTS), f32), d_gate, group * owned, 1
    )
    d_gate = lax.psum_scatter(d_gate, "group", scatter_dimension=0, tiled=True)
    layer_output = (h + owner_sum(moe).astype(f32)).astype(bf16)

    d_logits = (share * (d_gate - jnp.sum(share * d_gate, axis=1, keepdims=True))).astype(bf16)
    g_router = mm_tn(n2, d_logits)
    d_n2 = owner_sum(d_n2_all).astype(f32) + mm_nt(d_logits, router)
    g_gain_moe = jnp.sum(h * r2 * d_n2, axis=0)
    c = d_n2 * gain_moe
    d_h = cotangent.astype(f32) + r2 * (
        c - h * r2 * r2 * jnp.mean(c * h, axis=-1, keepdims=True)
    )
    d_y = d_h.astype(bf16)
    g_wo = mm_tn(ao, d_y).astype(bf16)
    d_o = mm_nt(d_y, wo).astype(bf16)

    dq, dk_all, dv_all = attend_grad(first_row, q, k_all, v_all, d_o, seg_q, seg_k)
    dkv = owner_sum(jnp.concatenate([dk_all, dv_all], axis=1))
    g_qkv, grad_input, g_gain_attn = project_grad(
        dq, dkv[:, :kv_width], dkv[:, kv_width:], n1, w_qkv, cosine, sine, layer_input,
        gain_attn, d_h,
    )

    g_attn = owner_sum(jnp.concatenate([g_qkv, g_wo], axis=1))
    g_small = owner_sum(
        jnp.concatenate([g_gain_attn.reshape(-1, 1), g_gain_moe[:, None], g_router], axis=1)
    )
    g_attn, g_small = (t.astype(f32) for t in lax.psum((g_attn, g_small), "replica"))
    return (
        layer_output,
        grad_input,
        g_small[:, 0],
        g_attn[:, :q_width],
        g_attn[:, q_width : q_width + kv_width],
        g_attn[:, q_width + kv_width : q_width + 2 * kv_width],
        g_attn[:, q_width + 2 * kv_width :],
        g_small[:, 1],
        g_small[:, 2:],
        g_in,
        g_out,
    )


def solution(mesh):
    tokens, weights = P(("replica", "group"), None), P("group", None)
    in_specs = (
        tokens, P(("replica", "group")), tokens, P("group"), weights, weights, weights, weights,
        P("group"), weights, P("group", None, None), P("group", None, None), tokens,
    )
    out_specs = (
        tokens, tokens, P("group"), weights, weights, weights, weights, P("group"), weights,
        P("group", None, None), P("group", None, None),
    )
    return jax.shard_map(
        on_device, mesh=mesh, in_specs=in_specs, out_specs=out_specs, check_vma=False
    )
```

```python
import functools

import jax
import jax.numpy as jnp
import numpy as np
from jax import lax
from jax.experimental import pallas as pl
from jax.experimental.pallas import tpu as pltpu
from jax.sharding import PartitionSpec as P

QUERY_HEADS = 16
KEY_VALUE_HEADS = 8
HEAD_SIZE = 64
EXPERTS = 16
EPS = 1e-06
MASKED = -1e30
SCALE = HEAD_SIZE ** (-0.5)

f32 = jnp.float32
bf16 = jnp.bfloat16
MIB = 1 << 20


def mm(a, b):
    return lax.dot_general(a, b, (((1,), (0,)), ((), ())), preferred_element_type=f32)


def mm_nt(a, b):
    return lax.dot_general(a, b, (((1,), (1,)), ((), ())), preferred_element_type=f32)


def mm_tn(a, b):
    return lax.dot_general(a, b, (((0,), (0,)), ((), ())), preferred_element_type=f32)


def params(mib):
    return pltpu.CompilerParams(vmem_limit_bytes=mib * MIB)


def cost(flops, moved):
    return pl.CostEstimate(flops=int(flops), bytes_accessed=int(moved), transcendentals=0)


def doc_positions(seg_ids):
    length = seg_ids.shape[0]
    index = jnp.arange(length, dtype=jnp.int32)
    previous = jnp.concatenate([seg_ids[:1] - 1, seg_ids[:-1]])
    is_start = (seg_ids != previous) | (index == 0)
    start = lax.cummax(jnp.where(is_start, index, 0), axis=0)
    return index - start


def turn_tables(position):
    half = HEAD_SIZE // 2
    exponent = jnp.arange(half, dtype=f32) * (-2.0 / HEAD_SIZE)
    inv_freq = jnp.power(10000.0, exponent)
    angles = position.astype(f32)[:, None] * inv_freq[None, :]
    cosine, sine = jnp.cos(angles), jnp.sin(angles)
    return (
        jnp.concatenate([cosine] * 4, axis=1),
        jnp.concatenate([-sine, sine, -sine, sine], axis=1),
    )


def swap_halves(t):
    lane = lax.broadcasted_iota(jnp.int32, t.shape, 1)
    return jnp.where(
        lane % HEAD_SIZE < HEAD_SIZE // 2, pltpu.roll(t, 96, 1), pltpu.roll(t, 32, 1)
    )


def qkv_kernel(x_ref, gain_ref, w_ref, cos_ref, sin_ref, n1_ref, q_ref, k_ref, v_ref):
    x = x_ref[...].astype(f32)
    factor = lax.rsqrt(jnp.mean(x * x, axis=-1, keepdims=True) + EPS)
    n1 = (x * factor * gain_ref[...]).astype(bf16)
    n1_ref[...] = n1
    cosine, sine = cos_ref[...], sin_ref[...]
    q_width, k_width = q_ref.shape[1], k_ref.shape[1]
    for start in range(0, q_width + k_width, 256):
        lin = mm(n1, w_ref[:, start : start + 256])
        for part in (0, 128):
            t = lin[:, part : part + 128]
            turned = (t * cosine + swap_halves(t) * sine).astype(bf16)
            at = start + part
            if at < q_width:
                q_ref[:, at : at + 128] = turned
            else:
                k_ref[:, at - q_width : at - q_width + 128] = turned
    v_ref[...] = mm(n1, w_ref[:, q_width + k_width :]).astype(bf16)


def project(x, gain, w, cosine, sine):
    rows, width = x.shape
    q_width, k_width = QUERY_HEADS * HEAD_SIZE, KEY_VALUE_HEADS * HEAD_SIZE
    shape = jax.ShapeDtypeStruct
    return pl.pallas_call(
        qkv_kernel,
        out_shape=(
            shape((rows, width), bf16),
            shape((rows, q_width), bf16),
            shape((rows, k_width), bf16),
            shape((rows, k_width), bf16),
        ),
        compiler_params=params(40),
        cost_estimate=cost(2 * rows * width * w.shape[1], 2 * w.size + 8 * x.size),
        name="project",
    )(x, gain, w, cosine, sine)


def qkv_grad_kernel(
    dq_ref, dk_ref, dv_ref, n1_ref, w_ref, cos_ref, sin_ref, x_ref, gain_ref, dh_ref,
    gw_ref, gx_ref, gg_ref, lin_ref,
):
    cosine, sine = cos_ref[...], sin_ref[...]
    q_width, k_width = dq_ref.shape[1], dk_ref.shape[1]
    for ref, width, base in ((dq_ref, q_width, 0), (dk_ref, k_width, q_width)):
        for at in range(0, width, 128):
            t = ref[:, at : at + 128].astype(f32)
            turned = (t * cosine - swap_halves(t) * sine).astype(bf16)
            lin_ref[:, base + at : base + at + 128] = turned
    lin_ref[:, q_width + k_width :] = dv_ref[...].astype(bf16)
    total = q_width + 2 * k_width
    n1 = n1_ref[...]
    for at in range(0, total, 512):
        gw_ref[:, at : at + 512] = mm_tn(n1, lin_ref[:, at : at + 512]).astype(bf16)
    dn1 = mm_nt(lin_ref[...], w_ref[...])
    x = x_ref[...].astype(f32)
    factor = lax.rsqrt(jnp.mean(x * x, axis=-1, keepdims=True) + EPS)
    gg_ref[...] = jnp.sum(x * factor * dn1, axis=0, keepdims=True)
    c = dn1 * gain_ref[...]
    mean = jnp.mean(c * x, axis=-1, keepdims=True)
    gx_ref[...] = dh_ref[...] + factor * (c - x * (factor * factor * mean))


def project_grad(dq, dk, dv, n1, w, cosine, sine, x, gain, dh):
    rows, width = x.shape
    shape = jax.ShapeDtypeStruct
    return pl.pallas_call(
        qkv_grad_kernel,
        out_shape=(
            shape(w.shape, bf16),
            shape((rows, width), f32),
            shape((1, width), f32),
        ),
        scratch_shapes=[pltpu.VMEM((rows, w.shape[1]), bf16)],
        compiler_params=params(56),
        cost_estimate=cost(4 * rows * width * w.shape[1], 4 * w.size + 16 * x.size),
        name="project_grad",
    )(dq, dk, dv, n1, w, cosine, sine, x, gain, dh)


def visible_bias(first_ref, seg_q_ref, seg_k_ref, bias_ref):
    rows, keys = bias_ref.shape
    row = first_ref[0] + lax.broadcasted_iota(jnp.int32, (rows, keys), 0)
    col = lax.broadcasted_iota(jnp.int32, (rows, keys), 1)
    seen = (seg_q_ref[...] == seg_k_ref[...]) & (row >= col)
    bias_ref[...] = jnp.where(seen, 0.0, MASKED).astype(f32)


def attend_kernel(first_ref, q_ref, k_ref, v_ref, seg_q_ref, seg_k_ref, o_ref, bias_ref):
    @pl.when(pl.program_id(0) == 0)
    def _():
        visible_bias(first_ref, seg_q_ref, seg_k_ref, bias_ref)

    bias = bias_ref[...]
    for head in range(4):
        at, kv = head * HEAD_SIZE, head // 2 * HEAD_SIZE
        s = mm_nt(q_ref[:, at : at + HEAD_SIZE], k_ref[:, kv : kv + HEAD_SIZE]) * SCALE + bias
        e = jnp.exp(s - jnp.max(s, axis=1, keepdims=True))
        total = jnp.sum(e, axis=1, keepdims=True)
        o = mm(e.astype(bf16), v_ref[:, kv : kv + HEAD_SIZE]) / total
        o_ref[:, at : at + HEAD_SIZE] = o.astype(bf16)


def attend(first, q, k, v, seg_q, seg_k):
    rows, width = q.shape
    keys = k.shape[0]
    wide = pl.BlockSpec((rows, 256), lambda i, first: (0, i))
    narrow = pl.BlockSpec((keys, 128), lambda i, first: (0, i))
    return pl.pallas_call(
        attend_kernel,
        out_shape=jax.ShapeDtypeStruct((rows, width), bf16),
        grid_spec=pltpu.PrefetchScalarGridSpec(
            num_scalar_prefetch=1,
            grid=(width // 256,),
            in_specs=[
                wide,
                narrow,
                narrow,
                pl.BlockSpec((rows, 1), lambda i, first: (0, 0)),
                pl.BlockSpec((1, keys), lambda i, first: (0, 0)),
            ],
            out_specs=wide,
            scratch_shapes=[pltpu.VMEM((rows, keys), f32)],
        ),
        compiler_params=params(48),
        cost_estimate=cost(16 * rows * keys * width, 4 * q.size + 4 * k.size),
        name="attend",
    )(first, q, k, v, seg_q, seg_k)


def attend_grad_kernel(
    first_ref, q_ref, k_ref, v_ref, do_ref, seg_q_ref, seg_k_ref,
    dq_ref, dk_ref, dv_ref, bias_ref,
):
    @pl.when(pl.program_id(0) == 0)
    def _():
        visible_bias(first_ref, seg_q_ref, seg_k_ref, bias_ref)

    bias = bias_ref[...]
    for pair in range(2):
        kv = pair * HEAD_SIZE
        k, v = k_ref[:, kv : kv + HEAD_SIZE], v_ref[:, kv : kv + HEAD_SIZE]
        dk = dv = None
        for head in (2 * pair, 2 * pair + 1):
            at = head * HEAD_SIZE
            q, do = q_ref[:, at : at + HEAD_SIZE], do_ref[:, at : at + HEAD_SIZE]
            s = mm_nt(q, k) * SCALE + bias
            e = jnp.exp(s - jnp.max(s, axis=1, keepdims=True))
            p = e * (1.0 / jnp.sum(e, axis=1, keepdims=True))
            dp = mm_nt(do, v)
            delta = jnp.sum(p * dp, axis=1, keepdims=True)
            ds = (p * (dp - delta) * SCALE).astype(bf16)
            dq_ref[:, at : at + HEAD_SIZE] = mm(ds, k)
            dk_part, dv_part = mm_tn(ds, q), mm_tn(p.astype(bf16), do)
            dk = dk_part if dk is None else dk + dk_part
            dv = dv_part if dv is None else dv + dv_part
        dk_ref[:, kv : kv + HEAD_SIZE] = dk.astype(bf16)
        dv_ref[:, kv : kv + HEAD_SIZE] = dv.astype(bf16)


def attend_grad(first, q, k, v, do, seg_q, seg_k):
    rows, width = q.shape
    keys = k.shape[0]
    wide = pl.BlockSpec((rows, 256), lambda i, first: (0, i))
    narrow = pl.BlockSpec((keys, 128), lambda i, first: (0, i))
    shape = jax.ShapeDtypeStruct
    return pl.pallas_call(
        attend_grad_kernel,
        out_shape=(
            shape((rows, width), f32),
            shape(k.shape, bf16),
            shape(k.shape, bf16),
        ),
        grid_spec=pltpu.PrefetchScalarGridSpec(
            num_scalar_prefetch=1,
            grid=(width // 256,),
            in_specs=[
                wide,
                narrow,
                narrow,
                wide,
                pl.BlockSpec((rows, 1), lambda i, first: (0, 0)),
                pl.BlockSpec((1, keys), lambda i, first: (0, 0)),
            ],
            out_specs=[wide, narrow, narrow],
            scratch_shapes=[pltpu.VMEM((rows, keys), f32)],
        ),
        compiler_params=params(56),
        cost_estimate=cost(40 * rows * keys * width // 4, 8 * q.size + 8 * k.size),
        name="attend_grad",
    )(first, q, k, v, do, seg_q, seg_k)


def gather(value):
    return lax.all_gather(value, "group", axis=0, tiled=True)


def owner_sum(value):
    return lax.psum_scatter(value.astype(bf16), "group", scatter_dimension=0, tiled=True)


def rms_factor(values):
    return lax.rsqrt(jnp.mean(values * values, axis=-1, keepdims=True) + EPS)


LAG = 2
PHASES = 7
SEMS = 8
(CORE, X_A, IN_B, IN_A, HALF_B, MID_A, RUNG_B, OUT_A, BACK_B, SPREAD_A, OUT_B, JOIN, KINDS) = range(13)
(Y_SHARE, Y_DN2, Y_MOE, Y_GATE, Y_DKV, Y_WEIGHT, Y_N2, Y_KINDS) = (0, 1, 2, 3, 4, 12, 18, 20)


def engine_scratch(quarter, width):
    def vmem(*shape):
        return pltpu.VMEM((*shape, quarter, width), bf16)

    return [
        vmem(4, 4),
        vmem(4, 4),
        vmem(4),
        vmem(8, 2),
        vmem(8),
        vmem(4),
        vmem(4),
        vmem(4),
        vmem(LAG, 4),
        vmem(LAG),
        vmem(LAG, 2),
        vmem(LAG),
        vmem(LAG),
        vmem(LAG),
        vmem(LAG),
        pltpu.SemaphoreType.DMA((KINDS, SEMS)),
        pltpu.SemaphoreType.DMA((KINDS, SEMS)),
        pltpu.SemaphoreType.DMA((3, SEMS)),
    ]


class Place:
    def __init__(self):
        r = lax.axis_index("replica")
        self.core, self.x, z = lax.rem(r, 2), lax.rem(r // 2, 2), r // 4
        self.group = lax.axis_index("group")
        self.inner = (z == 1) | (z == 2)
        self.outer = jnp.logical_not(self.inner)
        self.late = z // 2
        up = (z == 0) | (z == 2)
        self.core_peer = {"replica": r + 1 - 2 * self.core}
        self.x_peer = {"replica": r + 2 - 4 * self.x}
        self.line_peer = {"replica": jnp.where(up, r + 4, r - 4)}
        self.mid_peer = {"replica": jnp.where(z == 1, r + 4, r - 4)}
        self.y_peer = {"group": 1 - self.group}

    def greet(self):
        barrier = pltpu.get_barrier_semaphore()

        def signal(peer):
            pl.semaphore_signal(
                barrier, inc=1, device_id=peer, device_id_type=pl.DeviceIdType.MESH
            )

        for peer in (self.core_peer, self.x_peer, self.line_peer, self.y_peer):
            signal(peer)

        @pl.when(self.inner)
        def _():
            signal(self.mid_peer)
            pl.semaphore_wait(barrier, 5)

        @pl.when(self.outer)
        def _():
            pl.semaphore_wait(barrier, 4)


def remote_copy(src, dst, send_sem, recv_sem, peer):
    return pltpu.make_async_remote_copy(
        src_ref=src, dst_ref=dst, send_sem=send_sem, recv_sem=recv_sem, device_id=peer,
        device_id_type=pl.DeviceIdType.MESH,
    )


def make_engine(place, count, split, split_of, stage, out, scratch, late_piece):
    (mine, got_core, got_x, got_end_b, got_end_a, got_mid_b, got_mid_a, got_rung,
     summed, a_x, b_end, a_end, b_mid, a_all, b_all, send_sem, recv_sem, copy_sem) = scratch
    core, x, inner, outer, late = place.core, place.x, place.inner, place.outer, place.late

    owned = split_of // 6

    def spot(k):
        e, sub, part = k // 6, lax.rem(k // 2, 3), lax.rem(k, 2)
        inner_spot = jnp.where(sub == 0, 4 * owned + 2 * e, 4 * e + 2 * sub - 2) + part
        return jnp.where(k < split_of, inner_spot, k)

    def remote(kind, k, src, dst, peer):
        slot = lax.rem(k, SEMS)
        return remote_copy(src, dst, send_sem.at[kind, slot], recv_sem.at[kind, slot], peer)

    def local(kind, k, src, dst):
        return pltpu.make_async_copy(src, dst, copy_sem.at[kind, lax.rem(k, SEMS)])

    def core_copy(k):
        return remote(
            CORE, k, stage.at[k, 1 - core], got_core.at[lax.rem(k, 4)], place.core_peer
        )

    def mine_copy(k):
        return local(2, k, stage.at[k, core], mine.at[lax.rem(k, 4)])

    def x_copy(k):
        return remote(
            X_A, k, summed.at[lax.rem(k, LAG), 1 - x], got_x.at[lax.rem(k, 4)], place.x_peer
        )

    def in_b_copy(k):
        return remote(
            IN_B, k, summed.at[lax.rem(k, LAG), pl.ds(2, 2)], got_end_b.at[lax.rem(k, 8)],
            place.line_peer,
        )

    def in_a_copy(k):
        return remote(
            IN_A, k, a_x.at[lax.rem(k, LAG)], got_end_a.at[lax.rem(k, 8)], place.line_peer
        )

    def half_b_copy(k):
        return remote(
            HALF_B, k, b_end.at[lax.rem(k, LAG), 1 - late], got_mid_b.at[lax.rem(k, 4)],
            place.mid_peer,
        )

    def mid_a_copy(k):
        return remote(
            MID_A, k, a_end.at[lax.rem(k, LAG)], got_mid_a.at[lax.rem(k, 4)], place.mid_peer
        )

    def rung_copy(k):
        return remote(
            RUNG_B, k, b_mid.at[lax.rem(k, LAG)], got_rung.at[lax.rem(k, 4)], place.x_peer
        )

    def out_a_copy(k):
        return remote(OUT_A, k, a_all.at[lax.rem(k, LAG)], out.at[spot(k), core, x], place.line_peer)

    def back_b_copy(k, quarter):
        return remote(
            BACK_B, k, b_all.at[lax.rem(k, LAG)], out.at[spot(k), core, quarter], place.mid_peer
        )

    def spread_copy(k, quarter):
        return remote(SPREAD_A, k, out.at[spot(k), core, x], out.at[spot(k), core, quarter], place.x_peer)

    def out_b_copy(k):
        part = out.at[spot(k), core, pl.ds(2, 2)]
        return remote(OUT_B, k, part, part, place.line_peer)

    def join_copy(k, half):
        return remote(JOIN, k, out.at[spot(k), core], out.at[spot(k), half], place.core_peer)

    def keep_a(k):
        return local(0, k, a_all.at[lax.rem(k, LAG)], out.at[spot(k), core, x])

    def keep_b(k):
        return local(1, k, b_all.at[lax.rem(k, LAG)], out.at[spot(k), core, 2 + late])

    def phase1(k):
        i = lax.rem(k, LAG)

        @pl.when(k < split)
        def _():
            mine_copy(k).wait()
            core_copy(k).wait()
            summed[i] = mine[lax.rem(k, 4)] + got_core[lax.rem(k, 4)]

        if count > split:

            @pl.when(k >= split)
            def _():
                copy, own, other = late_piece(k)
                copy.wait()
                summed[i] = own[...] + other[...]

        x_copy(k).start()

        @pl.when(outer)
        def _():
            in_b_copy(k).start()

    def phase2(k):
        i = lax.rem(k, LAG)
        x_copy(k).wait()
        a_x[i] = summed[i, x] + got_x[lax.rem(k, 4)]

        @pl.when(outer)
        def _():
            in_a_copy(k).start()
            in_b_copy(k).wait_send()

        @pl.when(inner)
        def _():
            in_b_copy(k).wait_recv()
            b_end[i] = summed[i, 2:4] + got_end_b[lax.rem(k, 8)]
            half_b_copy(k).start()

    def phase3(k):
        i = lax.rem(k, LAG)

        @pl.when(outer)
        def _():
            in_a_copy(k).wait_send()

        @pl.when(inner)
        def _():
            in_a_copy(k).wait_recv()
            a_end[i] = a_x[i] + got_end_a[lax.rem(k, 8)]
            mid_a_copy(k).start()
            half_b_copy(k).wait()
            b_mid[i] = b_end[i, late] + got_mid_b[lax.rem(k, 4)]
            rung_copy(k).start()

    def phase4(k):
        i = lax.rem(k, LAG)

        @pl.when(inner)
        def _():
            mid_a_copy(k).wait()
            a_all[i] = a_end[i] + got_mid_a[lax.rem(k, 4)]
            out_a_copy(k).start()
            keep_a(k).start()
            rung_copy(k).wait()
            b_all[i] = b_mid[i] + got_rung[lax.rem(k, 4)]
            back_b_copy(k, 2 + late).start()
            keep_b(k).start()

    def phase5(k):
        @pl.when(outer)
        def _():
            out_a_copy(k).wait_recv()

        @pl.when(inner)
        def _():
            keep_a(k).wait()
            out_a_copy(k).wait_send()

        spread_copy(k, x).start()

        @pl.when(inner)
        def _():
            keep_b(k).wait()
            back_b_copy(k, 2 + late).wait_send()
            back_b_copy(k, 3 - late).wait_recv()
            out_b_copy(k).start()

    def phase6(k):
        spread_copy(k, x).wait_send()
        spread_copy(k, 1 - x).wait_recv()

        @pl.when(outer)
        def _():
            out_b_copy(k).wait_recv()

        @pl.when(inner)
        def _():
            out_b_copy(k).wait_send()

        join_copy(k, core).start()

    def phase7(k):
        join_copy(k, core).wait_send()
        join_copy(k, 1 - core).wait_recv()

    phases = (phase1, phase2, phase3, phase4, phase5, phase6, phase7)

    def tick(t):
        for number in range(PHASES, 0, -1):
            k = t - LAG * number

            @pl.when((k >= 0) & (k < count))
            def _():
                phases[number - 1](k)

    def send(k):
        @pl.when(k < split)
        def _():
            core_copy(k).start()
            mine_copy(k).start()

    return tick, send


def make_small_sum(place, values, got, send_sem, recv_sem):
    def copy(i, peer):
        return remote_copy(values.at[i], got.at[i], send_sem.at[i], recv_sem.at[i], peer)

    peers = (
        place.core_peer, place.x_peer, place.y_peer, place.line_peer, place.mid_peer,
        place.line_peer,
    )

    def add(i):
        values[i + 1] = values[i] + got[i]

    def step(i):
        if 1 <= i <= 3:
            copy(i - 1, peers[i - 1]).wait()
            add(i - 1)
        if i <= 2:
            copy(i, peers[i]).start()
        if i == 3:

            @pl.when(place.outer)
            def _():
                copy(3, peers[3]).start()

        if i == 4:

            @pl.when(place.outer)
            def _():
                copy(3, peers[3]).wait_send()

            @pl.when(place.inner)
            def _():
                copy(3, peers[3]).wait_recv()
                add(3)
                copy(4, peers[4]).start()

        if i == 5:

            @pl.when(place.inner)
            def _():
                copy(4, peers[4]).wait()
                add(4)
                copy(5, peers[5]).start()

        if i == 6:

            @pl.when(place.inner)
            def _():
                copy(5, peers[5]).wait_send()

            @pl.when(place.outer)
            def _():
                copy(5, peers[5]).wait_recv()
                values[5] = got[5]

    return step


TILE = 256
WIDE = 1024


(F_SMALL, F_SEG, F_WQ, F_WK, F_WV, F_WO, F_GRAD, F_KV) = range(8)
F_KINDS = F_KV + 8
W_KV, W_Q, W_OUT = 0, 1, 2
SMALL_ROWS = 32


def two_heads(t):
    return jnp.concatenate([t[:, :HEAD_SIZE], t[:, HEAD_SIZE:]], axis=0)


def side_by_side(t):
    half = t.shape[0] // 2
    return jnp.concatenate([t[:half], t[half:]], axis=1)


def layer_kernel(
    x_hbm, wq_hbm, wk_hbm, wv_hbm, wo_hbm, g_hbm, w1_hbm, w2_hbm, small_own, seg_own, routes, inv_freq,
    y_ref, gx_ref, small_ref, out, stage, q_hbm, kv_hbm, n1_hbm, g_all, w_all,
    ao, h, n2, lse, cosine_ref, sine_ref, seg_k, seg_q, router, gains, small_in, seg,
    f_send, f_recv, x_send, x_recv, c_send, c_recv, keep_sem,
    moe, dn2, share, gate, got_gate, y_send, y_got, got_kv, got_core_w, got_y_w, small, got_small,
    piece, piece_sem, w_sem, load_sem, ys_sem, yr_sem, cs_sem, cr_sem, ss_sem, sr_sem, *scratch,
):
    rows, width = x_hbm.shape
    tokens = 2 * rows
    owned, half = w2_hbm.shape[0], w2_hbm.shape[1]
    works = 3 * owned
    pieces = 2 * works
    count = pieces + 6
    place = Place()
    group, core = place.group, place.core
    here = pl.multiple_of(group * rows, rows)
    there = pl.multiple_of((1 - group) * rows, rows)

    def load(*pairs):
        copies = [
            pltpu.make_async_copy(src, dst, load_sem.at[i]) for i, (src, dst) in enumerate(pairs)
        ]
        for copy in copies:
            copy.start()
        for copy in copies:
            copy.wait()

    def y_copy(kind, src, dst):
        return remote_copy(src, dst, ys_sem.at[kind], yr_sem.at[kind], place.y_peer)

    def over_tiles(first, number, body, size=TILE):
        @pl.loop(0, number)
        def _(i):
            body(pl.ds(pl.multiple_of(first + i * size, size), size))

    def shifted(tile, by):
        return pl.ds(pl.multiple_of(tile.start + by, TILE), TILE)

    def after_core(gw):
        def late_piece(k):
            j, part = (k - pieces) // 2, lax.rem(k - pieces, 2)
            return (
                y_weight(gw, k - pieces), gw.at[j, group, part, core], got_y_w.at[j, part]
            )

        return late_piece

    def y_weight(gw, i):
        j, part = i // 2, i % 2
        return y_copy(Y_WEIGHT + i, gw.at[j, 1 - group, part, core], got_y_w.at[j, part])

    def fetch(w1, w2, e):
        slot = lax.rem(e, 2)
        return (
            pltpu.make_async_copy(w1_hbm.at[e], w1.at[slot], w_sem.at[0, slot]),
            pltpu.make_async_copy(w2_hbm.at[e], w2.at[slot], w_sem.at[1, slot]),
        )

    tick, send = make_engine(place, count, count, pieces, stage, out, scratch, None)

    def advance(t):
        tick(t)

        @pl.when(t < pieces)
        def _():
            send(t)

    def advance_all(first, number):
        @pl.loop(first, first + number)
        def _(t):
            advance(t)

    own_rows_here = pl.ds(here, rows)
    qkv_width = 2 * width
    kv_width = wk_hbm.shape[1]
    own_rows = wq_hbm.shape[0]
    part = own_rows // 4
    x = place.x
    w_here = pl.multiple_of(group * own_rows, own_rows)
    w_there = pl.multiple_of((1 - group) * own_rows, own_rows)
    quarter = pl.multiple_of((2 * core + x) * part, part)
    grad_copy = remote_copy(
        g_hbm, g_all.at[pl.ds(here, rows)], f_send.at[F_GRAD], f_recv.at[F_GRAD], place.y_peer
    )
    share_copy = y_copy(Y_SHARE, share.at[own_rows_here], share.at[own_rows_here])

    def n2_copy(i):
        tile = n2.at[pl.ds(pl.multiple_of(here + i * TILE, TILE), TILE)]
        return y_copy(Y_N2 + i, tile, tile)

    def keep(i, src, dst):
        return pltpu.make_async_copy(src, dst, keep_sem.at[i])

    def forward_part(w, kv, bias, n1_in, q, x_in):
        loads = [
            (x_hbm, x_in),
            (wk_hbm, w.at[pl.ds(w_here, own_rows), pl.ds(width, kv_width)]),
            (wv_hbm, w.at[pl.ds(w_here, own_rows), pl.ds(width + kv_width, kv_width)]),
            (wq_hbm, w.at[pl.ds(w_here, own_rows), pl.ds(0, width)]),
            (wo_hbm, w.at[pl.ds(w_here, own_rows), pl.ds(qkv_width, width)]),
        ]
        loads = [
            pltpu.make_async_copy(src, dst, load_sem.at[i]) for i, (src, dst) in enumerate(loads)
        ]
        for copy in loads:
            copy.start()
        place.greet()

        def f_copy(kind, src, dst):
            return remote_copy(src, dst, f_send.at[kind], f_recv.at[kind], place.y_peer)

        def weight_copy(kind, src, column, columns):
            return f_copy(
                kind, src.at[pl.ds(quarter, part)],
                w.at[pl.ds(w_here + quarter, part), pl.ds(column, columns)],
            )

        def x_copy(i, column, columns):
            block = w.at[pl.ds(w_there + quarter, part), pl.ds(column, columns)]
            return remote_copy(block, block, x_send.at[i], x_recv.at[i], place.x_peer)

        def core_copy(i, column, columns):
            first = pl.multiple_of(w_there + 2 * core * part, 2 * part)
            block = w.at[pl.ds(first, 2 * part), pl.ds(column, columns)]
            return remote_copy(block, block, c_send.at[i], c_recv.at[i], place.core_peer)

        small_copy = f_copy(F_SMALL, small_own, small_in.at[group])
        seg_copy = f_copy(F_SEG, seg_own, seg.at[group])
        kv_weights = [
            weight_copy(F_WK, wk_hbm, width, kv_width),
            weight_copy(F_WV, wv_hbm, width + kv_width, kv_width),
        ]
        wq_copy = weight_copy(F_WQ, wq_hbm, 0, width)
        wo_copy = weight_copy(F_WO, wo_hbm, qkv_width, width)
        for copy in (small_copy, seg_copy, *kv_weights):
            copy.start()
        small_in[group] = small_own[...]
        seg[group] = seg_own[...]

        small_copy.wait()
        seg_copy.wait()
        seg_row = jnp.concatenate([seg[0, 0:1, :], seg[1, 0:1, :]], axis=1)
        seg_k[...] = seg_row
        router[...] = jnp.concatenate([small_in[0, 0:EXPERTS, :], small_in[1, 0:EXPERTS, :]], axis=1)
        gains[...] = jnp.concatenate(
            [small_in[0, EXPERTS:, :], small_in[1, EXPERTS:, :]], axis=1
        ).astype(f32)[0 : gains.shape[0]]
        row = here + lax.broadcasted_iota(jnp.int32, bias.shape, 0)
        col = lax.broadcasted_iota(jnp.int32, bias.shape, 1)
        seg_column = seg_own[...].astype(f32).T[:, 0:1].astype(jnp.int32)
        seg_q[...] = seg_column
        same = seg_column == seg_row
        bias[...] = jnp.where(same & (row >= col), 0.0, MASKED).astype(f32)
        position = jnp.sum(jnp.where(same & (row > col), 1.0, 0.0), axis=1, keepdims=True)

        for copy in kv_weights:
            copy.wait()
        x_copy(W_KV, width, 2 * kv_width).start()
        wq_copy.start()

        expert = lax.broadcasted_iota(jnp.int32, (EXPERTS, rows), 0)
        named = jnp.zeros((EXPERTS, rows), f32)
        for k in range(routes.shape[0]):
            named = jnp.where(routes[k : k + 1, :] == expert, 1.0, named)
        share[own_rows_here, :] = named.T

        angle = position * inv_freq[...]
        lane = lax.broadcasted_iota(jnp.int32, angle.shape, 1)
        cosine_ref[...] = jnp.cos(angle)
        sine = jnp.sin(angle)
        sine_ref[...] = jnp.where(lax.rem(lane, HEAD_SIZE) < HEAD_SIZE // 2, -sine, sine)

        for copy in loads:
            copy.wait()
        xs = x_in[...].astype(f32)
        factor = lax.rsqrt(jnp.mean(xs * xs, axis=-1, keepdims=True) + EPS)
        n1_in[...] = (xs * factor * gains[0:1, :]).astype(bf16)

        x_copy(W_KV, width, 2 * kv_width).wait()
        core_copy(W_KV, width, 2 * kv_width).start()
        wq_copy.wait()
        x_copy(W_Q, 0, width).start()
        wo_copy.start()
        core_copy(W_KV, width, 2 * kv_width).wait()

        n1 = n1_in[...]
        keep(2, n1_in, n1_hbm).start()
        cosine, sine = cosine_ref[...], sine_ref[...]

        def turned(column):
            lin = mm(n1, w[:, column : column + 256])
            return [
                (t * cosine + swap_halves(t) * sine).astype(bf16)
                for t in (lin[:, :128], lin[:, 128:])
            ]

        own = own_rows_here

        def kv_copies(i):
            first = pl.multiple_of(i * 128, 128)
            return [
                f_copy(
                    F_KV + 2 * i + j,
                    kv.at[own, pl.ds(first + j * kv_width, 128)],
                    kv.at[own, pl.ds(first + j * kv_width, 128)],
                )
                for j in range(2)
            ]

        for i in range(2):
            at = 256 * i
            kv[own, at : at + 128], kv[own, at + 128 : at + 256] = turned(width + at)
            lin = mm(n1, w[:, width + kv_width + at : width + kv_width + at + 256])
            kv[own, kv_width + at : kv_width + at + 256] = lin.astype(bf16)

            @pl.when(group == 0)
            def _():
                for j in (2 * i, 2 * i + 1):
                    for copy in kv_copies(j):
                        copy.start()

        @pl.when(group == 0)
        def _():
            kv[rows:, :] = jnp.zeros((rows, kv.shape[1]), bf16)

        x_copy(W_Q, 0, width).wait()
        core_copy(W_Q, 0, width).start()
        wo_copy.wait()
        x_copy(W_OUT, qkv_width, width).start()

        @pl.when(group == 1)
        def _():
            grad_copy.start()

        core_copy(W_Q, 0, width).wait()
        for at in range(0, width, 256):
            q[:, at : at + 128], q[:, at + 128 : at + 256] = turned(at)
        lse[...] = jnp.zeros_like(lse)

        @pl.loop(0, 4)
        def _(i):
            @pl.when(group == 1)
            def _():
                for copy in kv_copies(i):
                    copy.wait_recv()

            @pl.when(i == 2)
            def _():
                x_copy(W_OUT, qkv_width, width).wait()
                core_copy(W_OUT, qkv_width, width).start()

            at_k = pl.ds(pl.multiple_of(i * 128, 128), 128)
            at_v = pl.ds(pl.multiple_of(kv_width + i * 128, 128), 128)
            keys, values = kv[:, at_k], kv[:, at_v]
            for pair in range(2):
                lanes = slice(pair * HEAD_SIZE, (pair + 1) * HEAD_SIZE)
                key, value = keys[:, lanes], values[:, lanes]
                at_q = pl.ds(pl.multiple_of(i * 256 + pair * 128, 128), 128)

                @pl.loop(0, rows // TILE)
                def _(number):
                    tile = pl.ds(pl.multiple_of(number * TILE, TILE), TILE)
                    s = mm_nt(two_heads(q[tile, at_q]) * SCALE, key)
                    s = s.reshape(2, TILE, -1) + bias[tile, :][None]
                    peak = jnp.max(s, axis=2, keepdims=True)
                    e = jnp.exp(s - peak)
                    total = jnp.sum(e, axis=2, keepdims=True)
                    o = mm(e.astype(bf16).reshape(2 * TILE, -1), value)
                    o = o / total.reshape(2 * TILE, 1)
                    ao[tile, at_q] = side_by_side(o).astype(bf16)
                    log_sum = peak + jnp.log(total)
                    lane = lax.broadcasted_iota(jnp.int32, (TILE, QUERY_HEADS), 1)
                    head = 4 * i + 2 * pair
                    lse[tile, :] = jnp.where(
                        lane == head, log_sum[0], jnp.where(lane == head + 1, log_sum[1], lse[tile, :])
                    )

        @pl.when(group == 0)
        def _():
            for i in range(4):
                for copy in kv_copies(i):
                    copy.wait_send()
            grad_copy.start()

        keep(3, q, q_hbm).start()
        keep(1, kv, kv_hbm).start()
        core_copy(W_OUT, qkv_width, width).wait()
        keep(0, w, w_all).start()

        @pl.loop(0, rows // TILE)
        def _(number):
            tile = pl.ds(pl.multiple_of(number * TILE, TILE), TILE)
            own_tile = shifted(tile, here)
            hidden = x_in[tile, :].astype(f32) + mm(ao[tile, :], w[:, qkv_width:])
            h[tile, :] = hidden
            factor = lax.rsqrt(jnp.mean(hidden * hidden, axis=-1, keepdims=True) + EPS)
            normed = (hidden * factor * gains[1:2, :]).astype(bf16)
            n2[own_tile, :] = normed
            n2_copy(number).start()
            logits = mm_nt(normed, router[...])
            chosen = share[own_tile, :] > 0.0
            picked = jnp.where(chosen, logits, MASKED)
            e = jnp.exp(picked - jnp.max(picked, axis=1, keepdims=True))
            e = jnp.where(chosen, e, 0.0)
            share[own_tile, :] = e / jnp.sum(e, axis=1, keepdims=True)

        share_copy.start()
        for i, (src, dst) in enumerate(((w, w_all), (kv, kv_hbm), (n1_in, n1_hbm), (q, q_hbm))):
            keep(i, src, dst).wait()

    pl.run_scoped(
        forward_part,
        pltpu.VMEM((width, 3 * width), bf16),
        pltpu.VMEM((tokens, width), bf16),
        pltpu.VMEM((rows, tokens), f32),
        *[pltpu.VMEM((rows, width), bf16)] * 3,
    )

    def expert_part(n2_turned, g, act, d_ye, d_gu, w1, w2):
        for copy in fetch(w1, w2, 0):
            copy.start()
        load((g_hbm, g.at[own_rows_here]))
        gate[...] = jnp.zeros_like(gate)

        def prepare(tile):
            n2_turned[:, tile] = n2[tile, :].T
            moe[tile, :] = jnp.zeros((TILE, width), f32)
            dn2[tile, :] = jnp.zeros((TILE, width), f32)

        over_tiles(here, rows // TILE, prepare)
        for i in range(rows // TILE):
            n2_copy(i).wait()
        share_copy.wait()
        over_tiles(there, rows // TILE, prepare)
        grad_copy.wait()
        load((g_all.at[pl.ds(there, rows)], g.at[pl.ds(there, rows)]))

        def pick(table, e):
            lane = lax.broadcasted_iota(jnp.int32, table.shape, 1)
            return jnp.sum(
                jnp.where(lane == group * owned + e, table, 0.0), axis=1, keepdims=True
            )

        def keep_piece(k):
            slot = lax.rem(k, 2)
            return pltpu.make_async_copy(piece.at[slot], stage.at[pl.ds(2 * k, 2)], piece_sem.at[slot])

        def work(k):
            e, sub = k // 3, lax.rem(k, 3)
            slot = lax.rem(e, 2)

            @pl.when(k == 2)
            def _():
                keep_piece(1).wait()

            @pl.when(k >= 4)
            def _():
                keep_piece(k - 2).wait()

            @pl.when(sub == 0)
            def _():
                for copy in fetch(w1, w2, e):
                    copy.wait()

                @pl.when(e + 1 < owned)
                def _():
                    for copy in fetch(w1, w2, e + 1):
                        copy.start()

                def body(tile):
                    gu = mm(n2[tile, :], w1[slot])
                    z, w = gu[:, :half], gu[:, half:]
                    sg = jax.nn.sigmoid(z)
                    silu = z * sg
                    act[tile, :] = (silu * w).astype(bf16)
                    dy = (pick(share[tile, :], e) * g[tile, :].astype(f32)).astype(bf16)
                    d_ye[tile, :] = dy
                    d_act = mm_nt(dy, w2[slot])
                    d_gu[tile, :half] = (d_act * w * sg * (1.0 + z * (1.0 - sg))).astype(bf16)
                    d_gu[tile, half:] = (d_act * silu).astype(bf16)

                over_tiles(0, tokens // WIDE, body, WIDE)
                for part in range(2):
                    columns = slice(part * half // 2, (part + 1) * half // 2)
                    grad = mm_tn(act[:, columns], d_ye[...])
                    piece[lax.rem(k, 2), part] = grad.astype(bf16).reshape(piece.shape[2:])

            @pl.when(sub == 1)
            def _():
                def body(tile):
                    ye = mm(act[tile, :], w2[slot]).astype(bf16).astype(f32)
                    value = jnp.sum(g[tile, :].astype(f32) * ye, axis=1, keepdims=True)
                    lane = lax.broadcasted_iota(jnp.int32, (WIDE, gate.shape[1]), 1)
                    gate[tile, :] = jnp.where(lane == group * owned + e, value, gate[tile, :])
                    moe[tile, :] += pick(share[tile, :], e) * ye

                over_tiles(0, tokens // WIDE, body, WIDE)

            @pl.when(sub == 2)
            def _():
                def body(tile):
                    dn2[tile, :] += mm_nt(d_gu[tile, :], w1[slot]).astype(bf16).astype(f32)

                over_tiles(0, tokens // WIDE, body, WIDE)

            @pl.when(sub > 0)
            def _():
                @pl.loop(0, 2)
                def _(part):
                    first = pl.multiple_of((2 * (sub - 1) + part) * (half // 2), half // 2)
                    grad = mm(n2_turned[pl.ds(first, half // 2), :], d_gu[...])
                    piece[lax.rem(k, 2), part] = grad.astype(bf16).reshape(piece.shape[2:])

            keep_piece(k).start()

            @pl.when(k == 0)
            def _():
                keep_piece(0).wait()

        @pl.loop(0, works)
        def _(k):
            work(k)
            advance(k)

        keep_piece(works - 2).wait()
        keep_piece(works - 1).wait()

        def leave(tile):
            to = shifted(tile, -there)
            y_send[0, to, :] = dn2[tile, :].astype(bf16)
            y_send[1, to, :] = moe[tile, :].astype(bf16)

        over_tiles(there, rows // TILE, leave)

    wide = (tokens, width)
    pl.run_scoped(
        expert_part,
        pltpu.VMEM((width, tokens), bf16),
        pltpu.VMEM(wide, bf16),
        pltpu.VMEM((tokens, half), bf16),
        pltpu.VMEM(wide, bf16),
        pltpu.VMEM((tokens, 2 * half), bf16),
        pltpu.VMEM((2, width, 2 * half), bf16),
        pltpu.VMEM((2, half, width), bf16),
    )
    t = works
    dn2_copy = y_copy(Y_DN2, y_send.at[0], y_got.at[0])
    gate_copy = y_copy(Y_GATE, gate.at[pl.ds(there, rows)], got_gate)
    moe_copy = y_copy(Y_MOE, y_send.at[1], y_got.at[1])
    dn2_copy.start()
    gate_copy.start()
    advance_all(t, 5)
    t += 5

    def attention_part(gw, d_o, dkv):
        tail = gw.shape[3:]

        def store_rows(j, i, grad):
            gw[j, i // 2, i % 2] = grad.astype(bf16).reshape(tail)

        def core_weight(j):
            return remote_copy(
                gw.at[j, :, :, 1 - core], got_core_w.at[j], cs_sem.at[j], cr_sem.at[j],
                place.core_peer,
            )

        def to_owner(j):
            core_weight(j).wait()
            for member in range(2):
                for part in range(2):
                    gw[j, member, part, core] += got_core_w[j, member, part]
            for part in range(2):
                y_weight(gw, 2 * j + part).start()

        def kv_copies(i):
            first = pl.multiple_of(i * 128, 128)
            return [
                y_copy(
                    Y_DKV + 2 * i + j,
                    dkv.at[pl.ds(0, rows), pl.ds(first + j * (width // 2), 128)],
                    got_kv.at[:, pl.ds(first + j * (width // 2), 128)],
                )
                for j in range(2)
            ]

        def middle(g, wo, d_y):
            load((g_hbm, g), (w_all.at[:, pl.ds(2 * width, width)], wo))
            dn2_copy.wait()
            gate_copy.wait()
            moe_copy.start()
            small[0] = jnp.zeros(small.shape[1:], f32)

            def body(tile):
                own = shifted(tile, here)
                s = share[own, :]
                dg = gate[own, :] + got_gate[tile, :]
                d_logits = (s * (dg - jnp.sum(s * dg, axis=1, keepdims=True))).astype(bf16)
                d_n2 = dn2[own, :] + y_got[0, tile, :].astype(f32) + mm(d_logits, router[...])
                hidden = h[tile, :]
                factor = lax.rsqrt(jnp.mean(hidden * hidden, axis=-1, keepdims=True) + EPS)
                small[0, 0:EXPERTS, :] += mm_tn(d_logits, n2[own, :])
                small[0, EXPERTS : EXPERTS + 1, :] += jnp.sum(
                    hidden * factor * d_n2, axis=0, keepdims=True
                )
                c = d_n2 * gains[1:2, :]
                mean = jnp.mean(c * hidden, axis=-1, keepdims=True)
                d_h = g[tile, :].astype(f32) + factor * (c - hidden * (factor * factor * mean))
                dn2[shifted(tile, there), :] = d_h
                d_y[tile, :] = d_h.astype(bf16)
                d_o[tile, :] = mm_nt(d_h.astype(bf16), wo[...]).astype(bf16)
                moe[own, :] += hidden

            @pl.loop(0, rows // TILE)
            def _(i):
                body(pl.ds(pl.multiple_of(i * TILE, TILE), TILE))
                advance(t + i)

            for i in range(4):
                columns = slice(i * width // 4, (i + 1) * width // 4)
                store_rows(0, i, mm_tn(ao[:, columns], d_y[...]))
            core_weight(0).start()

        pl.run_scoped(
            middle,
            pltpu.VMEM((rows, width), bf16),
            pltpu.VMEM((width, width), bf16),
            pltpu.VMEM((rows, width), bf16),
        )
        advance(t + 2)
        to_owner(0)

        def heads(q, kv, bias):
            load((q_hbm, q), (kv_hbm, kv))
            row = here + lax.broadcasted_iota(jnp.int32, bias.shape, 0)
            col = lax.broadcasted_iota(jnp.int32, bias.shape, 1)
            seen = (seg_q[...] == seg_k[...]) & (row >= col)
            bias[...] = jnp.where(seen, 0.0, MASKED).astype(f32)

            @pl.loop(0, 4)
            def _(i):
                at_k = pl.ds(pl.multiple_of(i * 128, 128), 128)
                at_v = pl.ds(pl.multiple_of(width // 2 + i * 128, 128), 128)
                keys, values = kv[:, at_k], kv[:, at_v]
                dks, dvs = [], []
                for pair in range(2):
                    lanes = slice(pair * HEAD_SIZE, (pair + 1) * HEAD_SIZE)
                    key, value = keys[:, lanes], values[:, lanes]
                    at_q = pl.ds(pl.multiple_of(i * 256 + pair * 128, 128), 128)

                    def body(part, sums):
                        dk, dv = sums
                        tile = pl.ds(pl.multiple_of(part * TILE, TILE), TILE)
                        qs = two_heads(q[tile, at_q]) * SCALE
                        dos = two_heads(d_o[tile, at_q])
                        os = two_heads(ao[tile, at_q])
                        delta = jnp.sum(
                            dos.astype(f32) * os.astype(f32), axis=1, keepdims=True
                        )
                        lane = lax.broadcasted_iota(jnp.int32, (TILE, QUERY_HEADS), 1)
                        peaks = jnp.concatenate(
                            [
                                jnp.sum(
                                    jnp.where(lane == 4 * i + 2 * pair + head, lse[tile, :], 0.0),
                                    axis=1, keepdims=True,
                                )
                                for head in range(2)
                            ],
                            axis=0,
                        )
                        s = mm_nt(qs, key) - peaks
                        s = s.reshape(2, TILE, -1) + bias[tile, :][None]
                        p = jnp.exp(s).reshape(2 * TILE, -1)
                        dp = mm_nt(dos, value)
                        ds = (p * (dp - delta)).astype(bf16)
                        dq = mm(ds, key) * SCALE
                        moe[shifted(tile, there), at_q] = side_by_side(dq)
                        return dk + mm_tn(qs, ds), dv + mm_tn(dos, p.astype(bf16))

                    zero = jnp.zeros((HEAD_SIZE, kv.shape[0]), f32)
                    dk, dv = lax.fori_loop(0, rows // TILE, body, (zero, zero))
                    dks.append(dk)
                    dvs.append(dv)
                dkv[:, at_k] = jnp.concatenate(dks, axis=0).T.astype(bf16)
                dkv[:, at_v] = jnp.concatenate(dvs, axis=0).T.astype(bf16)

                @pl.when(group == 1)
                def _():
                    for copy in kv_copies(i):
                        copy.start()

                advance(t + 3 + 2 * i)
                advance(t + 4 + 2 * i)

        pl.run_scoped(
            heads,
            pltpu.VMEM((rows, width), bf16),
            pltpu.VMEM((tokens, width), bf16),
            pltpu.VMEM((rows, tokens), f32),
        )

        def projections(n1, wqkv, lin, x_in):
            load((n1_hbm, n1), (w_all.at[:, pl.ds(0, 2 * width)], wqkv), (x_hbm, x_in))
            own = pl.ds(here, rows)

            def turn_back(to, source, where, at):
                value = source[where, at : at + 128].astype(f32)
                turned = value * cosine_ref[...] - swap_halves(value) * sine_ref[...]
                lin[:, to : to + 128] = turned.astype(bf16)

            def weight_grad(j, first):
                for i in range(4):
                    columns = slice(i * width // 4, (i + 1) * width // 4)
                    store_rows(j, i, mm_tn(n1[:, columns], lin[:, first : first + width]))
                core_weight(j).start()

            for j in range(0, width, 128):
                turn_back(j, moe, pl.ds(there, rows), j)
            weight_grad(1, 0)
            advance(t + 11)
            to_owner(1)
            advance(t + 12)

            @pl.when(group == 1)
            def _():
                for i in range(4):
                    for copy in kv_copies(i):
                        copy.wait_send()

            @pl.when(group == 0)
            def _():
                for i in range(4):
                    for copy in kv_copies(i):
                        copy.wait_recv()
                total = dkv[0:rows, :].astype(f32) + got_kv[...].astype(f32)
                dkv[0:rows, :] = total.astype(bf16)

            for j in range(0, width // 2, 128):
                turn_back(width + j, dkv, own, j)
            lin[:, 3 * width // 2 :] = dkv[own, width // 2 :]
            weight_grad(2, width)
            advance(t + 13)
            to_owner(2)
            advance(t + 14)

            def body(tile):
                dn1 = mm_nt(lin[tile, :], wqkv[...])
                xs = x_in[tile, :].astype(f32)
                factor = lax.rsqrt(jnp.mean(xs * xs, axis=-1, keepdims=True) + EPS)
                small[0, EXPERTS + 1 : EXPERTS + 2, :] += jnp.sum(
                    xs * factor * dn1, axis=0, keepdims=True
                )
                c = dn1 * gains[0:1, :]
                mean = jnp.mean(c * xs, axis=-1, keepdims=True)
                gx_ref[tile, :] = dn2[shifted(tile, there), :] + factor * (
                    c - xs * (factor * factor * mean)
                )
                total = moe[shifted(tile, here), :] + y_got[1, tile, :].astype(f32)
                y_ref[tile, :] = total.astype(bf16)

            moe_copy.wait()
            over_tiles(0, rows // TILE, body)

        pl.run_scoped(
            projections,
            pltpu.VMEM((rows, width), bf16),
            pltpu.VMEM((width, 2 * width), bf16),
            pltpu.VMEM((rows, 2 * width), bf16),
            pltpu.VMEM((rows, width), bf16),
        )
        last_tick, last_send = make_engine(
            place, count, pieces, pieces, stage, out, scratch, after_core(gw)
        )
        small_step = make_small_sum(place, small, got_small, ss_sem, sr_sem)

        first_last = t + 15

        @pl.loop(first_last, count + PHASES * LAG)
        def _(now):
            last_tick(now)

            @pl.when(now < pieces)
            def _():
                last_send(now)

            for i in range(7):

                @pl.when(now == first_last + 1 + 2 * i)
                def _():
                    small_step(i)

    pl.run_scoped(
        attention_part,
        pltpu.VMEM((3, 2, 2, *piece.shape[2:]), bf16),
        pltpu.VMEM((rows, width), bf16),
        pltpu.VMEM((tokens, width), bf16),
    )
    small_ref[...] = small[5]


DEPTH = 6


def finish_kernel(
    owned, pieces, small_ref, g_in, g_out, g_q, g_k, g_v, g_wo, router_ref, gain_ref,
    narrow, wide, in_sem, out_sem, last_sem,
):
    count = pieces.shape[0]
    whole = count - 2
    kv_width = g_k.shape[-1]

    def fetch(k):
        slot = lax.rem(k, DEPTH)
        return pltpu.make_async_copy(pieces.at[k], narrow.at[slot], in_sem.at[slot])

    def store(k, target):
        slot = lax.rem(k, DEPTH)
        return pltpu.make_async_copy(wide.at[slot], target, out_sem.at[slot])

    def convert(k):
        slot = lax.rem(k, DEPTH)
        fetch(k).wait()

        @pl.when(k >= DEPTH)
        def _():
            store(k, g_in.at[0]).wait()

        wide[slot] = narrow[slot].astype(f32)

        @pl.when(k + DEPTH < count)
        def _():
            fetch(k + DEPTH).start()

    for k in range(DEPTH):
        fetch(k).start()
    columns = router_ref.shape[1]
    first = pl.multiple_of(lax.axis_index("group") * columns, columns)
    router_ref[...] = small_ref[0:EXPERTS, pl.ds(first, columns)]
    gain_ref[...] = small_ref[EXPERTS:, pl.ds(first, columns)]

    @pl.loop(0, whole)
    def _(k):
        convert(k)
        base = 0
        for target in (g_in, g_out, g_wo, g_q):
            number = target.shape[0]

            @pl.when((k >= base) & (k < base + number))
            def _():
                store(k, target.at[k - base]).start()

            base += number

    last = []
    for i in range(2):
        k = whole + i
        convert(k)
        for j, target in enumerate((g_k, g_v)):
            copy = pltpu.make_async_copy(
                wide.at[k % DEPTH, :, pl.ds(j * kv_width, kv_width)], target.at[i],
                last_sem.at[2 * i + j],
            )
            copy.start()
            last.append(copy)
    for copy in last:
        copy.wait()
    for k in range(count - DEPTH, whole):
        store(k, g_in.at[0]).wait()


def finish(pieces, small, owned, kv_width):
    count, rows, width = pieces.shape
    shape = jax.ShapeDtypeStruct
    vmem = pl.BlockSpec(memory_space=pltpu.VMEM)
    hbm = pl.BlockSpec(memory_space=pl.ANY)
    dma = pltpu.SemaphoreType.DMA
    return pl.pallas_call(
        functools.partial(finish_kernel, owned),
        out_shape=(
            shape((4 * owned, rows, width), f32),
            shape((2 * owned, rows, width), f32),
            shape((2, rows, width), f32),
            shape((2, rows, kv_width), f32),
            shape((2, rows, kv_width), f32),
            shape((2, rows, width), f32),
            shape((EXPERTS, width // 2), f32),
            shape((8, width // 2), f32),
        ),
        in_specs=[hbm, vmem],
        out_specs=[hbm] * 6 + [vmem] * 2,
        scratch_shapes=[
            pltpu.VMEM((DEPTH, rows, width), bf16),
            pltpu.VMEM((DEPTH, rows, width), f32),
            dma((DEPTH,)),
            dma((DEPTH,)),
            dma((4,)),
        ],
        compiler_params=params(48),
        cost_estimate=cost(0, 6 * pieces.size),
        name="finish",
    )(pieces, small)


def layer(x, document_numbers, routes, gains, w_router, wq, wk, wv, wo, grad, w_in, w_out):
    rows, width = x.shape
    own_rows = wq.shape[0]
    small = jnp.concatenate(
        [w_router.T, *[gain[None] for gain in gains],
         jnp.zeros((SMALL_ROWS - EXPERTS - 2, own_rows), bf16)], axis=0,
    )
    exponent = (np.arange(128) % (HEAD_SIZE // 2)) * (-2.0 / HEAD_SIZE)
    inv_freq = jnp.asarray(np.power(10000.0, exponent)[None], f32)
    owned, half = w_out.shape[:2]
    tokens, quarter = 2 * rows, half // 16
    pieces = 6 * owned
    shape = jax.ShapeDtypeStruct
    vmem = pl.BlockSpec(memory_space=pltpu.VMEM)
    hbm = pl.BlockSpec(memory_space=pl.ANY)
    dma = pltpu.SemaphoreType.DMA
    small_rows = EXPERTS + 8
    return pl.pallas_call(
        layer_kernel,
        out_shape=(
            shape((rows, width), bf16),
            shape((rows, width), f32),
            shape((small_rows, width), f32),
            shape((pieces + 6, 2, 4, quarter, width), bf16),
            shape((pieces, 2, 4, quarter, width), bf16),
            shape((rows, width), bf16),
            shape((tokens, width), bf16),
            shape((rows, width), bf16),
            shape((tokens, width), bf16),
            shape((width, 3 * width), bf16),
        ),
        in_specs=[hbm] * 8 + [vmem] * 4,
        out_specs=[vmem, vmem, vmem] + [hbm] * 7,
        scratch_shapes=[
            pltpu.VMEM((rows, width), bf16),
            pltpu.VMEM((rows, width), f32),
            pltpu.VMEM((tokens, width), bf16),
            pltpu.VMEM((rows, QUERY_HEADS), f32),
            pltpu.VMEM((rows, 128), f32),
            pltpu.VMEM((rows, 128), f32),
            pltpu.VMEM((1, tokens), jnp.int32),
            pltpu.VMEM((rows, 1), jnp.int32),
            pltpu.VMEM((EXPERTS, width), bf16),
            pltpu.VMEM((8, width), f32),
            pltpu.VMEM((2, SMALL_ROWS, own_rows), bf16),
            pltpu.VMEM((2, 8, rows), jnp.int32),
            dma((F_KINDS,)),
            dma((F_KINDS,)),
            *[dma((3,))] * 4,
            dma((4,)),
            pltpu.VMEM((tokens, width), f32),
            pltpu.VMEM((tokens, width), f32),
            pltpu.VMEM((tokens, EXPERTS), f32),
            pltpu.VMEM((tokens, EXPERTS), f32),
            pltpu.VMEM((rows, EXPERTS), f32),
            pltpu.VMEM((2, rows, width), bf16),
            pltpu.VMEM((2, rows, width), bf16),
            pltpu.VMEM((rows, width), bf16),
            pltpu.VMEM((3, 2, 2, 4, quarter, width), bf16),
            pltpu.VMEM((3, 2, 4, quarter, width), bf16),
            pltpu.VMEM((6, small_rows, width), f32),
            pltpu.VMEM((6, small_rows, width), f32),
            pltpu.VMEM((2, 2, 2, 4, quarter, width), bf16),
            dma((2,)),
            dma((2, 2)),
            dma((5,)),
            dma((Y_KINDS,)),
            dma((Y_KINDS,)),
            dma((3,)),
            dma((3,)),
            dma((6,)),
            dma((6,)),
            *engine_scratch(quarter, width),
        ],
        compiler_params=pltpu.CompilerParams(
            collective_id=1, has_side_effects=True, vmem_limit_bytes=63 * MIB
        ),
        cost_estimate=cost(18 * tokens * width * half * owned, 6 * w_in.size),
        name="layer",
    )(
        x, wq, wk, wv, wo, grad, w_in, w_out, small,
        jnp.broadcast_to(document_numbers[None], (8, rows)), routes.T, inv_freq,
    )


def expert_pass(n2, grad, share, w_in, w_out):
    half = w_out.shape[0]
    gu = mm(n2, w_in)
    z, w = gu[:, :half], gu[:, half:]
    sg = jax.nn.sigmoid(z)
    act = (z * sg * w).astype(bf16)
    ye = mm(act, w_out).astype(bf16).astype(f32)
    d_gate = jnp.sum(grad * ye, axis=1)
    d_ye = (share * grad).astype(bf16)
    g_out = mm_tn(act, d_ye).astype(bf16)
    d_act = mm_nt(d_ye, w_out)
    d_gu = jnp.concatenate(
        [d_act * w * sg * (1.0 + z * (1.0 - sg)), d_act * z * sg], axis=1
    ).astype(bf16)
    g_in = mm_tn(n2, d_gu).astype(bf16)
    d_xe = mm_nt(d_gu, w_in).astype(bf16).astype(f32)
    return share * ye, d_gate, g_in, g_out, d_xe


def all_experts(n2, grad, share, w_in, w_out):
    moe = jnp.zeros(n2.shape, f32)
    d_n2 = jnp.zeros_like(moe)
    d_gate, g_in, g_out = [], [], []
    for i in range(w_in.shape[0]):
        y, dg, gi, go, dx = expert_pass(
            n2, grad.astype(f32), share[:, i : i + 1], w_in[i], w_out[i]
        )
        moe, d_n2 = moe + y, d_n2 + dx
        d_gate.append(dg)
        g_in.append(gi)
        g_out.append(go)
    g_in, g_out = lax.psum((jnp.stack(g_in), jnp.stack(g_out)), "replica")
    return moe, d_n2, jnp.stack(d_gate, 1), g_in.astype(f32), g_out.astype(f32)


def on_device(
    layer_input, document_numbers, routes, norm_attn, w_query, key_weight, value_weight, w_out,
    norm_moe, w_router, expert_in, expert_out, cotangent,
):
    rows, width = layer_input.shape
    group = lax.axis_index("group")
    first = group * rows
    owned = expert_in.shape[0]
    kv_width = KEY_VALUE_HEADS * HEAD_SIZE

    q_width = QUERY_HEADS * HEAD_SIZE
    if lax.axis_size("replica") == 16 and lax.axis_size("group") == 2:
        layer_output, grad_input, small_sum, sums, *_ = layer(
            layer_input, document_numbers, routes, (norm_attn, norm_moe), w_router, w_query,
            key_weight, value_weight, w_out, cotangent, expert_in, expert_out,
        )
        g_in, g_out, g_q, g_k, g_v, g_wo, g_router, g_gains = finish(
            sums.reshape(sums.shape[0], -1, width), small_sum, owned, kv_width
        )
        return (
            layer_output,
            grad_input,
            g_gains[1],
            g_q.reshape(w_query.shape),
            g_k.reshape(key_weight.shape),
            g_v.reshape(value_weight.shape),
            g_wo.reshape(w_out.shape),
            g_gains[0],
            g_router.T,
            g_in.reshape(expert_in.shape),
            g_out.reshape(expert_out.shape),
        )

    seg_all = gather(document_numbers)
    position = lax.dynamic_slice_in_dim(doc_positions(seg_all), first, rows, 0)
    cosine, sine = turn_tables(position)
    small = gather(jnp.concatenate([norm_attn[:, None], norm_moe[:, None], w_router], axis=1))
    gain_attn = small[:, 0].astype(f32)[None, :]
    gain_moe = small[:, 1].astype(f32)[None, :]
    router = small[:, 2:]
    w_qkv = gather(jnp.concatenate([w_query, key_weight, value_weight], axis=1))
    wo = gather(w_out)
    grad_all = gather(cotangent)

    n1, q, k, v = project(layer_input, gain_attn, w_qkv, cosine, sine)
    kv_all = gather(jnp.concatenate([k, v], axis=1))
    k_all, v_all = kv_all[:, :kv_width], kv_all[:, kv_width:]
    first_row = jnp.full((1,), first, jnp.int32)
    seg_q, seg_k = document_numbers[:, None], seg_all[None, :]
    ao = attend(first_row, q, k_all, v_all, seg_q, seg_k)

    x = layer_input.astype(f32)
    h = x + mm(ao, wo)
    r2 = rms_factor(h)
    n2 = (h * r2 * gain_moe).astype(bf16)
    logits = mm(n2, router)
    chosen = jnp.any(routes[:, :, None] == jnp.arange(EXPERTS, dtype=jnp.int32), axis=1)
    picked = jnp.where(chosen, logits, MASKED)
    e = jnp.where(chosen, jnp.exp(picked - jnp.max(picked, axis=1, keepdims=True)), 0.0)
    share = e / jnp.sum(e, axis=1, keepdims=True)

    n2_all = gather(n2)
    share_all = lax.dynamic_slice_in_dim(gather(share), group * owned, owned, 1)
    moe, d_n2_all, d_gate, g_in, g_out = all_experts(
        n2_all, grad_all, share_all, expert_in, expert_out
    )
    d_gate = lax.dynamic_update_slice_in_dim(
        jnp.zeros((n2_all.shape[0], EXPERTS), f32), d_gate, group * owned, 1
    )
    d_gate = lax.psum_scatter(d_gate, "group", scatter_dimension=0, tiled=True)
    layer_output = (h + owner_sum(moe).astype(f32)).astype(bf16)

    d_logits = (share * (d_gate - jnp.sum(share * d_gate, axis=1, keepdims=True))).astype(bf16)
    g_router = mm_tn(n2, d_logits)
    d_n2 = owner_sum(d_n2_all).astype(f32) + mm_nt(d_logits, router)
    g_gain_moe = jnp.sum(h * r2 * d_n2, axis=0)
    c = d_n2 * gain_moe
    d_h = cotangent.astype(f32) + r2 * (
        c - h * r2 * r2 * jnp.mean(c * h, axis=-1, keepdims=True)
    )
    d_y = d_h.astype(bf16)
    g_wo = mm_tn(ao, d_y).astype(bf16)
    d_o = mm_nt(d_y, wo).astype(bf16)

    dq, dk_all, dv_all = attend_grad(first_row, q, k_all, v_all, d_o, seg_q, seg_k)
    dkv = owner_sum(jnp.concatenate([dk_all, dv_all], axis=1))
    g_qkv, grad_input, g_gain_attn = project_grad(
        dq, dkv[:, :kv_width], dkv[:, kv_width:], n1, w_qkv, cosine, sine, layer_input,
        gain_attn, d_h,
    )

    g_attn = owner_sum(jnp.concatenate([g_qkv, g_wo], axis=1))
    g_small = owner_sum(
        jnp.concatenate([g_gain_attn.reshape(-1, 1), g_gain_moe[:, None], g_router], axis=1)
    )
    g_attn, g_small = (t.astype(f32) for t in lax.psum((g_attn, g_small), "replica"))
    return (
        layer_output,
        grad_input,
        g_small[:, 0],
        g_attn[:, :q_width],
        g_attn[:, q_width : q_width + kv_width],
        g_attn[:, q_width + kv_width : q_width + 2 * kv_width],
        g_attn[:, q_width + 2 * kv_width :],
        g_small[:, 1],
        g_small[:, 2:],
        g_in,
        g_out,
    )


def solution(mesh):
    tokens, weights = P(("replica", "group"), None), P("group", None)
    in_specs = (
        tokens, P(("replica", "group")), tokens, P("group"), weights, weights, weights, weights,
        P("group"), weights, P("group", None, None), P("group", None, None), tokens,
    )
    out_specs = (
        tokens, tokens, P("group"), weights, weights, weights, weights, P("group"), weights,
        P("group", None, None), P("group", None, None),
    )
    return jax.shard_map(
        on_device, mesh=mesh, in_specs=in_specs, out_specs=out_specs, check_vma=False
    )
```

```python
import functools

import jax
import jax.numpy as jnp
import numpy as np
from jax import lax
from jax.experimental import pallas as pl
from jax.experimental.pallas import tpu as pltpu
from jax.sharding import PartitionSpec as P

QUERY_HEADS = 16
KEY_VALUE_HEADS = 8
HEAD_SIZE = 64
EXPERTS = 16
EPS = 1e-06
MASKED = -1e30
SCALE = HEAD_SIZE ** (-0.5)

f32 = jnp.float32
bf16 = jnp.bfloat16
MIB = 1 << 20


def mm(a, b):
    return lax.dot_general(a, b, (((1,), (0,)), ((), ())), preferred_element_type=f32)


def mm_nt(a, b):
    return lax.dot_general(a, b, (((1,), (1,)), ((), ())), preferred_element_type=f32)


def mm_tn(a, b):
    return lax.dot_general(a, b, (((0,), (0,)), ((), ())), preferred_element_type=f32)


def params(mib):
    return pltpu.CompilerParams(vmem_limit_bytes=mib * MIB)


def cost(flops, moved):
    return pl.CostEstimate(flops=int(flops), bytes_accessed=int(moved), transcendentals=0)


def doc_positions(seg_ids):
    length = seg_ids.shape[0]
    index = jnp.arange(length, dtype=jnp.int32)
    previous = jnp.concatenate([seg_ids[:1] - 1, seg_ids[:-1]])
    is_start = (seg_ids != previous) | (index == 0)
    start = lax.cummax(jnp.where(is_start, index, 0), axis=0)
    return index - start


def turn_tables(position):
    half = HEAD_SIZE // 2
    exponent = jnp.arange(half, dtype=f32) * (-2.0 / HEAD_SIZE)
    inv_freq = jnp.power(10000.0, exponent)
    angles = position.astype(f32)[:, None] * inv_freq[None, :]
    cosine, sine = jnp.cos(angles), jnp.sin(angles)
    return (
        jnp.concatenate([cosine] * 4, axis=1),
        jnp.concatenate([-sine, sine, -sine, sine], axis=1),
    )


def swap_halves(t):
    lane = lax.broadcasted_iota(jnp.int32, t.shape, 1)
    return jnp.where(
        lane % HEAD_SIZE < HEAD_SIZE // 2, pltpu.roll(t, 96, 1), pltpu.roll(t, 32, 1)
    )


def qkv_kernel(x_ref, gain_ref, w_ref, cos_ref, sin_ref, n1_ref, q_ref, k_ref, v_ref):
    x = x_ref[...].astype(f32)
    factor = lax.rsqrt(jnp.mean(x * x, axis=-1, keepdims=True) + EPS)
    n1 = (x * factor * gain_ref[...]).astype(bf16)
    n1_ref[...] = n1
    cosine, sine = cos_ref[...], sin_ref[...]
    q_width, k_width = q_ref.shape[1], k_ref.shape[1]
    for start in range(0, q_width + k_width, 256):
        lin = mm(n1, w_ref[:, start : start + 256])
        for part in (0, 128):
            t = lin[:, part : part + 128]
            turned = (t * cosine + swap_halves(t) * sine).astype(bf16)
            at = start + part
            if at < q_width:
                q_ref[:, at : at + 128] = turned
            else:
                k_ref[:, at - q_width : at - q_width + 128] = turned
    v_ref[...] = mm(n1, w_ref[:, q_width + k_width :]).astype(bf16)


def project(x, gain, w, cosine, sine):
    rows, width = x.shape
    q_width, k_width = QUERY_HEADS * HEAD_SIZE, KEY_VALUE_HEADS * HEAD_SIZE
    shape = jax.ShapeDtypeStruct
    return pl.pallas_call(
        qkv_kernel,
        out_shape=(
            shape((rows, width), bf16),
            shape((rows, q_width), bf16),
            shape((rows, k_width), bf16),
            shape((rows, k_width), bf16),
        ),
        compiler_params=params(40),
        cost_estimate=cost(2 * rows * width * w.shape[1], 2 * w.size + 8 * x.size),
        name="project",
    )(x, gain, w, cosine, sine)


def qkv_grad_kernel(
    dq_ref, dk_ref, dv_ref, n1_ref, w_ref, cos_ref, sin_ref, x_ref, gain_ref, dh_ref,
    gw_ref, gx_ref, gg_ref, lin_ref,
):
    cosine, sine = cos_ref[...], sin_ref[...]
    q_width, k_width = dq_ref.shape[1], dk_ref.shape[1]
    for ref, width, base in ((dq_ref, q_width, 0), (dk_ref, k_width, q_width)):
        for at in range(0, width, 128):
            t = ref[:, at : at + 128].astype(f32)
            turned = (t * cosine - swap_halves(t) * sine).astype(bf16)
            lin_ref[:, base + at : base + at + 128] = turned
    lin_ref[:, q_width + k_width :] = dv_ref[...].astype(bf16)
    total = q_width + 2 * k_width
    n1 = n1_ref[...]
    for at in range(0, total, 512):
        gw_ref[:, at : at + 512] = mm_tn(n1, lin_ref[:, at : at + 512]).astype(bf16)
    dn1 = mm_nt(lin_ref[...], w_ref[...])
    x = x_ref[...].astype(f32)
    factor = lax.rsqrt(jnp.mean(x * x, axis=-1, keepdims=True) + EPS)
    gg_ref[...] = jnp.sum(x * factor * dn1, axis=0, keepdims=True)
    c = dn1 * gain_ref[...]
    mean = jnp.mean(c * x, axis=-1, keepdims=True)
    gx_ref[...] = dh_ref[...] + factor * (c - x * (factor * factor * mean))


def project_grad(dq, dk, dv, n1, w, cosine, sine, x, gain, dh):
    rows, width = x.shape
    shape = jax.ShapeDtypeStruct
    return pl.pallas_call(
        qkv_grad_kernel,
        out_shape=(
            shape(w.shape, bf16),
            shape((rows, width), f32),
            shape((1, width), f32),
        ),
        scratch_shapes=[pltpu.VMEM((rows, w.shape[1]), bf16)],
        compiler_params=params(56),
        cost_estimate=cost(4 * rows * width * w.shape[1], 4 * w.size + 16 * x.size),
        name="project_grad",
    )(dq, dk, dv, n1, w, cosine, sine, x, gain, dh)


def visible_bias(first_ref, seg_q_ref, seg_k_ref, bias_ref):
    rows, keys = bias_ref.shape
    row = first_ref[0] + lax.broadcasted_iota(jnp.int32, (rows, keys), 0)
    col = lax.broadcasted_iota(jnp.int32, (rows, keys), 1)
    seen = (seg_q_ref[...] == seg_k_ref[...]) & (row >= col)
    bias_ref[...] = jnp.where(seen, 0.0, MASKED).astype(f32)


def attend_kernel(first_ref, q_ref, k_ref, v_ref, seg_q_ref, seg_k_ref, o_ref, bias_ref):
    @pl.when(pl.program_id(0) == 0)
    def _():
        visible_bias(first_ref, seg_q_ref, seg_k_ref, bias_ref)

    bias = bias_ref[...]
    for head in range(4):
        at, kv = head * HEAD_SIZE, head // 2 * HEAD_SIZE
        s = mm_nt(q_ref[:, at : at + HEAD_SIZE], k_ref[:, kv : kv + HEAD_SIZE]) * SCALE + bias
        e = jnp.exp(s - jnp.max(s, axis=1, keepdims=True))
        total = jnp.sum(e, axis=1, keepdims=True)
        o = mm(e.astype(bf16), v_ref[:, kv : kv + HEAD_SIZE]) / total
        o_ref[:, at : at + HEAD_SIZE] = o.astype(bf16)


def attend(first, q, k, v, seg_q, seg_k):
    rows, width = q.shape
    keys = k.shape[0]
    wide = pl.BlockSpec((rows, 256), lambda i, first: (0, i))
    narrow = pl.BlockSpec((keys, 128), lambda i, first: (0, i))
    return pl.pallas_call(
        attend_kernel,
        out_shape=jax.ShapeDtypeStruct((rows, width), bf16),
        grid_spec=pltpu.PrefetchScalarGridSpec(
            num_scalar_prefetch=1,
            grid=(width // 256,),
            in_specs=[
                wide,
                narrow,
                narrow,
                pl.BlockSpec((rows, 1), lambda i, first: (0, 0)),
                pl.BlockSpec((1, keys), lambda i, first: (0, 0)),
            ],
            out_specs=wide,
            scratch_shapes=[pltpu.VMEM((rows, keys), f32)],
        ),
        compiler_params=params(48),
        cost_estimate=cost(16 * rows * keys * width, 4 * q.size + 4 * k.size),
        name="attend",
    )(first, q, k, v, seg_q, seg_k)


def attend_grad_kernel(
    first_ref, q_ref, k_ref, v_ref, do_ref, seg_q_ref, seg_k_ref,
    dq_ref, dk_ref, dv_ref, bias_ref,
):
    @pl.when(pl.program_id(0) == 0)
    def _():
        visible_bias(first_ref, seg_q_ref, seg_k_ref, bias_ref)

    bias = bias_ref[...]
    for pair in range(2):
        kv = pair * HEAD_SIZE
        k, v = k_ref[:, kv : kv + HEAD_SIZE], v_ref[:, kv : kv + HEAD_SIZE]
        dk = dv = None
        for head in (2 * pair, 2 * pair + 1):
            at = head * HEAD_SIZE
            q, do = q_ref[:, at : at + HEAD_SIZE], do_ref[:, at : at + HEAD_SIZE]
            s = mm_nt(q, k) * SCALE + bias
            e = jnp.exp(s - jnp.max(s, axis=1, keepdims=True))
            p = e * (1.0 / jnp.sum(e, axis=1, keepdims=True))
            dp = mm_nt(do, v)
            delta = jnp.sum(p * dp, axis=1, keepdims=True)
            ds = (p * (dp - delta) * SCALE).astype(bf16)
            dq_ref[:, at : at + HEAD_SIZE] = mm(ds, k)
            dk_part, dv_part = mm_tn(ds, q), mm_tn(p.astype(bf16), do)
            dk = dk_part if dk is None else dk + dk_part
            dv = dv_part if dv is None else dv + dv_part
        dk_ref[:, kv : kv + HEAD_SIZE] = dk.astype(bf16)
        dv_ref[:, kv : kv + HEAD_SIZE] = dv.astype(bf16)


def attend_grad(first, q, k, v, do, seg_q, seg_k):
    rows, width = q.shape
    keys = k.shape[0]
    wide = pl.BlockSpec((rows, 256), lambda i, first: (0, i))
    narrow = pl.BlockSpec((keys, 128), lambda i, first: (0, i))
    shape = jax.ShapeDtypeStruct
    return pl.pallas_call(
        attend_grad_kernel,
        out_shape=(
            shape((rows, width), f32),
            shape(k.shape, bf16),
            shape(k.shape, bf16),
        ),
        grid_spec=pltpu.PrefetchScalarGridSpec(
            num_scalar_prefetch=1,
            grid=(width // 256,),
            in_specs=[
                wide,
                narrow,
                narrow,
                wide,
                pl.BlockSpec((rows, 1), lambda i, first: (0, 0)),
                pl.BlockSpec((1, keys), lambda i, first: (0, 0)),
            ],
            out_specs=[wide, narrow, narrow],
            scratch_shapes=[pltpu.VMEM((rows, keys), f32)],
        ),
        compiler_params=params(56),
        cost_estimate=cost(40 * rows * keys * width // 4, 8 * q.size + 8 * k.size),
        name="attend_grad",
    )(first, q, k, v, do, seg_q, seg_k)


def gather(value):
    return lax.all_gather(value, "group", axis=0, tiled=True)


def owner_sum(value):
    return lax.psum_scatter(value.astype(bf16), "group", scatter_dimension=0, tiled=True)


def rms_factor(values):
    return lax.rsqrt(jnp.mean(values * values, axis=-1, keepdims=True) + EPS)


LAG = 2
PHASES = 7
SEMS = 8
(CORE, X_A, IN_B, IN_A, HALF_B, MID_A, RUNG_B, OUT_A, BACK_B, SPREAD_A, OUT_B, JOIN, KINDS) = range(13)
(Y_SHARE, Y_DN2, Y_MOE, Y_GATE, Y_DKV, Y_WEIGHT, Y_N2, Y_KINDS) = (0, 1, 2, 3, 4, 12, 18, 20)


def engine_scratch(quarter, width):
    def vmem(*shape):
        return pltpu.VMEM((*shape, quarter, width), bf16)

    return [
        vmem(4, 4),
        vmem(4, 4),
        vmem(4),
        vmem(8, 2),
        vmem(8),
        vmem(4),
        vmem(4),
        vmem(4),
        vmem(LAG, 4),
        vmem(LAG),
        vmem(LAG, 2),
        vmem(LAG),
        vmem(LAG),
        vmem(LAG),
        vmem(LAG),
        pltpu.SemaphoreType.DMA((KINDS, SEMS)),
        pltpu.SemaphoreType.DMA((KINDS, SEMS)),
        pltpu.SemaphoreType.DMA((3, SEMS)),
    ]


class Place:
    def __init__(self):
        r = lax.axis_index("replica")
        self.core, self.x, z = lax.rem(r, 2), lax.rem(r // 2, 2), r // 4
        self.group = lax.axis_index("group")
        self.inner = (z == 1) | (z == 2)
        self.outer = jnp.logical_not(self.inner)
        self.late = z // 2
        up = (z == 0) | (z == 2)
        self.core_peer = {"replica": r + 1 - 2 * self.core}
        self.x_peer = {"replica": r + 2 - 4 * self.x}
        self.line_peer = {"replica": jnp.where(up, r + 4, r - 4)}
        self.mid_peer = {"replica": jnp.where(z == 1, r + 4, r - 4)}
        self.y_peer = {"group": 1 - self.group}

    def greet(self):
        barrier = pltpu.get_barrier_semaphore()

        def signal(peer):
            pl.semaphore_signal(
                barrier, inc=1, device_id=peer, device_id_type=pl.DeviceIdType.MESH
            )

        for peer in (self.core_peer, self.x_peer, self.line_peer, self.y_peer):
            signal(peer)

        @pl.when(self.inner)
        def _():
            signal(self.mid_peer)
            pl.semaphore_wait(barrier, 5)

        @pl.when(self.outer)
        def _():
            pl.semaphore_wait(barrier, 4)


def remote_copy(src, dst, send_sem, recv_sem, peer):
    return pltpu.make_async_remote_copy(
        src_ref=src, dst_ref=dst, send_sem=send_sem, recv_sem=recv_sem, device_id=peer,
        device_id_type=pl.DeviceIdType.MESH,
    )


def make_engine(place, count, split, split_of, stage, out, scratch, late_piece):
    (mine, got_core, got_x, got_end_b, got_end_a, got_mid_b, got_mid_a, got_rung,
     summed, a_x, b_end, a_end, b_mid, a_all, b_all, send_sem, recv_sem, copy_sem) = scratch
    core, x, inner, outer, late = place.core, place.x, place.inner, place.outer, place.late

    owned = split_of // 6

    def spot(k):
        e, sub, part = k // 6, lax.rem(k // 2, 3), lax.rem(k, 2)
        inner_spot = jnp.where(sub == 0, 4 * owned + 2 * e, 4 * e + 2 * sub - 2) + part
        return jnp.where(k < split_of, inner_spot, k)

    def remote(kind, k, src, dst, peer):
        slot = lax.rem(k, SEMS)
        return remote_copy(src, dst, send_sem.at[kind, slot], recv_sem.at[kind, slot], peer)

    def local(kind, k, src, dst):
        return pltpu.make_async_copy(src, dst, copy_sem.at[kind, lax.rem(k, SEMS)])

    def core_copy(k):
        return remote(
            CORE, k, stage.at[k, 1 - core], got_core.at[lax.rem(k, 4)], place.core_peer
        )

    def mine_copy(k):
        return local(2, k, stage.at[k, core], mine.at[lax.rem(k, 4)])

    def x_copy(k):
        return remote(
            X_A, k, summed.at[lax.rem(k, LAG), 1 - x], got_x.at[lax.rem(k, 4)], place.x_peer
        )

    def in_b_copy(k):
        return remote(
            IN_B, k, summed.at[lax.rem(k, LAG), pl.ds(2, 2)], got_end_b.at[lax.rem(k, 8)],
            place.line_peer,
        )

    def in_a_copy(k):
        return remote(
            IN_A, k, a_x.at[lax.rem(k, LAG)], got_end_a.at[lax.rem(k, 8)], place.line_peer
        )

    def half_b_copy(k):
        return remote(
            HALF_B, k, b_end.at[lax.rem(k, LAG), 1 - late], got_mid_b.at[lax.rem(k, 4)],
            place.mid_peer,
        )

    def mid_a_copy(k):
        return remote(
            MID_A, k, a_end.at[lax.rem(k, LAG)], got_mid_a.at[lax.rem(k, 4)], place.mid_peer
        )

    def rung_copy(k):
        return remote(
            RUNG_B, k, b_mid.at[lax.rem(k, LAG)], got_rung.at[lax.rem(k, 4)], place.x_peer
        )

    def out_a_copy(k):
        return remote(OUT_A, k, a_all.at[lax.rem(k, LAG)], out.at[spot(k), core, x], place.line_peer)

    def back_b_copy(k, quarter):
        return remote(
            BACK_B, k, b_all.at[lax.rem(k, LAG)], out.at[spot(k), core, quarter], place.mid_peer
        )

    def spread_copy(k, quarter):
        return remote(SPREAD_A, k, out.at[spot(k), core, x], out.at[spot(k), core, quarter], place.x_peer)

    def out_b_copy(k):
        part = out.at[spot(k), core, pl.ds(2, 2)]
        return remote(OUT_B, k, part, part, place.line_peer)

    def join_copy(k, half):
        return remote(JOIN, k, out.at[spot(k), core], out.at[spot(k), half], place.core_peer)

    def keep_a(k):
        return local(0, k, a_all.at[lax.rem(k, LAG)], out.at[spot(k), core, x])

    def keep_b(k):
        return local(1, k, b_all.at[lax.rem(k, LAG)], out.at[spot(k), core, 2 + late])

    def phase1(k):
        i = lax.rem(k, LAG)

        @pl.when(k < split)
        def _():
            mine_copy(k).wait()
            core_copy(k).wait()
            summed[i] = mine[lax.rem(k, 4)] + got_core[lax.rem(k, 4)]

        if count > split:

            @pl.when(k >= split)
            def _():
                copy, own, other = late_piece(k)
                copy.wait()
                summed[i] = own[...] + other[...]

        x_copy(k).start()

        @pl.when(outer)
        def _():
            in_b_copy(k).start()

    def phase2(k):
        i = lax.rem(k, LAG)
        x_copy(k).wait()
        a_x[i] = summed[i, x] + got_x[lax.rem(k, 4)]

        @pl.when(outer)
        def _():
            in_a_copy(k).start()
            in_b_copy(k).wait_send()

        @pl.when(inner)
        def _():
            in_b_copy(k).wait_recv()
            b_end[i] = summed[i, 2:4] + got_end_b[lax.rem(k, 8)]
            half_b_copy(k).start()

    def phase3(k):
        i = lax.rem(k, LAG)

        @pl.when(outer)
        def _():
            in_a_copy(k).wait_send()

        @pl.when(inner)
        def _():
            in_a_copy(k).wait_recv()
            a_end[i] = a_x[i] + got_end_a[lax.rem(k, 8)]
            mid_a_copy(k).start()
            half_b_copy(k).wait()
            b_mid[i] = b_end[i, late] + got_mid_b[lax.rem(k, 4)]
            rung_copy(k).start()

    def phase4(k):
        i = lax.rem(k, LAG)

        @pl.when(inner)
        def _():
            mid_a_copy(k).wait()
            a_all[i] = a_end[i] + got_mid_a[lax.rem(k, 4)]
            out_a_copy(k).start()
            keep_a(k).start()
            rung_copy(k).wait()
            b_all[i] = b_mid[i] + got_rung[lax.rem(k, 4)]
            back_b_copy(k, 2 + late).start()
            keep_b(k).start()

    def phase5(k):
        @pl.when(outer)
        def _():
            out_a_copy(k).wait_recv()

        @pl.when(inner)
        def _():
            keep_a(k).wait()
            out_a_copy(k).wait_send()

        spread_copy(k, x).start()

        @pl.when(inner)
        def _():
            keep_b(k).wait()
            back_b_copy(k, 2 + late).wait_send()
            back_b_copy(k, 3 - late).wait_recv()
            out_b_copy(k).start()

    def phase6(k):
        spread_copy(k, x).wait_send()
        spread_copy(k, 1 - x).wait_recv()

        @pl.when(outer)
        def _():
            out_b_copy(k).wait_recv()

        @pl.when(inner)
        def _():
            out_b_copy(k).wait_send()

        join_copy(k, core).start()

    def phase7(k):
        join_copy(k, core).wait_send()
        join_copy(k, 1 - core).wait_recv()

    phases = (phase1, phase2, phase3, phase4, phase5, phase6, phase7)

    def tick(t):
        for number in range(PHASES, 0, -1):
            k = t - LAG * number

            @pl.when((k >= 0) & (k < count))
            def _():
                phases[number - 1](k)

    def send(k):
        @pl.when(k < split)
        def _():
            core_copy(k).start()
            mine_copy(k).start()

    return tick, send


def make_small_sum(place, values, got, send_sem, recv_sem):
    def copy(i, peer):
        return remote_copy(values.at[i], got.at[i], send_sem.at[i], recv_sem.at[i], peer)

    peers = (
        place.core_peer, place.x_peer, place.y_peer, place.line_peer, place.mid_peer,
        place.line_peer,
    )

    def add(i):
        values[i + 1] = values[i] + got[i]

    def step(i):
        if 1 <= i <= 3:
            copy(i - 1, peers[i - 1]).wait()
            add(i - 1)
        if i <= 2:
            copy(i, peers[i]).start()
        if i == 3:

            @pl.when(place.outer)
            def _():
                copy(3, peers[3]).start()

        if i == 4:

            @pl.when(place.outer)
            def _():
                copy(3, peers[3]).wait_send()

            @pl.when(place.inner)
            def _():
                copy(3, peers[3]).wait_recv()
                add(3)
                copy(4, peers[4]).start()

        if i == 5:

            @pl.when(place.inner)
            def _():
                copy(4, peers[4]).wait()
                add(4)
                copy(5, peers[5]).start()

        if i == 6:

            @pl.when(place.inner)
            def _():
                copy(5, peers[5]).wait_send()

            @pl.when(place.outer)
            def _():
                copy(5, peers[5]).wait_recv()
                values[5] = got[5]

    return step


TILE = 256
WIDE = 1024


(F_SMALL, F_SEG, F_WQ, F_WK, F_WV, F_WO, F_GRAD, F_KV) = range(8)
F_KINDS = F_KV + 8
W_KV, W_Q, W_OUT = 0, 1, 2
SMALL_ROWS = 32


def two_heads(t):
    return jnp.concatenate([t[:, :HEAD_SIZE], t[:, HEAD_SIZE:]], axis=0)


def side_by_side(t):
    half = t.shape[0] // 2
    return jnp.concatenate([t[:half], t[half:]], axis=1)


def layer_kernel(
    x_hbm, wq_hbm, wk_hbm, wv_hbm, wo_hbm, g_hbm, w1_hbm, w2_hbm, small_own, seg_own, routes, inv_freq,
    y_ref, gx_ref, small_ref, out, stage, q_hbm, kv_hbm, n1_hbm, g_all, w_all,
    ao, h, n2, lse, cosine_ref, sine_ref, seg_k, seg_q, router, gains, small_in, seg,
    f_send, f_recv, x_send, x_recv, c_send, c_recv, keep_sem,
    moe, dn2, share, share_t, gate, gate_t, y_send, y_got, got_kv, got_core_w, got_y_w, small, got_small,
    piece, piece_sem, w_sem, load_sem, ys_sem, yr_sem, cs_sem, cr_sem, ss_sem, sr_sem, *scratch,
):
    rows, width = x_hbm.shape
    tokens = 2 * rows
    owned, half = w2_hbm.shape[0], w2_hbm.shape[1]
    works = 3 * owned
    pieces = 2 * works
    count = pieces + 6
    place = Place()
    group, core = place.group, place.core
    here = pl.multiple_of(group * rows, rows)
    there = pl.multiple_of((1 - group) * rows, rows)

    def begin_load(*pairs):
        copies = [
            pltpu.make_async_copy(src, dst, load_sem.at[i]) for i, (src, dst) in enumerate(pairs)
        ]
        for copy in copies:
            copy.start()
        return copies

    def end_load(copies):
        for copy in copies:
            copy.wait()

    def y_copy(kind, src, dst):
        return remote_copy(src, dst, ys_sem.at[kind], yr_sem.at[kind], place.y_peer)

    def over_tiles(first, number, body, size=TILE):
        @pl.loop(0, number)
        def _(i):
            body(pl.ds(pl.multiple_of(first + i * size, size), size))

    def shifted(tile, by):
        return pl.ds(pl.multiple_of(tile.start + by, TILE), TILE)

    def after_core(gw):
        def late_piece(k):
            j, part = (k - pieces) // 2, lax.rem(k - pieces, 2)
            return (
                y_weight(gw, k - pieces), gw.at[j, group, part, core], got_y_w.at[j, part]
            )

        return late_piece

    def y_weight(gw, i):
        j, part = i // 2, i % 2
        return y_copy(Y_WEIGHT + i, gw.at[j, 1 - group, part, core], got_y_w.at[j, part])

    def fetch(w1, w2, e):
        slot = lax.rem(e, 2)
        return (
            pltpu.make_async_copy(w1_hbm.at[e], w1.at[slot], w_sem.at[0, slot]),
            pltpu.make_async_copy(w2_hbm.at[e], w2.at[slot], w_sem.at[1, slot]),
        )

    tick, send = make_engine(place, count, count, pieces, stage, out, scratch, None)

    def advance(t):
        tick(t)

        @pl.when(t < pieces)
        def _():
            send(t)

    def advance_all(first, number):
        @pl.loop(first, first + number)
        def _(t):
            advance(t)

    own_rows_here = pl.ds(here, rows)
    qkv_width = 2 * width
    kv_width = wk_hbm.shape[1]
    own_rows = wq_hbm.shape[0]
    part = own_rows // 4
    x = place.x
    w_here = pl.multiple_of(group * own_rows, own_rows)
    w_there = pl.multiple_of((1 - group) * own_rows, own_rows)
    quarter = pl.multiple_of((2 * core + x) * part, part)
    grad_copy = remote_copy(
        g_hbm, g_all.at[pl.ds(here, rows)], f_send.at[F_GRAD], f_recv.at[F_GRAD], place.y_peer
    )
    share_copy = y_copy(Y_SHARE, share_t.at[0], share_t.at[1])

    def n2_copy(i):
        tile = n2.at[pl.ds(pl.multiple_of(here + i * TILE, TILE), TILE)]
        return y_copy(Y_N2 + i, tile, tile)

    def keep(i, src, dst):
        return pltpu.make_async_copy(src, dst, keep_sem.at[i])

    def forward_part(w, kv, bias, n1_in, q, x_in):
        loads = [
            (x_hbm, x_in),
            (wk_hbm, w.at[pl.ds(w_here, own_rows), pl.ds(width, kv_width)]),
            (wv_hbm, w.at[pl.ds(w_here, own_rows), pl.ds(width + kv_width, kv_width)]),
            (wq_hbm, w.at[pl.ds(w_here, own_rows), pl.ds(0, width)]),
            (wo_hbm, w.at[pl.ds(w_here, own_rows), pl.ds(qkv_width, width)]),
        ]
        loads = [
            pltpu.make_async_copy(src, dst, load_sem.at[i]) for i, (src, dst) in enumerate(loads)
        ]
        for copy in loads:
            copy.start()
        place.greet()

        def f_copy(kind, src, dst):
            return remote_copy(src, dst, f_send.at[kind], f_recv.at[kind], place.y_peer)

        def weight_copy(kind, src, column, columns):
            return f_copy(
                kind, src.at[pl.ds(quarter, part)],
                w.at[pl.ds(w_here + quarter, part), pl.ds(column, columns)],
            )

        def x_copy(i, column, columns):
            block = w.at[pl.ds(w_there + quarter, part), pl.ds(column, columns)]
            return remote_copy(block, block, x_send.at[i], x_recv.at[i], place.x_peer)

        def core_copy(i, column, columns):
            first = pl.multiple_of(w_there + 2 * core * part, 2 * part)
            block = w.at[pl.ds(first, 2 * part), pl.ds(column, columns)]
            return remote_copy(block, block, c_send.at[i], c_recv.at[i], place.core_peer)

        small_copy = f_copy(F_SMALL, small_own, small_in.at[group])
        seg_copy = f_copy(F_SEG, seg_own, seg.at[group])
        kv_weights = [
            weight_copy(F_WK, wk_hbm, width, kv_width),
            weight_copy(F_WV, wv_hbm, width + kv_width, kv_width),
        ]
        wq_copy = weight_copy(F_WQ, wq_hbm, 0, width)
        wo_copy = weight_copy(F_WO, wo_hbm, qkv_width, width)
        for copy in (small_copy, seg_copy, *kv_weights):
            copy.start()
        small_in[group] = small_own[...]
        seg[group] = seg_own[...]

        small_copy.wait()
        seg_copy.wait()
        seg_row = jnp.concatenate([seg[0, 0:1, :], seg[1, 0:1, :]], axis=1)
        seg_k[...] = seg_row
        router[...] = jnp.concatenate([small_in[0, 0:EXPERTS, :], small_in[1, 0:EXPERTS, :]], axis=1)
        gains[...] = jnp.concatenate(
            [small_in[0, EXPERTS:, :], small_in[1, EXPERTS:, :]], axis=1
        ).astype(f32)[0 : gains.shape[0]]
        row = here + lax.broadcasted_iota(jnp.int32, bias.shape, 0)
        col = lax.broadcasted_iota(jnp.int32, bias.shape, 1)
        seg_column = seg_own[...].astype(f32).T[:, 0:1].astype(jnp.int32)
        seg_q[...] = seg_column
        same = seg_column == seg_row
        bias[...] = jnp.where(same & (row >= col), 0.0, MASKED).astype(f32)
        position = jnp.sum(jnp.where(same & (row > col), 1.0, 0.0), axis=1, keepdims=True)

        for copy in kv_weights:
            copy.wait()
        x_copy(W_KV, width, 2 * kv_width).start()
        wq_copy.start()

        expert = lax.broadcasted_iota(jnp.int32, (EXPERTS, rows), 0)
        named = jnp.zeros((EXPERTS, rows), f32)
        for k in range(routes.shape[0]):
            named = jnp.where(routes[k : k + 1, :] == expert, 1.0, named)
        share[own_rows_here, :] = named.T

        angle = position * inv_freq[...]
        lane = lax.broadcasted_iota(jnp.int32, angle.shape, 1)
        cosine_ref[...] = jnp.cos(angle)
        sine = jnp.sin(angle)
        sine_ref[...] = jnp.where(lax.rem(lane, HEAD_SIZE) < HEAD_SIZE // 2, -sine, sine)

        for copy in loads:
            copy.wait()
        xs = x_in[...].astype(f32)
        factor = lax.rsqrt(jnp.mean(xs * xs, axis=-1, keepdims=True) + EPS)
        n1_in[...] = (xs * factor * gains[0:1, :]).astype(bf16)

        x_copy(W_KV, width, 2 * kv_width).wait()
        core_copy(W_KV, width, 2 * kv_width).start()
        wq_copy.wait()
        x_copy(W_Q, 0, width).start()
        wo_copy.start()
        core_copy(W_KV, width, 2 * kv_width).wait()

        n1 = n1_in[...]
        keep(2, n1_in, n1_hbm).start()
        cosine, sine = cosine_ref[...], sine_ref[...]

        def turned(column):
            lin = mm(n1, w[:, column : column + 256])
            return [
                (t * cosine + swap_halves(t) * sine).astype(bf16)
                for t in (lin[:, :128], lin[:, 128:])
            ]

        own = own_rows_here

        def kv_copies(i):
            first = pl.multiple_of(i * 128, 128)
            return [
                f_copy(
                    F_KV + 2 * i + j,
                    kv.at[own, pl.ds(first + j * kv_width, 128)],
                    kv.at[own, pl.ds(first + j * kv_width, 128)],
                )
                for j in range(2)
            ]

        for i in range(2):
            at = 256 * i
            kv[own, at : at + 128], kv[own, at + 128 : at + 256] = turned(width + at)
            lin = mm(n1, w[:, width + kv_width + at : width + kv_width + at + 256])
            kv[own, kv_width + at : kv_width + at + 256] = lin.astype(bf16)

            @pl.when(group == 0)
            def _():
                for j in (2 * i, 2 * i + 1):
                    for copy in kv_copies(j):
                        copy.start()

        @pl.when(group == 0)
        def _():
            kv[rows:, :] = jnp.zeros((rows, kv.shape[1]), bf16)

        x_copy(W_Q, 0, width).wait()
        core_copy(W_Q, 0, width).start()
        wo_copy.wait()
        x_copy(W_OUT, qkv_width, width).start()

        @pl.when(group == 1)
        def _():
            grad_copy.start()

        core_copy(W_Q, 0, width).wait()
        for at in range(0, width, 256):
            q[:, at : at + 128], q[:, at + 128 : at + 256] = turned(at)
        lse[...] = jnp.zeros_like(lse)

        @pl.loop(0, 4)
        def _(i):
            @pl.when(group == 1)
            def _():
                for copy in kv_copies(i):
                    copy.wait_recv()

            @pl.when(i == 2)
            def _():
                x_copy(W_OUT, qkv_width, width).wait()
                core_copy(W_OUT, qkv_width, width).start()

            at_k = pl.ds(pl.multiple_of(i * 128, 128), 128)
            at_v = pl.ds(pl.multiple_of(kv_width + i * 128, 128), 128)
            keys, values = kv[:, at_k], kv[:, at_v]
            for pair in range(2):
                lanes = slice(pair * HEAD_SIZE, (pair + 1) * HEAD_SIZE)
                key, value = keys[:, lanes], values[:, lanes]
                at_q = pl.ds(pl.multiple_of(i * 256 + pair * 128, 128), 128)

                @pl.loop(0, rows // TILE)
                def _(number):
                    tile = pl.ds(pl.multiple_of(number * TILE, TILE), TILE)
                    s = mm_nt(two_heads(q[tile, at_q]) * SCALE, key)
                    s = s.reshape(2, TILE, -1) + bias[tile, :][None]
                    peak = jnp.max(s, axis=2, keepdims=True)
                    e = jnp.exp(s - peak)
                    total = jnp.sum(e, axis=2, keepdims=True)
                    o = mm(e.astype(bf16).reshape(2 * TILE, -1), value)
                    o = o / total.reshape(2 * TILE, 1)
                    ao[tile, at_q] = side_by_side(o).astype(bf16)
                    log_sum = peak + jnp.log(total)
                    lane = lax.broadcasted_iota(jnp.int32, (TILE, QUERY_HEADS), 1)
                    head = 4 * i + 2 * pair
                    lse[tile, :] = jnp.where(
                        lane == head, log_sum[0], jnp.where(lane == head + 1, log_sum[1], lse[tile, :])
                    )

        @pl.when(group == 0)
        def _():
            for i in range(4):
                for copy in kv_copies(i):
                    copy.wait_send()
            grad_copy.start()

        keep(3, q, q_hbm).start()
        keep(1, kv, kv_hbm).start()
        core_copy(W_OUT, qkv_width, width).wait()
        keep(0, w, w_all).start()

        @pl.loop(0, rows // TILE)
        def _(number):
            tile = pl.ds(pl.multiple_of(number * TILE, TILE), TILE)
            own_tile = shifted(tile, here)
            hidden = x_in[tile, :].astype(f32) + mm(ao[tile, :], w[:, qkv_width:])
            h[tile, :] = hidden
            factor = lax.rsqrt(jnp.mean(hidden * hidden, axis=-1, keepdims=True) + EPS)
            normed = (hidden * factor * gains[1:2, :]).astype(bf16)
            n2[own_tile, :] = normed
            n2_copy(number).start()
            logits = mm_nt(normed, router[...])
            chosen = share[own_tile, :] > 0.0
            picked = jnp.where(chosen, logits, MASKED)
            e = jnp.exp(picked - jnp.max(picked, axis=1, keepdims=True))
            e = jnp.where(chosen, e, 0.0)
            share[own_tile, :] = e / jnp.sum(e, axis=1, keepdims=True)

        share_t[0] = share[own_rows_here, :].T
        share_copy.start()
        for i, (src, dst) in enumerate(((w, w_all), (kv, kv_hbm), (n1_in, n1_hbm), (q, q_hbm))):
            keep(i, src, dst).wait()

    pl.run_scoped(
        forward_part,
        pltpu.VMEM((width, 3 * width), bf16),
        pltpu.VMEM((tokens, width), bf16),
        pltpu.VMEM((rows, tokens), f32),
        *[pltpu.VMEM((rows, width), bf16)] * 3,
    )

    dn2_copy = y_copy(Y_DN2, y_send.at[0], y_got.at[0])

    def leave(i, terms, tile):
        y_send[i, shifted(tile, -there), :] = terms[tile, :].astype(bf16)

    def expert_part(n2_turned, g, act, d_ye, d_gu, w1, w2):
        for copy in fetch(w1, w2, 0):
            copy.start()
        loads = begin_load((g_hbm, g.at[own_rows_here]))
        gate[...] = jnp.zeros_like(gate)

        def prepare(tile):
            n2_turned[:, tile] = n2[tile, :].T
            moe[tile, :] = jnp.zeros((TILE, width), f32)
            dn2[tile, :] = jnp.zeros((TILE, width), f32)

        over_tiles(here, rows // TILE, prepare)
        for i in range(rows // TILE):
            n2_copy(i).wait()
        share_copy.wait()
        share[pl.ds(there, rows), :] = share_t[1].T
        over_tiles(there, rows // TILE, prepare)
        grad_copy.wait()
        end_load(loads)
        end_load(begin_load((g_all.at[pl.ds(there, rows)], g.at[pl.ds(there, rows)])))

        def pick(table, e):
            lane = lax.broadcasted_iota(jnp.int32, table.shape, 1)
            return jnp.sum(
                jnp.where(lane == group * owned + e, table, 0.0), axis=1, keepdims=True
            )

        def keep_piece(k):
            slot = lax.rem(k, 2)
            return pltpu.make_async_copy(piece.at[slot], stage.at[pl.ds(2 * k, 2)], piece_sem.at[slot])

        def work(k):
            e, sub = k // 3, lax.rem(k, 3)
            slot = lax.rem(e, 2)

            @pl.when(k == 2)
            def _():
                keep_piece(1).wait()

            @pl.when(k >= 4)
            def _():
                keep_piece(k - 2).wait()

            @pl.when(sub == 0)
            def _():
                for copy in fetch(w1, w2, e):
                    copy.wait()

                @pl.when(e + 1 < owned)
                def _():
                    for copy in fetch(w1, w2, e + 1):
                        copy.start()

                def body(tile):
                    gu = mm(n2[tile, :], w1[slot])
                    z, w = gu[:, :half], gu[:, half:]
                    sg = jax.nn.sigmoid(z)
                    silu = z * sg
                    act[tile, :] = (silu * w).astype(bf16)
                    dy = (pick(share[tile, :], e) * g[tile, :].astype(f32)).astype(bf16)
                    d_ye[tile, :] = dy
                    d_act = mm_nt(dy, w2[slot])
                    d_gu[tile, :half] = (d_act * w * sg * (1.0 + z * (1.0 - sg))).astype(bf16)
                    d_gu[tile, half:] = (d_act * silu).astype(bf16)

                over_tiles(0, tokens // WIDE, body, WIDE)
                for part in range(2):
                    columns = slice(part * half // 2, (part + 1) * half // 2)
                    grad = mm_tn(act[:, columns], d_ye[...])
                    piece[lax.rem(k, 2), part] = grad.astype(bf16).reshape(piece.shape[2:])

            @pl.when(sub == 2)
            def _():
                @pl.when(k == works - 1)
                def _():
                    over_tiles(there, rows // TILE, functools.partial(leave, 0, dn2))
                    dn2_copy.start()

                def body(tile):
                    ye = mm(act[tile, :], w2[slot]).astype(bf16).astype(f32)
                    value = jnp.sum(g[tile, :].astype(f32) * ye, axis=1, keepdims=True)
                    lane = lax.broadcasted_iota(jnp.int32, (WIDE, gate.shape[1]), 1)
                    gate[tile, :] = jnp.where(lane == group * owned + e, value, gate[tile, :])
                    moe[tile, :] += pick(share[tile, :], e) * ye

                over_tiles(0, tokens // WIDE, body, WIDE)

            @pl.when(sub == 1)
            def _():
                def body(tile):
                    dn2[tile, :] += mm_nt(d_gu[tile, :], w1[slot]).astype(bf16).astype(f32)

                over_tiles(0, tokens // WIDE, body, WIDE)

            @pl.when(sub > 0)
            def _():
                @pl.loop(0, 2)
                def _(part):
                    first = pl.multiple_of((2 * (sub - 1) + part) * (half // 2), half // 2)
                    grad = mm(n2_turned[pl.ds(first, half // 2), :], d_gu[...])
                    piece[lax.rem(k, 2), part] = grad.astype(bf16).reshape(piece.shape[2:])

            keep_piece(k).start()

            @pl.when(k == 0)
            def _():
                keep_piece(0).wait()

        @pl.loop(0, works)
        def _(k):
            work(k)
            pl.loop(6 * k // 5, 6 * (k + 1) // 5)(advance)

        keep_piece(works - 2).wait()
        keep_piece(works - 1).wait()

        over_tiles(there, rows // TILE, functools.partial(leave, 1, moe))

    wide = (tokens, width)
    pl.run_scoped(
        expert_part,
        pltpu.VMEM((width, tokens), bf16),
        pltpu.VMEM(wide, bf16),
        pltpu.VMEM((tokens, half), bf16),
        pltpu.VMEM(wide, bf16),
        pltpu.VMEM((tokens, 2 * half), bf16),
        pltpu.VMEM((2, width, 2 * half), bf16),
        pltpu.VMEM((2, half, width), bf16),
    )
    t = 6 * works // 5
    gate_copy = y_copy(Y_GATE, gate_t.at[0], gate_t.at[1])
    gate_t[0] = gate[pl.ds(there, rows), :].T
    moe_copy = y_copy(Y_MOE, y_send.at[1], y_got.at[1])
    gate_copy.start()
    t += 5

    def attention_part(gw, d_o, dkv):
        tail = gw.shape[3:]

        def store_rows(j, i, grad):
            gw[j, i // 2, i % 2] = grad.astype(bf16).reshape(tail)

        def core_weight(j):
            return remote_copy(
                gw.at[j, :, :, 1 - core], got_core_w.at[j], cs_sem.at[j], cr_sem.at[j],
                place.core_peer,
            )

        def to_owner(j):
            core_weight(j).wait()
            for member in range(2):
                for part in range(2):
                    gw[j, member, part, core] += got_core_w[j, member, part]
            for part in range(2):
                y_weight(gw, 2 * j + part).start()

        def kv_copies(i):
            first = pl.multiple_of(i * 128, 128)
            return [
                y_copy(
                    Y_DKV + 2 * i + j,
                    dkv.at[pl.ds(0, rows), pl.ds(first + j * (width // 2), 128)],
                    got_kv.at[:, pl.ds(first + j * (width // 2), 128)],
                )
                for j in range(2)
            ]

        def middle(g, wo, d_y):
            loads = begin_load((g_hbm, g), (w_all.at[:, pl.ds(2 * width, width)], wo))
            advance_all(t - 5, 5)
            end_load(loads)
            dn2_copy.wait()
            gate_copy.wait()
            gate[own_rows_here, :] += gate_t[1].T
            moe_copy.start()
            small[0] = jnp.zeros(small.shape[1:], f32)

            def body(tile):
                own = shifted(tile, here)
                s = share[own, :]
                dg = gate[own, :]
                d_logits = (s * (dg - jnp.sum(s * dg, axis=1, keepdims=True))).astype(bf16)
                d_n2 = dn2[own, :] + y_got[0, tile, :].astype(f32) + mm(d_logits, router[...])
                hidden = h[tile, :]
                factor = lax.rsqrt(jnp.mean(hidden * hidden, axis=-1, keepdims=True) + EPS)
                small[0, 0:EXPERTS, :] += mm_tn(d_logits, n2[own, :])
                small[0, EXPERTS : EXPERTS + 1, :] += jnp.sum(
                    hidden * factor * d_n2, axis=0, keepdims=True
                )
                c = d_n2 * gains[1:2, :]
                mean = jnp.mean(c * hidden, axis=-1, keepdims=True)
                d_h = g[tile, :].astype(f32) + factor * (c - hidden * (factor * factor * mean))
                dn2[shifted(tile, there), :] = d_h
                d_y[tile, :] = d_h.astype(bf16)
                d_o[tile, :] = mm_nt(d_h.astype(bf16), wo[...]).astype(bf16)
                moe[own, :] += hidden

            @pl.loop(0, rows // TILE)
            def _(i):
                body(pl.ds(pl.multiple_of(i * TILE, TILE), TILE))
                advance(t + i)

            for i in range(4):
                columns = slice(i * width // 4, (i + 1) * width // 4)
                store_rows(0, i, mm_tn(ao[:, columns], d_y[...]))
            core_weight(0).start()

        pl.run_scoped(
            middle,
            pltpu.VMEM((rows, width), bf16),
            pltpu.VMEM((width, width), bf16),
            pltpu.VMEM((rows, width), bf16),
        )
        advance(t + 2)
        to_owner(0)

        def heads(q, kv, bias):
            loads = begin_load((q_hbm, q), (kv_hbm, kv))
            row = here + lax.broadcasted_iota(jnp.int32, bias.shape, 0)
            col = lax.broadcasted_iota(jnp.int32, bias.shape, 1)
            seen = (seg_q[...] == seg_k[...]) & (row >= col)
            bias[...] = jnp.where(seen, 0.0, MASKED).astype(f32)
            end_load(loads)

            @pl.loop(0, 4)
            def _(i):
                at_k = pl.ds(pl.multiple_of(i * 128, 128), 128)
                at_v = pl.ds(pl.multiple_of(width // 2 + i * 128, 128), 128)
                keys, values = kv[:, at_k], kv[:, at_v]
                dks, dvs = [], []
                for pair in range(2):
                    lanes = slice(pair * HEAD_SIZE, (pair + 1) * HEAD_SIZE)
                    key, value = keys[:, lanes], values[:, lanes]
                    at_q = pl.ds(pl.multiple_of(i * 256 + pair * 128, 128), 128)

                    def body(part, sums):
                        dk, dv = sums
                        tile = pl.ds(pl.multiple_of(part * TILE, TILE), TILE)
                        qs = two_heads(q[tile, at_q]) * SCALE
                        dos = two_heads(d_o[tile, at_q])
                        os = two_heads(ao[tile, at_q])
                        delta = jnp.sum(
                            dos.astype(f32) * os.astype(f32), axis=1, keepdims=True
                        )
                        lane = lax.broadcasted_iota(jnp.int32, (TILE, QUERY_HEADS), 1)
                        peaks = jnp.concatenate(
                            [
                                jnp.sum(
                                    jnp.where(lane == 4 * i + 2 * pair + head, lse[tile, :], 0.0),
                                    axis=1, keepdims=True,
                                )
                                for head in range(2)
                            ],
                            axis=0,
                        )
                        s = mm_nt(qs, key) - peaks
                        s = s.reshape(2, TILE, -1) + bias[tile, :][None]
                        p = jnp.exp(s).reshape(2 * TILE, -1)
                        dp = mm_nt(dos, value)
                        ds = (p * (dp - delta)).astype(bf16)
                        dq = mm(ds, key) * SCALE
                        moe[shifted(tile, there), at_q] = side_by_side(dq)
                        return dk + mm_tn(qs, ds), dv + mm_tn(dos, p.astype(bf16))

                    zero = jnp.zeros((HEAD_SIZE, kv.shape[0]), f32)
                    dk, dv = lax.fori_loop(0, rows // TILE, body, (zero, zero))
                    dks.append(dk)
                    dvs.append(dv)
                dkv[:, at_k] = jnp.concatenate(dks, axis=0).T.astype(bf16)
                dkv[:, at_v] = jnp.concatenate(dvs, axis=0).T.astype(bf16)

                @pl.when(group == 1)
                def _():
                    for copy in kv_copies(i):
                        copy.start()

                advance(t + 3 + 2 * i)
                advance(t + 4 + 2 * i)

        pl.run_scoped(
            heads,
            pltpu.VMEM((rows, width), bf16),
            pltpu.VMEM((tokens, width), bf16),
            pltpu.VMEM((rows, tokens), f32),
        )

        def projections(n1, wqkv, lin, x_in):
            loads = begin_load(
                (n1_hbm, n1), (x_hbm, x_in), (w_all.at[:, pl.ds(0, 2 * width)], wqkv)
            )
            own = pl.ds(here, rows)

            def turn_back(to, source, where, at):
                value = source[where, at : at + 128].astype(f32)
                turned = value * cosine_ref[...] - swap_halves(value) * sine_ref[...]
                lin[:, to : to + 128] = turned.astype(bf16)

            def weight_grad(j, first):
                for i in range(4):
                    columns = slice(i * width // 4, (i + 1) * width // 4)
                    store_rows(j, i, mm_tn(n1[:, columns], lin[:, first : first + width]))
                core_weight(j).start()

            for j in range(0, width, 128):
                turn_back(j, moe, pl.ds(there, rows), j)
            end_load(loads[:1])
            weight_grad(1, 0)
            advance(t + 11)
            to_owner(1)
            advance(t + 12)

            @pl.when(group == 1)
            def _():
                for i in range(4):
                    for copy in kv_copies(i):
                        copy.wait_send()

            @pl.when(group == 0)
            def _():
                for i in range(4):
                    for copy in kv_copies(i):
                        copy.wait_recv()
                total = dkv[0:rows, :].astype(f32) + got_kv[...].astype(f32)
                dkv[0:rows, :] = total.astype(bf16)

            for j in range(0, width // 2, 128):
                turn_back(width + j, dkv, own, j)
            lin[:, 3 * width // 2 :] = dkv[own, width // 2 :]
            weight_grad(2, width)
            advance(t + 13)
            to_owner(2)
            advance(t + 14)

            def body(tile):
                dn1 = mm_nt(lin[tile, :], wqkv[...])
                xs = x_in[tile, :].astype(f32)
                factor = lax.rsqrt(jnp.mean(xs * xs, axis=-1, keepdims=True) + EPS)
                small[0, EXPERTS + 1 : EXPERTS + 2, :] += jnp.sum(
                    xs * factor * dn1, axis=0, keepdims=True
                )
                c = dn1 * gains[0:1, :]
                mean = jnp.mean(c * xs, axis=-1, keepdims=True)
                gx_ref[tile, :] = dn2[shifted(tile, there), :] + factor * (
                    c - xs * (factor * factor * mean)
                )
                total = moe[shifted(tile, here), :] + y_got[1, tile, :].astype(f32)
                y_ref[tile, :] = total.astype(bf16)

            end_load(loads[1:])
            moe_copy.wait()
            last_tick, last_send = make_engine(
                place, count, pieces, pieces, stage, out, scratch, after_core(gw)
            )
            small_step = make_small_sum(place, small, got_small, ss_sem, sr_sem)
            first_last = t + 15
            tiles = rows // TILE

            @pl.loop(first_last, count + PHASES * LAG)
            def _(now):
                last_tick(now)

                @pl.when(now < pieces)
                def _():
                    last_send(now)

                @pl.when(now < first_last + tiles)
                def _():
                    body(pl.ds(pl.multiple_of((now - first_last) * TILE, TILE), TILE))

                for i in range(7):

                    @pl.when(now == first_last + tiles + 2 * i)
                    def _():
                        small_step(i)

        pl.run_scoped(
            projections,
            pltpu.VMEM((rows, width), bf16),
            pltpu.VMEM((width, 2 * width), bf16),
            pltpu.VMEM((rows, 2 * width), bf16),
            pltpu.VMEM((rows, width), bf16),
        )

    pl.run_scoped(
        attention_part,
        pltpu.VMEM((3, 2, 2, *piece.shape[2:]), bf16),
        pltpu.VMEM((rows, width), bf16),
        pltpu.VMEM((tokens, width), bf16),
    )
    small_ref[...] = small[5]


DEPTH = 6


def finish_kernel(
    owned, pieces, small_ref, g_in, g_out, g_q, g_k, g_v, g_wo, router_ref, gain_ref,
    narrow, wide, in_sem, out_sem, last_sem,
):
    count = pieces.shape[0]
    whole = count - 2
    kv_width = g_k.shape[-1]

    def fetch(k):
        slot = lax.rem(k, DEPTH)
        return pltpu.make_async_copy(pieces.at[k], narrow.at[slot], in_sem.at[slot])

    def store(k, target):
        slot = lax.rem(k, DEPTH)
        return pltpu.make_async_copy(wide.at[slot], target, out_sem.at[slot])

    def convert(k):
        slot = lax.rem(k, DEPTH)
        fetch(k).wait()

        @pl.when(k >= DEPTH)
        def _():
            store(k, g_in.at[0]).wait()

        wide[slot] = narrow[slot].astype(f32)

        @pl.when(k + DEPTH < count)
        def _():
            fetch(k + DEPTH).start()

    for k in range(DEPTH):
        fetch(k).start()
    columns = router_ref.shape[1]
    first = pl.multiple_of(lax.axis_index("group") * columns, columns)
    router_ref[...] = small_ref[0:EXPERTS, pl.ds(first, columns)]
    gain_ref[...] = small_ref[EXPERTS:, pl.ds(first, columns)]

    @pl.loop(0, whole)
    def _(k):
        convert(k)
        base = 0
        for target in (g_in, g_out, g_wo, g_q):
            number = target.shape[0]

            @pl.when((k >= base) & (k < base + number))
            def _():
                store(k, target.at[k - base]).start()

            base += number

    last = []
    for i in range(2):
        k = whole + i
        convert(k)
        for j, target in enumerate((g_k, g_v)):
            copy = pltpu.make_async_copy(
                wide.at[k % DEPTH, :, pl.ds(j * kv_width, kv_width)], target.at[i],
                last_sem.at[2 * i + j],
            )
            copy.start()
            last.append(copy)
    for copy in last:
        copy.wait()
    for k in range(count - DEPTH, whole):
        store(k, g_in.at[0]).wait()


def finish(pieces, small, owned, kv_width):
    count, rows, width = pieces.shape
    shape = jax.ShapeDtypeStruct
    vmem = pl.BlockSpec(memory_space=pltpu.VMEM)
    hbm = pl.BlockSpec(memory_space=pl.ANY)
    dma = pltpu.SemaphoreType.DMA
    return pl.pallas_call(
        functools.partial(finish_kernel, owned),
        out_shape=(
            shape((4 * owned, rows, width), f32),
            shape((2 * owned, rows, width), f32),
            shape((2, rows, width), f32),
            shape((2, rows, kv_width), f32),
            shape((2, rows, kv_width), f32),
            shape((2, rows, width), f32),
            shape((EXPERTS, width // 2), f32),
            shape((8, width // 2), f32),
        ),
        in_specs=[hbm, vmem],
        out_specs=[hbm] * 6 + [vmem] * 2,
        scratch_shapes=[
            pltpu.VMEM((DEPTH, rows, width), bf16),
            pltpu.VMEM((DEPTH, rows, width), f32),
            dma((DEPTH,)),
            dma((DEPTH,)),
            dma((4,)),
        ],
        compiler_params=params(48),
        cost_estimate=cost(0, 6 * pieces.size),
        name="finish",
    )(pieces, small)


def layer(x, document_numbers, routes, gains, w_router, wq, wk, wv, wo, grad, w_in, w_out):
    rows, width = x.shape
    own_rows = wq.shape[0]
    small = jnp.concatenate(
        [w_router.T, *[gain[None] for gain in gains],
         jnp.zeros((SMALL_ROWS - EXPERTS - 2, own_rows), bf16)], axis=0,
    )
    exponent = (np.arange(128) % (HEAD_SIZE // 2)) * (-2.0 / HEAD_SIZE)
    inv_freq = jnp.asarray(np.power(10000.0, exponent)[None], f32)
    owned, half = w_out.shape[:2]
    tokens, quarter = 2 * rows, half // 16
    pieces = 6 * owned
    shape = jax.ShapeDtypeStruct
    vmem = pl.BlockSpec(memory_space=pltpu.VMEM)
    hbm = pl.BlockSpec(memory_space=pl.ANY)
    dma = pltpu.SemaphoreType.DMA
    small_rows = EXPERTS + 8
    return pl.pallas_call(
        layer_kernel,
        out_shape=(
            shape((rows, width), bf16),
            shape((rows, width), f32),
            shape((small_rows, width), f32),
            shape((pieces + 6, 2, 4, quarter, width), bf16),
            shape((pieces, 2, 4, quarter, width), bf16),
            shape((rows, width), bf16),
            shape((tokens, width), bf16),
            shape((rows, width), bf16),
            shape((tokens, width), bf16),
            shape((width, 3 * width), bf16),
        ),
        in_specs=[hbm] * 8 + [vmem] * 4,
        out_specs=[vmem, vmem, vmem] + [hbm] * 7,
        scratch_shapes=[
            pltpu.VMEM((rows, width), bf16),
            pltpu.VMEM((rows, width), f32),
            pltpu.VMEM((tokens, width), bf16),
            pltpu.VMEM((rows, QUERY_HEADS), f32),
            pltpu.VMEM((rows, 128), f32),
            pltpu.VMEM((rows, 128), f32),
            pltpu.VMEM((1, tokens), jnp.int32),
            pltpu.VMEM((rows, 1), jnp.int32),
            pltpu.VMEM((EXPERTS, width), bf16),
            pltpu.VMEM((8, width), f32),
            pltpu.VMEM((2, SMALL_ROWS, own_rows), bf16),
            pltpu.VMEM((2, 8, rows), jnp.int32),
            dma((F_KINDS,)),
            dma((F_KINDS,)),
            *[dma((3,))] * 4,
            dma((4,)),
            pltpu.VMEM((tokens, width), f32),
            pltpu.VMEM((tokens, width), f32),
            pltpu.VMEM((tokens, EXPERTS), f32),
            pltpu.VMEM((2, EXPERTS, rows), f32),
            pltpu.VMEM((tokens, EXPERTS), f32),
            pltpu.VMEM((2, EXPERTS, rows), f32),
            pltpu.VMEM((2, rows, width), bf16),
            pltpu.VMEM((2, rows, width), bf16),
            pltpu.VMEM((rows, width), bf16),
            pltpu.VMEM((3, 2, 2, 4, quarter, width), bf16),
            pltpu.VMEM((3, 2, 4, quarter, width), bf16),
            pltpu.VMEM((6, small_rows, width), f32),
            pltpu.VMEM((6, small_rows, width), f32),
            pltpu.VMEM((2, 2, 2, 4, quarter, width), bf16),
            dma((2,)),
            dma((2, 2)),
            dma((5,)),
            dma((Y_KINDS,)),
            dma((Y_KINDS,)),
            dma((3,)),
            dma((3,)),
            dma((6,)),
            dma((6,)),
            *engine_scratch(quarter, width),
        ],
        compiler_params=pltpu.CompilerParams(
            collective_id=1, has_side_effects=True, vmem_limit_bytes=63 * MIB
        ),
        cost_estimate=cost(18 * tokens * width * half * owned, 6 * w_in.size),
        name="layer",
    )(
        x, wq, wk, wv, wo, grad, w_in, w_out, small,
        jnp.broadcast_to(document_numbers[None], (8, rows)), routes.T, inv_freq,
    )


def expert_pass(n2, grad, share, w_in, w_out):
    half = w_out.shape[0]
    gu = mm(n2, w_in)
    z, w = gu[:, :half], gu[:, half:]
    sg = jax.nn.sigmoid(z)
    act = (z * sg * w).astype(bf16)
    ye = mm(act, w_out).astype(bf16).astype(f32)
    d_gate = jnp.sum(grad * ye, axis=1)
    d_ye = (share * grad).astype(bf16)
    g_out = mm_tn(act, d_ye).astype(bf16)
    d_act = mm_nt(d_ye, w_out)
    d_gu = jnp.concatenate(
        [d_act * w * sg * (1.0 + z * (1.0 - sg)), d_act * z * sg], axis=1
    ).astype(bf16)
    g_in = mm_tn(n2, d_gu).astype(bf16)
    d_xe = mm_nt(d_gu, w_in).astype(bf16).astype(f32)
    return share * ye, d_gate, g_in, g_out, d_xe


def all_experts(n2, grad, share, w_in, w_out):
    moe = jnp.zeros(n2.shape, f32)
    d_n2 = jnp.zeros_like(moe)
    d_gate, g_in, g_out = [], [], []
    for i in range(w_in.shape[0]):
        y, dg, gi, go, dx = expert_pass(
            n2, grad.astype(f32), share[:, i : i + 1], w_in[i], w_out[i]
        )
        moe, d_n2 = moe + y, d_n2 + dx
        d_gate.append(dg)
        g_in.append(gi)
        g_out.append(go)
    g_in, g_out = lax.psum((jnp.stack(g_in), jnp.stack(g_out)), "replica")
    return moe, d_n2, jnp.stack(d_gate, 1), g_in.astype(f32), g_out.astype(f32)


def on_device(
    layer_input, document_numbers, routes, norm_attn, w_query, key_weight, value_weight, w_out,
    norm_moe, w_router, expert_in, expert_out, cotangent,
):
    rows, width = layer_input.shape
    group = lax.axis_index("group")
    first = group * rows
    owned = expert_in.shape[0]
    kv_width = KEY_VALUE_HEADS * HEAD_SIZE

    q_width = QUERY_HEADS * HEAD_SIZE
    if lax.axis_size("replica") == 16 and lax.axis_size("group") == 2:
        layer_output, grad_input, small_sum, sums, *_ = layer(
            layer_input, document_numbers, routes, (norm_attn, norm_moe), w_router, w_query,
            key_weight, value_weight, w_out, cotangent, expert_in, expert_out,
        )
        g_in, g_out, g_q, g_k, g_v, g_wo, g_router, g_gains = finish(
            sums.reshape(sums.shape[0], -1, width), small_sum, owned, kv_width
        )
        return (
            layer_output,
            grad_input,
            g_gains[1],
            g_q.reshape(w_query.shape),
            g_k.reshape(key_weight.shape),
            g_v.reshape(value_weight.shape),
            g_wo.reshape(w_out.shape),
            g_gains[0],
            g_router.T,
            g_in.reshape(expert_in.shape),
            g_out.reshape(expert_out.shape),
        )

    seg_all = gather(document_numbers)
    position = lax.dynamic_slice_in_dim(doc_positions(seg_all), first, rows, 0)
    cosine, sine = turn_tables(position)
    small = gather(jnp.concatenate([norm_attn[:, None], norm_moe[:, None], w_router], axis=1))
    gain_attn = small[:, 0].astype(f32)[None, :]
    gain_moe = small[:, 1].astype(f32)[None, :]
    router = small[:, 2:]
    w_qkv = gather(jnp.concatenate([w_query, key_weight, value_weight], axis=1))
    wo = gather(w_out)
    grad_all = gather(cotangent)

    n1, q, k, v = project(layer_input, gain_attn, w_qkv, cosine, sine)
    kv_all = gather(jnp.concatenate([k, v], axis=1))
    k_all, v_all = kv_all[:, :kv_width], kv_all[:, kv_width:]
    first_row = jnp.full((1,), first, jnp.int32)
    seg_q, seg_k = document_numbers[:, None], seg_all[None, :]
    ao = attend(first_row, q, k_all, v_all, seg_q, seg_k)

    x = layer_input.astype(f32)
    h = x + mm(ao, wo)
    r2 = rms_factor(h)
    n2 = (h * r2 * gain_moe).astype(bf16)
    logits = mm(n2, router)
    chosen = jnp.any(routes[:, :, None] == jnp.arange(EXPERTS, dtype=jnp.int32), axis=1)
    picked = jnp.where(chosen, logits, MASKED)
    e = jnp.where(chosen, jnp.exp(picked - jnp.max(picked, axis=1, keepdims=True)), 0.0)
    share = e / jnp.sum(e, axis=1, keepdims=True)

    n2_all = gather(n2)
    share_all = lax.dynamic_slice_in_dim(gather(share), group * owned, owned, 1)
    moe, d_n2_all, d_gate, g_in, g_out = all_experts(
        n2_all, grad_all, share_all, expert_in, expert_out
    )
    d_gate = lax.dynamic_update_slice_in_dim(
        jnp.zeros((n2_all.shape[0], EXPERTS), f32), d_gate, group * owned, 1
    )
    d_gate = lax.psum_scatter(d_gate, "group", scatter_dimension=0, tiled=True)
    layer_output = (h + owner_sum(moe).astype(f32)).astype(bf16)

    d_logits = (share * (d_gate - jnp.sum(share * d_gate, axis=1, keepdims=True))).astype(bf16)
    g_router = mm_tn(n2, d_logits)
    d_n2 = owner_sum(d_n2_all).astype(f32) + mm_nt(d_logits, router)
    g_gain_moe = jnp.sum(h * r2 * d_n2, axis=0)
    c = d_n2 * gain_moe
    d_h = cotangent.astype(f32) + r2 * (
        c - h * r2 * r2 * jnp.mean(c * h, axis=-1, keepdims=True)
    )
    d_y = d_h.astype(bf16)
    g_wo = mm_tn(ao, d_y).astype(bf16)
    d_o = mm_nt(d_y, wo).astype(bf16)

    dq, dk_all, dv_all = attend_grad(first_row, q, k_all, v_all, d_o, seg_q, seg_k)
    dkv = owner_sum(jnp.concatenate([dk_all, dv_all], axis=1))
    g_qkv, grad_input, g_gain_attn = project_grad(
        dq, dkv[:, :kv_width], dkv[:, kv_width:], n1, w_qkv, cosine, sine, layer_input,
        gain_attn, d_h,
    )

    g_attn = owner_sum(jnp.concatenate([g_qkv, g_wo], axis=1))
    g_small = owner_sum(
        jnp.concatenate([g_gain_attn.reshape(-1, 1), g_gain_moe[:, None], g_router], axis=1)
    )
    g_attn, g_small = (t.astype(f32) for t in lax.psum((g_attn, g_small), "replica"))
    return (
        layer_output,
        grad_input,
        g_small[:, 0],
        g_attn[:, :q_width],
        g_attn[:, q_width : q_width + kv_width],
        g_attn[:, q_width + kv_width : q_width + 2 * kv_width],
        g_attn[:, q_width + 2 * kv_width :],
        g_small[:, 1],
        g_small[:, 2:],
        g_in,
        g_out,
    )


def solution(mesh):
    tokens, weights = P(("replica", "group"), None), P("group", None)
    in_specs = (
        tokens, P(("replica", "group")), tokens, P("group"), weights, weights, weights, weights,
        P("group"), weights, P("group", None, None), P("group", None, None), tokens,
    )
    out_specs = (
        tokens, tokens, P("group"), weights, weights, weights, weights, P("group"), weights,
        P("group", None, None), P("group", None, None),
    )
    return jax.shard_map(
        on_device, mesh=mesh, in_specs=in_specs, out_specs=out_specs, check_vma=False
    )
```

```python
import functools

import jax
import jax.numpy as jnp
import numpy as np
from jax import lax
from jax.experimental import pallas as pl
from jax.experimental.pallas import tpu as pltpu
from jax.sharding import PartitionSpec as P

QUERY_HEADS = 16
KEY_VALUE_HEADS = 8
HEAD_SIZE = 64
EXPERTS = 16
EPS = 1e-06
MASKED = -1e30
SCALE = HEAD_SIZE ** (-0.5)

f32 = jnp.float32
bf16 = jnp.bfloat16
MIB = 1 << 20


def mm(a, b):
    return lax.dot_general(a, b, (((1,), (0,)), ((), ())), preferred_element_type=f32)


def mm_nt(a, b):
    return lax.dot_general(a, b, (((1,), (1,)), ((), ())), preferred_element_type=f32)


def mm_tn(a, b):
    return lax.dot_general(a, b, (((0,), (0,)), ((), ())), preferred_element_type=f32)


def params(mib):
    return pltpu.CompilerParams(vmem_limit_bytes=mib * MIB)


def cost(flops, moved):
    return pl.CostEstimate(flops=int(flops), bytes_accessed=int(moved), transcendentals=0)


def doc_positions(seg_ids):
    length = seg_ids.shape[0]
    index = jnp.arange(length, dtype=jnp.int32)
    previous = jnp.concatenate([seg_ids[:1] - 1, seg_ids[:-1]])
    is_start = (seg_ids != previous) | (index == 0)
    start = lax.cummax(jnp.where(is_start, index, 0), axis=0)
    return index - start


def turn_tables(position):
    half = HEAD_SIZE // 2
    exponent = jnp.arange(half, dtype=f32) * (-2.0 / HEAD_SIZE)
    inv_freq = jnp.power(10000.0, exponent)
    angles = position.astype(f32)[:, None] * inv_freq[None, :]
    cosine, sine = jnp.cos(angles), jnp.sin(angles)
    return (
        jnp.concatenate([cosine] * 4, axis=1),
        jnp.concatenate([-sine, sine, -sine, sine], axis=1),
    )


def swap_halves(t):
    lane = lax.broadcasted_iota(jnp.int32, t.shape, 1)
    return jnp.where(
        lane % HEAD_SIZE < HEAD_SIZE // 2, pltpu.roll(t, 96, 1), pltpu.roll(t, 32, 1)
    )


def qkv_kernel(x_ref, gain_ref, w_ref, cos_ref, sin_ref, n1_ref, q_ref, k_ref, v_ref):
    x = x_ref[...].astype(f32)
    factor = lax.rsqrt(jnp.mean(x * x, axis=-1, keepdims=True) + EPS)
    n1 = (x * factor * gain_ref[...]).astype(bf16)
    n1_ref[...] = n1
    cosine, sine = cos_ref[...], sin_ref[...]
    q_width, k_width = q_ref.shape[1], k_ref.shape[1]
    for start in range(0, q_width + k_width, 256):
        lin = mm(n1, w_ref[:, start : start + 256])
        for part in (0, 128):
            t = lin[:, part : part + 128]
            turned = (t * cosine + swap_halves(t) * sine).astype(bf16)
            at = start + part
            if at < q_width:
                q_ref[:, at : at + 128] = turned
            else:
                k_ref[:, at - q_width : at - q_width + 128] = turned
    v_ref[...] = mm(n1, w_ref[:, q_width + k_width :]).astype(bf16)


def project(x, gain, w, cosine, sine):
    rows, width = x.shape
    q_width, k_width = QUERY_HEADS * HEAD_SIZE, KEY_VALUE_HEADS * HEAD_SIZE
    shape = jax.ShapeDtypeStruct
    return pl.pallas_call(
        qkv_kernel,
        out_shape=(
            shape((rows, width), bf16),
            shape((rows, q_width), bf16),
            shape((rows, k_width), bf16),
            shape((rows, k_width), bf16),
        ),
        compiler_params=params(40),
        cost_estimate=cost(2 * rows * width * w.shape[1], 2 * w.size + 8 * x.size),
        name="project",
    )(x, gain, w, cosine, sine)


def qkv_grad_kernel(
    dq_ref, dk_ref, dv_ref, n1_ref, w_ref, cos_ref, sin_ref, x_ref, gain_ref, dh_ref,
    gw_ref, gx_ref, gg_ref, lin_ref,
):
    cosine, sine = cos_ref[...], sin_ref[...]
    q_width, k_width = dq_ref.shape[1], dk_ref.shape[1]
    for ref, width, base in ((dq_ref, q_width, 0), (dk_ref, k_width, q_width)):
        for at in range(0, width, 128):
            t = ref[:, at : at + 128].astype(f32)
            turned = (t * cosine - swap_halves(t) * sine).astype(bf16)
            lin_ref[:, base + at : base + at + 128] = turned
    lin_ref[:, q_width + k_width :] = dv_ref[...].astype(bf16)
    total = q_width + 2 * k_width
    n1 = n1_ref[...]
    for at in range(0, total, 512):
        gw_ref[:, at : at + 512] = mm_tn(n1, lin_ref[:, at : at + 512]).astype(bf16)
    dn1 = mm_nt(lin_ref[...], w_ref[...])
    x = x_ref[...].astype(f32)
    factor = lax.rsqrt(jnp.mean(x * x, axis=-1, keepdims=True) + EPS)
    gg_ref[...] = jnp.sum(x * factor * dn1, axis=0, keepdims=True)
    c = dn1 * gain_ref[...]
    mean = jnp.mean(c * x, axis=-1, keepdims=True)
    gx_ref[...] = dh_ref[...] + factor * (c - x * (factor * factor * mean))


def project_grad(dq, dk, dv, n1, w, cosine, sine, x, gain, dh):
    rows, width = x.shape
    shape = jax.ShapeDtypeStruct
    return pl.pallas_call(
        qkv_grad_kernel,
        out_shape=(
            shape(w.shape, bf16),
            shape((rows, width), f32),
            shape((1, width), f32),
        ),
        scratch_shapes=[pltpu.VMEM((rows, w.shape[1]), bf16)],
        compiler_params=params(56),
        cost_estimate=cost(4 * rows * width * w.shape[1], 4 * w.size + 16 * x.size),
        name="project_grad",
    )(dq, dk, dv, n1, w, cosine, sine, x, gain, dh)


def visible_bias(first_ref, seg_q_ref, seg_k_ref, bias_ref):
    rows, keys = bias_ref.shape
    row = first_ref[0] + lax.broadcasted_iota(jnp.int32, (rows, keys), 0)
    col = lax.broadcasted_iota(jnp.int32, (rows, keys), 1)
    seen = (seg_q_ref[...] == seg_k_ref[...]) & (row >= col)
    bias_ref[...] = jnp.where(seen, 0.0, MASKED).astype(f32)


def attend_kernel(first_ref, q_ref, k_ref, v_ref, seg_q_ref, seg_k_ref, o_ref, bias_ref):
    @pl.when(pl.program_id(0) == 0)
    def _():
        visible_bias(first_ref, seg_q_ref, seg_k_ref, bias_ref)

    bias = bias_ref[...]
    for head in range(4):
        at, kv = head * HEAD_SIZE, head // 2 * HEAD_SIZE
        s = mm_nt(q_ref[:, at : at + HEAD_SIZE], k_ref[:, kv : kv + HEAD_SIZE]) * SCALE + bias
        e = jnp.exp(s - jnp.max(s, axis=1, keepdims=True))
        total = jnp.sum(e, axis=1, keepdims=True)
        o = mm(e.astype(bf16), v_ref[:, kv : kv + HEAD_SIZE]) / total
        o_ref[:, at : at + HEAD_SIZE] = o.astype(bf16)


def attend(first, q, k, v, seg_q, seg_k):
    rows, width = q.shape
    keys = k.shape[0]
    wide = pl.BlockSpec((rows, 256), lambda i, first: (0, i))
    narrow = pl.BlockSpec((keys, 128), lambda i, first: (0, i))
    return pl.pallas_call(
        attend_kernel,
        out_shape=jax.ShapeDtypeStruct((rows, width), bf16),
        grid_spec=pltpu.PrefetchScalarGridSpec(
            num_scalar_prefetch=1,
            grid=(width // 256,),
            in_specs=[
                wide,
                narrow,
                narrow,
                pl.BlockSpec((rows, 1), lambda i, first: (0, 0)),
                pl.BlockSpec((1, keys), lambda i, first: (0, 0)),
            ],
            out_specs=wide,
            scratch_shapes=[pltpu.VMEM((rows, keys), f32)],
        ),
        compiler_params=params(48),
        cost_estimate=cost(16 * rows * keys * width, 4 * q.size + 4 * k.size),
        name="attend",
    )(first, q, k, v, seg_q, seg_k)


def attend_grad_kernel(
    first_ref, q_ref, k_ref, v_ref, do_ref, seg_q_ref, seg_k_ref,
    dq_ref, dk_ref, dv_ref, bias_ref,
):
    @pl.when(pl.program_id(0) == 0)
    def _():
        visible_bias(first_ref, seg_q_ref, seg_k_ref, bias_ref)

    bias = bias_ref[...]
    for pair in range(2):
        kv = pair * HEAD_SIZE
        k, v = k_ref[:, kv : kv + HEAD_SIZE], v_ref[:, kv : kv + HEAD_SIZE]
        dk = dv = None
        for head in (2 * pair, 2 * pair + 1):
            at = head * HEAD_SIZE
            q, do = q_ref[:, at : at + HEAD_SIZE], do_ref[:, at : at + HEAD_SIZE]
            s = mm_nt(q, k) * SCALE + bias
            e = jnp.exp(s - jnp.max(s, axis=1, keepdims=True))
            p = e * (1.0 / jnp.sum(e, axis=1, keepdims=True))
            dp = mm_nt(do, v)
            delta = jnp.sum(p * dp, axis=1, keepdims=True)
            ds = (p * (dp - delta) * SCALE).astype(bf16)
            dq_ref[:, at : at + HEAD_SIZE] = mm(ds, k)
            dk_part, dv_part = mm_tn(ds, q), mm_tn(p.astype(bf16), do)
            dk = dk_part if dk is None else dk + dk_part
            dv = dv_part if dv is None else dv + dv_part
        dk_ref[:, kv : kv + HEAD_SIZE] = dk.astype(bf16)
        dv_ref[:, kv : kv + HEAD_SIZE] = dv.astype(bf16)


def attend_grad(first, q, k, v, do, seg_q, seg_k):
    rows, width = q.shape
    keys = k.shape[0]
    wide = pl.BlockSpec((rows, 256), lambda i, first: (0, i))
    narrow = pl.BlockSpec((keys, 128), lambda i, first: (0, i))
    shape = jax.ShapeDtypeStruct
    return pl.pallas_call(
        attend_grad_kernel,
        out_shape=(
            shape((rows, width), f32),
            shape(k.shape, bf16),
            shape(k.shape, bf16),
        ),
        grid_spec=pltpu.PrefetchScalarGridSpec(
            num_scalar_prefetch=1,
            grid=(width // 256,),
            in_specs=[
                wide,
                narrow,
                narrow,
                wide,
                pl.BlockSpec((rows, 1), lambda i, first: (0, 0)),
                pl.BlockSpec((1, keys), lambda i, first: (0, 0)),
            ],
            out_specs=[wide, narrow, narrow],
            scratch_shapes=[pltpu.VMEM((rows, keys), f32)],
        ),
        compiler_params=params(56),
        cost_estimate=cost(40 * rows * keys * width // 4, 8 * q.size + 8 * k.size),
        name="attend_grad",
    )(first, q, k, v, do, seg_q, seg_k)


def gather(value):
    return lax.all_gather(value, "group", axis=0, tiled=True)


def owner_sum(value):
    return lax.psum_scatter(value.astype(bf16), "group", scatter_dimension=0, tiled=True)


def rms_factor(values):
    return lax.rsqrt(jnp.mean(values * values, axis=-1, keepdims=True) + EPS)


LAG = 2
PHASES = 7
SEMS = 8
(CORE, X_A, IN_B, IN_A, HALF_B, MID_A, RUNG_B, OUT_A, BACK_B, SPREAD_A, OUT_B, JOIN, KINDS) = range(13)
(Y_SHARE, Y_DN2, Y_MOE, Y_GATE, Y_DKV, Y_WEIGHT, Y_N2, Y_KINDS) = (0, 1, 2, 3, 4, 12, 18, 20)


def engine_scratch(quarter, width):
    def vmem(*shape):
        return pltpu.VMEM((*shape, quarter, width), bf16)

    return [
        vmem(4, 4),
        vmem(4, 4),
        vmem(4),
        vmem(8, 2),
        vmem(8),
        vmem(4),
        vmem(4),
        vmem(4),
        vmem(LAG, 4),
        vmem(LAG),
        vmem(LAG, 2),
        vmem(LAG),
        vmem(LAG),
        vmem(LAG),
        vmem(LAG),
        pltpu.SemaphoreType.DMA((KINDS, SEMS)),
        pltpu.SemaphoreType.DMA((KINDS, SEMS)),
        pltpu.SemaphoreType.DMA((3, SEMS)),
    ]


class Place:
    def __init__(self):
        r = lax.axis_index("replica")
        self.core, self.x, z = lax.rem(r, 2), lax.rem(r // 2, 2), r // 4
        self.group = lax.axis_index("group")
        self.inner = (z == 1) | (z == 2)
        self.outer = jnp.logical_not(self.inner)
        self.late = z // 2
        self.odd = lax.rem(z, 2)
        up = (z == 0) | (z == 2)
        self.core_peer = {"replica": r + 1 - 2 * self.core}
        self.x_peer = {"replica": r + 2 - 4 * self.x}
        self.line_peer = {"replica": jnp.where(up, r + 4, r - 4)}
        self.mid_peer = {"replica": jnp.where(z == 1, r + 4, r - 4)}
        self.y_peer = {"group": 1 - self.group}

    def greet(self):
        barrier = pltpu.get_barrier_semaphore()

        def signal(peer):
            pl.semaphore_signal(
                barrier, inc=1, device_id=peer, device_id_type=pl.DeviceIdType.MESH
            )

        for peer in (self.core_peer, self.x_peer, self.line_peer, self.y_peer):
            signal(peer)

        @pl.when(self.inner)
        def _():
            signal(self.mid_peer)
            pl.semaphore_wait(barrier, 5)

        @pl.when(self.outer)
        def _():
            pl.semaphore_wait(barrier, 4)


def remote_copy(src, dst, send_sem, recv_sem, peer):
    return pltpu.make_async_remote_copy(
        src_ref=src, dst_ref=dst, send_sem=send_sem, recv_sem=recv_sem, device_id=peer,
        device_id_type=pl.DeviceIdType.MESH,
    )


def make_engine(place, count, split, split_of, stage, out, scratch, late_piece):
    (mine, got_core, got_x, got_end_b, got_end_a, got_mid_b, got_mid_a, got_rung,
     summed, a_x, b_end, a_end, b_mid, a_all, b_all, send_sem, recv_sem, copy_sem) = scratch
    core, x, inner, outer, late = place.core, place.x, place.inner, place.outer, place.late

    owned = split_of // 6

    def spot(k):
        e, sub, part = k // 6, lax.rem(k // 2, 3), lax.rem(k, 2)
        inner_spot = jnp.where(sub == 0, 4 * owned + 2 * e, 4 * e + 2 * sub - 2) + part
        return jnp.where(k < split_of, inner_spot, k)

    def remote(kind, k, src, dst, peer):
        slot = lax.rem(k, SEMS)
        return remote_copy(src, dst, send_sem.at[kind, slot], recv_sem.at[kind, slot], peer)

    def local(kind, k, src, dst):
        return pltpu.make_async_copy(src, dst, copy_sem.at[kind, lax.rem(k, SEMS)])

    def core_copy(k):
        return remote(
            CORE, k, stage.at[k, 1 - core], got_core.at[lax.rem(k, 4)], place.core_peer
        )

    def mine_copy(k):
        return local(2, k, stage.at[k, core], mine.at[lax.rem(k, 4)])

    def x_copy(k):
        return remote(
            X_A, k, summed.at[lax.rem(k, LAG), 1 - x], got_x.at[lax.rem(k, 4)], place.x_peer
        )

    def in_b_copy(k):
        return remote(
            IN_B, k, summed.at[lax.rem(k, LAG), pl.ds(2, 2)], got_end_b.at[lax.rem(k, 8)],
            place.line_peer,
        )

    def in_a_copy(k):
        return remote(
            IN_A, k, a_x.at[lax.rem(k, LAG)], got_end_a.at[lax.rem(k, 8)], place.line_peer
        )

    def half_b_copy(k):
        return remote(
            HALF_B, k, b_end.at[lax.rem(k, LAG), 1 - late], got_mid_b.at[lax.rem(k, 4)],
            place.mid_peer,
        )

    def mid_a_copy(k):
        return remote(
            MID_A, k, a_end.at[lax.rem(k, LAG)], got_mid_a.at[lax.rem(k, 4)], place.mid_peer
        )

    def rung_copy(k):
        return remote(
            RUNG_B, k, b_mid.at[lax.rem(k, LAG)], got_rung.at[lax.rem(k, 4)], place.x_peer
        )

    def out_a_copy(k):
        return remote(OUT_A, k, a_all.at[lax.rem(k, LAG)], out.at[spot(k), core, x], place.line_peer)

    def back_b_copy(k, quarter):
        return remote(
            BACK_B, k, b_all.at[lax.rem(k, LAG)], out.at[spot(k), core, quarter], place.mid_peer
        )

    def spread_copy(k, quarter):
        return remote(SPREAD_A, k, out.at[spot(k), core, x], out.at[spot(k), core, quarter], place.x_peer)

    def out_b_copy(k):
        part = out.at[spot(k), core, pl.ds(2, 2)]
        return remote(OUT_B, k, part, part, place.line_peer)

    def join_copy(k, half):
        return remote(JOIN, k, out.at[spot(k), core], out.at[spot(k), half], place.core_peer)

    def keep_a(k):
        return local(0, k, a_all.at[lax.rem(k, LAG)], out.at[spot(k), core, x])

    def keep_b(k):
        return local(1, k, b_all.at[lax.rem(k, LAG)], out.at[spot(k), core, 2 + late])

    def phase1(k):
        i = lax.rem(k, LAG)

        @pl.when(k < split)
        def _():
            mine_copy(k).wait()
            core_copy(k).wait()
            summed[i] = mine[lax.rem(k, 4)] + got_core[lax.rem(k, 4)]

        if count > split:

            @pl.when(k >= split)
            def _():
                copy, own, other = late_piece(k)
                copy.wait()
                summed[i] = own[...] + other[...]

        x_copy(k).start()

        @pl.when(outer)
        def _():
            in_b_copy(k).start()

    def phase2(k):
        i = lax.rem(k, LAG)
        x_copy(k).wait()
        a_x[i] = summed[i, x] + got_x[lax.rem(k, 4)]

        @pl.when(outer)
        def _():
            in_a_copy(k).start()
            in_b_copy(k).wait_send()

        @pl.when(inner)
        def _():
            in_b_copy(k).wait_recv()
            b_end[i] = summed[i, 2:4] + got_end_b[lax.rem(k, 8)]
            half_b_copy(k).start()

    def phase3(k):
        i = lax.rem(k, LAG)

        @pl.when(outer)
        def _():
            in_a_copy(k).wait_send()

        @pl.when(inner)
        def _():
            in_a_copy(k).wait_recv()
            a_end[i] = a_x[i] + got_end_a[lax.rem(k, 8)]
            mid_a_copy(k).start()
            half_b_copy(k).wait()
            b_mid[i] = b_end[i, late] + got_mid_b[lax.rem(k, 4)]
            rung_copy(k).start()

    def phase4(k):
        i = lax.rem(k, LAG)

        @pl.when(inner)
        def _():
            mid_a_copy(k).wait()
            a_all[i] = a_end[i] + got_mid_a[lax.rem(k, 4)]
            out_a_copy(k).start()
            keep_a(k).start()
            rung_copy(k).wait()
            b_all[i] = b_mid[i] + got_rung[lax.rem(k, 4)]
            back_b_copy(k, 2 + late).start()
            keep_b(k).start()

    def phase5(k):
        @pl.when(outer)
        def _():
            out_a_copy(k).wait_recv()

        @pl.when(inner)
        def _():
            keep_a(k).wait()
            out_a_copy(k).wait_send()

        spread_copy(k, x).start()

        @pl.when(inner)
        def _():
            keep_b(k).wait()
            back_b_copy(k, 2 + late).wait_send()
            back_b_copy(k, 3 - late).wait_recv()
            out_b_copy(k).start()

    def phase6(k):
        spread_copy(k, x).wait_send()
        spread_copy(k, 1 - x).wait_recv()

        @pl.when(outer)
        def _():
            out_b_copy(k).wait_recv()

        @pl.when(inner)
        def _():
            out_b_copy(k).wait_send()

        join_copy(k, core).start()

    def phase7(k):
        join_copy(k, core).wait_send()
        join_copy(k, 1 - core).wait_recv()

    phases = (phase1, phase2, phase3, phase4, phase5, phase6, phase7)

    def tick(t):
        for number in range(PHASES, 0, -1):
            k = t - LAG * number

            @pl.when((k >= 0) & (k < count))
            def _():
                phases[number - 1](k)

    def send(k):
        @pl.when(k < split)
        def _():
            core_copy(k).start()
            mine_copy(k).start()

    return tick, send


def make_small_sum(place, values, got, send_sem, recv_sem):
    def copy(i, peer):
        return remote_copy(values.at[i], got.at[i], send_sem.at[i], recv_sem.at[i], peer)

    peers = (
        place.core_peer, place.x_peer, place.y_peer, place.line_peer, place.mid_peer,
        place.line_peer,
    )

    def add(i):
        values[i + 1] = values[i] + got[i]

    def step(i):
        if 1 <= i <= 3:
            copy(i - 1, peers[i - 1]).wait()
            add(i - 1)
        if i <= 2:
            copy(i, peers[i]).start()
        if i == 3:

            @pl.when(place.outer)
            def _():
                copy(3, peers[3]).start()

        if i == 4:

            @pl.when(place.outer)
            def _():
                copy(3, peers[3]).wait_send()

            @pl.when(place.inner)
            def _():
                copy(3, peers[3]).wait_recv()
                add(3)
                copy(4, peers[4]).start()

        if i == 5:

            @pl.when(place.inner)
            def _():
                copy(4, peers[4]).wait()
                add(4)
                copy(5, peers[5]).start()

        if i == 6:

            @pl.when(place.inner)
            def _():
                copy(5, peers[5]).wait_send()

            @pl.when(place.outer)
            def _():
                copy(5, peers[5]).wait_recv()
                values[5] = got[5]

    return step


TILE = 256
WIDE = 1024


(F_SMALL, F_SEG, F_WQ, F_WK, F_WV, F_WO, F_GRAD) = range(7)
F_KV = F_GRAD + 2
F_KINDS = F_KV + 8
W_KV, W_Q, W_OUT = 0, 1, 2
SMALL_ROWS = 32


def two_heads(t):
    return jnp.concatenate([t[:, :HEAD_SIZE], t[:, HEAD_SIZE:]], axis=0)


def side_by_side(t):
    half = t.shape[0] // 2
    return jnp.concatenate([t[:half], t[half:]], axis=1)


def layer_kernel(
    x_hbm, wq_hbm, wk_hbm, wv_hbm, wo_hbm, g_hbm, w1_hbm, w2_hbm, small_own, seg_own, routes, inv_freq,
    y_ref, gx_ref, small_ref, out, stage, q_hbm, kv_hbm, n1_hbm, g_all, w_all,
    ao, h, n2, lse, cosine_ref, sine_ref, seg_k, seg_q, router, gains, small_in, seg,
    f_send, f_recv, l_send, l_recv, x_send, x_recv, c_send, c_recv, keep_sem,
    moe, dn2, share, share_t, gate, gate_t, y_send, y_got, got_kv, got_core_w, got_y_w, small, got_small,
    piece, piece_sem, w_sem, load_sem, ys_sem, yr_sem, cs_sem, cr_sem, ss_sem, sr_sem, *scratch,
):
    rows, width = x_hbm.shape
    tokens = 2 * rows
    owned, half = w2_hbm.shape[0], w2_hbm.shape[1]
    works = 3 * owned
    pieces = 2 * works
    count = pieces + 6
    place = Place()
    group, core = place.group, place.core
    here = pl.multiple_of(group * rows, rows)
    there = pl.multiple_of((1 - group) * rows, rows)

    def begin_load(*pairs):
        copies = [
            pltpu.make_async_copy(src, dst, load_sem.at[i]) for i, (src, dst) in enumerate(pairs)
        ]
        for copy in copies:
            copy.start()
        return copies

    def end_load(copies):
        for copy in copies:
            copy.wait()

    def y_copy(kind, src, dst):
        return remote_copy(src, dst, ys_sem.at[kind], yr_sem.at[kind], place.y_peer)

    def over_tiles(first, number, body, size=TILE):
        @pl.loop(0, number)
        def _(i):
            body(pl.ds(pl.multiple_of(first + i * size, size), size))

    def shifted(tile, by):
        return pl.ds(pl.multiple_of(tile.start + by, TILE), TILE)

    def after_core(gw):
        def late_piece(k):
            j, part = (k - pieces) // 2, lax.rem(k - pieces, 2)
            return (
                y_weight(gw, k - pieces), gw.at[j, group, part, core], got_y_w.at[j, part]
            )

        return late_piece

    def y_weight(gw, i):
        j, part = i // 2, i % 2
        return y_copy(Y_WEIGHT + i, gw.at[j, 1 - group, part, core], got_y_w.at[j, part])

    def fetch(w1, w2, e):
        slot = lax.rem(e, 2)
        return (
            pltpu.make_async_copy(w1_hbm.at[e], w1.at[slot], w_sem.at[0, slot]),
            pltpu.make_async_copy(w2_hbm.at[e], w2.at[slot], w_sem.at[1, slot]),
        )

    tick, send = make_engine(place, count, count, pieces, stage, out, scratch, None)

    def advance(t):
        tick(t)

        @pl.when(t < pieces)
        def _():
            send(t)

    def advance_all(first, number):
        @pl.loop(first, first + number)
        def _(t):
            advance(t)

    own_rows_here = pl.ds(here, rows)
    qkv_width = 2 * width
    kv_width = wk_hbm.shape[1]
    own_rows = wq_hbm.shape[0]
    part = own_rows // 4
    small_part = part // 2
    x = place.x
    w_here = pl.multiple_of(group * own_rows, own_rows)
    w_there = pl.multiple_of((1 - group) * own_rows, own_rows)
    quarter = pl.multiple_of((2 * core + x) * part, part)
    eighth = pl.multiple_of(quarter + place.odd * small_part, small_part)
    grad_copies = [
        remote_copy(
            g_hbm.at[pl.ds(i * rows // 2, rows // 2)],
            g_all.at[pl.ds(pl.multiple_of(here + i * rows // 2, rows // 2), rows // 2)],
            f_send.at[F_GRAD + i], f_recv.at[F_GRAD + i], place.y_peer,
        )
        for i in range(2)
    ]
    share_copy = y_copy(Y_SHARE, share_t.at[0], share_t.at[1])

    def n2_copy(i):
        tile = n2.at[pl.ds(pl.multiple_of(here + i * TILE, TILE), TILE)]
        return y_copy(Y_N2 + i, tile, tile)

    def keep(i, src, dst):
        return pltpu.make_async_copy(src, dst, keep_sem.at[i])

    def forward_part(w, kv, bias, n1_in, q, x_in):
        loads = [
            (x_hbm, x_in),
            (wk_hbm, w.at[pl.ds(w_here, own_rows), pl.ds(width, kv_width)]),
            (wv_hbm, w.at[pl.ds(w_here, own_rows), pl.ds(width + kv_width, kv_width)]),
            (wq_hbm, w.at[pl.ds(w_here, own_rows), pl.ds(0, width)]),
            (wo_hbm, w.at[pl.ds(w_here, own_rows), pl.ds(qkv_width, width)]),
        ]
        loads = [
            pltpu.make_async_copy(src, dst, load_sem.at[i]) for i, (src, dst) in enumerate(loads)
        ]
        for copy in loads:
            copy.start()
        place.greet()

        def f_copy(kind, src, dst):
            return remote_copy(src, dst, f_send.at[kind], f_recv.at[kind], place.y_peer)

        def weight_copy(kind, src, column, columns):
            return f_copy(
                kind, src.at[pl.ds(eighth, small_part)],
                w.at[pl.ds(w_here + eighth, small_part), pl.ds(column, columns)],
            )

        def line_copy(i, column, columns):
            block = w.at[pl.ds(w_there + eighth, small_part), pl.ds(column, columns)]
            return remote_copy(block, block, l_send.at[i], l_recv.at[i], place.line_peer)

        def x_copy(i, column, columns):
            block = w.at[pl.ds(w_there + quarter, part), pl.ds(column, columns)]
            return remote_copy(block, block, x_send.at[i], x_recv.at[i], place.x_peer)

        def core_copy(i, column, columns):
            first = pl.multiple_of(w_there + 2 * core * part, 2 * part)
            block = w.at[pl.ds(first, 2 * part), pl.ds(column, columns)]
            return remote_copy(block, block, c_send.at[i], c_recv.at[i], place.core_peer)

        small_copy = f_copy(F_SMALL, small_own, small_in.at[group])
        seg_copy = f_copy(F_SEG, seg_own, seg.at[group])
        kv_weights = [
            weight_copy(F_WK, wk_hbm, width, kv_width),
            weight_copy(F_WV, wv_hbm, width + kv_width, kv_width),
        ]
        wq_copy = weight_copy(F_WQ, wq_hbm, 0, width)
        wo_copy = weight_copy(F_WO, wo_hbm, qkv_width, width)
        for copy in (small_copy, seg_copy, *kv_weights):
            copy.start()
        small_in[group] = small_own[...]
        seg[group] = seg_own[...]

        small_copy.wait()
        seg_copy.wait()
        seg_row = jnp.concatenate([seg[0, 0:1, :], seg[1, 0:1, :]], axis=1)
        seg_k[...] = seg_row
        router[...] = jnp.concatenate([small_in[0, 0:EXPERTS, :], small_in[1, 0:EXPERTS, :]], axis=1)
        gains[...] = jnp.concatenate(
            [small_in[0, EXPERTS:, :], small_in[1, EXPERTS:, :]], axis=1
        ).astype(f32)[0 : gains.shape[0]]
        row = here + lax.broadcasted_iota(jnp.int32, bias.shape, 0)
        col = lax.broadcasted_iota(jnp.int32, bias.shape, 1)
        seg_column = seg_own[...].astype(f32).T[:, 0:1].astype(jnp.int32)
        seg_q[...] = seg_column
        same = seg_column == seg_row
        bias[...] = jnp.where(same & (row >= col), 0.0, MASKED).astype(f32)
        position = jnp.sum(jnp.where(same & (row > col), 1.0, 0.0), axis=1, keepdims=True)

        for copy in kv_weights:
            copy.wait()
        line_copy(W_KV, width, 2 * kv_width).start()
        wq_copy.start()

        expert = lax.broadcasted_iota(jnp.int32, (EXPERTS, rows), 0)
        named = jnp.zeros((EXPERTS, rows), f32)
        for k in range(routes.shape[0]):
            named = jnp.where(routes[k : k + 1, :] == expert, 1.0, named)
        share[own_rows_here, :] = named.T

        angle = position * inv_freq[...]
        lane = lax.broadcasted_iota(jnp.int32, angle.shape, 1)
        cosine_ref[...] = jnp.cos(angle)
        sine = jnp.sin(angle)
        sine_ref[...] = jnp.where(lax.rem(lane, HEAD_SIZE) < HEAD_SIZE // 2, -sine, sine)

        line_copy(W_KV, width, 2 * kv_width).wait()
        x_copy(W_KV, width, 2 * kv_width).start()
        wq_copy.wait()
        line_copy(W_Q, 0, width).start()
        wo_copy.start()
        for copy in loads:
            copy.wait()
        xs = x_in[...].astype(f32)
        factor = lax.rsqrt(jnp.mean(xs * xs, axis=-1, keepdims=True) + EPS)
        n1_in[...] = (xs * factor * gains[0:1, :]).astype(bf16)

        x_copy(W_KV, width, 2 * kv_width).wait()
        core_copy(W_KV, width, 2 * kv_width).start()
        line_copy(W_Q, 0, width).wait()
        x_copy(W_Q, 0, width).start()
        wo_copy.wait()
        line_copy(W_OUT, qkv_width, width).start()
        grad_copies[0].start()
        core_copy(W_KV, width, 2 * kv_width).wait()

        n1 = n1_in[...]
        keep(2, n1_in, n1_hbm).start()
        cosine, sine = cosine_ref[...], sine_ref[...]

        def turned(column):
            lin = mm(n1, w[:, column : column + 256])
            return [
                (t * cosine + swap_halves(t) * sine).astype(bf16)
                for t in (lin[:, :128], lin[:, 128:])
            ]

        own = own_rows_here

        def kv_copies(i):
            first = pl.multiple_of(i * 128, 128)
            return [
                f_copy(
                    F_KV + 2 * i + j,
                    kv.at[own, pl.ds(first + j * kv_width, 128)],
                    kv.at[own, pl.ds(first + j * kv_width, 128)],
                )
                for j in range(2)
            ]

        for i in range(2):
            at = 256 * i
            kv[own, at : at + 128], kv[own, at + 128 : at + 256] = turned(width + at)
            lin = mm(n1, w[:, width + kv_width + at : width + kv_width + at + 256])
            kv[own, kv_width + at : kv_width + at + 256] = lin.astype(bf16)

            @pl.when(group == 0)
            def _():
                for j in (2 * i, 2 * i + 1):
                    for copy in kv_copies(j):
                        copy.start()

        @pl.when(group == 0)
        def _():
            kv[rows:, :] = jnp.zeros((rows, kv.shape[1]), bf16)

        x_copy(W_Q, 0, width).wait()
        core_copy(W_Q, 0, width).start()
        line_copy(W_OUT, qkv_width, width).wait()
        x_copy(W_OUT, qkv_width, width).start()

        @pl.when(group == 1)
        def _():
            grad_copies[1].start()

        core_copy(W_Q, 0, width).wait()
        for at in range(0, width, 256):
            q[:, at : at + 128], q[:, at + 128 : at + 256] = turned(at)
        lse[...] = jnp.zeros_like(lse)

        @pl.loop(0, 4)
        def _(i):
            @pl.when(group == 1)
            def _():
                for copy in kv_copies(i):
                    copy.wait_recv()

            @pl.when(i == 2)
            def _():
                x_copy(W_OUT, qkv_width, width).wait()
                core_copy(W_OUT, qkv_width, width).start()

            at_k = pl.ds(pl.multiple_of(i * 128, 128), 128)
            at_v = pl.ds(pl.multiple_of(kv_width + i * 128, 128), 128)
            keys, values = kv[:, at_k], kv[:, at_v]
            for pair in range(2):
                lanes = slice(pair * HEAD_SIZE, (pair + 1) * HEAD_SIZE)
                key, value = keys[:, lanes], values[:, lanes]
                at_q = pl.ds(pl.multiple_of(i * 256 + pair * 128, 128), 128)

                @pl.loop(0, rows // TILE)
                def _(number):
                    tile = pl.ds(pl.multiple_of(number * TILE, TILE), TILE)
                    s = mm_nt(two_heads(q[tile, at_q]) * SCALE, key)
                    s = s.reshape(2, TILE, -1) + bias[tile, :][None]
                    peak = jnp.max(s, axis=2, keepdims=True)
                    e = jnp.exp(s - peak)
                    total = jnp.sum(e, axis=2, keepdims=True)
                    o = mm(e.astype(bf16).reshape(2 * TILE, -1), value)
                    o = o / total.reshape(2 * TILE, 1)
                    ao[tile, at_q] = side_by_side(o).astype(bf16)
                    log_sum = peak + jnp.log(total)
                    lane = lax.broadcasted_iota(jnp.int32, (TILE, QUERY_HEADS), 1)
                    head = 4 * i + 2 * pair
                    lse[tile, :] = jnp.where(
                        lane == head, log_sum[0], jnp.where(lane == head + 1, log_sum[1], lse[tile, :])
                    )

        @pl.when(group == 0)
        def _():
            for i in range(4):
                for copy in kv_copies(i):
                    copy.wait_send()
            grad_copies[1].start()

        keep(3, q, q_hbm).start()
        keep(1, kv, kv_hbm).start()
        core_copy(W_OUT, qkv_width, width).wait()
        keep(0, w, w_all).start()

        @pl.loop(0, rows // TILE)
        def _(number):
            tile = pl.ds(pl.multiple_of(number * TILE, TILE), TILE)
            own_tile = shifted(tile, here)
            hidden = x_in[tile, :].astype(f32) + mm(ao[tile, :], w[:, qkv_width:])
            h[tile, :] = hidden
            factor = lax.rsqrt(jnp.mean(hidden * hidden, axis=-1, keepdims=True) + EPS)
            normed = (hidden * factor * gains[1:2, :]).astype(bf16)
            n2[own_tile, :] = normed
            n2_copy(number).start()
            logits = mm_nt(normed, router[...])
            chosen = share[own_tile, :] > 0.0
            picked = jnp.where(chosen, logits, MASKED)
            e = jnp.exp(picked - jnp.max(picked, axis=1, keepdims=True))
            e = jnp.where(chosen, e, 0.0)
            share[own_tile, :] = e / jnp.sum(e, axis=1, keepdims=True)

        share_t[0] = share[own_rows_here, :].T
        share_copy.start()
        for i, (src, dst) in enumerate(((w, w_all), (kv, kv_hbm), (n1_in, n1_hbm), (q, q_hbm))):
            keep(i, src, dst).wait()

    pl.run_scoped(
        forward_part,
        pltpu.VMEM((width, 3 * width), bf16),
        pltpu.VMEM((tokens, width), bf16),
        pltpu.VMEM((rows, tokens), f32),
        *[pltpu.VMEM((rows, width), bf16)] * 3,
    )

    dn2_copy = y_copy(Y_DN2, y_send.at[0], y_got.at[0])

    def leave(i, terms, tile):
        y_send[i, shifted(tile, -there), :] = terms[tile, :].astype(bf16)

    def expert_part(n2_turned, g, act, d_ye, d_gu, w1, w2):
        for copy in fetch(w1, w2, 0):
            copy.start()
        loads = begin_load((g_hbm, g.at[own_rows_here]))
        gate[...] = jnp.zeros_like(gate)

        def prepare(tile):
            n2_turned[:, tile] = n2[tile, :].T
            moe[tile, :] = jnp.zeros((TILE, width), f32)
            dn2[tile, :] = jnp.zeros((TILE, width), f32)

        over_tiles(here, rows // TILE, prepare)
        for i in range(rows // TILE):
            n2_copy(i).wait()
        share_copy.wait()
        share[pl.ds(there, rows), :] = share_t[1].T
        over_tiles(there, rows // TILE, prepare)
        for copy in grad_copies:
            copy.wait()
        end_load(loads)
        end_load(begin_load((g_all.at[pl.ds(there, rows)], g.at[pl.ds(there, rows)])))

        def pick(table, e):
            lane = lax.broadcasted_iota(jnp.int32, table.shape, 1)
            return jnp.sum(
                jnp.where(lane == group * owned + e, table, 0.0), axis=1, keepdims=True
            )

        def keep_piece(k):
            slot = lax.rem(k, 2)
            return pltpu.make_async_copy(piece.at[slot], stage.at[pl.ds(2 * k, 2)], piece_sem.at[slot])

        def work(k):
            e, sub = k // 3, lax.rem(k, 3)
            slot = lax.rem(e, 2)

            @pl.when(k == 2)
            def _():
                keep_piece(1).wait()

            @pl.when(k >= 4)
            def _():
                keep_piece(k - 2).wait()

            @pl.when(sub == 0)
            def _():
                for copy in fetch(w1, w2, e):
                    copy.wait()

                @pl.when(e + 1 < owned)
                def _():
                    for copy in fetch(w1, w2, e + 1):
                        copy.start()

                def body(tile):
                    gu = mm(n2[tile, :], w1[slot])
                    z, w = gu[:, :half], gu[:, half:]
                    sg = jax.nn.sigmoid(z)
                    silu = z * sg
                    act[tile, :] = (silu * w).astype(bf16)
                    dy = (pick(share[tile, :], e) * g[tile, :].astype(f32)).astype(bf16)
                    d_ye[tile, :] = dy
                    d_act = mm_nt(dy, w2[slot])
                    d_gu[tile, :half] = (d_act * w * sg * (1.0 + z * (1.0 - sg))).astype(bf16)
                    d_gu[tile, half:] = (d_act * silu).astype(bf16)

                over_tiles(0, tokens // WIDE, body, WIDE)
                for part in range(2):
                    columns = slice(part * half // 2, (part + 1) * half // 2)
                    grad = mm_tn(act[:, columns], d_ye[...])
                    piece[lax.rem(k, 2), part] = grad.astype(bf16).reshape(piece.shape[2:])

            @pl.when(sub == 2)
            def _():
                @pl.when(k == works - 1)
                def _():
                    over_tiles(there, rows // TILE, functools.partial(leave, 0, dn2))
                    dn2_copy.start()

                def body(tile):
                    ye = mm(act[tile, :], w2[slot]).astype(bf16).astype(f32)
                    value = jnp.sum(g[tile, :].astype(f32) * ye, axis=1, keepdims=True)
                    lane = lax.broadcasted_iota(jnp.int32, (WIDE, gate.shape[1]), 1)
                    gate[tile, :] = jnp.where(lane == group * owned + e, value, gate[tile, :])
                    moe[tile, :] += pick(share[tile, :], e) * ye

                over_tiles(0, tokens // WIDE, body, WIDE)

            @pl.when(sub == 1)
            def _():
                def body(tile):
                    dn2[tile, :] += mm_nt(d_gu[tile, :], w1[slot]).astype(bf16).astype(f32)

                over_tiles(0, tokens // WIDE, body, WIDE)

            @pl.when(sub > 0)
            def _():
                @pl.loop(0, 2)
                def _(part):
                    first = pl.multiple_of((2 * (sub - 1) + part) * (half // 2), half // 2)
                    grad = mm(n2_turned[pl.ds(first, half // 2), :], d_gu[...])
                    piece[lax.rem(k, 2), part] = grad.astype(bf16).reshape(piece.shape[2:])

            keep_piece(k).start()

            @pl.when(k == 0)
            def _():
                keep_piece(0).wait()

        @pl.loop(0, works)
        def _(k):
            work(k)
            pl.loop(6 * k // 5, 6 * (k + 1) // 5)(advance)

        keep_piece(works - 2).wait()
        keep_piece(works - 1).wait()

        over_tiles(there, rows // TILE, functools.partial(leave, 1, moe))

    wide = (tokens, width)
    pl.run_scoped(
        expert_part,
        pltpu.VMEM((width, tokens), bf16),
        pltpu.VMEM(wide, bf16),
        pltpu.VMEM((tokens, half), bf16),
        pltpu.VMEM(wide, bf16),
        pltpu.VMEM((tokens, 2 * half), bf16),
        pltpu.VMEM((2, width, 2 * half), bf16),
        pltpu.VMEM((2, half, width), bf16),
    )
    t = 6 * works // 5
    gate_copy = y_copy(Y_GATE, gate_t.at[0], gate_t.at[1])
    gate_t[0] = gate[pl.ds(there, rows), :].T
    moe_copy = y_copy(Y_MOE, y_send.at[1], y_got.at[1])
    gate_copy.start()
    t += 5

    def attention_part(gw, d_o, dkv):
        tail = gw.shape[3:]

        def store_rows(j, i, grad):
            gw[j, i // 2, i % 2] = grad.astype(bf16).reshape(tail)

        def core_weight(j):
            return remote_copy(
                gw.at[j, :, :, 1 - core], got_core_w.at[j], cs_sem.at[j], cr_sem.at[j],
                place.core_peer,
            )

        def to_owner(j):
            core_weight(j).wait()
            for member in range(2):
                for part in range(2):
                    gw[j, member, part, core] += got_core_w[j, member, part]
            for part in range(2):
                y_weight(gw, 2 * j + part).start()

        def kv_copies(i):
            first = pl.multiple_of(i * 128, 128)
            return [
                y_copy(
                    Y_DKV + 2 * i + j,
                    dkv.at[pl.ds(0, rows), pl.ds(first + j * (width // 2), 128)],
                    got_kv.at[:, pl.ds(first + j * (width // 2), 128)],
                )
                for j in range(2)
            ]

        def middle(g, wo, d_y):
            loads = begin_load((g_hbm, g), (w_all.at[:, pl.ds(2 * width, width)], wo))
            advance_all(t - 5, 5)
            end_load(loads)
            dn2_copy.wait()
            gate_copy.wait()
            gate[own_rows_here, :] += gate_t[1].T
            moe_copy.start()
            small[0] = jnp.zeros(small.shape[1:], f32)

            def body(tile):
                own = shifted(tile, here)
                s = share[own, :]
                dg = gate[own, :]
                d_logits = (s * (dg - jnp.sum(s * dg, axis=1, keepdims=True))).astype(bf16)
                d_n2 = dn2[own, :] + y_got[0, tile, :].astype(f32) + mm(d_logits, router[...])
                hidden = h[tile, :]
                factor = lax.rsqrt(jnp.mean(hidden * hidden, axis=-1, keepdims=True) + EPS)
                small[0, 0:EXPERTS, :] += mm_tn(d_logits, n2[own, :])
                small[0, EXPERTS : EXPERTS + 1, :] += jnp.sum(
                    hidden * factor * d_n2, axis=0, keepdims=True
                )
                c = d_n2 * gains[1:2, :]
                mean = jnp.mean(c * hidden, axis=-1, keepdims=True)
                d_h = g[tile, :].astype(f32) + factor * (c - hidden * (factor * factor * mean))
                dn2[shifted(tile, there), :] = d_h
                d_y[tile, :] = d_h.astype(bf16)
                d_o[tile, :] = mm_nt(d_h.astype(bf16), wo[...]).astype(bf16)
                moe[own, :] += hidden

            @pl.loop(0, rows // TILE)
            def _(i):
                body(pl.ds(pl.multiple_of(i * TILE, TILE), TILE))
                advance(t + i)

            for i in range(4):
                columns = slice(i * width // 4, (i + 1) * width // 4)
                store_rows(0, i, mm_tn(ao[:, columns], d_y[...]))
            core_weight(0).start()

        pl.run_scoped(
            middle,
            pltpu.VMEM((rows, width), bf16),
            pltpu.VMEM((width, width), bf16),
            pltpu.VMEM((rows, width), bf16),
        )
        advance(t + 2)
        to_owner(0)

        def heads(q, kv, bias):
            loads = begin_load((q_hbm, q), (kv_hbm, kv))
            row = here + lax.broadcasted_iota(jnp.int32, bias.shape, 0)
            col = lax.broadcasted_iota(jnp.int32, bias.shape, 1)
            seen = (seg_q[...] == seg_k[...]) & (row >= col)
            bias[...] = jnp.where(seen, 0.0, MASKED).astype(f32)
            end_load(loads)

            @pl.loop(0, 4)
            def _(i):
                at_k = pl.ds(pl.multiple_of(i * 128, 128), 128)
                at_v = pl.ds(pl.multiple_of(width // 2 + i * 128, 128), 128)
                keys, values = kv[:, at_k], kv[:, at_v]
                dks, dvs = [], []
                for pair in range(2):
                    lanes = slice(pair * HEAD_SIZE, (pair + 1) * HEAD_SIZE)
                    key, value = keys[:, lanes], values[:, lanes]
                    at_q = pl.ds(pl.multiple_of(i * 256 + pair * 128, 128), 128)

                    def body(part, sums):
                        dk, dv = sums
                        tile = pl.ds(pl.multiple_of(part * TILE, TILE), TILE)
                        qs = two_heads(q[tile, at_q]) * SCALE
                        dos = two_heads(d_o[tile, at_q])
                        os = two_heads(ao[tile, at_q])
                        delta = jnp.sum(
                            dos.astype(f32) * os.astype(f32), axis=1, keepdims=True
                        )
                        lane = lax.broadcasted_iota(jnp.int32, (TILE, QUERY_HEADS), 1)
                        peaks = jnp.concatenate(
                            [
                                jnp.sum(
                                    jnp.where(lane == 4 * i + 2 * pair + head, lse[tile, :], 0.0),
                                    axis=1, keepdims=True,
                                )
                                for head in range(2)
                            ],
                            axis=0,
                        )
                        s = mm_nt(qs, key) - peaks
                        s = s.reshape(2, TILE, -1) + bias[tile, :][None]
                        p = jnp.exp(s).reshape(2 * TILE, -1)
                        dp = mm_nt(dos, value)
                        ds = (p * (dp - delta)).astype(bf16)
                        dq = mm(ds, key) * SCALE
                        moe[shifted(tile, there), at_q] = side_by_side(dq)
                        return dk + mm_tn(qs, ds), dv + mm_tn(dos, p.astype(bf16))

                    zero = jnp.zeros((HEAD_SIZE, kv.shape[0]), f32)
                    dk, dv = lax.fori_loop(0, rows // TILE, body, (zero, zero))
                    dks.append(dk)
                    dvs.append(dv)
                dkv[:, at_k] = jnp.concatenate(dks, axis=0).T.astype(bf16)
                dkv[:, at_v] = jnp.concatenate(dvs, axis=0).T.astype(bf16)

                @pl.when(group == 1)
                def _():
                    for copy in kv_copies(i):
                        copy.start()

                advance(t + 3 + 2 * i)
                advance(t + 4 + 2 * i)

        pl.run_scoped(
            heads,
            pltpu.VMEM((rows, width), bf16),
            pltpu.VMEM((tokens, width), bf16),
            pltpu.VMEM((rows, tokens), f32),
        )

        def projections(n1, wqkv, lin, x_in):
            loads = begin_load(
                (n1_hbm, n1), (x_hbm, x_in), (w_all.at[:, pl.ds(0, 2 * width)], wqkv)
            )
            own = pl.ds(here, rows)

            def turn_back(to, source, where, at):
                value = source[where, at : at + 128].astype(f32)
                turned = value * cosine_ref[...] - swap_halves(value) * sine_ref[...]
                lin[:, to : to + 128] = turned.astype(bf16)

            def weight_grad(j, first):
                for i in range(4):
                    columns = slice(i * width // 4, (i + 1) * width // 4)
                    store_rows(j, i, mm_tn(n1[:, columns], lin[:, first : first + width]))
                core_weight(j).start()

            for j in range(0, width, 128):
                turn_back(j, moe, pl.ds(there, rows), j)
            end_load(loads[:1])
            weight_grad(1, 0)
            advance(t + 11)
            to_owner(1)
            advance(t + 12)

            @pl.when(group == 1)
            def _():
                for i in range(4):
                    for copy in kv_copies(i):
                        copy.wait_send()

            @pl.when(group == 0)
            def _():
                for i in range(4):
                    for copy in kv_copies(i):
                        copy.wait_recv()
                total = dkv[0:rows, :].astype(f32) + got_kv[...].astype(f32)
                dkv[0:rows, :] = total.astype(bf16)

            for j in range(0, width // 2, 128):
                turn_back(width + j, dkv, own, j)
            lin[:, 3 * width // 2 :] = dkv[own, width // 2 :]
            weight_grad(2, width)
            advance(t + 13)
            to_owner(2)
            advance(t + 14)

            def body(tile):
                dn1 = mm_nt(lin[tile, :], wqkv[...])
                xs = x_in[tile, :].astype(f32)
                factor = lax.rsqrt(jnp.mean(xs * xs, axis=-1, keepdims=True) + EPS)
                small[0, EXPERTS + 1 : EXPERTS + 2, :] += jnp.sum(
                    xs * factor * dn1, axis=0, keepdims=True
                )
                c = dn1 * gains[0:1, :]
                mean = jnp.mean(c * xs, axis=-1, keepdims=True)
                gx_ref[tile, :] = dn2[shifted(tile, there), :] + factor * (
                    c - xs * (factor * factor * mean)
                )
                total = moe[shifted(tile, here), :] + y_got[1, tile, :].astype(f32)
                y_ref[tile, :] = total.astype(bf16)

            end_load(loads[1:])
            moe_copy.wait()
            last_tick, last_send = make_engine(
                place, count, pieces, pieces, stage, out, scratch, after_core(gw)
            )
            small_step = make_small_sum(place, small, got_small, ss_sem, sr_sem)
            first_last = t + 15
            tiles = rows // TILE

            @pl.loop(first_last, count + PHASES * LAG)
            def _(now):
                last_tick(now)

                @pl.when(now < pieces)
                def _():
                    last_send(now)

                @pl.when(now < first_last + tiles)
                def _():
                    body(pl.ds(pl.multiple_of((now - first_last) * TILE, TILE), TILE))

                for i in range(7):

                    @pl.when(now == first_last + tiles + 2 * i)
                    def _():
                        small_step(i)

        pl.run_scoped(
            projections,
            pltpu.VMEM((rows, width), bf16),
            pltpu.VMEM((width, 2 * width), bf16),
            pltpu.VMEM((rows, 2 * width), bf16),
            pltpu.VMEM((rows, width), bf16),
        )

    pl.run_scoped(
        attention_part,
        pltpu.VMEM((3, 2, 2, *piece.shape[2:]), bf16),
        pltpu.VMEM((rows, width), bf16),
        pltpu.VMEM((tokens, width), bf16),
    )
    small_ref[...] = small[5]


DEPTH = 6


def finish_kernel(
    owned, pieces, small_ref, g_in, g_out, g_q, g_k, g_v, g_wo, router_ref, gain_ref,
    narrow, wide, in_sem, out_sem, last_sem,
):
    count = pieces.shape[0]
    whole = count - 2
    kv_width = g_k.shape[-1]

    def fetch(k):
        slot = lax.rem(k, DEPTH)
        return pltpu.make_async_copy(pieces.at[k], narrow.at[slot], in_sem.at[slot])

    def store(k, target):
        slot = lax.rem(k, DEPTH)
        return pltpu.make_async_copy(wide.at[slot], target, out_sem.at[slot])

    def convert(k):
        slot = lax.rem(k, DEPTH)
        fetch(k).wait()

        @pl.when(k >= DEPTH)
        def _():
            store(k, g_in.at[0]).wait()

        wide[slot] = narrow[slot].astype(f32)

        @pl.when(k + DEPTH < count)
        def _():
            fetch(k + DEPTH).start()

    for k in range(DEPTH):
        fetch(k).start()
    columns = router_ref.shape[1]
    first = pl.multiple_of(lax.axis_index("group") * columns, columns)
    router_ref[...] = small_ref[0:EXPERTS, pl.ds(first, columns)]
    gain_ref[...] = small_ref[EXPERTS:, pl.ds(first, columns)]

    @pl.loop(0, whole)
    def _(k):
        convert(k)
        base = 0
        for target in (g_in, g_out, g_wo, g_q):
            number = target.shape[0]

            @pl.when((k >= base) & (k < base + number))
            def _():
                store(k, target.at[k - base]).start()

            base += number

    last = []
    for i in range(2):
        k = whole + i
        convert(k)
        for j, target in enumerate((g_k, g_v)):
            copy = pltpu.make_async_copy(
                wide.at[k % DEPTH, :, pl.ds(j * kv_width, kv_width)], target.at[i],
                last_sem.at[2 * i + j],
            )
            copy.start()
            last.append(copy)
    for copy in last:
        copy.wait()
    for k in range(count - DEPTH, whole):
        store(k, g_in.at[0]).wait()


def finish(pieces, small, owned, kv_width):
    count, rows, width = pieces.shape
    shape = jax.ShapeDtypeStruct
    vmem = pl.BlockSpec(memory_space=pltpu.VMEM)
    hbm = pl.BlockSpec(memory_space=pl.ANY)
    dma = pltpu.SemaphoreType.DMA
    return pl.pallas_call(
        functools.partial(finish_kernel, owned),
        out_shape=(
            shape((4 * owned, rows, width), f32),
            shape((2 * owned, rows, width), f32),
            shape((2, rows, width), f32),
            shape((2, rows, kv_width), f32),
            shape((2, rows, kv_width), f32),
            shape((2, rows, width), f32),
            shape((EXPERTS, width // 2), f32),
            shape((8, width // 2), f32),
        ),
        in_specs=[hbm, vmem],
        out_specs=[hbm] * 6 + [vmem] * 2,
        scratch_shapes=[
            pltpu.VMEM((DEPTH, rows, width), bf16),
            pltpu.VMEM((DEPTH, rows, width), f32),
            dma((DEPTH,)),
            dma((DEPTH,)),
            dma((4,)),
        ],
        compiler_params=params(48),
        cost_estimate=cost(0, 6 * pieces.size),
        name="finish",
    )(pieces, small)


def layer(x, document_numbers, routes, gains, w_router, wq, wk, wv, wo, grad, w_in, w_out):
    rows, width = x.shape
    own_rows = wq.shape[0]
    small = jnp.concatenate(
        [w_router.T, *[gain[None] for gain in gains],
         jnp.zeros((SMALL_ROWS - EXPERTS - 2, own_rows), bf16)], axis=0,
    )
    exponent = (np.arange(128) % (HEAD_SIZE // 2)) * (-2.0 / HEAD_SIZE)
    inv_freq = jnp.asarray(np.power(10000.0, exponent)[None], f32)
    owned, half = w_out.shape[:2]
    tokens, quarter = 2 * rows, half // 16
    pieces = 6 * owned
    shape = jax.ShapeDtypeStruct
    vmem = pl.BlockSpec(memory_space=pltpu.VMEM)
    hbm = pl.BlockSpec(memory_space=pl.ANY)
    dma = pltpu.SemaphoreType.DMA
    small_rows = EXPERTS + 8
    return pl.pallas_call(
        layer_kernel,
        out_shape=(
            shape((rows, width), bf16),
            shape((rows, width), f32),
            shape((small_rows, width), f32),
            shape((pieces + 6, 2, 4, quarter, width), bf16),
            shape((pieces, 2, 4, quarter, width), bf16),
            shape((rows, width), bf16),
            shape((tokens, width), bf16),
            shape((rows, width), bf16),
            shape((tokens, width), bf16),
            shape((width, 3 * width), bf16),
        ),
        in_specs=[hbm] * 8 + [vmem] * 4,
        out_specs=[vmem, vmem, vmem] + [hbm] * 7,
        scratch_shapes=[
            pltpu.VMEM((rows, width), bf16),
            pltpu.VMEM((rows, width), f32),
            pltpu.VMEM((tokens, width), bf16),
            pltpu.VMEM((rows, QUERY_HEADS), f32),
            pltpu.VMEM((rows, 128), f32),
            pltpu.VMEM((rows, 128), f32),
            pltpu.VMEM((1, tokens), jnp.int32),
            pltpu.VMEM((rows, 1), jnp.int32),
            pltpu.VMEM((EXPERTS, width), bf16),
            pltpu.VMEM((8, width), f32),
            pltpu.VMEM((2, SMALL_ROWS, own_rows), bf16),
            pltpu.VMEM((2, 8, rows), jnp.int32),
            dma((F_KINDS,)),
            dma((F_KINDS,)),
            *[dma((3,))] * 6,
            dma((4,)),
            pltpu.VMEM((tokens, width), f32),
            pltpu.VMEM((tokens, width), f32),
            pltpu.VMEM((tokens, EXPERTS), f32),
            pltpu.VMEM((2, EXPERTS, rows), f32),
            pltpu.VMEM((tokens, EXPERTS), f32),
            pltpu.VMEM((2, EXPERTS, rows), f32),
            pltpu.VMEM((2, rows, width), bf16),
            pltpu.VMEM((2, rows, width), bf16),
            pltpu.VMEM((rows, width), bf16),
            pltpu.VMEM((3, 2, 2, 4, quarter, width), bf16),
            pltpu.VMEM((3, 2, 4, quarter, width), bf16),
            pltpu.VMEM((6, small_rows, width), f32),
            pltpu.VMEM((6, small_rows, width), f32),
            pltpu.VMEM((2, 2, 2, 4, quarter, width), bf16),
            dma((2,)),
            dma((2, 2)),
            dma((5,)),
            dma((Y_KINDS,)),
            dma((Y_KINDS,)),
            dma((3,)),
            dma((3,)),
            dma((6,)),
            dma((6,)),
            *engine_scratch(quarter, width),
        ],
        compiler_params=pltpu.CompilerParams(
            collective_id=1, has_side_effects=True, vmem_limit_bytes=63 * MIB
        ),
        cost_estimate=cost(18 * tokens * width * half * owned, 6 * w_in.size),
        name="layer",
    )(
        x, wq, wk, wv, wo, grad, w_in, w_out, small,
        jnp.broadcast_to(document_numbers[None], (8, rows)), routes.T, inv_freq,
    )


def expert_pass(n2, grad, share, w_in, w_out):
    half = w_out.shape[0]
    gu = mm(n2, w_in)
    z, w = gu[:, :half], gu[:, half:]
    sg = jax.nn.sigmoid(z)
    act = (z * sg * w).astype(bf16)
    ye = mm(act, w_out).astype(bf16).astype(f32)
    d_gate = jnp.sum(grad * ye, axis=1)
    d_ye = (share * grad).astype(bf16)
    g_out = mm_tn(act, d_ye).astype(bf16)
    d_act = mm_nt(d_ye, w_out)
    d_gu = jnp.concatenate(
        [d_act * w * sg * (1.0 + z * (1.0 - sg)), d_act * z * sg], axis=1
    ).astype(bf16)
    g_in = mm_tn(n2, d_gu).astype(bf16)
    d_xe = mm_nt(d_gu, w_in).astype(bf16).astype(f32)
    return share * ye, d_gate, g_in, g_out, d_xe


def all_experts(n2, grad, share, w_in, w_out):
    moe = jnp.zeros(n2.shape, f32)
    d_n2 = jnp.zeros_like(moe)
    d_gate, g_in, g_out = [], [], []
    for i in range(w_in.shape[0]):
        y, dg, gi, go, dx = expert_pass(
            n2, grad.astype(f32), share[:, i : i + 1], w_in[i], w_out[i]
        )
        moe, d_n2 = moe + y, d_n2 + dx
        d_gate.append(dg)
        g_in.append(gi)
        g_out.append(go)
    g_in, g_out = lax.psum((jnp.stack(g_in), jnp.stack(g_out)), "replica")
    return moe, d_n2, jnp.stack(d_gate, 1), g_in.astype(f32), g_out.astype(f32)


def on_device(
    layer_input, document_numbers, routes, norm_attn, w_query, key_weight, value_weight, w_out,
    norm_moe, w_router, expert_in, expert_out, cotangent,
):
    rows, width = layer_input.shape
    group = lax.axis_index("group")
    first = group * rows
    owned = expert_in.shape[0]
    kv_width = KEY_VALUE_HEADS * HEAD_SIZE

    q_width = QUERY_HEADS * HEAD_SIZE
    if lax.axis_size("replica") == 16 and lax.axis_size("group") == 2:
        layer_output, grad_input, small_sum, sums, *_ = layer(
            layer_input, document_numbers, routes, (norm_attn, norm_moe), w_router, w_query,
            key_weight, value_weight, w_out, cotangent, expert_in, expert_out,
        )
        g_in, g_out, g_q, g_k, g_v, g_wo, g_router, g_gains = finish(
            sums.reshape(sums.shape[0], -1, width), small_sum, owned, kv_width
        )
        return (
            layer_output,
            grad_input,
            g_gains[1],
            g_q.reshape(w_query.shape),
            g_k.reshape(key_weight.shape),
            g_v.reshape(value_weight.shape),
            g_wo.reshape(w_out.shape),
            g_gains[0],
            g_router.T,
            g_in.reshape(expert_in.shape),
            g_out.reshape(expert_out.shape),
        )

    seg_all = gather(document_numbers)
    position = lax.dynamic_slice_in_dim(doc_positions(seg_all), first, rows, 0)
    cosine, sine = turn_tables(position)
    small = gather(jnp.concatenate([norm_attn[:, None], norm_moe[:, None], w_router], axis=1))
    gain_attn = small[:, 0].astype(f32)[None, :]
    gain_moe = small[:, 1].astype(f32)[None, :]
    router = small[:, 2:]
    w_qkv = gather(jnp.concatenate([w_query, key_weight, value_weight], axis=1))
    wo = gather(w_out)
    grad_all = gather(cotangent)

    n1, q, k, v = project(layer_input, gain_attn, w_qkv, cosine, sine)
    kv_all = gather(jnp.concatenate([k, v], axis=1))
    k_all, v_all = kv_all[:, :kv_width], kv_all[:, kv_width:]
    first_row = jnp.full((1,), first, jnp.int32)
    seg_q, seg_k = document_numbers[:, None], seg_all[None, :]
    ao = attend(first_row, q, k_all, v_all, seg_q, seg_k)

    x = layer_input.astype(f32)
    h = x + mm(ao, wo)
    r2 = rms_factor(h)
    n2 = (h * r2 * gain_moe).astype(bf16)
    logits = mm(n2, router)
    chosen = jnp.any(routes[:, :, None] == jnp.arange(EXPERTS, dtype=jnp.int32), axis=1)
    picked = jnp.where(chosen, logits, MASKED)
    e = jnp.where(chosen, jnp.exp(picked - jnp.max(picked, axis=1, keepdims=True)), 0.0)
    share = e / jnp.sum(e, axis=1, keepdims=True)

    n2_all = gather(n2)
    share_all = lax.dynamic_slice_in_dim(gather(share), group * owned, owned, 1)
    moe, d_n2_all, d_gate, g_in, g_out = all_experts(
        n2_all, grad_all, share_all, expert_in, expert_out
    )
    d_gate = lax.dynamic_update_slice_in_dim(
        jnp.zeros((n2_all.shape[0], EXPERTS), f32), d_gate, group * owned, 1
    )
    d_gate = lax.psum_scatter(d_gate, "group", scatter_dimension=0, tiled=True)
    layer_output = (h + owner_sum(moe).astype(f32)).astype(bf16)

    d_logits = (share * (d_gate - jnp.sum(share * d_gate, axis=1, keepdims=True))).astype(bf16)
    g_router = mm_tn(n2, d_logits)
    d_n2 = owner_sum(d_n2_all).astype(f32) + mm_nt(d_logits, router)
    g_gain_moe = jnp.sum(h * r2 * d_n2, axis=0)
    c = d_n2 * gain_moe
    d_h = cotangent.astype(f32) + r2 * (
        c - h * r2 * r2 * jnp.mean(c * h, axis=-1, keepdims=True)
    )
    d_y = d_h.astype(bf16)
    g_wo = mm_tn(ao, d_y).astype(bf16)
    d_o = mm_nt(d_y, wo).astype(bf16)

    dq, dk_all, dv_all = attend_grad(first_row, q, k_all, v_all, d_o, seg_q, seg_k)
    dkv = owner_sum(jnp.concatenate([dk_all, dv_all], axis=1))
    g_qkv, grad_input, g_gain_attn = project_grad(
        dq, dkv[:, :kv_width], dkv[:, kv_width:], n1, w_qkv, cosine, sine, layer_input,
        gain_attn, d_h,
    )

    g_attn = owner_sum(jnp.concatenate([g_qkv, g_wo], axis=1))
    g_small = owner_sum(
        jnp.concatenate([g_gain_attn.reshape(-1, 1), g_gain_moe[:, None], g_router], axis=1)
    )
    g_attn, g_small = (t.astype(f32) for t in lax.psum((g_attn, g_small), "replica"))
    return (
        layer_output,
        grad_input,
        g_small[:, 0],
        g_attn[:, :q_width],
        g_attn[:, q_width : q_width + kv_width],
        g_attn[:, q_width + kv_width : q_width + 2 * kv_width],
        g_attn[:, q_width + 2 * kv_width :],
        g_small[:, 1],
        g_small[:, 2:],
        g_in,
        g_out,
    )


def solution(mesh):
    tokens, weights = P(("replica", "group"), None), P("group", None)
    in_specs = (
        tokens, P(("replica", "group")), tokens, P("group"), weights, weights, weights, weights,
        P("group"), weights, P("group", None, None), P("group", None, None), tokens,
    )
    out_specs = (
        tokens, tokens, P("group"), weights, weights, weights, weights, P("group"), weights,
        P("group", None, None), P("group", None, None),
    )
    return jax.shard_map(
        on_device, mesh=mesh, in_specs=in_specs, out_specs=out_specs, check_vma=False
    )
```

```python
import functools

import jax
import jax.numpy as jnp
import numpy as np
from jax import lax
from jax.experimental import pallas as pl
from jax.experimental.pallas import tpu as pltpu
from jax.sharding import PartitionSpec as P

QUERY_HEADS = 16
KEY_VALUE_HEADS = 8
HEAD_SIZE = 64
EXPERTS = 16
EPS = 1e-06
MASKED = -1e30
SCALE = HEAD_SIZE ** (-0.5)

f32 = jnp.float32
bf16 = jnp.bfloat16
MIB = 1 << 20


def mm(a, b):
    return lax.dot_general(a, b, (((1,), (0,)), ((), ())), preferred_element_type=f32)


def mm_nt(a, b):
    return lax.dot_general(a, b, (((1,), (1,)), ((), ())), preferred_element_type=f32)


def mm_tn(a, b):
    return lax.dot_general(a, b, (((0,), (0,)), ((), ())), preferred_element_type=f32)


def params(mib):
    return pltpu.CompilerParams(vmem_limit_bytes=mib * MIB)


def cost(flops, moved):
    return pl.CostEstimate(flops=int(flops), bytes_accessed=int(moved), transcendentals=0)


def doc_positions(seg_ids):
    length = seg_ids.shape[0]
    index = jnp.arange(length, dtype=jnp.int32)
    previous = jnp.concatenate([seg_ids[:1] - 1, seg_ids[:-1]])
    is_start = (seg_ids != previous) | (index == 0)
    start = lax.cummax(jnp.where(is_start, index, 0), axis=0)
    return index - start


def turn_tables(position):
    half = HEAD_SIZE // 2
    exponent = jnp.arange(half, dtype=f32) * (-2.0 / HEAD_SIZE)
    inv_freq = jnp.power(10000.0, exponent)
    angles = position.astype(f32)[:, None] * inv_freq[None, :]
    cosine, sine = jnp.cos(angles), jnp.sin(angles)
    return (
        jnp.concatenate([cosine] * 4, axis=1),
        jnp.concatenate([-sine, sine, -sine, sine], axis=1),
    )


def swap_halves(t):
    lane = lax.broadcasted_iota(jnp.int32, t.shape, 1)
    return jnp.where(
        lane % HEAD_SIZE < HEAD_SIZE // 2, pltpu.roll(t, 96, 1), pltpu.roll(t, 32, 1)
    )


def qkv_kernel(x_ref, gain_ref, w_ref, cos_ref, sin_ref, n1_ref, q_ref, k_ref, v_ref):
    x = x_ref[...].astype(f32)
    factor = lax.rsqrt(jnp.mean(x * x, axis=-1, keepdims=True) + EPS)
    n1 = (x * factor * gain_ref[...]).astype(bf16)
    n1_ref[...] = n1
    cosine, sine = cos_ref[...], sin_ref[...]
    q_width, k_width = q_ref.shape[1], k_ref.shape[1]
    for start in range(0, q_width + k_width, 256):
        lin = mm(n1, w_ref[:, start : start + 256])
        for part in (0, 128):
            t = lin[:, part : part + 128]
            turned = (t * cosine + swap_halves(t) * sine).astype(bf16)
            at = start + part
            if at < q_width:
                q_ref[:, at : at + 128] = turned
            else:
                k_ref[:, at - q_width : at - q_width + 128] = turned
    v_ref[...] = mm(n1, w_ref[:, q_width + k_width :]).astype(bf16)


def project(x, gain, w, cosine, sine):
    rows, width = x.shape
    q_width, k_width = QUERY_HEADS * HEAD_SIZE, KEY_VALUE_HEADS * HEAD_SIZE
    shape = jax.ShapeDtypeStruct
    return pl.pallas_call(
        qkv_kernel,
        out_shape=(
            shape((rows, width), bf16),
            shape((rows, q_width), bf16),
            shape((rows, k_width), bf16),
            shape((rows, k_width), bf16),
        ),
        compiler_params=params(40),
        cost_estimate=cost(2 * rows * width * w.shape[1], 2 * w.size + 8 * x.size),
        name="project",
    )(x, gain, w, cosine, sine)


def qkv_grad_kernel(
    dq_ref, dk_ref, dv_ref, n1_ref, w_ref, cos_ref, sin_ref, x_ref, gain_ref, dh_ref,
    gw_ref, gx_ref, gg_ref, lin_ref,
):
    cosine, sine = cos_ref[...], sin_ref[...]
    q_width, k_width = dq_ref.shape[1], dk_ref.shape[1]
    for ref, width, base in ((dq_ref, q_width, 0), (dk_ref, k_width, q_width)):
        for at in range(0, width, 128):
            t = ref[:, at : at + 128].astype(f32)
            turned = (t * cosine - swap_halves(t) * sine).astype(bf16)
            lin_ref[:, base + at : base + at + 128] = turned
    lin_ref[:, q_width + k_width :] = dv_ref[...].astype(bf16)
    total = q_width + 2 * k_width
    n1 = n1_ref[...]
    for at in range(0, total, 512):
        gw_ref[:, at : at + 512] = mm_tn(n1, lin_ref[:, at : at + 512]).astype(bf16)
    dn1 = mm_nt(lin_ref[...], w_ref[...])
    x = x_ref[...].astype(f32)
    factor = lax.rsqrt(jnp.mean(x * x, axis=-1, keepdims=True) + EPS)
    gg_ref[...] = jnp.sum(x * factor * dn1, axis=0, keepdims=True)
    c = dn1 * gain_ref[...]
    mean = jnp.mean(c * x, axis=-1, keepdims=True)
    gx_ref[...] = dh_ref[...] + factor * (c - x * (factor * factor * mean))


def project_grad(dq, dk, dv, n1, w, cosine, sine, x, gain, dh):
    rows, width = x.shape
    shape = jax.ShapeDtypeStruct
    return pl.pallas_call(
        qkv_grad_kernel,
        out_shape=(
            shape(w.shape, bf16),
            shape((rows, width), f32),
            shape((1, width), f32),
        ),
        scratch_shapes=[pltpu.VMEM((rows, w.shape[1]), bf16)],
        compiler_params=params(56),
        cost_estimate=cost(4 * rows * width * w.shape[1], 4 * w.size + 16 * x.size),
        name="project_grad",
    )(dq, dk, dv, n1, w, cosine, sine, x, gain, dh)


def visible_bias(first_ref, seg_q_ref, seg_k_ref, bias_ref):
    rows, keys = bias_ref.shape
    row = first_ref[0] + lax.broadcasted_iota(jnp.int32, (rows, keys), 0)
    col = lax.broadcasted_iota(jnp.int32, (rows, keys), 1)
    seen = (seg_q_ref[...] == seg_k_ref[...]) & (row >= col)
    bias_ref[...] = jnp.where(seen, 0.0, MASKED).astype(f32)


def attend_kernel(first_ref, q_ref, k_ref, v_ref, seg_q_ref, seg_k_ref, o_ref, bias_ref):
    @pl.when(pl.program_id(0) == 0)
    def _():
        visible_bias(first_ref, seg_q_ref, seg_k_ref, bias_ref)

    bias = bias_ref[...]
    for head in range(4):
        at, kv = head * HEAD_SIZE, head // 2 * HEAD_SIZE
        s = mm_nt(q_ref[:, at : at + HEAD_SIZE], k_ref[:, kv : kv + HEAD_SIZE]) * SCALE + bias
        e = jnp.exp(s - jnp.max(s, axis=1, keepdims=True))
        total = jnp.sum(e, axis=1, keepdims=True)
        o = mm(e.astype(bf16), v_ref[:, kv : kv + HEAD_SIZE]) / total
        o_ref[:, at : at + HEAD_SIZE] = o.astype(bf16)


def attend(first, q, k, v, seg_q, seg_k):
    rows, width = q.shape
    keys = k.shape[0]
    wide = pl.BlockSpec((rows, 256), lambda i, first: (0, i))
    narrow = pl.BlockSpec((keys, 128), lambda i, first: (0, i))
    return pl.pallas_call(
        attend_kernel,
        out_shape=jax.ShapeDtypeStruct((rows, width), bf16),
        grid_spec=pltpu.PrefetchScalarGridSpec(
            num_scalar_prefetch=1,
            grid=(width // 256,),
            in_specs=[
                wide,
                narrow,
                narrow,
                pl.BlockSpec((rows, 1), lambda i, first: (0, 0)),
                pl.BlockSpec((1, keys), lambda i, first: (0, 0)),
            ],
            out_specs=wide,
            scratch_shapes=[pltpu.VMEM((rows, keys), f32)],
        ),
        compiler_params=params(48),
        cost_estimate=cost(16 * rows * keys * width, 4 * q.size + 4 * k.size),
        name="attend",
    )(first, q, k, v, seg_q, seg_k)


def attend_grad_kernel(
    first_ref, q_ref, k_ref, v_ref, do_ref, seg_q_ref, seg_k_ref,
    dq_ref, dk_ref, dv_ref, bias_ref,
):
    @pl.when(pl.program_id(0) == 0)
    def _():
        visible_bias(first_ref, seg_q_ref, seg_k_ref, bias_ref)

    bias = bias_ref[...]
    for pair in range(2):
        kv = pair * HEAD_SIZE
        k, v = k_ref[:, kv : kv + HEAD_SIZE], v_ref[:, kv : kv + HEAD_SIZE]
        dk = dv = None
        for head in (2 * pair, 2 * pair + 1):
            at = head * HEAD_SIZE
            q, do = q_ref[:, at : at + HEAD_SIZE], do_ref[:, at : at + HEAD_SIZE]
            s = mm_nt(q, k) * SCALE + bias
            e = jnp.exp(s - jnp.max(s, axis=1, keepdims=True))
            p = e * (1.0 / jnp.sum(e, axis=1, keepdims=True))
            dp = mm_nt(do, v)
            delta = jnp.sum(p * dp, axis=1, keepdims=True)
            ds = (p * (dp - delta) * SCALE).astype(bf16)
            dq_ref[:, at : at + HEAD_SIZE] = mm(ds, k)
            dk_part, dv_part = mm_tn(ds, q), mm_tn(p.astype(bf16), do)
            dk = dk_part if dk is None else dk + dk_part
            dv = dv_part if dv is None else dv + dv_part
        dk_ref[:, kv : kv + HEAD_SIZE] = dk.astype(bf16)
        dv_ref[:, kv : kv + HEAD_SIZE] = dv.astype(bf16)


def attend_grad(first, q, k, v, do, seg_q, seg_k):
    rows, width = q.shape
    keys = k.shape[0]
    wide = pl.BlockSpec((rows, 256), lambda i, first: (0, i))
    narrow = pl.BlockSpec((keys, 128), lambda i, first: (0, i))
    shape = jax.ShapeDtypeStruct
    return pl.pallas_call(
        attend_grad_kernel,
        out_shape=(
            shape((rows, width), f32),
            shape(k.shape, bf16),
            shape(k.shape, bf16),
        ),
        grid_spec=pltpu.PrefetchScalarGridSpec(
            num_scalar_prefetch=1,
            grid=(width // 256,),
            in_specs=[
                wide,
                narrow,
                narrow,
                wide,
                pl.BlockSpec((rows, 1), lambda i, first: (0, 0)),
                pl.BlockSpec((1, keys), lambda i, first: (0, 0)),
            ],
            out_specs=[wide, narrow, narrow],
            scratch_shapes=[pltpu.VMEM((rows, keys), f32)],
        ),
        compiler_params=params(56),
        cost_estimate=cost(40 * rows * keys * width // 4, 8 * q.size + 8 * k.size),
        name="attend_grad",
    )(first, q, k, v, do, seg_q, seg_k)


def gather(value):
    return lax.all_gather(value, "group", axis=0, tiled=True)


def owner_sum(value):
    return lax.psum_scatter(value.astype(bf16), "group", scatter_dimension=0, tiled=True)


def rms_factor(values):
    return lax.rsqrt(jnp.mean(values * values, axis=-1, keepdims=True) + EPS)


LAG = 2
PHASES = 7
SEMS = 8
(CORE, X_A, IN_B, IN_A, HALF_B, MID_A, RUNG_B, OUT_A, BACK_B, SPREAD_A, OUT_B, JOIN, KINDS) = range(13)
(Y_SHARE, Y_DN2, Y_MOE, Y_GATE, Y_DKV, Y_WEIGHT, Y_N2, Y_KINDS) = (0, 1, 2, 3, 4, 12, 18, 20)


def engine_scratch(quarter, width):
    def vmem(*shape):
        return pltpu.VMEM((*shape, quarter, width), bf16)

    return [
        vmem(4, 4),
        vmem(4, 4),
        vmem(4),
        vmem(8, 2),
        vmem(8),
        vmem(4),
        vmem(4),
        vmem(4),
        vmem(LAG, 4),
        vmem(LAG),
        vmem(LAG, 2),
        vmem(LAG),
        vmem(LAG),
        vmem(LAG),
        vmem(LAG),
        pltpu.SemaphoreType.DMA((KINDS, SEMS)),
        pltpu.SemaphoreType.DMA((KINDS, SEMS)),
        pltpu.SemaphoreType.DMA((3, SEMS)),
    ]


class Place:
    def __init__(self):
        r = lax.axis_index("replica")
        self.core, self.x, z = lax.rem(r, 2), lax.rem(r // 2, 2), r // 4
        self.group = lax.axis_index("group")
        self.inner = (z == 1) | (z == 2)
        self.outer = jnp.logical_not(self.inner)
        self.late = z // 2
        self.odd = lax.rem(z, 2)
        up = (z == 0) | (z == 2)
        self.core_peer = {"replica": r + 1 - 2 * self.core}
        self.x_peer = {"replica": r + 2 - 4 * self.x}
        self.line_peer = {"replica": jnp.where(up, r + 4, r - 4)}
        self.mid_peer = {"replica": jnp.where(z == 1, r + 4, r - 4)}
        self.y_peer = {"group": 1 - self.group}

    def greet(self):
        barrier = pltpu.get_barrier_semaphore()

        def signal(peer):
            pl.semaphore_signal(
                barrier, inc=1, device_id=peer, device_id_type=pl.DeviceIdType.MESH
            )

        for peer in (self.core_peer, self.x_peer, self.line_peer, self.y_peer):
            signal(peer)

        @pl.when(self.inner)
        def _():
            signal(self.mid_peer)
            pl.semaphore_wait(barrier, 5)

        @pl.when(self.outer)
        def _():
            pl.semaphore_wait(barrier, 4)


def remote_copy(src, dst, send_sem, recv_sem, peer):
    return pltpu.make_async_remote_copy(
        src_ref=src, dst_ref=dst, send_sem=send_sem, recv_sem=recv_sem, device_id=peer,
        device_id_type=pl.DeviceIdType.MESH,
    )


def make_engine(place, count, split, split_of, stage, out, scratch, late_piece):
    (mine, got_core, got_x, got_end_b, got_end_a, got_mid_b, got_mid_a, got_rung,
     summed, a_x, b_end, a_end, b_mid, a_all, b_all, send_sem, recv_sem, copy_sem) = scratch
    core, x, inner, outer, late = place.core, place.x, place.inner, place.outer, place.late

    owned = split_of // 6

    def spot(k):
        e, sub, part = k // 6, lax.rem(k // 2, 3), lax.rem(k, 2)
        inner_spot = jnp.where(sub == 0, 4 * owned + 2 * e, 4 * e + 2 * sub - 2) + part
        return jnp.where(k < split_of, inner_spot, k)

    def remote(kind, k, src, dst, peer):
        slot = lax.rem(k, SEMS)
        return remote_copy(src, dst, send_sem.at[kind, slot], recv_sem.at[kind, slot], peer)

    def local(kind, k, src, dst):
        return pltpu.make_async_copy(src, dst, copy_sem.at[kind, lax.rem(k, SEMS)])

    def core_copy(k):
        return remote(
            CORE, k, stage.at[k, 1 - core], got_core.at[lax.rem(k, 4)], place.core_peer
        )

    def mine_copy(k):
        return local(2, k, stage.at[k, core], mine.at[lax.rem(k, 4)])

    def x_copy(k):
        return remote(
            X_A, k, summed.at[lax.rem(k, LAG), 1 - x], got_x.at[lax.rem(k, 4)], place.x_peer
        )

    def in_b_copy(k):
        return remote(
            IN_B, k, summed.at[lax.rem(k, LAG), pl.ds(2, 2)], got_end_b.at[lax.rem(k, 8)],
            place.line_peer,
        )

    def in_a_copy(k):
        return remote(
            IN_A, k, a_x.at[lax.rem(k, LAG)], got_end_a.at[lax.rem(k, 8)], place.line_peer
        )

    def half_b_copy(k):
        return remote(
            HALF_B, k, b_end.at[lax.rem(k, LAG), 1 - late], got_mid_b.at[lax.rem(k, 4)],
            place.mid_peer,
        )

    def mid_a_copy(k):
        return remote(
            MID_A, k, a_end.at[lax.rem(k, LAG)], got_mid_a.at[lax.rem(k, 4)], place.mid_peer
        )

    def rung_copy(k):
        return remote(
            RUNG_B, k, b_mid.at[lax.rem(k, LAG)], got_rung.at[lax.rem(k, 4)], place.x_peer
        )

    def out_a_copy(k):
        return remote(OUT_A, k, a_all.at[lax.rem(k, LAG)], out.at[spot(k), core, x], place.line_peer)

    def back_b_copy(k, quarter):
        return remote(
            BACK_B, k, b_all.at[lax.rem(k, LAG)], out.at[spot(k), core, quarter], place.mid_peer
        )

    def spread_copy(k, quarter):
        return remote(SPREAD_A, k, out.at[spot(k), core, x], out.at[spot(k), core, quarter], place.x_peer)

    def out_b_copy(k):
        part = out.at[spot(k), core, pl.ds(2, 2)]
        return remote(OUT_B, k, part, part, place.line_peer)

    def join_copy(k, half):
        return remote(JOIN, k, out.at[spot(k), core], out.at[spot(k), half], place.core_peer)

    def keep_a(k):
        return local(0, k, a_all.at[lax.rem(k, LAG)], out.at[spot(k), core, x])

    def keep_b(k):
        return local(1, k, b_all.at[lax.rem(k, LAG)], out.at[spot(k), core, 2 + late])

    def phase1(k):
        i = lax.rem(k, LAG)

        @pl.when(k < split)
        def _():
            mine_copy(k).wait()
            core_copy(k).wait()
            summed[i] = mine[lax.rem(k, 4)] + got_core[lax.rem(k, 4)]

        if count > split:

            @pl.when(k >= split)
            def _():
                copy, own, other = late_piece(k)
                copy.wait()
                summed[i] = own[...] + other[...]

        x_copy(k).start()

        @pl.when(outer)
        def _():
            in_b_copy(k).start()

    def phase2(k):
        i = lax.rem(k, LAG)
        x_copy(k).wait()
        a_x[i] = summed[i, x] + got_x[lax.rem(k, 4)]

        @pl.when(outer)
        def _():
            in_a_copy(k).start()
            in_b_copy(k).wait_send()

        @pl.when(inner)
        def _():
            in_b_copy(k).wait_recv()
            b_end[i] = summed[i, 2:4] + got_end_b[lax.rem(k, 8)]
            half_b_copy(k).start()

    def phase3(k):
        i = lax.rem(k, LAG)

        @pl.when(outer)
        def _():
            in_a_copy(k).wait_send()

        @pl.when(inner)
        def _():
            in_a_copy(k).wait_recv()
            a_end[i] = a_x[i] + got_end_a[lax.rem(k, 8)]
            mid_a_copy(k).start()
            half_b_copy(k).wait()
            b_mid[i] = b_end[i, late] + got_mid_b[lax.rem(k, 4)]
            rung_copy(k).start()

    def phase4(k):
        i = lax.rem(k, LAG)

        @pl.when(inner)
        def _():
            mid_a_copy(k).wait()
            a_all[i] = a_end[i] + got_mid_a[lax.rem(k, 4)]
            out_a_copy(k).start()
            keep_a(k).start()
            rung_copy(k).wait()
            b_all[i] = b_mid[i] + got_rung[lax.rem(k, 4)]
            back_b_copy(k, 2 + late).start()
            keep_b(k).start()

    def phase5(k):
        @pl.when(outer)
        def _():
            out_a_copy(k).wait_recv()

        @pl.when(inner)
        def _():
            keep_a(k).wait()
            out_a_copy(k).wait_send()

        spread_copy(k, x).start()

        @pl.when(inner)
        def _():
            keep_b(k).wait()
            back_b_copy(k, 2 + late).wait_send()
            back_b_copy(k, 3 - late).wait_recv()
            out_b_copy(k).start()

    def phase6(k):
        spread_copy(k, x).wait_send()
        spread_copy(k, 1 - x).wait_recv()

        @pl.when(outer)
        def _():
            out_b_copy(k).wait_recv()

        @pl.when(inner)
        def _():
            out_b_copy(k).wait_send()

        join_copy(k, core).start()

    def phase7(k):
        join_copy(k, core).wait_send()
        join_copy(k, 1 - core).wait_recv()

    phases = (phase1, phase2, phase3, phase4, phase5, phase6, phase7)

    def tick(t):
        for number in range(PHASES, 0, -1):
            k = t - LAG * number

            @pl.when((k >= 0) & (k < count))
            def _():
                phases[number - 1](k)

    def send(k):
        @pl.when(k < split)
        def _():
            core_copy(k).start()
            mine_copy(k).start()

    return tick, send


def make_small_sum(place, values, got, send_sem, recv_sem):
    def copy(i, peer):
        return remote_copy(values.at[i], got.at[i], send_sem.at[i], recv_sem.at[i], peer)

    peers = (
        place.core_peer, place.x_peer, place.y_peer, place.line_peer, place.mid_peer,
        place.line_peer,
    )

    def add(i):
        values[i + 1] = values[i] + got[i]

    def step(i):
        if 1 <= i <= 3:
            copy(i - 1, peers[i - 1]).wait()
            add(i - 1)
        if i <= 2:
            copy(i, peers[i]).start()
        if i == 3:

            @pl.when(place.outer)
            def _():
                copy(3, peers[3]).start()

        if i == 4:

            @pl.when(place.outer)
            def _():
                copy(3, peers[3]).wait_send()

            @pl.when(place.inner)
            def _():
                copy(3, peers[3]).wait_recv()
                add(3)
                copy(4, peers[4]).start()

        if i == 5:

            @pl.when(place.inner)
            def _():
                copy(4, peers[4]).wait()
                add(4)
                copy(5, peers[5]).start()

        if i == 6:

            @pl.when(place.inner)
            def _():
                copy(5, peers[5]).wait_send()

            @pl.when(place.outer)
            def _():
                copy(5, peers[5]).wait_recv()
                values[5] = got[5]

    return step


TILE = 256
WIDE = 1024


(F_SMALL, F_SEG, F_WQ, F_WK, F_WV, F_WO, F_GRAD) = range(7)
F_KV = F_GRAD + 2
F_KINDS = F_KV + 8
W_KV, W_Q, W_OUT = 0, 1, 2
SMALL_ROWS = 32


def two_heads(t):
    return jnp.concatenate([t[:, :HEAD_SIZE], t[:, HEAD_SIZE:]], axis=0)


def side_by_side(t):
    half = t.shape[0] // 2
    return jnp.concatenate([t[:half], t[half:]], axis=1)


def layer_kernel(
    x_hbm, wq_hbm, wk_hbm, wv_hbm, wo_hbm, g_hbm, w1_hbm, w2_hbm, small_own, seg_own, routes, inv_freq,
    y_ref, gx_ref, small_ref, out, stage, q_hbm, kv_hbm, n1_hbm, g_all, w_all,
    ao, h, n2, lse, cosine_ref, sine_ref, seg_k, seg_q, router, gains, small_in, seg,
    f_send, f_recv, l_send, l_recv, x_send, x_recv, c_send, c_recv, keep_sem,
    moe, dn2, share, share_t, gate, gate_t, y_send, y_got, got_kv, got_core_w, got_y_w, small, got_small,
    piece, piece_sem, w_sem, load_sem, ys_sem, yr_sem, cs_sem, cr_sem, ss_sem, sr_sem, *scratch,
):
    rows, width = x_hbm.shape
    tokens = 2 * rows
    owned, half = w2_hbm.shape[0], w2_hbm.shape[1]
    works = 3 * owned
    pieces = 2 * works
    count = pieces + 6
    place = Place()
    group, core = place.group, place.core
    here = pl.multiple_of(group * rows, rows)
    there = pl.multiple_of((1 - group) * rows, rows)

    def begin_load(*pairs):
        copies = [
            pltpu.make_async_copy(src, dst, load_sem.at[i]) for i, (src, dst) in enumerate(pairs)
        ]
        for copy in copies:
            copy.start()
        return copies

    def end_load(copies):
        for copy in copies:
            copy.wait()

    def y_copy(kind, src, dst):
        return remote_copy(src, dst, ys_sem.at[kind], yr_sem.at[kind], place.y_peer)

    def over_tiles(first, number, body, size=TILE):
        @pl.loop(0, number)
        def _(i):
            body(pl.ds(pl.multiple_of(first + i * size, size), size))

    def shifted(tile, by):
        return pl.ds(pl.multiple_of(tile.start + by, TILE), TILE)

    def after_core(gw):
        def late_piece(k):
            j, part = (k - pieces) // 2, lax.rem(k - pieces, 2)
            return (
                y_weight(gw, k - pieces), gw.at[j, group, part, core], got_y_w.at[j, part]
            )

        return late_piece

    def y_weight(gw, i):
        j, part = i // 2, i % 2
        return y_copy(Y_WEIGHT + i, gw.at[j, 1 - group, part, core], got_y_w.at[j, part])

    def fetch(w1, w2, e):
        slot = lax.rem(e, 2)
        return (
            pltpu.make_async_copy(w1_hbm.at[e], w1.at[slot], w_sem.at[0, slot]),
            pltpu.make_async_copy(w2_hbm.at[e], w2.at[slot], w_sem.at[1, slot]),
        )

    tick, send = make_engine(place, count, count, pieces, stage, out, scratch, None)

    def advance(t):
        tick(t)

        @pl.when(t < pieces)
        def _():
            send(t)

    def advance_all(first, number):
        @pl.loop(first, first + number)
        def _(t):
            advance(t)

    own_rows_here = pl.ds(here, rows)
    qkv_width = 2 * width
    kv_width = wk_hbm.shape[1]
    own_rows = wq_hbm.shape[0]
    part = own_rows // 4
    small_part = part // 2
    x = place.x
    w_here = pl.multiple_of(group * own_rows, own_rows)
    w_there = pl.multiple_of((1 - group) * own_rows, own_rows)
    quarter = pl.multiple_of((2 * core + x) * part, part)
    eighth = pl.multiple_of(quarter + place.odd * small_part, small_part)
    grad_copies = [
        remote_copy(
            g_hbm.at[pl.ds(i * rows // 2, rows // 2)],
            g_all.at[pl.ds(pl.multiple_of(here + i * rows // 2, rows // 2), rows // 2)],
            f_send.at[F_GRAD + i], f_recv.at[F_GRAD + i], place.y_peer,
        )
        for i in range(2)
    ]
    share_copy = y_copy(Y_SHARE, share_t.at[0], share_t.at[1])

    def n2_copy(i):
        tile = n2.at[pl.ds(pl.multiple_of(here + i * TILE, TILE), TILE)]
        return y_copy(Y_N2 + i, tile, tile)

    def keep(i, src, dst):
        return pltpu.make_async_copy(src, dst, keep_sem.at[i])

    def forward_part(w, kv, bias, n1_in, q, x_in):
        loads = [
            (x_hbm, x_in),
            (wk_hbm, w.at[pl.ds(w_here, own_rows), pl.ds(width, kv_width)]),
            (wv_hbm, w.at[pl.ds(w_here, own_rows), pl.ds(width + kv_width, kv_width)]),
            (wq_hbm, w.at[pl.ds(w_here, own_rows), pl.ds(0, width)]),
            (wo_hbm, w.at[pl.ds(w_here, own_rows), pl.ds(qkv_width, width)]),
        ]
        loads = [
            pltpu.make_async_copy(src, dst, load_sem.at[i]) for i, (src, dst) in enumerate(loads)
        ]
        for copy in loads:
            copy.start()
        place.greet()

        def f_copy(kind, src, dst):
            return remote_copy(src, dst, f_send.at[kind], f_recv.at[kind], place.y_peer)

        def weight_copy(kind, src, column, columns):
            return f_copy(
                kind, src.at[pl.ds(eighth, small_part)],
                w.at[pl.ds(w_here + eighth, small_part), pl.ds(column, columns)],
            )

        def line_copy(i, column, columns):
            block = w.at[pl.ds(w_there + eighth, small_part), pl.ds(column, columns)]
            return remote_copy(block, block, l_send.at[i], l_recv.at[i], place.line_peer)

        def x_copy(i, column, columns):
            block = w.at[pl.ds(w_there + quarter, part), pl.ds(column, columns)]
            return remote_copy(block, block, x_send.at[i], x_recv.at[i], place.x_peer)

        def core_copy(i, column, columns):
            first = pl.multiple_of(w_there + 2 * core * part, 2 * part)
            block = w.at[pl.ds(first, 2 * part), pl.ds(column, columns)]
            return remote_copy(block, block, c_send.at[i], c_recv.at[i], place.core_peer)

        small_copy = f_copy(F_SMALL, small_own, small_in.at[group])
        seg_copy = f_copy(F_SEG, seg_own, seg.at[group])
        kv_weights = [
            weight_copy(F_WK, wk_hbm, width, kv_width),
            weight_copy(F_WV, wv_hbm, width + kv_width, kv_width),
        ]
        wq_copy = weight_copy(F_WQ, wq_hbm, 0, width)
        wo_copy = weight_copy(F_WO, wo_hbm, qkv_width, width)
        for copy in (small_copy, seg_copy, *kv_weights):
            copy.start()
        small_in[group] = small_own[...]
        seg[group] = seg_own[...]

        small_copy.wait()
        seg_copy.wait()
        seg_row = jnp.concatenate([seg[0, 0:1, :], seg[1, 0:1, :]], axis=1)
        seg_k[...] = seg_row
        router[...] = jnp.concatenate([small_in[0, 0:EXPERTS, :], small_in[1, 0:EXPERTS, :]], axis=1)
        gains[...] = jnp.concatenate(
            [small_in[0, EXPERTS:, :], small_in[1, EXPERTS:, :]], axis=1
        ).astype(f32)[0 : gains.shape[0]]
        row = here + lax.broadcasted_iota(jnp.int32, bias.shape, 0)
        col = lax.broadcasted_iota(jnp.int32, bias.shape, 1)
        seg_column = seg_own[...].astype(f32).T[:, 0:1].astype(jnp.int32)
        seg_q[...] = seg_column
        same = seg_column == seg_row
        bias[...] = jnp.where(same & (row >= col), 0.0, MASKED).astype(f32)
        position = jnp.sum(jnp.where(same & (row > col), 1.0, 0.0), axis=1, keepdims=True)

        for copy in kv_weights:
            copy.wait()
        line_copy(W_KV, width, 2 * kv_width).start()
        wq_copy.start()

        expert = lax.broadcasted_iota(jnp.int32, (EXPERTS, rows), 0)
        named = jnp.zeros((EXPERTS, rows), f32)
        for k in range(routes.shape[0]):
            named = jnp.where(routes[k : k + 1, :] == expert, 1.0, named)
        share[own_rows_here, :] = named.T

        angle = position * inv_freq[...]
        lane = lax.broadcasted_iota(jnp.int32, angle.shape, 1)
        cosine_ref[...] = jnp.cos(angle)
        sine = jnp.sin(angle)
        sine_ref[...] = jnp.where(lax.rem(lane, HEAD_SIZE) < HEAD_SIZE // 2, -sine, sine)

        line_copy(W_KV, width, 2 * kv_width).wait()
        x_copy(W_KV, width, 2 * kv_width).start()
        wq_copy.wait()
        line_copy(W_Q, 0, width).start()
        wo_copy.start()
        for copy in loads:
            copy.wait()
        xs = x_in[...].astype(f32)
        factor = lax.rsqrt(jnp.mean(xs * xs, axis=-1, keepdims=True) + EPS)
        n1_in[...] = (xs * factor * gains[0:1, :]).astype(bf16)

        x_copy(W_KV, width, 2 * kv_width).wait()
        core_copy(W_KV, width, 2 * kv_width).start()
        line_copy(W_Q, 0, width).wait()
        x_copy(W_Q, 0, width).start()
        wo_copy.wait()
        line_copy(W_OUT, qkv_width, width).start()
        grad_copies[0].start()
        core_copy(W_KV, width, 2 * kv_width).wait()

        n1 = n1_in[...]
        keep(2, n1_in, n1_hbm).start()
        cosine, sine = cosine_ref[...], sine_ref[...]

        def turned(column):
            lin = mm(n1, w[:, column : column + 256])
            return [
                (t * cosine + swap_halves(t) * sine).astype(bf16)
                for t in (lin[:, :128], lin[:, 128:])
            ]

        own = own_rows_here

        def kv_copies(i):
            first = pl.multiple_of(i * 128, 128)
            return [
                f_copy(
                    F_KV + 2 * i + j,
                    kv.at[own, pl.ds(first + j * kv_width, 128)],
                    kv.at[own, pl.ds(first + j * kv_width, 128)],
                )
                for j in range(2)
            ]

        for i in range(2):
            at = 256 * i
            kv[own, at : at + 128], kv[own, at + 128 : at + 256] = turned(width + at)
            lin = mm(n1, w[:, width + kv_width + at : width + kv_width + at + 256])
            kv[own, kv_width + at : kv_width + at + 256] = lin.astype(bf16)

            @pl.when(group == 0)
            def _():
                for j in (2 * i, 2 * i + 1):
                    for copy in kv_copies(j):
                        copy.start()

        @pl.when(group == 0)
        def _():
            kv[rows:, :] = jnp.zeros((rows, kv.shape[1]), bf16)

        x_copy(W_Q, 0, width).wait()
        core_copy(W_Q, 0, width).start()
        line_copy(W_OUT, qkv_width, width).wait()
        x_copy(W_OUT, qkv_width, width).start()

        @pl.when(group == 1)
        def _():
            grad_copies[1].start()

        core_copy(W_Q, 0, width).wait()
        for at in range(0, width, 256):
            q[:, at : at + 128], q[:, at + 128 : at + 256] = turned(at)
        lse[...] = jnp.zeros_like(lse)

        @pl.loop(0, 4)
        def _(i):
            @pl.when(group == 1)
            def _():
                for copy in kv_copies(i):
                    copy.wait_recv()

            @pl.when(i == 2)
            def _():
                x_copy(W_OUT, qkv_width, width).wait()
                core_copy(W_OUT, qkv_width, width).start()

            at_k = pl.ds(pl.multiple_of(i * 128, 128), 128)
            at_v = pl.ds(pl.multiple_of(kv_width + i * 128, 128), 128)
            keys, values = kv[:, at_k], kv[:, at_v]
            for pair in range(2):
                lanes = slice(pair * HEAD_SIZE, (pair + 1) * HEAD_SIZE)
                key, value = keys[:, lanes], values[:, lanes]
                at_q = pl.ds(pl.multiple_of(i * 256 + pair * 128, 128), 128)

                @pl.loop(0, rows // TILE)
                def _(number):
                    tile = pl.ds(pl.multiple_of(number * TILE, TILE), TILE)
                    s = mm_nt(two_heads(q[tile, at_q]) * SCALE, key)
                    s = s.reshape(2, TILE, -1) + bias[tile, :][None]
                    peak = jnp.max(s, axis=2, keepdims=True)
                    e = jnp.exp(s - peak)
                    total = jnp.sum(e, axis=2, keepdims=True)
                    o = mm(e.astype(bf16).reshape(2 * TILE, -1), value)
                    o = o / total.reshape(2 * TILE, 1)
                    ao[tile, at_q] = side_by_side(o).astype(bf16)
                    log_sum = peak + jnp.log(total)
                    lane = lax.broadcasted_iota(jnp.int32, (TILE, QUERY_HEADS), 1)
                    head = 4 * i + 2 * pair
                    lse[tile, :] = jnp.where(
                        lane == head, log_sum[0], jnp.where(lane == head + 1, log_sum[1], lse[tile, :])
                    )

        @pl.when(group == 0)
        def _():
            for i in range(4):
                for copy in kv_copies(i):
                    copy.wait_send()
            grad_copies[1].start()

        keep(3, q, q_hbm).start()
        keep(1, kv, kv_hbm).start()
        core_copy(W_OUT, qkv_width, width).wait()
        keep(0, w, w_all).start()

        @pl.loop(0, rows // TILE)
        def _(number):
            tile = pl.ds(pl.multiple_of(number * TILE, TILE), TILE)
            own_tile = shifted(tile, here)
            hidden = x_in[tile, :].astype(f32) + mm(ao[tile, :], w[:, qkv_width:])
            h[tile, :] = hidden
            factor = lax.rsqrt(jnp.mean(hidden * hidden, axis=-1, keepdims=True) + EPS)
            normed = (hidden * factor * gains[1:2, :]).astype(bf16)
            n2[own_tile, :] = normed
            n2_copy(number).start()
            logits = mm_nt(normed, router[...])
            chosen = share[own_tile, :] > 0.0
            picked = jnp.where(chosen, logits, MASKED)
            e = jnp.exp(picked - jnp.max(picked, axis=1, keepdims=True))
            e = jnp.where(chosen, e, 0.0)
            share[own_tile, :] = e / jnp.sum(e, axis=1, keepdims=True)

        share_t[0] = share[own_rows_here, :].T
        share_copy.start()
        for i, (src, dst) in enumerate(((w, w_all), (kv, kv_hbm), (n1_in, n1_hbm), (q, q_hbm))):
            keep(i, src, dst).wait()

    pl.run_scoped(
        forward_part,
        pltpu.VMEM((width, 3 * width), bf16),
        pltpu.VMEM((tokens, width), bf16),
        pltpu.VMEM((rows, tokens), f32),
        *[pltpu.VMEM((rows, width), bf16)] * 3,
    )

    dn2_copy = y_copy(Y_DN2, y_send.at[0], y_got.at[0])

    def leave(i, terms, tile):
        y_send[i, shifted(tile, -there), :] = terms[tile, :].astype(bf16)

    def expert_part(n2_turned, g, act, d_ye, d_gu, w1, w2):
        for copy in fetch(w1, w2, 0):
            copy.start()
        loads = begin_load((g_hbm, g.at[own_rows_here]))
        gate[...] = jnp.zeros_like(gate)

        def prepare(tile):
            n2_turned[:, tile] = n2[tile, :].T
            moe[tile, :] = jnp.zeros((TILE, width), f32)
            dn2[tile, :] = jnp.zeros((TILE, width), f32)

        over_tiles(here, rows // TILE, prepare)
        for i in range(rows // TILE):
            n2_copy(i).wait()
        share_copy.wait()
        share[pl.ds(there, rows), :] = share_t[1].T
        over_tiles(there, rows // TILE, prepare)
        for copy in grad_copies:
            copy.wait()
        end_load(loads)
        end_load(begin_load((g_all.at[pl.ds(there, rows)], g.at[pl.ds(there, rows)])))

        def pick(table, e):
            lane = lax.broadcasted_iota(jnp.int32, table.shape, 1)
            return jnp.sum(
                jnp.where(lane == group * owned + e, table, 0.0), axis=1, keepdims=True
            )

        def keep_piece(k):
            slot = lax.rem(k, 2)
            return pltpu.make_async_copy(piece.at[slot], stage.at[pl.ds(2 * k, 2)], piece_sem.at[slot])

        def work(k):
            e, sub = k // 3, lax.rem(k, 3)
            slot = lax.rem(e, 2)

            @pl.when(k == 2)
            def _():
                keep_piece(1).wait()

            @pl.when(k >= 4)
            def _():
                keep_piece(k - 2).wait()

            @pl.when(sub == 0)
            def _():
                for copy in fetch(w1, w2, e):
                    copy.wait()

                @pl.when(e + 1 < owned)
                def _():
                    for copy in fetch(w1, w2, e + 1):
                        copy.start()

                def body(tile):
                    gu = mm(n2[tile, :], w1[slot])
                    z, w = gu[:, :half], gu[:, half:]
                    sg = jax.nn.sigmoid(z)
                    silu = z * sg
                    act[tile, :] = (silu * w).astype(bf16)
                    dy = (pick(share[tile, :], e) * g[tile, :].astype(f32)).astype(bf16)
                    d_ye[tile, :] = dy
                    d_act = mm_nt(dy, w2[slot])
                    d_gu[tile, :half] = (d_act * w * sg * (1.0 + z * (1.0 - sg))).astype(bf16)
                    d_gu[tile, half:] = (d_act * silu).astype(bf16)

                over_tiles(0, tokens // WIDE, body, WIDE)
                for part in range(2):
                    columns = slice(part * half // 2, (part + 1) * half // 2)
                    grad = mm_tn(act[:, columns], d_ye[...])
                    piece[lax.rem(k, 2), part] = grad.astype(bf16).reshape(piece.shape[2:])

            @pl.when(sub == 2)
            def _():
                @pl.when(k == works - 1)
                def _():
                    over_tiles(there, rows // TILE, functools.partial(leave, 0, dn2))
                    dn2_copy.start()

                def body(tile):
                    ye = mm(act[tile, :], w2[slot]).astype(bf16).astype(f32)
                    value = jnp.sum(g[tile, :].astype(f32) * ye, axis=1, keepdims=True)
                    lane = lax.broadcasted_iota(jnp.int32, (WIDE, gate.shape[1]), 1)
                    gate[tile, :] = jnp.where(lane == group * owned + e, value, gate[tile, :])
                    moe[tile, :] += pick(share[tile, :], e) * ye

                over_tiles(0, tokens // WIDE, body, WIDE)

            @pl.when(sub == 1)
            def _():
                def body(tile):
                    dn2[tile, :] += mm_nt(d_gu[tile, :], w1[slot]).astype(bf16).astype(f32)

                over_tiles(0, tokens // WIDE, body, WIDE)

            @pl.when(sub > 0)
            def _():
                @pl.loop(0, 2)
                def _(part):
                    first = pl.multiple_of((2 * (sub - 1) + part) * (half // 2), half // 2)
                    grad = mm(n2_turned[pl.ds(first, half // 2), :], d_gu[...])
                    piece[lax.rem(k, 2), part] = grad.astype(bf16).reshape(piece.shape[2:])

            keep_piece(k).start()

            @pl.when(k == 0)
            def _():
                keep_piece(0).wait()

        @pl.loop(0, works)
        def _(k):
            work(k)
            pl.loop(6 * k // 5, 6 * (k + 1) // 5)(advance)

        keep_piece(works - 2).wait()
        keep_piece(works - 1).wait()

        over_tiles(there, rows // TILE, functools.partial(leave, 1, moe))

    wide = (tokens, width)
    pl.run_scoped(
        expert_part,
        pltpu.VMEM((width, tokens), bf16),
        pltpu.VMEM(wide, bf16),
        pltpu.VMEM((tokens, half), bf16),
        pltpu.VMEM(wide, bf16),
        pltpu.VMEM((tokens, 2 * half), bf16),
        pltpu.VMEM((2, width, 2 * half), bf16),
        pltpu.VMEM((2, half, width), bf16),
    )
    t = 6 * works // 5
    gate_copy = y_copy(Y_GATE, gate_t.at[0], gate_t.at[1])
    gate_t[0] = gate[pl.ds(there, rows), :].T
    moe_copy = y_copy(Y_MOE, y_send.at[1], y_got.at[1])
    gate_copy.start()
    t += 5

    def attention_part(gw, d_o, dkv):
        tail = gw.shape[3:]

        def store_rows(j, i, grad):
            gw[j, i // 2, i % 2] = grad.astype(bf16).reshape(tail)

        def core_weight(j):
            return remote_copy(
                gw.at[j, :, :, 1 - core], got_core_w.at[j], cs_sem.at[j], cr_sem.at[j],
                place.core_peer,
            )

        def to_owner(j):
            core_weight(j).wait()
            for member in range(2):
                for part in range(2):
                    gw[j, member, part, core] += got_core_w[j, member, part]
            for part in range(2):
                y_weight(gw, 2 * j + part).start()

        def kv_copies(i):
            first = pl.multiple_of(i * 128, 128)
            return [
                y_copy(
                    Y_DKV + 2 * i + j,
                    dkv.at[pl.ds(0, rows), pl.ds(first + j * (width // 2), 128)],
                    got_kv.at[:, pl.ds(first + j * (width // 2), 128)],
                )
                for j in range(2)
            ]

        def middle(g, wo, d_y):
            loads = begin_load((g_hbm, g), (w_all.at[:, pl.ds(2 * width, width)], wo))
            advance_all(t - 5, 5)
            end_load(loads)
            dn2_copy.wait()
            gate_copy.wait()
            gate[own_rows_here, :] += gate_t[1].T
            moe_copy.start()
            small[0] = jnp.zeros(small.shape[1:], f32)

            def body(tile):
                own = shifted(tile, here)
                s = share[own, :]
                dg = gate[own, :]
                d_logits = (s * (dg - jnp.sum(s * dg, axis=1, keepdims=True))).astype(bf16)
                d_n2 = dn2[own, :] + y_got[0, tile, :].astype(f32) + mm(d_logits, router[...])
                hidden = h[tile, :]
                factor = lax.rsqrt(jnp.mean(hidden * hidden, axis=-1, keepdims=True) + EPS)
                small[0, 0:EXPERTS, :] += mm_tn(d_logits, n2[own, :])
                small[0, EXPERTS : EXPERTS + 1, :] += jnp.sum(
                    hidden * factor * d_n2, axis=0, keepdims=True
                )
                c = d_n2 * gains[1:2, :]
                mean = jnp.mean(c * hidden, axis=-1, keepdims=True)
                d_h = g[tile, :].astype(f32) + factor * (c - hidden * (factor * factor * mean))
                dn2[shifted(tile, there), :] = d_h
                d_y[tile, :] = d_h.astype(bf16)
                d_o[tile, :] = mm_nt(d_h.astype(bf16), wo[...]).astype(bf16)
                moe[own, :] += hidden

            @pl.loop(0, rows // TILE)
            def _(i):
                body(pl.ds(pl.multiple_of(i * TILE, TILE), TILE))
                advance(t + i)

            for i in range(4):
                columns = slice(i * width // 4, (i + 1) * width // 4)
                store_rows(0, i, mm_tn(ao[:, columns], d_y[...]))
            core_weight(0).start()

        pl.run_scoped(
            middle,
            pltpu.VMEM((rows, width), bf16),
            pltpu.VMEM((width, width), bf16),
            pltpu.VMEM((rows, width), bf16),
        )
        advance(t + 2)
        to_owner(0)

        def heads(q, kv, bias):
            loads = begin_load((q_hbm, q), (kv_hbm, kv))
            row = here + lax.broadcasted_iota(jnp.int32, bias.shape, 0)
            col = lax.broadcasted_iota(jnp.int32, bias.shape, 1)
            seen = (seg_q[...] == seg_k[...]) & (row >= col)
            bias[...] = jnp.where(seen, 0.0, MASKED).astype(f32)
            end_load(loads)

            @pl.loop(0, 4)
            def _(i):
                at_k = pl.ds(pl.multiple_of(i * 128, 128), 128)
                at_v = pl.ds(pl.multiple_of(width // 2 + i * 128, 128), 128)
                keys, values = kv[:, at_k], kv[:, at_v]
                dks, dvs = [], []
                for pair in range(2):
                    lanes = slice(pair * HEAD_SIZE, (pair + 1) * HEAD_SIZE)
                    key, value = keys[:, lanes], values[:, lanes]
                    at_q = pl.ds(pl.multiple_of(i * 256 + pair * 128, 128), 128)

                    def body(part, sums):
                        dk, dv = sums
                        tile = pl.ds(pl.multiple_of(part * TILE, TILE), TILE)
                        qs = two_heads(q[tile, at_q]) * SCALE
                        dos = two_heads(d_o[tile, at_q])
                        os = two_heads(ao[tile, at_q])
                        delta = jnp.sum(
                            dos.astype(f32) * os.astype(f32), axis=1, keepdims=True
                        )
                        lane = lax.broadcasted_iota(jnp.int32, (TILE, QUERY_HEADS), 1)
                        peaks = jnp.concatenate(
                            [
                                jnp.sum(
                                    jnp.where(lane == 4 * i + 2 * pair + head, lse[tile, :], 0.0),
                                    axis=1, keepdims=True,
                                )
                                for head in range(2)
                            ],
                            axis=0,
                        )
                        s = mm_nt(qs, key) - peaks
                        s = s.reshape(2, TILE, -1) + bias[tile, :][None]
                        p = jnp.exp(s).reshape(2 * TILE, -1)
                        dp = mm_nt(dos, value)
                        ds = (p * (dp - delta)).astype(bf16)
                        dq = mm(ds, key) * SCALE
                        moe[shifted(tile, there), at_q] = side_by_side(dq)
                        return dk + mm_tn(qs, ds), dv + mm_tn(dos, p.astype(bf16))

                    zero = jnp.zeros((HEAD_SIZE, kv.shape[0]), f32)
                    dk, dv = lax.fori_loop(0, rows // TILE, body, (zero, zero))
                    dks.append(dk)
                    dvs.append(dv)
                dkv[:, at_k] = jnp.concatenate(dks, axis=0).T.astype(bf16)
                dkv[:, at_v] = jnp.concatenate(dvs, axis=0).T.astype(bf16)

                @pl.when(group == 1)
                def _():
                    for copy in kv_copies(i):
                        copy.start()

                advance(t + 3 + 2 * i)
                advance(t + 4 + 2 * i)

        pl.run_scoped(
            heads,
            pltpu.VMEM((rows, width), bf16),
            pltpu.VMEM((tokens, width), bf16),
            pltpu.VMEM((rows, tokens), f32),
        )

        def projections(n1, wqkv, lin, x_in):
            loads = begin_load(
                (n1_hbm, n1), (x_hbm, x_in), (w_all.at[:, pl.ds(0, 2 * width)], wqkv)
            )
            own = pl.ds(here, rows)

            def turn_back(to, source, where, at):
                value = source[where, at : at + 128].astype(f32)
                turned = value * cosine_ref[...] - swap_halves(value) * sine_ref[...]
                lin[:, to : to + 128] = turned.astype(bf16)

            def weight_grad(j, first):
                for i in range(4):
                    columns = slice(i * width // 4, (i + 1) * width // 4)
                    store_rows(j, i, mm_tn(n1[:, columns], lin[:, first : first + width]))
                core_weight(j).start()

            for j in range(0, width, 128):
                turn_back(j, moe, pl.ds(there, rows), j)
            end_load(loads[:1])
            weight_grad(1, 0)
            advance(t + 11)
            to_owner(1)
            advance(t + 12)

            @pl.when(group == 1)
            def _():
                for i in range(4):
                    for copy in kv_copies(i):
                        copy.wait_send()

            @pl.when(group == 0)
            def _():
                for i in range(4):
                    for copy in kv_copies(i):
                        copy.wait_recv()
                total = dkv[0:rows, :].astype(f32) + got_kv[...].astype(f32)
                dkv[0:rows, :] = total.astype(bf16)

            for j in range(0, width // 2, 128):
                turn_back(width + j, dkv, own, j)
            lin[:, 3 * width // 2 :] = dkv[own, width // 2 :]
            weight_grad(2, width)
            advance(t + 13)
            to_owner(2)
            advance(t + 14)

            def body(tile):
                dn1 = mm_nt(lin[tile, :], wqkv[...])
                xs = x_in[tile, :].astype(f32)
                factor = lax.rsqrt(jnp.mean(xs * xs, axis=-1, keepdims=True) + EPS)
                small[0, EXPERTS + 1 : EXPERTS + 2, :] += jnp.sum(
                    xs * factor * dn1, axis=0, keepdims=True
                )
                c = dn1 * gains[0:1, :]
                mean = jnp.mean(c * xs, axis=-1, keepdims=True)
                gx_ref[tile, :] = dn2[shifted(tile, there), :] + factor * (
                    c - xs * (factor * factor * mean)
                )
                total = moe[shifted(tile, here), :] + y_got[1, tile, :].astype(f32)
                y_ref[tile, :] = total.astype(bf16)

            end_load(loads[1:])
            moe_copy.wait()
            last_tick, last_send = make_engine(
                place, count, pieces, pieces, stage, out, scratch, after_core(gw)
            )
            small_step = make_small_sum(place, small, got_small, ss_sem, sr_sem)
            first_last = t + 15
            tiles = rows // TILE

            @pl.loop(first_last, count + PHASES * LAG)
            def _(now):
                last_tick(now)

                @pl.when(now < pieces)
                def _():
                    last_send(now)

                @pl.when(now < first_last + tiles)
                def _():
                    body(pl.ds(pl.multiple_of((now - first_last) * TILE, TILE), TILE))

                for i in range(7):

                    @pl.when(now == first_last + tiles + 2 * i)
                    def _():
                        small_step(i)

        pl.run_scoped(
            projections,
            pltpu.VMEM((rows, width), bf16),
            pltpu.VMEM((width, 2 * width), bf16),
            pltpu.VMEM((rows, 2 * width), bf16),
            pltpu.VMEM((rows, width), bf16),
        )

    pl.run_scoped(
        attention_part,
        pltpu.VMEM((3, 2, 2, *piece.shape[2:]), bf16),
        pltpu.VMEM((rows, width), bf16),
        pltpu.VMEM((tokens, width), bf16),
    )
    small_ref[...] = small[5]


DEPTH = 12


def finish_kernel(
    owned, pieces, small_ref, g_in, g_out, g_q, g_k, g_v, g_wo, router_ref, gain_ref,
    narrow, wide, in_sem, out_sem, last_sem,
):
    count = pieces.shape[0]
    whole = count - 2
    kv_width = g_k.shape[-1]

    def fetch(k):
        slot = lax.rem(k, DEPTH)
        return pltpu.make_async_copy(pieces.at[k], narrow.at[slot], in_sem.at[slot])

    def store(k, target):
        slot = lax.rem(k, DEPTH)
        return pltpu.make_async_copy(wide.at[slot], target, out_sem.at[slot])

    def convert(k):
        slot = lax.rem(k, DEPTH)
        fetch(k).wait()

        @pl.when(k >= DEPTH)
        def _():
            store(k, g_in.at[0]).wait()

        wide[slot] = narrow[slot].astype(f32)

        @pl.when(k + DEPTH < count)
        def _():
            fetch(k + DEPTH).start()

    for k in range(DEPTH):
        fetch(k).start()
    columns = router_ref.shape[1]
    first = pl.multiple_of(lax.axis_index("group") * columns, columns)
    router_ref[...] = small_ref[0:EXPERTS, pl.ds(first, columns)]
    gain_ref[...] = small_ref[EXPERTS:, pl.ds(first, columns)]

    @pl.loop(0, whole)
    def _(k):
        convert(k)
        base = 0
        for target in (g_in, g_out, g_wo, g_q):
            number = target.shape[0]

            @pl.when((k >= base) & (k < base + number))
            def _():
                store(k, target.at[k - base]).start()

            base += number

    last = []
    for i in range(2):
        k = whole + i
        convert(k)
        for j, target in enumerate((g_k, g_v)):
            copy = pltpu.make_async_copy(
                wide.at[k % DEPTH, :, pl.ds(j * kv_width, kv_width)], target.at[i],
                last_sem.at[2 * i + j],
            )
            copy.start()
            last.append(copy)
    for copy in last:
        copy.wait()
    for k in range(count - DEPTH, whole):
        store(k, g_in.at[0]).wait()


def finish(pieces, small, owned, kv_width):
    count, rows, width = pieces.shape
    shape = jax.ShapeDtypeStruct
    vmem = pl.BlockSpec(memory_space=pltpu.VMEM)
    hbm = pl.BlockSpec(memory_space=pl.ANY)
    dma = pltpu.SemaphoreType.DMA
    return pl.pallas_call(
        functools.partial(finish_kernel, owned),
        out_shape=(
            shape((4 * owned, rows, width), f32),
            shape((2 * owned, rows, width), f32),
            shape((2, rows, width), f32),
            shape((2, rows, kv_width), f32),
            shape((2, rows, kv_width), f32),
            shape((2, rows, width), f32),
            shape((EXPERTS, width // 2), f32),
            shape((8, width // 2), f32),
        ),
        in_specs=[hbm, vmem],
        out_specs=[hbm] * 6 + [vmem] * 2,
        scratch_shapes=[
            pltpu.VMEM((DEPTH, rows, width), bf16),
            pltpu.VMEM((DEPTH, rows, width), f32),
            dma((DEPTH,)),
            dma((DEPTH,)),
            dma((4,)),
        ],
        compiler_params=params(48),
        cost_estimate=cost(0, 6 * pieces.size),
        name="finish",
    )(pieces, small)


def layer(x, document_numbers, routes, gains, w_router, wq, wk, wv, wo, grad, w_in, w_out):
    rows, width = x.shape
    own_rows = wq.shape[0]
    small = jnp.concatenate(
        [w_router.T, *[gain[None] for gain in gains],
         jnp.zeros((SMALL_ROWS - EXPERTS - 2, own_rows), bf16)], axis=0,
    )
    exponent = (np.arange(128) % (HEAD_SIZE // 2)) * (-2.0 / HEAD_SIZE)
    inv_freq = jnp.asarray(np.power(10000.0, exponent)[None], f32)
    owned, half = w_out.shape[:2]
    tokens, quarter = 2 * rows, half // 16
    pieces = 6 * owned
    shape = jax.ShapeDtypeStruct
    vmem = pl.BlockSpec(memory_space=pltpu.VMEM)
    hbm = pl.BlockSpec(memory_space=pl.ANY)
    dma = pltpu.SemaphoreType.DMA
    small_rows = EXPERTS + 8
    return pl.pallas_call(
        layer_kernel,
        out_shape=(
            shape((rows, width), bf16),
            shape((rows, width), f32),
            shape((small_rows, width), f32),
            shape((pieces + 6, 2, 4, quarter, width), bf16),
            shape((pieces, 2, 4, quarter, width), bf16),
            shape((rows, width), bf16),
            shape((tokens, width), bf16),
            shape((rows, width), bf16),
            shape((tokens, width), bf16),
            shape((width, 3 * width), bf16),
        ),
        in_specs=[hbm] * 8 + [vmem] * 4,
        out_specs=[vmem, vmem, vmem] + [hbm] * 7,
        scratch_shapes=[
            pltpu.VMEM((rows, width), bf16),
            pltpu.VMEM((rows, width), f32),
            pltpu.VMEM((tokens, width), bf16),
            pltpu.VMEM((rows, QUERY_HEADS), f32),
            pltpu.VMEM((rows, 128), f32),
            pltpu.VMEM((rows, 128), f32),
            pltpu.VMEM((1, tokens), jnp.int32),
            pltpu.VMEM((rows, 1), jnp.int32),
            pltpu.VMEM((EXPERTS, width), bf16),
            pltpu.VMEM((8, width), f32),
            pltpu.VMEM((2, SMALL_ROWS, own_rows), bf16),
            pltpu.VMEM((2, 8, rows), jnp.int32),
            dma((F_KINDS,)),
            dma((F_KINDS,)),
            *[dma((3,))] * 6,
            dma((4,)),
            pltpu.VMEM((tokens, width), f32),
            pltpu.VMEM((tokens, width), f32),
            pltpu.VMEM((tokens, EXPERTS), f32),
            pltpu.VMEM((2, EXPERTS, rows), f32),
            pltpu.VMEM((tokens, EXPERTS), f32),
            pltpu.VMEM((2, EXPERTS, rows), f32),
            pltpu.VMEM((2, rows, width), bf16),
            pltpu.VMEM((2, rows, width), bf16),
            pltpu.VMEM((rows, width), bf16),
            pltpu.VMEM((3, 2, 2, 4, quarter, width), bf16),
            pltpu.VMEM((3, 2, 4, quarter, width), bf16),
            pltpu.VMEM((6, small_rows, width), f32),
            pltpu.VMEM((6, small_rows, width), f32),
            pltpu.VMEM((2, 2, 2, 4, quarter, width), bf16),
            dma((2,)),
            dma((2, 2)),
            dma((5,)),
            dma((Y_KINDS,)),
            dma((Y_KINDS,)),
            dma((3,)),
            dma((3,)),
            dma((6,)),
            dma((6,)),
            *engine_scratch(quarter, width),
        ],
        compiler_params=pltpu.CompilerParams(
            collective_id=1, has_side_effects=True, vmem_limit_bytes=63 * MIB
        ),
        cost_estimate=cost(18 * tokens * width * half * owned, 6 * w_in.size),
        name="layer",
    )(
        x, wq, wk, wv, wo, grad, w_in, w_out, small,
        jnp.broadcast_to(document_numbers[None], (8, rows)), routes.T, inv_freq,
    )


def expert_pass(n2, grad, share, w_in, w_out):
    half = w_out.shape[0]
    gu = mm(n2, w_in)
    z, w = gu[:, :half], gu[:, half:]
    sg = jax.nn.sigmoid(z)
    act = (z * sg * w).astype(bf16)
    ye = mm(act, w_out).astype(bf16).astype(f32)
    d_gate = jnp.sum(grad * ye, axis=1)
    d_ye = (share * grad).astype(bf16)
    g_out = mm_tn(act, d_ye).astype(bf16)
    d_act = mm_nt(d_ye, w_out)
    d_gu = jnp.concatenate(
        [d_act * w * sg * (1.0 + z * (1.0 - sg)), d_act * z * sg], axis=1
    ).astype(bf16)
    g_in = mm_tn(n2, d_gu).astype(bf16)
    d_xe = mm_nt(d_gu, w_in).astype(bf16).astype(f32)
    return share * ye, d_gate, g_in, g_out, d_xe


def all_experts(n2, grad, share, w_in, w_out):
    moe = jnp.zeros(n2.shape, f32)
    d_n2 = jnp.zeros_like(moe)
    d_gate, g_in, g_out = [], [], []
    for i in range(w_in.shape[0]):
        y, dg, gi, go, dx = expert_pass(
            n2, grad.astype(f32), share[:, i : i + 1], w_in[i], w_out[i]
        )
        moe, d_n2 = moe + y, d_n2 + dx
        d_gate.append(dg)
        g_in.append(gi)
        g_out.append(go)
    g_in, g_out = lax.psum((jnp.stack(g_in), jnp.stack(g_out)), "replica")
    return moe, d_n2, jnp.stack(d_gate, 1), g_in.astype(f32), g_out.astype(f32)


def on_device(
    layer_input, document_numbers, routes, norm_attn, w_query, key_weight, value_weight, w_out,
    norm_moe, w_router, expert_in, expert_out, cotangent,
):
    rows, width = layer_input.shape
    group = lax.axis_index("group")
    first = group * rows
    owned = expert_in.shape[0]
    kv_width = KEY_VALUE_HEADS * HEAD_SIZE

    q_width = QUERY_HEADS * HEAD_SIZE
    if lax.axis_size("replica") == 16 and lax.axis_size("group") == 2:
        layer_output, grad_input, small_sum, sums, *_ = layer(
            layer_input, document_numbers, routes, (norm_attn, norm_moe), w_router, w_query,
            key_weight, value_weight, w_out, cotangent, expert_in, expert_out,
        )
        g_in, g_out, g_q, g_k, g_v, g_wo, g_router, g_gains = finish(
            sums.reshape(sums.shape[0], -1, width), small_sum, owned, kv_width
        )
        return (
            layer_output,
            grad_input,
            g_gains[1],
            g_q.reshape(w_query.shape),
            g_k.reshape(key_weight.shape),
            g_v.reshape(value_weight.shape),
            g_wo.reshape(w_out.shape),
            g_gains[0],
            g_router.T,
            g_in.reshape(expert_in.shape),
            g_out.reshape(expert_out.shape),
        )

    seg_all = gather(document_numbers)
    position = lax.dynamic_slice_in_dim(doc_positions(seg_all), first, rows, 0)
    cosine, sine = turn_tables(position)
    small = gather(jnp.concatenate([norm_attn[:, None], norm_moe[:, None], w_router], axis=1))
    gain_attn = small[:, 0].astype(f32)[None, :]
    gain_moe = small[:, 1].astype(f32)[None, :]
    router = small[:, 2:]
    w_qkv = gather(jnp.concatenate([w_query, key_weight, value_weight], axis=1))
    wo = gather(w_out)
    grad_all = gather(cotangent)

    n1, q, k, v = project(layer_input, gain_attn, w_qkv, cosine, sine)
    kv_all = gather(jnp.concatenate([k, v], axis=1))
    k_all, v_all = kv_all[:, :kv_width], kv_all[:, kv_width:]
    first_row = jnp.full((1,), first, jnp.int32)
    seg_q, seg_k = document_numbers[:, None], seg_all[None, :]
    ao = attend(first_row, q, k_all, v_all, seg_q, seg_k)

    x = layer_input.astype(f32)
    h = x + mm(ao, wo)
    r2 = rms_factor(h)
    n2 = (h * r2 * gain_moe).astype(bf16)
    logits = mm(n2, router)
    chosen = jnp.any(routes[:, :, None] == jnp.arange(EXPERTS, dtype=jnp.int32), axis=1)
    picked = jnp.where(chosen, logits, MASKED)
    e = jnp.where(chosen, jnp.exp(picked - jnp.max(picked, axis=1, keepdims=True)), 0.0)
    share = e / jnp.sum(e, axis=1, keepdims=True)

    n2_all = gather(n2)
    share_all = lax.dynamic_slice_in_dim(gather(share), group * owned, owned, 1)
    moe, d_n2_all, d_gate, g_in, g_out = all_experts(
        n2_all, grad_all, share_all, expert_in, expert_out
    )
    d_gate = lax.dynamic_update_slice_in_dim(
        jnp.zeros((n2_all.shape[0], EXPERTS), f32), d_gate, group * owned, 1
    )
    d_gate = lax.psum_scatter(d_gate, "group", scatter_dimension=0, tiled=True)
    layer_output = (h + owner_sum(moe).astype(f32)).astype(bf16)

    d_logits = (share * (d_gate - jnp.sum(share * d_gate, axis=1, keepdims=True))).astype(bf16)
    g_router = mm_tn(n2, d_logits)
    d_n2 = owner_sum(d_n2_all).astype(f32) + mm_nt(d_logits, router)
    g_gain_moe = jnp.sum(h * r2 * d_n2, axis=0)
    c = d_n2 * gain_moe
    d_h = cotangent.astype(f32) + r2 * (
        c - h * r2 * r2 * jnp.mean(c * h, axis=-1, keepdims=True)
    )
    d_y = d_h.astype(bf16)
    g_wo = mm_tn(ao, d_y).astype(bf16)
    d_o = mm_nt(d_y, wo).astype(bf16)

    dq, dk_all, dv_all = attend_grad(first_row, q, k_all, v_all, d_o, seg_q, seg_k)
    dkv = owner_sum(jnp.concatenate([dk_all, dv_all], axis=1))
    g_qkv, grad_input, g_gain_attn = project_grad(
        dq, dkv[:, :kv_width], dkv[:, kv_width:], n1, w_qkv, cosine, sine, layer_input,
        gain_attn, d_h,
    )

    g_attn = owner_sum(jnp.concatenate([g_qkv, g_wo], axis=1))
    g_small = owner_sum(
        jnp.concatenate([g_gain_attn.reshape(-1, 1), g_gain_moe[:, None], g_router], axis=1)
    )
    g_attn, g_small = (t.astype(f32) for t in lax.psum((g_attn, g_small), "replica"))
    return (
        layer_output,
        grad_input,
        g_small[:, 0],
        g_attn[:, :q_width],
        g_attn[:, q_width : q_width + kv_width],
        g_attn[:, q_width + kv_width : q_width + 2 * kv_width],
        g_attn[:, q_width + 2 * kv_width :],
        g_small[:, 1],
        g_small[:, 2:],
        g_in,
        g_out,
    )


def solution(mesh):
    tokens, weights = P(("replica", "group"), None), P("group", None)
    in_specs = (
        tokens, P(("replica", "group")), tokens, P("group"), weights, weights, weights, weights,
        P("group"), weights, P("group", None, None), P("group", None, None), tokens,
    )
    out_specs = (
        tokens, tokens, P("group"), weights, weights, weights, weights, P("group"), weights,
        P("group", None, None), P("group", None, None),
    )
    return jax.shard_map(
        on_device, mesh=mesh, in_specs=in_specs, out_specs=out_specs, check_vma=False
    )
```
